32 devices in a mesh: scene: 2 (over y), tok: 4 (over z), col: 2 (over x), rep: 2 (over core).
Axes of the slice: x: 2, y: 2, z: 4, core: 2. Of those that a mesh axis runs over, the one named last changes fastest.
Arguments:
- tokens: float32 [8192, 512], P(('scene', 'tok'), ('col', 'rep')), parts along dimension 0
- w_qkv: float32 [2, 3, 512, 512], P(None, None, None, ('col', 'rep'))
- w_out: float32 [2, 512, 512], P(None, ('col', 'rep')), may hold values from -0.25 to 0.25
- w_up: float32 [2, 512, 2048], P(None, None, ('col', 'rep')), may hold values from -0.25 to 0.25
- w_down: float32 [2, 2048, 512], P(None, ('col', 'rep')), may hold values from -0.125 to 0.125
- attn_gain: float32 [2, 512], replicated, may hold values from 0.1 to 1.9
- mlp_gain: float32 [2, 512], replicated, may hold values from 0.1 to 1.9
- dest_device: int32 [128], P(('scene', 'tok')), parts along dimension 0, may hold values from 0 to 3, as said below
- dest_slot: int32 [128], P(('scene', 'tok')), parts along dimension 0, may hold values from 0 to 15, as said below
- pillar: int32 [8192], P(('scene', 'tok')), parts along dimension 0, may hold values from -1 to 2047, as said below
- depth_weight: float32 [2, 3, 3, 512], replicated, may hold values from -2 to 2
- point_weight: float32 [2, 512, 1024], replicated, may hold values from -0.25 to 0.25
- raster_gain: float32 [2, 512], replicated, may hold values from 0.1 to 1.9
Outputs:
- raster: float32 [128, 32, 512], P(('scene', 'tok', 'rep'), 'col'), parts along dimension 0
The draws below stay inside these ranges and needn't reach their ends.
There are 2 independent parts, one for each index of `scene`. The reference program is written for one: setup_inputs(seed, part) draws one part's arguments, and reference() takes and returns one part's arrays. A program takes and returns all parts, laid end to end along the dimension named above; an argument that names none is the same for every part. Nothing has to cross between parts.
Inputs may be any that keep to these rules, and one draw needn't show every extreme that they name: `dest_device`: together with dest_slot the blocks fill every index of tok's 16 slots exactly once. At most 5 blocks of one index of tok go to one index, and every index sends exactly 5 blocks to some index. `dest_slot`: the slot of the block among the 16 of its destination. The token at Hilbert position t has a cell in raster rows i * 16 to (i + 1) * 16 - 1 with i = t // 1024, or -1 if it has no pillar; several tokens may share a cell.
All inputs are finite; a program needn't handle non-finite values.
Results may differ from the reference program's by a relative error of at most 0.00012.
Values sent between devices are 32-bit elements; how exact they have to be, the bound alone decides.
A program may use at most 128 MiB of HBM per device.

```python
import jax
import jax.numpy as jnp
from jax import lax

D = 512
HEADS = 32
FF = 2048
PATCH = 1024
BLOCK = 64
TR = 16
TC = 16
HD = 16
TOK_DEV = 1024
TOKENS = 4096
BLK_DEV = 16
NB = 64
H = 64
W = 32
N_TOK = 4
N_COL = 2


def draw_tokens(key, part):
    first_key = jax.random.fold_in(jax.random.fold_in(key, 3), 0)
    values = jax.random.normal(first_key, (TOKENS, D), jnp.float32)
    return values


def draw_w_qkv(key, part):
    first_key = jax.random.fold_in(jax.random.fold_in(key, 5), 0)
    base = jax.random.normal(first_key, (2, 3, D, D), jnp.float32) * D ** (-0.5)
    return base


def route_tables(key):
    first_key, second_key, third_key, fourth_key = jax.random.split(jax.random.fold_in(key, 29), 4)
    owners = jax.random.permutation(first_key, N_TOK).astype(jnp.int32)
    spread = jax.random.permutation(second_key, BLK_DEV - 2).astype(jnp.int32)
    shifts = jnp.concatenate([jnp.zeros((2,), jnp.int32), 1 + spread % (N_TOK - 1)])

    def permute_single_block(subkey):
        return jax.random.permutation(subkey, BLK_DEV).astype(jnp.int32)
    order = jax.vmap(permute_single_block)(jax.random.split(third_key, N_TOK))
    arrival = jax.vmap(permute_single_block)(jax.random.split(fourth_key, N_TOK))
    source = jnp.arange(N_TOK, dtype=jnp.int32)[:, None]
    target = owners[(source + shifts[order]) % N_TOK]
    slots = arrival[target, order]
    return (target.reshape(-1).astype(jnp.int32), slots.reshape(-1).astype(jnp.int32))


def draw_dest_device(key, part):
    return route_tables(key)[0]


def draw_dest_slot(key, part):
    return route_tables(key)[1]


def draw_pillar(key, part):
    first_key, second_key, third_key = jax.random.split(jax.random.fold_in(key, 41), 3)
    full_width = TC * N_COL
    band = jnp.arange(TOKENS, dtype=jnp.int32) // TOK_DEV
    row_in = jax.random.randint(first_key, (TOKENS,), 0, TR, jnp.int32)
    col_in = jax.random.randint(second_key, (TOKENS,), 0, full_width, jnp.int32)
    present = jax.random.randint(third_key, (TOKENS,), 0, 8, jnp.int32) < 7
    return jnp.where(present, (band * TR + row_in) * full_width + col_in, -1).astype(jnp.int32)


def shard_levels(own_key, dims, pieces, low, high):
    gain = 1.0
    for axis_at, shards_of in pieces:
        draws = jax.random.uniform(jax.random.fold_in(jax.random.fold_in(own_key, 6), axis_at), (shards_of,), jnp.float32, low / len(pieces), high / len(pieces))
        gain = gain * jnp.repeat(jnp.exp(draws), dims[axis_at] // shards_of).reshape((-1,) + (1,) * (len(dims) - 1 - axis_at))
    return gain


def centred(rng, dims, deviation, limit, cuts=(), kind=jnp.bfloat16):
    gain = shard_levels(rng, dims, cuts, -0.22, 0.18) if cuts else 1.0
    array = jax.random.normal(rng, dims, jnp.float32) * deviation * gain
    return jnp.minimum(jnp.maximum(array, -limit), limit).astype(kind)


def setup_inputs(seed: int = 0, part: int = 0) -> dict:
    seeds = jax.random.split(jax.random.key(seed), 14)
    part_keys = jax.random.split(jax.random.fold_in(seeds[13], part), 14)
    tokens = draw_tokens(jax.random.fold_in(jax.random.fold_in(seeds[13], part), 71), part)
    w_qkv = draw_w_qkv(jax.random.fold_in(seeds[13], 71), part)
    w_out = centred(seeds[2], (2, D, D), D ** -0.5, 0.25, ((1, 4),), jnp.float32)
    w_up = centred(seeds[3], (2, D, FF), D ** -0.5, 0.25, ((2, 4),), jnp.float32)
    w_down = centred(seeds[4], (2, FF, D), FF ** -0.5, 0.125, ((1, 4),), jnp.float32)
    attn_gain = jnp.clip(1.0 + 0.18 * jax.random.normal(seeds[5], (2, D), jnp.float32), 0.1, 1.9)
    mlp_gain = jnp.clip(1.0 + 0.18 * jax.random.normal(seeds[6], (2, D), jnp.float32), 0.1, 1.9)
    dest_device = draw_dest_device(jax.random.fold_in(jax.random.fold_in(seeds[13], part), 71), part)
    dest_slot = draw_dest_slot(jax.random.fold_in(jax.random.fold_in(seeds[13], part), 71), part)
    pillar = draw_pillar(jax.random.fold_in(jax.random.fold_in(seeds[13], part), 71), part)
    depth_weight = centred(seeds[10], (2, 3, 3, D), 0.35, 2.0, (), jnp.float32)
    point_weight = centred(seeds[11], (2, D, 2 * D), D ** -0.5, 0.25, (), jnp.float32)
    raster_gain = jnp.clip(1.0 + 0.18 * jax.random.normal(seeds[12], (2, D), jnp.float32), 0.1, 1.9)
    return dict(tokens=tokens, w_qkv=w_qkv, w_out=w_out, w_up=w_up, w_down=w_down, attn_gain=attn_gain, mlp_gain=mlp_gain, dest_device=dest_device, dest_slot=dest_slot, pillar=pillar, depth_weight=depth_weight, point_weight=point_weight, raster_gain=raster_gain)


MATMUL_PRECISION = lax.Precision.HIGHEST
EPSILON = 1e-05

def layer_norm(values, gain_row):
    average = lax.optimization_barrier(jnp.mean(values, axis=-1, keepdims=True))
    centered = values - average
    variance = lax.optimization_barrier(jnp.mean(centered * centered, axis=-1, keepdims=True))
    return centered * lax.rsqrt(variance + EPSILON) * gain_row

def patch_attention(query_projection, key_proj, value_proj):
    scores = jnp.einsum('qhd,khd->hqk', query_projection, key_proj, precision=MATMUL_PRECISION) * HD ** (-0.5)
    scores = scores - lax.optimization_barrier(jnp.max(scores, axis=-1, keepdims=True))
    weights = jnp.exp(scores)
    weights = weights / lax.optimization_barrier(jnp.sum(weights, axis=-1, keepdims=True))
    return jnp.einsum('hqk,khd->qhd', weights, value_proj, precision=MATMUL_PRECISION)

def matmul(left, right):
    return jnp.dot(left, right, precision=MATMUL_PRECISION, preferred_element_type=jnp.float32)

def block_layer(stream, w_qkv, w_out, w_up, w_down, attn_gain, mlp_gain):
    row_count = stream.shape[0]
    normed = layer_norm(stream, attn_gain)
    shaped = tuple((matmul(normed, w_qkv[j]).reshape(row_count // PATCH, PATCH, HEADS, HD) for j in range(3)))

    def attend_patch(operands):
        return patch_attention(operands[0], operands[1], operands[2]).reshape(PATCH, D)
    attended = lax.map(attend_patch, shaped).reshape(row_count, D)
    stream = stream + matmul(attended, w_out)
    normed = layer_norm(stream, mlp_gain)
    hidden = jax.nn.gelu(matmul(normed, w_up), approximate=False)
    return stream + matmul(hidden, w_down)

def raster_layer(raster_grid, depth_weight, point_weight, gain_row):
    row_count, col_count, count_of_channels = raster_grid.shape
    normed = raster_grid * lax.rsqrt(lax.optimization_barrier(jnp.mean(raster_grid * raster_grid, axis=-1, keepdims=True)) + EPSILON) * gain_row
    padded = jnp.pad(normed, ((1, 1), (1, 1), (0, 0)))
    mixed_cells = jnp.zeros_like(raster_grid)
    for row_tap in range(3):
        for col_tap in range(3):
            mixed_cells = mixed_cells + padded[row_tap:row_tap + row_count, col_tap:col_tap + col_count] * depth_weight[row_tap, col_tap]
    combined = matmul(mixed_cells.reshape(row_count * col_count, count_of_channels), point_weight)
    combined = combined.reshape(row_count, col_count, 2 * count_of_channels)
    return raster_grid + combined[..., :count_of_channels] * jax.nn.sigmoid(combined[..., count_of_channels:])

def reference(tokens, w_qkv, w_out, w_up, w_down, attn_gain, mlp_gain, dest_device, dest_slot, pillar, depth_weight, point_weight, raster_gain):
    stream = block_layer(tokens, w_qkv[0], w_out[0], w_up[0], w_down[0], attn_gain[0], mlp_gain[0])
    block_list = stream.reshape(NB, BLOCK, D)
    position = (dest_device * BLK_DEV + dest_slot).astype(jnp.int32)
    reordered_tokens = jnp.zeros_like(block_list).at[position].set(block_list).reshape(TOKENS, D)
    stream = block_layer(reordered_tokens, w_qkv[1], w_out[1], w_up[1], w_down[1], attn_gain[1], mlp_gain[1])
    cell_ids = jnp.where(pillar < 0, H * W, pillar).astype(jnp.int32)
    pooled = jax.ops.segment_sum(stream, cell_ids, num_segments=H * W + 1)[:H * W]
    raster_grid = pooled.reshape(H, W, D)
    for layer_index in range(2):
        raster_grid = raster_layer(raster_grid, depth_weight[layer_index], point_weight[layer_index], raster_gain[layer_index])
    return raster_grid
```

```python
import functools
import math

import jax
import jax.numpy as jnp
from jax import lax
from jax.experimental import pallas as pl
from jax.experimental.pallas import tpu as pltpu
from jax.sharding import PartitionSpec as P

PATCH = 1024
TR = 16
TC = 16
HD = 16


MATMUL_PRECISION = lax.Precision.HIGH
EPSILON = 1e-05


def layer_norm(values, gain_row):
    average = jnp.mean(values, axis=-1, keepdims=True)
    centered = values - average
    variance = jnp.mean(centered * centered, axis=-1, keepdims=True)
    return centered * lax.rsqrt(variance + EPSILON) * gain_row


def split(values):
    high = values.astype(jnp.bfloat16)
    return high, (values - high.astype(jnp.float32)).astype(jnp.bfloat16)


def bdot(left, right, dims=(((1,), (0,)), ((), ()))):
    return lax.dot_general(left, right, dims, preferred_element_type=jnp.float32)


def dot3(left, right):
    lh, ll = left
    rh, rl = right
    return bdot(lh, rh) + bdot(lh, rl) + bdot(ll, rh)


def attention_kernel(share, source_ref, x_ref, gain_ref, w_ref, o_ref, out_ref, q_s, k_s, v_s, att_s):
    cols = w_ref.shape[-1]
    heads = cols // HD
    rows = out_ref.shape[0]
    chunk = att_s.shape[0]
    slots, each, block = x_ref.shape[1:4]
    first_block = pl.program_id(0) * (rows // block)

    def stream_rows(i):
        parts = []
        for n in range(chunk // block):
            at = source_ref[first_block + i * (chunk // block) + n]
            places = [x_ref[at // each, j, at % each] for j in range(slots)]
            parts.append(jnp.concatenate(places, axis=-1))
        return jnp.concatenate(parts, axis=0)

    lanes = q_s.shape[-1]

    r = lax.broadcasted_iota(jnp.int32, (cols, lanes), 0)
    c = lax.broadcasted_iota(jnp.int32, (cols, lanes), 1)
    lane = lax.broadcasted_iota(jnp.int32, (1, cols), 1)
    w = [split(w_ref[j]) for j in range(3)]
    for i in range(rows // chunk):
        at = pl.ds(i * chunk, chunk)
        normed = split(layer_norm(stream_rows(i), gain_ref[...]))
        qh, ql = split(dot3(normed, w[0]) * (HD ** (-0.5) * math.log2(math.e)))
        kh, kl = split(dot3(normed, w[1]))
        vh, vl = split(dot3(normed, w[2]))
        for h in range(heads):
            part = c // HD
            inside = (r // HD == h) & (r % HD == c % HD)
            first = (inside & ((part == 0) | (part == 1))).astype(jnp.bfloat16)
            third = (inside & (part == 2)).astype(jnp.bfloat16)
            outer = (inside & ((part == 0) | (part == 2))).astype(jnp.bfloat16)
            middle = (inside & (part == 1)).astype(jnp.bfloat16)
            q_s[h, at, :] = (bdot(qh, first) + bdot(ql, third)).astype(jnp.bfloat16)
            k_s[h, at, :] = (bdot(kh, outer) + bdot(kl, middle)).astype(jnp.bfloat16)
            own = lane // HD == h
            v_s[h, at, :cols] = jnp.where(own, vh.astype(jnp.float32), 0.0).astype(jnp.bfloat16)
            v_s[h, at, cols:] = jnp.where(own, vl.astype(jnp.float32), 1.0).astype(jnp.bfloat16)

    projection = split(o_ref[...])

    def query_rows(i, carry):
        at = pl.ds(pl.multiple_of(i * chunk, chunk), chunk)
        att_s[...] = jnp.zeros_like(att_s)

        def one_head(h, carry):
            scores = bdot(q_s[h, at, :], k_s[h], (((1,), (1,)), ((), ())))
            weights = jnp.exp2(scores - jnp.max(scores, axis=-1, keepdims=True))
            wh, wl = split(weights)
            sums = bdot(wh, v_s[h]) + bdot(wl, v_s[h])
            top, low = sums[:, :cols], sums[:, cols:]
            own = lane // HD == h
            total = jnp.max(jnp.where(own, 0.0, low), axis=-1, keepdims=True)
            att_s[...] += jnp.where(own, (top + low) / total, 0.0)
            return carry

        lax.fori_loop(0, heads, one_head, 0, unroll=4)
        out_ref[at, :] = dot3(split(att_s[...]), projection) + stream_rows(i) * share
        return carry

    lax.fori_loop(0, rows // chunk, query_rows, 0)


def attend(blocks, source, gain_row, weights, w_out, group):
    block, width = blocks.shape[3], blocks.shape[1] * blocks.shape[4]
    rows = source.shape[0] * block
    cols = weights.shape[-1]
    heads = cols // HD
    lanes = max(128, 3 * HD)
    return pl.pallas_call(
        functools.partial(attention_kernel, 1.0 / group),
        grid_spec=pltpu.PrefetchScalarGridSpec(
            num_scalar_prefetch=1,
            grid=(rows // PATCH,),
            in_specs=[
                pl.BlockSpec(blocks.shape, lambda i, source: (0, 0, 0, 0, 0)),
                pl.BlockSpec((1, width), lambda i, source: (0, 0)),
                pl.BlockSpec(weights.shape, lambda i, source: (0, 0, 0)),
                pl.BlockSpec(w_out.shape, lambda i, source: (0, 0)),
            ],
            out_specs=pl.BlockSpec((PATCH, width), lambda i, source: (i, 0)),
            scratch_shapes=[
                pltpu.VMEM((heads, PATCH, lanes), jnp.bfloat16),
                pltpu.VMEM((heads, PATCH, lanes), jnp.bfloat16),
                pltpu.VMEM((heads, PATCH, 2 * cols), jnp.bfloat16),
                pltpu.VMEM((256, cols), jnp.float32),
            ],
        ),
        out_shape=jax.ShapeDtypeStruct((rows, width), jnp.float32),
        compiler_params=pltpu.CompilerParams(vmem_limit_bytes=48 * 1024 * 1024),
        name="attend",
    )(source, blocks, gain_row[None, :], weights, w_out)


def matmul(left, right):
    return jnp.dot(left, right, precision=MATMUL_PRECISION, preferred_element_type=jnp.float32)


VMEM_LIMIT = 56 * 1024 * 1024
MESH = pl.DeviceIdType.MESH


def position():
    cols, reps = lax.axis_size("col"), lax.axis_size("rep")
    return cols, reps, lax.axis_index("col"), lax.axis_index("rep")


def greet(devices):
    barrier = pltpu.get_barrier_semaphore()
    for device in devices:
        pl.semaphore_signal(barrier, inc=1, device_id=device, device_id_type=MESH)
    pl.semaphore_wait(barrier, len(devices))


def remote(src, dst, send, recv, device):
    return pltpu.make_async_remote_copy(
        src_ref=src, dst_ref=dst, send_sem=send, recv_sem=recv, device_id=device, device_id_type=MESH
    )


def chunks_of(rows):
    for pieces in (8, 5, 4, 2):
        if rows % (8 * pieces) == 0:
            return pieces, rows // pieces
    return 1, rows


def gather_kernel(x_ref, out_ref, xs, xr, fs, fr, ps, pr, local):
    cols, reps, c, r = position()
    rows = x_ref.shape[0]
    pieces, size = chunks_of(rows)
    me = c * reps + r
    mate = {"col": c, "rep": 1 - r}
    others = [{"col": lax.rem(c + d, cols), "rep": r} for d in range(1, cols)]
    greet([mate] + others)
    across, onward = [], []
    for k in range(pieces):
        at = pl.ds(k * size, size)
        for d in range(1, cols):
            copy = remote(
                x_ref.at[at], out_ref.at[me, at], xs.at[d - 1, k], xr.at[d - 1, k], others[d - 1]
            )
            copy.start()
            across.append(copy)
    share = remote(x_ref, out_ref.at[me], ps, pr, mate)
    share.start()
    keep = pltpu.make_async_copy(x_ref, out_ref.at[me], local)
    keep.start()
    for k in range(pieces):
        at = pl.ds(k * size, size)
        for d in range(1, cols):
            across[k * (cols - 1) + d - 1].wait_recv()
            slot = lax.rem(c + cols - d, cols) * reps + r
            copy = remote(
                out_ref.at[slot, at], out_ref.at[slot, at], fs.at[d - 1, k], fr.at[d - 1, k], mate
            )
            copy.start()
            onward.append(copy)
    for copy in across:
        copy.wait_send()
    share.wait()
    keep.wait()
    for copy in onward:
        copy.wait()


def gather(block, collective_id):
    cols, reps = lax.axis_size("col"), lax.axis_size("rep")
    if reps != 2 or cols < 2:
        return lax.all_gather(block, ("col", "rep"), axis=0)
    pieces, _ = chunks_of(block.shape[0])
    dma = pltpu.SemaphoreType.DMA
    return pl.pallas_call(
        gather_kernel,
        out_shape=jax.ShapeDtypeStruct((cols * reps,) + block.shape, block.dtype),
        in_specs=[pl.BlockSpec(memory_space=pltpu.VMEM)],
        out_specs=pl.BlockSpec(memory_space=pltpu.VMEM),
        scratch_shapes=[dma((cols - 1, pieces))] * 4 + [dma, dma, dma],
        compiler_params=pltpu.CompilerParams(
            collective_id=collective_id, has_side_effects=True, vmem_limit_bytes=VMEM_LIMIT
        ),
        name="gather",
    )(block)


def scatter_kernel(edge, p_ref, out_ref, a_ref, s_ref, b_ref, a_s, a_r, b_s, b_r, *halo):
    cols, reps, c, r = position()
    rows = p_ref.shape[1]
    pieces, size = chunks_of(rows)
    mate = {"col": c, "rep": 1 - r}
    others = [{"col": lax.rem(c + d, cols), "rep": r} for d in range(1, cols)]
    greeted = [mate] + others
    if edge:
        ntok, t = lax.axis_size("tok"), lax.axis_index("tok")
        partner = {"tok": lax.rem(t + jnp.where(r == 0, ntok - 1, 1), ntok), "rep": 1 - r}
        greeted = greeted + [partner]
    greet(greeted)
    order = [(k, d) for k in range(pieces) for d in range(1, cols)]
    order += [(k, 0) for k in range(pieces)]
    near, far = {}, {}
    for k, d in order:
        at = pl.ds(k * size, size)
        slot = lax.rem(c + d, cols) * reps + 1 - r
        near[k, d] = remote(
            p_ref.at[slot, at], a_ref.at[d, at], a_s.at[d, k], a_r.at[d, k], mate
        )
        near[k, d].start()
    for k, d in order:
        at = pl.ds(k * size, size)
        slot = lax.rem(c + d, cols) * reps + r
        near[k, d].wait_recv()
        total = p_ref[slot, at] + a_ref[d, at]
        if d == 0:
            out_ref[at] = total
        else:
            s_ref[d - 1, at] = total
            far[k, d] = remote(
                s_ref.at[d - 1, at],
                b_ref.at[d - 1, at],
                b_s.at[d - 1, k],
                b_r.at[d - 1, k],
                others[d - 1],
            )
            far[k, d].start()
    for (k, d), copy in far.items():
        at = pl.ds(k * size, size)
        copy.wait_recv()
        out_ref[at] += b_ref[d - 1, at]
    if edge:
        h_ref, e_ref, h_s, h_r = halo
        inner = pl.multiple_of(jnp.where(r == 0, edge, rows - 2 * edge), 8)
        outer = pl.multiple_of(jnp.where(r == 0, 0, rows - edge), 8)
        e_ref[...] = out_ref[pl.ds(inner, edge)]
        copy = remote(e_ref, h_ref, h_s, h_r, partner)
        copy.start()
        copy.wait()
        wrapped = jnp.where(r == 0, t == 0, t == ntok - 1)
        out_ref[pl.ds(outer, edge)] = jnp.where(wrapped, 0.0, h_ref[...])
    for copy in list(near.values()) + list(far.values()):
        copy.wait_send()


def scatter(parts, collective_id, edge=0):
    cols, reps = lax.axis_size("col"), lax.axis_size("rep")
    if reps != 2 or cols < 2:
        return lax.psum_scatter(parts, ("col", "rep"), scatter_dimension=0)
    shape, kind = parts.shape[1:], parts.dtype
    pieces, _ = chunks_of(shape[0])
    dma = pltpu.SemaphoreType.DMA
    return pl.pallas_call(
        functools.partial(scatter_kernel, edge),
        out_shape=jax.ShapeDtypeStruct(shape, kind),
        in_specs=[pl.BlockSpec(memory_space=pltpu.VMEM)],
        out_specs=pl.BlockSpec(memory_space=pltpu.VMEM),
        scratch_shapes=[
            pltpu.VMEM((cols,) + shape, kind),
            pltpu.VMEM((cols - 1,) + shape, kind),
            pltpu.VMEM((cols - 1,) + shape, kind),
            dma((cols, pieces)),
            dma((cols, pieces)),
            dma((cols - 1, pieces)),
            dma((cols - 1, pieces)),
        ]
        + ([pltpu.VMEM((edge, shape[1]), kind)] * 2 + [dma, dma] if edge else []),
        compiler_params=pltpu.CompilerParams(
            collective_id=collective_id, has_side_effects=True, vmem_limit_bytes=VMEM_LIMIT
        ),
        name="scatter",
    )(parts)


def total_kernel(
    p_ref, out_ref, a_ref, s_ref, b_ref, a_s, a_r, b_s, b_r, xs, xr, fs, fr, ps, pr
):
    cols, reps, c, r = position()
    rows = p_ref.shape[1]
    pieces, size = chunks_of(rows)
    me = c * reps + r
    mate = {"col": c, "rep": 1 - r}
    others = [{"col": lax.rem(c + d, cols), "rep": r} for d in range(1, cols)]
    greet([mate] + others)
    order = [(k, d) for k in range(pieces) for d in range(1, cols)]
    order += [(k, 0) for k in range(pieces)]
    near, far, across, share, onward = {}, {}, {}, {}, {}
    for k, d in order:
        at = pl.ds(k * size, size)
        slot = lax.rem(c + d, cols) * reps + 1 - r
        near[k, d] = remote(
            p_ref.at[slot, at], a_ref.at[d, at], a_s.at[d, k], a_r.at[d, k], mate
        )
        near[k, d].start()
    for k, d in order:
        if d == 0:
            continue
        at = pl.ds(k * size, size)
        slot = lax.rem(c + d, cols) * reps + r
        near[k, d].wait_recv()
        s_ref[d - 1, at] = p_ref[slot, at] + a_ref[d, at]
        far[k, d] = remote(
            s_ref.at[d - 1, at], b_ref.at[d - 1, at], b_s.at[d - 1, k], b_r.at[d - 1, k], others[d - 1]
        )
        far[k, d].start()
    for k in range(pieces):
        at = pl.ds(k * size, size)
        near[k, 0].wait_recv()
        total = p_ref[me, at] + a_ref[0, at]
        for d in range(1, cols):
            far[k, d].wait_recv()
            total = total + b_ref[d - 1, at]
        out_ref[me, at] = total
        for d in range(1, cols):
            across[k, d] = remote(
                out_ref.at[me, at], out_ref.at[me, at], xs.at[d - 1, k], xr.at[d - 1, k], others[d - 1]
            )
            across[k, d].start()
        share[k] = remote(out_ref.at[me, at], out_ref.at[me, at], ps.at[k], pr.at[k], mate)
        share[k].start()
    for (k, d), copy in across.items():
        at = pl.ds(k * size, size)
        copy.wait_recv()
        slot = lax.rem(c + cols - d, cols) * reps + r
        onward[k, d] = remote(
            out_ref.at[slot, at], out_ref.at[slot, at], fs.at[d - 1, k], fr.at[d - 1, k], mate
        )
        onward[k, d].start()
    for copies in (near, far, across):
        for copy in copies.values():
            copy.wait_send()
    for copies in (share, onward):
        for copy in copies.values():
            copy.wait()


def total(parts, collective_id):
    cols, reps = lax.axis_size("col"), lax.axis_size("rep")
    if reps != 2 or cols < 2:
        return lax.psum(parts, ("col", "rep"))
    shape, kind = parts.shape[1:], parts.dtype
    pieces, _ = chunks_of(shape[0])
    dma = pltpu.SemaphoreType.DMA
    return pl.pallas_call(
        total_kernel,
        out_shape=jax.ShapeDtypeStruct(parts.shape, kind),
        in_specs=[pl.BlockSpec(memory_space=pltpu.VMEM)],
        out_specs=pl.BlockSpec(memory_space=pltpu.VMEM),
        scratch_shapes=[
            pltpu.VMEM((cols,) + shape, kind),
            pltpu.VMEM((cols - 1,) + shape, kind),
            pltpu.VMEM((cols - 1,) + shape, kind),
            dma((cols, pieces)),
            dma((cols, pieces)),
        ]
        + [dma((cols - 1, pieces))] * 6
        + [dma((pieces,))] * 2,
        compiler_params=pltpu.CompilerParams(
            collective_id=collective_id, has_side_effects=True, vmem_limit_bytes=VMEM_LIMIT
        ),
        name="total",
    )(parts)


def move_kernel(o_ref, code_ref, out_ref, arrived_ref, zs, zr, cs, cr, xs, xr, fs, fr, ps, pr, local):
    cols, reps, c, r = position()
    ntok, t = lax.axis_size("tok"), lax.axis_index("tok")
    me = c * reps + r
    mate = {"col": c, "rep": 1 - r}
    others = [{"col": lax.rem(c + d, cols), "rep": r} for d in range(1, cols)]
    peers = [{"tok": lax.rem(t + e, ntok)} for e in range(1, ntok)]
    greet([mate] + others + peers)
    along, codes, across, share, onward = [], [], {}, [], []
    for e in range(1, ntok):
        target = lax.rem(t + e, ntok)
        copy = remote(o_ref.at[target], out_ref.at[t, me], zs.at[e - 1], zr.at[e - 1], peers[e - 1])
        copy.start()
        along.append(copy)
        copy = remote(
            code_ref.at[target], arrived_ref.at[t], cs.at[e - 1], cr.at[e - 1], peers[e - 1]
        )
        copy.start()
        codes.append(copy)
    keep = pltpu.make_async_copy(o_ref.at[t], out_ref.at[t, me], local.at[0])
    keep.start()
    keep_code = pltpu.make_async_copy(code_ref.at[t], arrived_ref.at[t], local.at[1])
    keep_code.start()

    def hand_on(e):
        u = lax.rem(t + ntok - e, ntok)
        for d in range(1, cols):
            across[e, d].wait_recv()
            slot = lax.rem(c + cols - d, cols) * reps + r
            copy = remote(
                out_ref.at[u, slot], out_ref.at[u, slot], fs.at[e, d - 1], fr.at[e, d - 1], mate
            )
            copy.start()
            onward.append(copy)

    for e in range(ntok):
        u = lax.rem(t + ntok - e, ntok)
        if e:
            along[e - 1].wait_recv()
        origin = out_ref.at[u, me] if e else o_ref.at[t]
        for d in range(1, cols):
            across[e, d] = remote(
                origin, out_ref.at[u, me], xs.at[e, d - 1], xr.at[e, d - 1], others[d - 1]
            )
            across[e, d].start()
        copy = remote(origin, out_ref.at[u, me], ps.at[e], pr.at[e], mate)
        copy.start()
        share.append(copy)
        if e:
            hand_on(e - 1)
    hand_on(ntok - 1)
    keep.wait()
    keep_code.wait()
    for copy in along + list(across.values()):
        copy.wait_send()
    for copy in codes + share + onward:
        copy.wait()


def move(outgoing, codes, collective_id):
    cols, reps, ntok = lax.axis_size("col"), lax.axis_size("rep"), lax.axis_size("tok")
    if reps != 2 or cols < 2 or ntok < 2:
        incoming = lax.all_to_all(outgoing, "tok", split_axis=0, concat_axis=0, tiled=True)
        arrived = lax.all_to_all(codes, "tok", split_axis=0, concat_axis=0, tiled=True)
        return lax.all_gather(incoming, ("col", "rep"), axis=1), arrived
    dma = pltpu.SemaphoreType.DMA
    shape = (ntok, cols * reps) + outgoing.shape[1:]
    return pl.pallas_call(
        move_kernel,
        out_shape=(
            jax.ShapeDtypeStruct(shape, outgoing.dtype),
            jax.ShapeDtypeStruct(codes.shape, codes.dtype),
        ),
        in_specs=[pl.BlockSpec(memory_space=pltpu.VMEM)] * 2,
        out_specs=[pl.BlockSpec(memory_space=pltpu.VMEM)] * 2,
        scratch_shapes=[dma((ntok - 1,))] * 4
        + [dma((ntok, cols - 1))] * 4
        + [dma((ntok,))] * 2
        + [dma((2,))],
        compiler_params=pltpu.CompilerParams(
            collective_id=collective_id, has_side_effects=True, vmem_limit_bytes=VMEM_LIMIT
        ),
        name="move",
    )(outgoing, codes)


def pick_kernel(index_ref, x_ref, out_ref):
    for j in range(out_ref.shape[0]):
        out_ref[j] = x_ref[index_ref[j]]


def pick(blocks, index):
    return pl.pallas_call(
        pick_kernel,
        out_shape=jax.ShapeDtypeStruct(index.shape + blocks.shape[1:], blocks.dtype),
        in_specs=[pl.BlockSpec(memory_space=pltpu.SMEM), pl.BlockSpec(memory_space=pltpu.VMEM)],
        out_specs=pl.BlockSpec(memory_space=pltpu.VMEM),
        name="pick",
    )(index, blocks)


def attention_layer(blocks, source, layer, w_qkv, w_out, attn_gain, collective_id):
    group = blocks.shape[1]
    terms = attend(blocks, source, attn_gain[layer], w_qkv[layer], w_out[layer], group)
    rows, width = terms.shape
    return total(terms.reshape(group, rows // group, width), collective_id).reshape(rows, width)


def mlp_kernel(x_ref, gain_ref, up_ref, down_ref, share, out_ref):
    x = x_ref[...]
    hidden = dot3(split(layer_norm(x, gain_ref[...])), split(up_ref[...]))
    hidden = 0.5 * hidden * (1.0 + lax.erf(hidden * (0.5**0.5)))
    total = dot3(split(hidden), split(down_ref[...])) + x * share
    width = out_ref.shape[-1]
    for j in range(out_ref.shape[0]):
        out_ref[j] = total[:, j * width : (j + 1) * width]


def mlp_partial(stream, layer, w_up, w_down, mlp_gain, slots):
    rows, width = stream.shape
    tile = min(256, rows)
    hidden = w_up.shape[-1]
    group = lax.axis_size("col") * lax.axis_size("rep")

    def kernel(x_ref, gain_ref, up_ref, down_ref, out_ref):
        mlp_kernel(x_ref, gain_ref, up_ref, down_ref, 1.0 / group, out_ref)

    return pl.pallas_call(
        kernel,
        grid=(rows // tile,),
        in_specs=[
            pl.BlockSpec((tile, width), lambda i: (i, 0)),
            pl.BlockSpec((1, width), lambda i: (0, 0)),
            pl.BlockSpec((width, hidden), lambda i: (0, 0)),
            pl.BlockSpec((hidden, width), lambda i: (0, 0)),
        ],
        out_specs=pl.BlockSpec((slots, tile, width // slots), lambda i: (0, i, 0)),
        out_shape=jax.ShapeDtypeStruct((slots, rows, width // slots), jnp.float32),
        compiler_params=pltpu.CompilerParams(vmem_limit_bytes=48 * 1024 * 1024),
        name="mlp",
    )(stream, mlp_gain[layer][None, :], w_up[layer], w_down[layer])


def gelu(values):
    return 0.5 * values * (1.0 + lax.erf(values * (0.5**0.5)))


NEAR, FAR, SHARE, NEAR2, FAR2, ACROSS, OVER, RELAY = range(8)


def layer_kernel(layer, first, heads, chunk, *refs):
    refs = list(refs)
    source_ref = None if first else refs.pop(0)
    x_ref, ga_ref, gm_ref, wqkv_hbm, wo_hbm, wu_hbm, wd_hbm, out_ref = refs[:8]
    (
        wqkv_f, wo_f, wu_f, wd_f, wqkv_s, wo_s, wu_s, wd_s,
        q_s, k_s, v_s, att_s, p_s, n1_s, s1_s, f1_s, a_s, sem, wsem,
    ) = refs[8:27]
    rest = refs[27:]
    cols, reps, c, r = position()
    me = c * reps + r
    mate, peer = {"rep": 1 - r}, {"col": 1 - c}
    lanes = q_s.shape[-1] // 2
    width = a_s.shape[-1]
    rows = a_s.shape[0]
    n = rows // chunk
    half_rows = chunk // 2
    half_lanes = lanes // 2
    half_heads = heads // 2

    def piece(i, size):
        return pl.ds(pl.multiple_of(i * size, size), size)

    def sent(kind, i, src, dst, device):
        return remote(src, dst, sem.at[kind, 0, i], sem.at[kind, 1, i], device)

    loads = [
        pltpu.make_async_copy(src.at[layer], dst, wsem.at[j])
        for j, (src, dst) in enumerate(
            ((wqkv_hbm, wqkv_f), (wo_hbm, wo_f), (wu_hbm, wu_f), (wd_hbm, wd_f))
        )
    ]
    for load in loads:
        load.start()
    greet([mate, peer])

    if first:
        g_s, m_s, n2_s, s2_s, f2_s = rest

        def across(i):
            at = piece(i, chunk)
            return sent(ACROSS, i, x_ref.at[at], g_s.at[me, at], peer)

        def over(i):
            at = piece(i, chunk)
            return sent(OVER, i, x_ref.at[at], g_s.at[me, at], mate)

        def relay(i):
            at = piece(i, chunk)
            slot = (1 - c) * reps + r
            return sent(RELAY, i, g_s.at[slot, at], g_s.at[slot, at], mate)

        for i in range(n):
            across(i).start()
        for i in range(n):
            over(i).start()
        g_s[me] = x_ref[...]

        def stream_rows(start, count):
            at = pl.ds(pl.multiple_of(start, count), count)
            return jnp.concatenate([g_s[j, at] for j in range(cols * reps)], axis=-1)

    else:
        each, block = x_ref.shape[2:4]

        def stream_rows(start, count):
            parts = []
            for m in range(count // block):
                at = source_ref[start // block + m]
                places = [x_ref[at // each, j, at % each] for j in range(cols * reps)]
                parts.append(jnp.concatenate(places, axis=-1))
            return jnp.concatenate(parts, axis=0)

    for j, (load, src, dst) in enumerate(
        zip(loads, (wqkv_f, wo_f, wu_f, wd_f), (wqkv_s, wo_s, wu_s, wd_s))
    ):
        load.wait()
        if j == 0:
            for m in range(3):
                dst[0, m], dst[1, m] = split(src[m])
        else:
            dst[0], dst[1] = split(src[...])

    lane = lax.broadcasted_iota(jnp.int32, (1, lanes), 1)

    def project(i):
        at = piece(i, chunk)
        normed = split(layer_norm(stream_rows(i * chunk, chunk), ga_ref[...]))
        q = dot3(normed, (wqkv_s[0, 0], wqkv_s[1, 0])) * (HD ** (-0.5) * math.log2(math.e))
        k = dot3(normed, (wqkv_s[0, 1], wqkv_s[1, 1]))
        v = dot3(normed, (wqkv_s[0, 2], wqkv_s[1, 2]))
        qh, ql = split(q)
        kh, kl = [part.astype(jnp.float32) for part in split(k)]
        vh, vl = [part.astype(jnp.float32) for part in split(v)]
        lower = lane < half_lanes
        qf, qlf = qh.astype(jnp.float32), ql.astype(jnp.float32)
        q_s[0, at, :lanes] = qh
        q_s[1, at, :lanes] = qh
        q_s[0, at, lanes:] = jnp.where(lower, qf, pltpu.roll(qlf, half_lanes, 1)).astype(jnp.bfloat16)
        q_s[1, at, lanes:] = jnp.where(lower, pltpu.roll(qf, half_lanes, 1), qlf).astype(jnp.bfloat16)
        kh_r, kl_r = pltpu.roll(kh, half_lanes, 1), pltpu.roll(kl, half_lanes, 1)
        for h in range(heads):
            own = lane // HD == h
            other = lane // HD == (h + half_heads) % heads
            k_s[h, at, :lanes] = jnp.where(own, kh, 0.0).astype(jnp.bfloat16)
            if h < half_heads:
                mixed = jnp.where(own, kl, jnp.where(other, kh_r, 0.0))
            else:
                mixed = jnp.where(own, kh, jnp.where(other, kl_r, 0.0))
            k_s[h, at, lanes:] = mixed.astype(jnp.bfloat16)
            v_s[h, at, :lanes] = jnp.where(own, vh, 0.0).astype(jnp.bfloat16)
            v_s[h, at, lanes:] = jnp.where(own, vl, 1.0).astype(jnp.bfloat16)

    def gather_step(i, carry):
        if first:
            @pl.when(i < n)
            def _():
                across(i).wait_recv()
                relay(i).start()

            @pl.when(i > 0)
            def _():
                over(i - 1).wait_recv()
                relay(i - 1).wait_recv()
                project(i - 1)

        else:
            project(i)
        return carry

    lax.fori_loop(0, n + 1 if first else n, gather_step, 0)

    def near(i):
        return sent(
            NEAR, i, p_s.at[pl.ds(pl.multiple_of(i * chunk + (1 - r) * half_rows, half_rows), half_rows)],
            n1_s.at[piece(i, half_rows)], mate,
        )

    def far(i):
        at = piece(i, half_rows)
        return sent(FAR, i, s1_s.at[at], f1_s.at[at], peer)

    def own_half(i):
        return pl.ds(pl.multiple_of(i * chunk + r * half_rows, half_rows), half_rows)

    def share(i):
        at = own_half(i)
        return sent(SHARE, i, a_s.at[at], a_s.at[at], mate)

    def attention(k):
        i, half = k // 2, k % 2
        at = piece(i, chunk)
        total = jnp.zeros((chunk, lanes), jnp.float32)
        for m in range(half_heads):
            h = half * half_heads + m
            scores = bdot(q_s[half, at, :], k_s[h], (((1,), (1,)), ((), ())))
            weights = jnp.exp2(scores - jnp.max(scores, axis=-1, keepdims=True))
            wh, wl = split(weights)
            sums = bdot(wh, v_s[h]) + bdot(wl, v_s[h])
            top, low = sums[:, :lanes], sums[:, lanes:]
            total += jnp.where(lane // HD == h, (top + low) / pltpu.roll(low, half_lanes, 1), 0.0)
        att_s[half] = total

    def finish(i):
        p_s[piece(i, chunk)] = dot3(split(att_s[0] + att_s[1]), (wo_s[0], wo_s[1]))
        near(i).start()

    def reduce_near(i):
        near(i).wait_recv()
        at = piece(i, half_rows)
        s1_s[at] = p_s[own_half(i)] + n1_s[at]
        far(i).start()

    def reduce_far(i):
        far(i).wait_recv()
        at = piece(i, half_rows)
        stream = stream_rows(i * chunk + r * half_rows, half_rows)
        a_s[own_half(i)] = (s1_s[at] + f1_s[at]) + stream
        share(i).start()

    def feed(i):
        share(i).wait_recv()
        at = piece(i, chunk)
        x = a_s[at]
        hidden = gelu(dot3(split(layer_norm(x, gm_ref[...])), (wu_s[0], wu_s[1])))
        total = dot3(split(hidden), (wd_s[0], wd_s[1]))
        if first:
            for j in range(cols * reps):
                m_s[j % reps, j // reps, at] = total[:, j * lanes : (j + 1) * lanes]
            near2(i).start()
        else:
            out_ref[at] = total + x * (1.0 / (cols * reps))

    def near2(i):
        at = piece(i, chunk)
        return sent(NEAR2, i, m_s.at[1 - r, :, at], n2_s.at[:, at], mate)

    def far2(i):
        at = piece(i, chunk)
        return sent(FAR2, i, s2_s.at[at], f2_s.at[at], peer)

    def scatter_near(i):
        near2(i).wait_recv()
        at = piece(i, chunk)
        s2_s[at] = m_s[r, 1 - c, at] + n2_s[1 - c, at]
        far2(i).start()

    def scatter_far(i):
        far2(i).wait_recv()
        at = piece(i, chunk)
        own = a_s[at, pl.ds(pl.multiple_of(me * lanes, lanes), lanes)]
        out_ref[at] = (m_s[r, c, at] + n2_s[c, at]) + f2_s[at] + own

    stages = [(9, scatter_far), (7, scatter_near), (6, feed), (5, reduce_far), (2, reduce_near), (1, finish)]
    if not first:
        stages = stages[2:]

    def tick(k, carry):
        @pl.when(k < 2 * n)
        def _():
            attention(k)

        for offset, stage in stages:
            @pl.when((k >= offset) & (k < offset + 2 * n) & ((k - offset) % 2 == 0))
            def _(offset=offset, stage=stage):
                stage((k - offset) // 2)

        return carry

    lax.fori_loop(0, 2 * n + stages[0][0] - 1, tick, 0)

    kinds = [near, far, share] + ([near2, far2, across, over, relay] if first else [])
    for copy in kinds:
        for i in range(n):
            copy(i).wait_send()


def run_layer(layer, first, x, source, w_qkv, w_out, w_up, w_down, attn_gain, mlp_gain, collective_id):
    cols, reps = lax.axis_size("col"), lax.axis_size("rep")
    group = cols * reps
    lanes = w_qkv.shape[-1]
    width = w_qkv.shape[-2]
    hidden = w_up.shape[-1]
    heads = lanes // HD
    rows = PATCH
    chunk = min(256, rows)
    n = rows // chunk
    dma, f32, b16 = pltpu.SemaphoreType.DMA, jnp.float32, jnp.bfloat16
    vmem = pl.BlockSpec(memory_space=pltpu.VMEM)
    hbm = pl.BlockSpec(memory_space=pl.ANY)
    scratch = [
        pltpu.VMEM((3, width, lanes), f32),
        pltpu.VMEM((lanes, width), f32),
        pltpu.VMEM((width, hidden), f32),
        pltpu.VMEM((hidden, width), f32),
        pltpu.VMEM((2, 3, width, lanes), b16),
        pltpu.VMEM((2, lanes, width), b16),
        pltpu.VMEM((2, width, hidden), b16),
        pltpu.VMEM((2, hidden, width), b16),
        pltpu.VMEM((2, rows, 2 * lanes), b16),
        pltpu.VMEM((heads, rows, 2 * lanes), b16),
        pltpu.VMEM((heads, rows, 2 * lanes), b16),
        pltpu.VMEM((2, chunk, lanes), f32),
        pltpu.VMEM((rows, width), f32),
        pltpu.VMEM((rows // 2, width), f32),
        pltpu.VMEM((rows // 2, width), f32),
        pltpu.VMEM((rows // 2, width), f32),
        pltpu.VMEM((rows, width), f32),
        dma((8 if first else 3, 2, n)),
        dma((4,)),
    ]
    if first:
        scratch += [
            pltpu.VMEM((group, rows, lanes), f32),
            pltpu.VMEM((reps, cols, rows, lanes), f32),
            pltpu.VMEM((cols, rows, lanes), f32),
            pltpu.VMEM((rows, lanes), f32),
            pltpu.VMEM((rows, lanes), f32),
        ]
    operands = [x, attn_gain[layer][None, :], mlp_gain[layer][None, :], w_qkv, w_out, w_up, w_down]
    specs = [vmem] * 3 + [hbm] * 4
    if not first:
        operands = [source] + operands
        specs = [pl.BlockSpec(memory_space=pltpu.SMEM)] + specs
    return pl.pallas_call(
        functools.partial(layer_kernel, layer, first, heads, chunk),
        out_shape=jax.ShapeDtypeStruct((rows, lanes if first else width), f32),
        in_specs=specs,
        out_specs=vmem,
        scratch_shapes=scratch,
        compiler_params=pltpu.CompilerParams(
            collective_id=collective_id, has_side_effects=True, vmem_limit_bytes=VMEM_LIMIT
        ),
        name="first_layer" if first else "second_layer",
    )(*operands)


def routes(dest_device, dest_slot):
    count = dest_device.shape[0]
    peers = lax.axis_size("tok")
    capacity = max(2, (count + peers - 4) // (peers - 1))
    order = jnp.arange(count, dtype=jnp.int32)
    earlier = (dest_device[:, None] == dest_device[None, :]) & (order[None, :] < order[:, None])
    place = dest_device * capacity + jnp.sum(earlier.astype(jnp.int32), axis=1)
    chosen = jnp.arange(peers * capacity, dtype=jnp.int32)[:, None] == place[None, :]
    index = jnp.sum(jnp.where(chosen, order[None, :], 0), axis=1)
    code = jnp.sum(jnp.where(chosen, dest_slot[None, :] + 1, 0), axis=1)
    code = jnp.pad(code.reshape(peers, capacity), ((0, 0), (0, 128 - capacity)))
    code = jnp.broadcast_to(code[:, None, :], (peers, 8, 128)).astype(jnp.float32)
    return index, code, capacity


def raster_cells(extended, depth_weight, point_weight, gain_row):
    row_count = extended.shape[0] - 2
    col_count = extended.shape[1] - 2
    channels = extended.shape[2]
    normed = (
        extended
        * lax.rsqrt(jnp.mean(extended * extended, axis=-1, keepdims=True) + EPSILON)
        * gain_row
    )
    mixed = jnp.zeros((row_count, col_count, channels), jnp.float32)
    for a in range(3):
        for b in range(3):
            mixed = mixed + normed[a : a + row_count, b : b + col_count] * depth_weight[a, b]
    combined = matmul(mixed.reshape(row_count * col_count, channels), point_weight)
    combined = combined.reshape(row_count, col_count, 2 * channels)
    centre = extended[1:-1, 1:-1]
    return centre + combined[..., :channels] * jax.nn.sigmoid(combined[..., channels:])


HALO = 2


def extended_cells(tok, members, rep_rows, full_width):
    cols, reps = members
    tile = []
    for col in range(cols):
        for rep in range(reps):
            y = rep * rep_rows - HALO + jnp.arange(rep_rows + 2 * HALO, dtype=jnp.int32)[:, None]
            x = col * TC - HALO + jnp.arange(TC + 2 * HALO, dtype=jnp.int32)[None, :]
            good = (y >= 0) & (y < TR) & (x >= 0) & (x < full_width)
            tile.append(jnp.where(good, (tok * TR + y) * full_width + x, -2).reshape(-1))
    return jnp.concatenate(tile)


def pool(partial, pillar, cells):
    onehot = (cells[:, None] == pillar[None, :]).astype(jnp.float32)
    return matmul(onehot, partial)


def exchange_rows(tile, ntok, reps):
    count = ntok * reps
    rep = lax.axis_index("rep")
    forward = [(i, i + 1) for i in range(count - 1)]
    backward = [(i + 1, i) for i in range(count - 1)]
    above = lax.ppermute(tile[-2 * HALO : -HALO], ("tok", "rep"), forward)
    below = lax.ppermute(tile[HALO : 2 * HALO], ("tok", "rep"), backward)
    above = jnp.where(rep == 0, above, tile[:HALO])
    below = jnp.where(rep == reps - 1, below, tile[-HALO:])
    return jnp.concatenate([above, tile[HALO:-HALO], below], axis=0)


def on_device(
    tokens,
    w_qkv,
    w_out,
    w_up,
    w_down,
    attn_gain,
    mlp_gain,
    dest_device,
    dest_slot,
    pillar,
    depth_weight,
    point_weight,
    raster_gain,
):
    members = (lax.axis_size("col"), lax.axis_size("rep"))
    group = members[0] * members[1]
    ntok = lax.axis_size("tok")
    block_count = dest_device.shape[0]
    order = jnp.arange(block_count, dtype=jnp.int32)
    index, codes, capacity = routes(dest_device, dest_slot)
    width = tokens.shape[1]
    rows = tokens.shape[0]
    pair = members == (2, 2) and rows == PATCH
    weights = (w_qkv, w_out, w_up, w_down, attn_gain, mlp_gain)
    if pair:
        share = run_layer(0, True, tokens, None, *weights, 1)
    else:
        blocks = gather(tokens, 1).reshape(1, group, block_count, -1, width)
        stream = attention_layer(blocks, order, 0, w_qkv, w_out, attn_gain, 2)
        share = scatter(mlp_partial(stream, 0, w_up, w_down, mlp_gain, group), 3)
    outgoing = pick(share.reshape(block_count, -1, width), index)
    outgoing = outgoing.reshape(ntok, -1, width)
    moved, arrived = move(outgoing, codes, 4)
    blocks = moved.reshape(ntok, group, capacity, -1, width)
    held = arrived[:, 0, :capacity].reshape(-1).astype(jnp.int32)
    found = held[None, :] == order[:, None] + 1
    source = jnp.sum(jnp.where(found, jnp.arange(held.shape[0], dtype=jnp.int32)[None, :], 0), axis=1)
    if pair:
        partial = run_layer(1, False, blocks, source, *weights, 5)
    else:
        stream = attention_layer(blocks, source, 1, w_qkv, w_out, attn_gain, 5)
        partial = mlp_partial(stream, 1, w_up, w_down, mlp_gain, 1)[0]

    rep_rows = TR // members[1]
    full_width = TC * members[0]
    cells = extended_cells(lax.axis_index("tok"), members, rep_rows, full_width)
    pooled = pool(partial, pillar, cells)
    parts = pooled.reshape(group, -1, pooled.shape[1])
    edge = HALO * (TC + 2 * HALO)
    inside_kernel = members[0] > 1 and members[1] == 2 and ntok > 1 and edge % 8 == 0
    tile = scatter(parts, 6, edge if inside_kernel else 0)
    tile = tile.reshape(rep_rows + 2 * HALO, TC + 2 * HALO, -1)
    if not inside_kernel:
        tile = exchange_rows(tile, ntok, members[1])
    first = raster_cells(tile, depth_weight[0], point_weight[0], raster_gain[0])
    y = lax.axis_index(("tok", "rep")) * rep_rows - 1 + jnp.arange(rep_rows + 2)[:, None, None]
    x = lax.axis_index("col") * TC - 1 + jnp.arange(TC + 2)[None, :, None]
    inside = (y >= 0) & (y < TR * ntok) & (x >= 0) & (x < full_width)
    first = jnp.where(inside, first, 0.0)
    return raster_cells(first, depth_weight[1], point_weight[1], raster_gain[1])


def solution(mesh):
    placed = (
        P(("scene", "tok"), ("col", "rep")),
        P(None, None, None, ("col", "rep")),
        P(None, ("col", "rep"), None),
        P(None, None, ("col", "rep")),
        P(None, ("col", "rep"), None),
        P(),
        P(),
        P(("scene", "tok")),
        P(("scene", "tok")),
        P(("scene", "tok")),
        P(),
        P(),
        P(),
    )
    return jax.shard_map(
        on_device,
        mesh=mesh,
        in_specs=placed,
        out_specs=P(("scene", "tok", "rep"), "col", None),
        check_vma=False,
    )
```

```python
import functools
import math

import jax
import jax.numpy as jnp
from jax import lax
from jax.experimental import pallas as pl
from jax.experimental.pallas import tpu as pltpu
from jax.sharding import PartitionSpec as P

PATCH = 1024
TR = 16
TC = 16
HD = 16


MATMUL_PRECISION = lax.Precision.HIGH
EPSILON = 1e-05


def layer_norm(values, gain_row):
    average = jnp.mean(values, axis=-1, keepdims=True)
    centered = values - average
    variance = jnp.mean(centered * centered, axis=-1, keepdims=True)
    return centered * lax.rsqrt(variance + EPSILON) * gain_row


def split(values):
    high = values.astype(jnp.bfloat16)
    return high, (values - high.astype(jnp.float32)).astype(jnp.bfloat16)


def bdot(left, right, dims=(((1,), (0,)), ((), ()))):
    return lax.dot_general(left, right, dims, preferred_element_type=jnp.float32)


def dot3(left, right):
    lh, ll = left
    rh, rl = right
    return bdot(lh, rh) + bdot(lh, rl) + bdot(ll, rh)


def attention_kernel(share, source_ref, x_ref, gain_ref, w_ref, o_ref, out_ref, q_s, k_s, v_s, att_s):
    cols = w_ref.shape[-1]
    heads = cols // HD
    rows = out_ref.shape[0]
    chunk = att_s.shape[0]
    slots, each, block = x_ref.shape[1:4]
    first_block = pl.program_id(0) * (rows // block)

    def stream_rows(i):
        parts = []
        for n in range(chunk // block):
            at = source_ref[first_block + i * (chunk // block) + n]
            places = [x_ref[at // each, j, at % each] for j in range(slots)]
            parts.append(jnp.concatenate(places, axis=-1))
        return jnp.concatenate(parts, axis=0)

    lanes = q_s.shape[-1]

    r = lax.broadcasted_iota(jnp.int32, (cols, lanes), 0)
    c = lax.broadcasted_iota(jnp.int32, (cols, lanes), 1)
    lane = lax.broadcasted_iota(jnp.int32, (1, cols), 1)
    w = [split(w_ref[j]) for j in range(3)]
    for i in range(rows // chunk):
        at = pl.ds(i * chunk, chunk)
        normed = split(layer_norm(stream_rows(i), gain_ref[...]))
        qh, ql = split(dot3(normed, w[0]) * (HD ** (-0.5) * math.log2(math.e)))
        kh, kl = split(dot3(normed, w[1]))
        vh, vl = split(dot3(normed, w[2]))
        for h in range(heads):
            part = c // HD
            inside = (r // HD == h) & (r % HD == c % HD)
            first = (inside & ((part == 0) | (part == 1))).astype(jnp.bfloat16)
            third = (inside & (part == 2)).astype(jnp.bfloat16)
            outer = (inside & ((part == 0) | (part == 2))).astype(jnp.bfloat16)
            middle = (inside & (part == 1)).astype(jnp.bfloat16)
            q_s[h, at, :] = (bdot(qh, first) + bdot(ql, third)).astype(jnp.bfloat16)
            k_s[h, at, :] = (bdot(kh, outer) + bdot(kl, middle)).astype(jnp.bfloat16)
            own = lane // HD == h
            v_s[h, at, :cols] = jnp.where(own, vh.astype(jnp.float32), 0.0).astype(jnp.bfloat16)
            v_s[h, at, cols:] = jnp.where(own, vl.astype(jnp.float32), 1.0).astype(jnp.bfloat16)

    projection = split(o_ref[...])

    def query_rows(i, carry):
        at = pl.ds(pl.multiple_of(i * chunk, chunk), chunk)
        att_s[...] = jnp.zeros_like(att_s)

        def one_head(h, carry):
            scores = bdot(q_s[h, at, :], k_s[h], (((1,), (1,)), ((), ())))
            weights = jnp.exp2(scores - jnp.max(scores, axis=-1, keepdims=True))
            wh, wl = split(weights)
            sums = bdot(wh, v_s[h]) + bdot(wl, v_s[h])
            top, low = sums[:, :cols], sums[:, cols:]
            own = lane // HD == h
            total = jnp.max(jnp.where(own, 0.0, low), axis=-1, keepdims=True)
            att_s[...] += jnp.where(own, (top + low) / total, 0.0)
            return carry

        lax.fori_loop(0, heads, one_head, 0, unroll=4)
        out_ref[at, :] = dot3(split(att_s[...]), projection) + stream_rows(i) * share
        return carry

    lax.fori_loop(0, rows // chunk, query_rows, 0)


def attend(blocks, source, gain_row, weights, w_out, group):
    block, width = blocks.shape[3], blocks.shape[1] * blocks.shape[4]
    rows = source.shape[0] * block
    cols = weights.shape[-1]
    heads = cols // HD
    lanes = max(128, 3 * HD)
    return pl.pallas_call(
        functools.partial(attention_kernel, 1.0 / group),
        grid_spec=pltpu.PrefetchScalarGridSpec(
            num_scalar_prefetch=1,
            grid=(rows // PATCH,),
            in_specs=[
                pl.BlockSpec(blocks.shape, lambda i, source: (0, 0, 0, 0, 0)),
                pl.BlockSpec((1, width), lambda i, source: (0, 0)),
                pl.BlockSpec(weights.shape, lambda i, source: (0, 0, 0)),
                pl.BlockSpec(w_out.shape, lambda i, source: (0, 0)),
            ],
            out_specs=pl.BlockSpec((PATCH, width), lambda i, source: (i, 0)),
            scratch_shapes=[
                pltpu.VMEM((heads, PATCH, lanes), jnp.bfloat16),
                pltpu.VMEM((heads, PATCH, lanes), jnp.bfloat16),
                pltpu.VMEM((heads, PATCH, 2 * cols), jnp.bfloat16),
                pltpu.VMEM((256, cols), jnp.float32),
            ],
        ),
        out_shape=jax.ShapeDtypeStruct((rows, width), jnp.float32),
        compiler_params=pltpu.CompilerParams(vmem_limit_bytes=48 * 1024 * 1024),
        name="attend",
    )(source, blocks, gain_row[None, :], weights, w_out)


def matmul(left, right):
    return jnp.dot(left, right, precision=MATMUL_PRECISION, preferred_element_type=jnp.float32)


VMEM_LIMIT = 56 * 1024 * 1024
MESH = pl.DeviceIdType.MESH


def position():
    cols, reps = lax.axis_size("col"), lax.axis_size("rep")
    return cols, reps, lax.axis_index("col"), lax.axis_index("rep")


def greet(devices):
    barrier = pltpu.get_barrier_semaphore()
    for device in devices:
        pl.semaphore_signal(barrier, inc=1, device_id=device, device_id_type=MESH)
    pl.semaphore_wait(barrier, len(devices))


def remote(src, dst, send, recv, device):
    return pltpu.make_async_remote_copy(
        src_ref=src, dst_ref=dst, send_sem=send, recv_sem=recv, device_id=device, device_id_type=MESH
    )


def chunks_of(rows):
    for pieces in (8, 5, 4, 2):
        if rows % (8 * pieces) == 0:
            return pieces, rows // pieces
    return 1, rows


def gather_kernel(x_ref, out_ref, xs, xr, fs, fr, ps, pr, local):
    cols, reps, c, r = position()
    rows = x_ref.shape[0]
    pieces, size = chunks_of(rows)
    me = c * reps + r
    mate = {"col": c, "rep": 1 - r}
    others = [{"col": lax.rem(c + d, cols), "rep": r} for d in range(1, cols)]
    greet([mate] + others)
    across, onward = [], []
    for k in range(pieces):
        at = pl.ds(k * size, size)
        for d in range(1, cols):
            copy = remote(
                x_ref.at[at], out_ref.at[me, at], xs.at[d - 1, k], xr.at[d - 1, k], others[d - 1]
            )
            copy.start()
            across.append(copy)
    share = remote(x_ref, out_ref.at[me], ps, pr, mate)
    share.start()
    keep = pltpu.make_async_copy(x_ref, out_ref.at[me], local)
    keep.start()
    for k in range(pieces):
        at = pl.ds(k * size, size)
        for d in range(1, cols):
            across[k * (cols - 1) + d - 1].wait_recv()
            slot = lax.rem(c + cols - d, cols) * reps + r
            copy = remote(
                out_ref.at[slot, at], out_ref.at[slot, at], fs.at[d - 1, k], fr.at[d - 1, k], mate
            )
            copy.start()
            onward.append(copy)
    for copy in across:
        copy.wait_send()
    share.wait()
    keep.wait()
    for copy in onward:
        copy.wait()


def gather(block, collective_id):
    cols, reps = lax.axis_size("col"), lax.axis_size("rep")
    if reps != 2 or cols < 2:
        return lax.all_gather(block, ("col", "rep"), axis=0)
    pieces, _ = chunks_of(block.shape[0])
    dma = pltpu.SemaphoreType.DMA
    return pl.pallas_call(
        gather_kernel,
        out_shape=jax.ShapeDtypeStruct((cols * reps,) + block.shape, block.dtype),
        in_specs=[pl.BlockSpec(memory_space=pltpu.VMEM)],
        out_specs=pl.BlockSpec(memory_space=pltpu.VMEM),
        scratch_shapes=[dma((cols - 1, pieces))] * 4 + [dma, dma, dma],
        compiler_params=pltpu.CompilerParams(
            collective_id=collective_id, has_side_effects=True, vmem_limit_bytes=VMEM_LIMIT
        ),
        name="gather",
    )(block)


def scatter_kernel(edge, p_ref, out_ref, a_ref, s_ref, b_ref, a_s, a_r, b_s, b_r, *halo):
    cols, reps, c, r = position()
    rows = p_ref.shape[1]
    pieces, size = chunks_of(rows)
    mate = {"col": c, "rep": 1 - r}
    others = [{"col": lax.rem(c + d, cols), "rep": r} for d in range(1, cols)]
    greeted = [mate] + others
    if edge:
        ntok, t = lax.axis_size("tok"), lax.axis_index("tok")
        partner = {"tok": lax.rem(t + jnp.where(r == 0, ntok - 1, 1), ntok), "rep": 1 - r}
        greeted = greeted + [partner]
    greet(greeted)
    order = [(k, d) for k in range(pieces) for d in range(1, cols)]
    order += [(k, 0) for k in range(pieces)]
    near, far = {}, {}
    for k, d in order:
        at = pl.ds(k * size, size)
        slot = lax.rem(c + d, cols) * reps + 1 - r
        near[k, d] = remote(
            p_ref.at[slot, at], a_ref.at[d, at], a_s.at[d, k], a_r.at[d, k], mate
        )
        near[k, d].start()
    for k, d in order:
        at = pl.ds(k * size, size)
        slot = lax.rem(c + d, cols) * reps + r
        near[k, d].wait_recv()
        total = p_ref[slot, at] + a_ref[d, at]
        if d == 0:
            out_ref[at] = total
        else:
            s_ref[d - 1, at] = total
            far[k, d] = remote(
                s_ref.at[d - 1, at],
                b_ref.at[d - 1, at],
                b_s.at[d - 1, k],
                b_r.at[d - 1, k],
                others[d - 1],
            )
            far[k, d].start()
    for (k, d), copy in far.items():
        at = pl.ds(k * size, size)
        copy.wait_recv()
        out_ref[at] += b_ref[d - 1, at]
    if edge:
        h_ref, e_ref, h_s, h_r = halo
        inner = pl.multiple_of(jnp.where(r == 0, edge, rows - 2 * edge), 8)
        outer = pl.multiple_of(jnp.where(r == 0, 0, rows - edge), 8)
        e_ref[...] = out_ref[pl.ds(inner, edge)]
        copy = remote(e_ref, h_ref, h_s, h_r, partner)
        copy.start()
        copy.wait()
        wrapped = jnp.where(r == 0, t == 0, t == ntok - 1)
        out_ref[pl.ds(outer, edge)] = jnp.where(wrapped, 0.0, h_ref[...])
    for copy in list(near.values()) + list(far.values()):
        copy.wait_send()


def scatter(parts, collective_id, edge=0):
    cols, reps = lax.axis_size("col"), lax.axis_size("rep")
    if reps != 2 or cols < 2:
        return lax.psum_scatter(parts, ("col", "rep"), scatter_dimension=0)
    shape, kind = parts.shape[1:], parts.dtype
    pieces, _ = chunks_of(shape[0])
    dma = pltpu.SemaphoreType.DMA
    return pl.pallas_call(
        functools.partial(scatter_kernel, edge),
        out_shape=jax.ShapeDtypeStruct(shape, kind),
        in_specs=[pl.BlockSpec(memory_space=pltpu.VMEM)],
        out_specs=pl.BlockSpec(memory_space=pltpu.VMEM),
        scratch_shapes=[
            pltpu.VMEM((cols,) + shape, kind),
            pltpu.VMEM((cols - 1,) + shape, kind),
            pltpu.VMEM((cols - 1,) + shape, kind),
            dma((cols, pieces)),
            dma((cols, pieces)),
            dma((cols - 1, pieces)),
            dma((cols - 1, pieces)),
        ]
        + ([pltpu.VMEM((edge, shape[1]), kind)] * 2 + [dma, dma] if edge else []),
        compiler_params=pltpu.CompilerParams(
            collective_id=collective_id, has_side_effects=True, vmem_limit_bytes=VMEM_LIMIT
        ),
        name="scatter",
    )(parts)


def total_kernel(
    p_ref, out_ref, a_ref, s_ref, b_ref, a_s, a_r, b_s, b_r, xs, xr, fs, fr, ps, pr
):
    cols, reps, c, r = position()
    rows = p_ref.shape[1]
    pieces, size = chunks_of(rows)
    me = c * reps + r
    mate = {"col": c, "rep": 1 - r}
    others = [{"col": lax.rem(c + d, cols), "rep": r} for d in range(1, cols)]
    greet([mate] + others)
    order = [(k, d) for k in range(pieces) for d in range(1, cols)]
    order += [(k, 0) for k in range(pieces)]
    near, far, across, share, onward = {}, {}, {}, {}, {}
    for k, d in order:
        at = pl.ds(k * size, size)
        slot = lax.rem(c + d, cols) * reps + 1 - r
        near[k, d] = remote(
            p_ref.at[slot, at], a_ref.at[d, at], a_s.at[d, k], a_r.at[d, k], mate
        )
        near[k, d].start()
    for k, d in order:
        if d == 0:
            continue
        at = pl.ds(k * size, size)
        slot = lax.rem(c + d, cols) * reps + r
        near[k, d].wait_recv()
        s_ref[d - 1, at] = p_ref[slot, at] + a_ref[d, at]
        far[k, d] = remote(
            s_ref.at[d - 1, at], b_ref.at[d - 1, at], b_s.at[d - 1, k], b_r.at[d - 1, k], others[d - 1]
        )
        far[k, d].start()
    for k in range(pieces):
        at = pl.ds(k * size, size)
        near[k, 0].wait_recv()
        total = p_ref[me, at] + a_ref[0, at]
        for d in range(1, cols):
            far[k, d].wait_recv()
            total = total + b_ref[d - 1, at]
        out_ref[me, at] = total
        for d in range(1, cols):
            across[k, d] = remote(
                out_ref.at[me, at], out_ref.at[me, at], xs.at[d - 1, k], xr.at[d - 1, k], others[d - 1]
            )
            across[k, d].start()
        share[k] = remote(out_ref.at[me, at], out_ref.at[me, at], ps.at[k], pr.at[k], mate)
        share[k].start()
    for (k, d), copy in across.items():
        at = pl.ds(k * size, size)
        copy.wait_recv()
        slot = lax.rem(c + cols - d, cols) * reps + r
        onward[k, d] = remote(
            out_ref.at[slot, at], out_ref.at[slot, at], fs.at[d - 1, k], fr.at[d - 1, k], mate
        )
        onward[k, d].start()
    for copies in (near, far, across):
        for copy in copies.values():
            copy.wait_send()
    for copies in (share, onward):
        for copy in copies.values():
            copy.wait()


def total(parts, collective_id):
    cols, reps = lax.axis_size("col"), lax.axis_size("rep")
    if reps != 2 or cols < 2:
        return lax.psum(parts, ("col", "rep"))
    shape, kind = parts.shape[1:], parts.dtype
    pieces, _ = chunks_of(shape[0])
    dma = pltpu.SemaphoreType.DMA
    return pl.pallas_call(
        total_kernel,
        out_shape=jax.ShapeDtypeStruct(parts.shape, kind),
        in_specs=[pl.BlockSpec(memory_space=pltpu.VMEM)],
        out_specs=pl.BlockSpec(memory_space=pltpu.VMEM),
        scratch_shapes=[
            pltpu.VMEM((cols,) + shape, kind),
            pltpu.VMEM((cols - 1,) + shape, kind),
            pltpu.VMEM((cols - 1,) + shape, kind),
            dma((cols, pieces)),
            dma((cols, pieces)),
        ]
        + [dma((cols - 1, pieces))] * 6
        + [dma((pieces,))] * 2,
        compiler_params=pltpu.CompilerParams(
            collective_id=collective_id, has_side_effects=True, vmem_limit_bytes=VMEM_LIMIT
        ),
        name="total",
    )(parts)


def move_kernel(o_ref, code_ref, out_ref, arrived_ref, zs, zr, cs, cr, xs, xr, fs, fr, ps, pr, local):
    cols, reps, c, r = position()
    ntok, t = lax.axis_size("tok"), lax.axis_index("tok")
    me = c * reps + r
    mate = {"col": c, "rep": 1 - r}
    others = [{"col": lax.rem(c + d, cols), "rep": r} for d in range(1, cols)]
    peers = [{"tok": lax.rem(t + e, ntok)} for e in range(1, ntok)]
    greet([mate] + others + peers)
    along, codes, across, share, onward = [], [], {}, [], []
    for e in range(1, ntok):
        target = lax.rem(t + e, ntok)
        copy = remote(o_ref.at[target], out_ref.at[t, me], zs.at[e - 1], zr.at[e - 1], peers[e - 1])
        copy.start()
        along.append(copy)
        copy = remote(
            code_ref.at[target], arrived_ref.at[t], cs.at[e - 1], cr.at[e - 1], peers[e - 1]
        )
        copy.start()
        codes.append(copy)
    keep = pltpu.make_async_copy(o_ref.at[t], out_ref.at[t, me], local.at[0])
    keep.start()
    keep_code = pltpu.make_async_copy(code_ref.at[t], arrived_ref.at[t], local.at[1])
    keep_code.start()

    def hand_on(e):
        u = lax.rem(t + ntok - e, ntok)
        for d in range(1, cols):
            across[e, d].wait_recv()
            slot = lax.rem(c + cols - d, cols) * reps + r
            copy = remote(
                out_ref.at[u, slot], out_ref.at[u, slot], fs.at[e, d - 1], fr.at[e, d - 1], mate
            )
            copy.start()
            onward.append(copy)

    for e in range(ntok):
        u = lax.rem(t + ntok - e, ntok)
        if e:
            along[e - 1].wait_recv()
        origin = out_ref.at[u, me] if e else o_ref.at[t]
        for d in range(1, cols):
            across[e, d] = remote(
                origin, out_ref.at[u, me], xs.at[e, d - 1], xr.at[e, d - 1], others[d - 1]
            )
            across[e, d].start()
        copy = remote(origin, out_ref.at[u, me], ps.at[e], pr.at[e], mate)
        copy.start()
        share.append(copy)
        if e:
            hand_on(e - 1)
    hand_on(ntok - 1)
    keep.wait()
    keep_code.wait()
    for copy in along + list(across.values()):
        copy.wait_send()
    for copy in codes + share + onward:
        copy.wait()


def move(outgoing, codes, collective_id):
    cols, reps, ntok = lax.axis_size("col"), lax.axis_size("rep"), lax.axis_size("tok")
    if reps != 2 or cols < 2 or ntok < 2:
        incoming = lax.all_to_all(outgoing, "tok", split_axis=0, concat_axis=0, tiled=True)
        arrived = lax.all_to_all(codes, "tok", split_axis=0, concat_axis=0, tiled=True)
        return lax.all_gather(incoming, ("col", "rep"), axis=1), arrived
    dma = pltpu.SemaphoreType.DMA
    shape = (ntok, cols * reps) + outgoing.shape[1:]
    return pl.pallas_call(
        move_kernel,
        out_shape=(
            jax.ShapeDtypeStruct(shape, outgoing.dtype),
            jax.ShapeDtypeStruct(codes.shape, codes.dtype),
        ),
        in_specs=[pl.BlockSpec(memory_space=pltpu.VMEM)] * 2,
        out_specs=[pl.BlockSpec(memory_space=pltpu.VMEM)] * 2,
        scratch_shapes=[dma((ntok - 1,))] * 4
        + [dma((ntok, cols - 1))] * 4
        + [dma((ntok,))] * 2
        + [dma((2,))],
        compiler_params=pltpu.CompilerParams(
            collective_id=collective_id, has_side_effects=True, vmem_limit_bytes=VMEM_LIMIT
        ),
        name="move",
    )(outgoing, codes)


def pick_kernel(index_ref, x_ref, out_ref):
    for j in range(out_ref.shape[0]):
        out_ref[j] = x_ref[index_ref[j]]


def pick(blocks, index):
    return pl.pallas_call(
        pick_kernel,
        out_shape=jax.ShapeDtypeStruct(index.shape + blocks.shape[1:], blocks.dtype),
        in_specs=[pl.BlockSpec(memory_space=pltpu.SMEM), pl.BlockSpec(memory_space=pltpu.VMEM)],
        out_specs=pl.BlockSpec(memory_space=pltpu.VMEM),
        name="pick",
    )(index, blocks)


def attention_layer(blocks, source, layer, w_qkv, w_out, attn_gain, collective_id):
    group = blocks.shape[1]
    terms = attend(blocks, source, attn_gain[layer], w_qkv[layer], w_out[layer], group)
    rows, width = terms.shape
    return total(terms.reshape(group, rows // group, width), collective_id).reshape(rows, width)


def mlp_kernel(x_ref, gain_ref, up_ref, down_ref, share, out_ref):
    x = x_ref[...]
    hidden = dot3(split(layer_norm(x, gain_ref[...])), split(up_ref[...]))
    hidden = 0.5 * hidden * (1.0 + lax.erf(hidden * (0.5**0.5)))
    total = dot3(split(hidden), split(down_ref[...])) + x * share
    width = out_ref.shape[-1]
    for j in range(out_ref.shape[0]):
        out_ref[j] = total[:, j * width : (j + 1) * width]


def mlp_partial(stream, layer, w_up, w_down, mlp_gain, slots):
    rows, width = stream.shape
    tile = min(256, rows)
    hidden = w_up.shape[-1]
    group = lax.axis_size("col") * lax.axis_size("rep")

    def kernel(x_ref, gain_ref, up_ref, down_ref, out_ref):
        mlp_kernel(x_ref, gain_ref, up_ref, down_ref, 1.0 / group, out_ref)

    return pl.pallas_call(
        kernel,
        grid=(rows // tile,),
        in_specs=[
            pl.BlockSpec((tile, width), lambda i: (i, 0)),
            pl.BlockSpec((1, width), lambda i: (0, 0)),
            pl.BlockSpec((width, hidden), lambda i: (0, 0)),
            pl.BlockSpec((hidden, width), lambda i: (0, 0)),
        ],
        out_specs=pl.BlockSpec((slots, tile, width // slots), lambda i: (0, i, 0)),
        out_shape=jax.ShapeDtypeStruct((slots, rows, width // slots), jnp.float32),
        compiler_params=pltpu.CompilerParams(vmem_limit_bytes=48 * 1024 * 1024),
        name="mlp",
    )(stream, mlp_gain[layer][None, :], w_up[layer], w_down[layer])


def gelu(values):
    return 0.5 * values * (1.0 + lax.erf(values * (0.5**0.5)))


def piece(i, size):
    return pl.ds(pl.multiple_of(i * size, size), size)


class Layer:
    def __init__(self, layer, refs, heads, chunk, kinds):
        self.__dict__.update(refs)
        self.layer, self.heads, self.chunk, self.kinds = layer, heads, chunk, kinds
        self.cols, self.reps, self.c, self.r = position()
        self.ntok, self.t = lax.axis_size("tok"), lax.axis_index("tok")
        self.me = self.c * self.reps + self.r
        self.mate, self.peer = {"rep": 1 - self.r}, {"col": 1 - self.c}
        self.peers = [{"tok": lax.rem(self.t + e, self.ntok)} for e in range(1, self.ntok)]
        self.rows, self.width = self.a_s.shape
        self.lanes = self.q_s.shape[-1] // 2
        self.n = self.rows // chunk
        self.started = []

    def sent(self, kind, i, src, dst, device):
        k = self.kinds.index(kind)
        return remote(src, dst, self.sem.at[k, 0, i], self.sem.at[k, 1, i], device)

    def load_weights(self):
        pairs = (
            (self.wqkv_ref, self.wqkv_f), (self.wo_ref, self.wo_f),
            (self.wu_ref, self.wu_f), (self.wd_ref, self.wd_f),
        )
        self.loads = [
            pltpu.make_async_copy(src.at[self.layer], dst, self.wsem.at[j])
            for j, (src, dst) in enumerate(pairs)
        ]
        for load in self.loads:
            load.start()

    def split_weights(self):
        self.loads[0].wait()
        for m in range(3):
            self.wqkv_s[0, m], self.wqkv_s[1, m] = split(self.wqkv_f[m])
        rest = ((self.wo_f, self.wo_s), (self.wu_f, self.wu_s), (self.wd_f, self.wd_s))
        for load, (src, dst) in zip(self.loads[1:], rest):
            load.wait()
            dst[0], dst[1] = split(src[...])

    def project(self, stream):
        normed = split(layer_norm(stream, self.ga_ref[pl.ds(self.layer, 1)]))
        return [dot3(normed, (self.wqkv_s[0, m], self.wqkv_s[1, m])) for m in range(3)]

    def pack(self, at, q, k, v):
        lanes, heads = self.lanes, self.heads
        half_lanes, half_heads = lanes // 2, heads // 2
        lane = lax.broadcasted_iota(jnp.int32, (1, lanes), 1)
        low = lane < half_lanes
        qh, ql = split(q * (HD ** (-0.5) * math.log2(math.e)))
        kh, kl = [part.astype(jnp.float32) for part in split(k)]
        vh, vl = [part.astype(jnp.float32) for part in split(v)]
        qf, qlf = qh.astype(jnp.float32), ql.astype(jnp.float32)
        q_s, k_s, v_s = self.q_s, self.k_s, self.v_s
        q_s[0, at, :lanes] = qh
        q_s[1, at, :lanes] = qh
        q_s[0, at, lanes:] = jnp.where(low, qf, pltpu.roll(qlf, half_lanes, 1)).astype(jnp.bfloat16)
        q_s[1, at, lanes:] = jnp.where(low, pltpu.roll(qf, half_lanes, 1), qlf).astype(jnp.bfloat16)
        kh_r, kl_r = pltpu.roll(kh, half_lanes, 1), pltpu.roll(kl, half_lanes, 1)
        for h in range(heads):
            own = lane // HD == h
            other = lane // HD == (h + half_heads) % heads
            k_s[h, at, :lanes] = jnp.where(own, kh, 0.0).astype(jnp.bfloat16)
            if h < half_heads:
                mixed = jnp.where(own, kl, jnp.where(other, kh_r, 0.0))
            else:
                mixed = jnp.where(own, kh, jnp.where(other, kl_r, 0.0))
            k_s[h, at, lanes:] = mixed.astype(jnp.bfloat16)
            v_s[h, at, :lanes] = jnp.where(own, vh, 0.0).astype(jnp.bfloat16)
            v_s[h, at, lanes:] = jnp.where(own, vl, 1.0).astype(jnp.bfloat16)

    def near(self, i):
        half = self.chunk // 2
        start = pl.multiple_of(i * self.chunk + (1 - self.r) * half, half)
        return self.sent("near", i, self.p_s.at[pl.ds(start, half)], self.n1_s.at[piece(i, half)], self.mate)

    def far(self, i):
        at = piece(i, self.chunk // 2)
        return self.sent("far", i, self.s1_s.at[at], self.f1_s.at[at], self.peer)

    def own_half(self, i):
        half = self.chunk // 2
        return pl.ds(pl.multiple_of(i * self.chunk + self.r * half, half), half)

    def share(self, i):
        at = self.own_half(i)
        return self.sent("share", i, self.a_s.at[at], self.a_s.at[at], self.mate)

    def attention(self, k):
        lanes, half_heads = self.lanes, self.heads // 2
        lane = lax.broadcasted_iota(jnp.int32, (1, lanes), 1)
        i, half = k // 2, k % 2
        at = piece(i, self.chunk)
        total = jnp.zeros((self.chunk, lanes), jnp.float32)
        for m in range(half_heads):
            h = half * half_heads + m
            scores = bdot(self.q_s[half, at, :], self.k_s[h], (((1,), (1,)), ((), ())))
            weights = jnp.exp2(scores - jnp.max(scores, axis=-1, keepdims=True))
            wh, wl = split(weights)
            sums = bdot(wh, self.v_s[h]) + bdot(wl, self.v_s[h])
            top, low = sums[:, :lanes], sums[:, lanes:]
            total += jnp.where(lane // HD == h, (top + low) / pltpu.roll(low, lanes // 2, 1), 0.0)
        self.att_s[half] = total

    def finish(self, i):
        projection = (self.wo_s[0], self.wo_s[1])
        self.p_s[piece(i, self.chunk)] = dot3(split(self.att_s[0] + self.att_s[1]), projection)
        self.near(i).start()

    def reduce_near(self, i):
        self.near(i).wait_recv()
        at = piece(i, self.chunk // 2)
        self.s1_s[at] = self.p_s[self.own_half(i)] + self.n1_s[at]
        self.far(i).start()

    def reduce_far(self, i):
        self.far(i).wait_recv()
        half = self.chunk // 2
        at = piece(i, half)
        stream = self.stream_rows(i * self.chunk + self.r * half, half)
        self.a_s[self.own_half(i)] = (self.s1_s[at] + self.f1_s[at]) + stream
        self.share(i).start()

    def mlp(self, x):
        normed = split(layer_norm(x, self.gm_ref[pl.ds(self.layer, 1)]))
        hidden = gelu(dot3(normed, (self.wu_s[0], self.wu_s[1])))
        return dot3(split(hidden), (self.wd_s[0], self.wd_s[1]))

    def run(self, stages):
        n = self.n

        def tick(k, carry):
            @pl.when(k < 2 * n)
            def _():
                self.attention(k)

            for offset, stage in stages:
                @pl.when((k >= offset) & (k < offset + 2 * n) & ((k - offset) % 2 == 0))
                def _(offset=offset, stage=stage):
                    stage((k - offset) // 2)

            return carry

        lax.fori_loop(0, 2 * n + stages[0][0] - 1, tick, 0)


class First(Layer):
    def stream_rows(self, start, count):
        at = pl.ds(pl.multiple_of(start, count), count)
        return jnp.concatenate([self.g_s[j, at] for j in range(self.cols * self.reps)], axis=-1)

    def across(self, i):
        at = piece(i, self.chunk)
        return self.sent("across", i, self.x_ref.at[at], self.g_s.at[self.me, at], self.peer)

    def over(self, i):
        at = piece(i, self.chunk)
        return self.sent("over", i, self.x_ref.at[at], self.g_s.at[self.me, at], self.mate)

    def relay(self, i):
        at = piece(i, self.chunk)
        slot = (1 - self.c) * self.reps + self.r
        return self.sent("relay", i, self.g_s.at[slot, at], self.g_s.at[slot, at], self.mate)

    def code(self, e):
        target = lax.rem(self.t + e, self.ntok)
        return self.sent(
            "code", e, self.code_ref.at[target], self.arrived_ref.at[self.t], {"tok": target}
        )

    def near2(self, i):
        at = piece(i, self.chunk)
        return self.sent("near2", i, self.m_s.at[1 - self.r, :, at], self.n2_s.at[:, at], self.mate)

    def far2(self, i):
        at = piece(i, self.chunk)
        return self.sent("far2", i, self.s2_s.at[at], self.f2_s.at[at], self.peer)

    def feed(self, i):
        self.share(i).wait_recv()
        at = piece(i, self.chunk)
        total = self.mlp(self.a_s[at])
        for j in range(self.cols * self.reps):
            self.m_s[j % self.reps, j // self.reps, at] = total[:, j * self.lanes : (j + 1) * self.lanes]
        self.near2(i).start()

    def scatter_near(self, i):
        self.near2(i).wait_recv()
        at = piece(i, self.chunk)
        self.s2_s[at] = self.m_s[self.r, 1 - self.c, at] + self.n2_s[1 - self.c, at]
        self.far2(i).start()

    def scatter_far(self, i):
        self.far2(i).wait_recv()
        at = piece(i, self.chunk)
        own = self.a_s[at, piece(self.me, self.lanes)]
        total = (self.m_s[self.r, self.c, at] + self.n2_s[self.c, at]) + self.f2_s[at]
        self.out_ref[at] = total + own

    def body(self):
        n = self.n
        self.load_weights()
        greet([self.mate, self.peer] + self.peers)
        for i in range(n):
            self.across(i).start()
        for i in range(n):
            self.over(i).start()
        for e in range(1, self.ntok):
            self.code(e).start()
        self.arrived_ref[self.t] = self.code_ref[self.t]
        self.g_s[self.me] = self.x_ref[...]
        self.split_weights()

        def step(i, carry):
            @pl.when(i < n)
            def _():
                self.across(i).wait_recv()
                self.relay(i).start()

            @pl.when(i > 0)
            def _():
                self.over(i - 1).wait_recv()
                self.relay(i - 1).wait_recv()
                stream = self.stream_rows((i - 1) * self.chunk, self.chunk)
                self.pack(piece(i - 1, self.chunk), *self.project(stream))

            return carry

        lax.fori_loop(0, n + 1, step, 0)
        self.run(
            [
                (9, self.scatter_far), (7, self.scatter_near), (6, self.feed),
                (5, self.reduce_far), (2, self.reduce_near), (1, self.finish),
            ]
        )
        for copy in (
            self.near, self.far, self.share, self.near2, self.far2, self.across, self.over, self.relay
        ):
            for i in range(n):
                copy(i).wait_send()
        for e in range(1, self.ntok):
            self.code(e).wait()


class Second(Layer):
    def stream_rows(self, start, count):
        parts = []
        for m in range(count // self.block):
            at = self.source_ref[start // self.block + m]
            places = [self.g_s[at // self.cap, j, at % self.cap] for j in range(self.cols * self.reps)]
            parts.append(jnp.concatenate(places, axis=-1))
        return jnp.concatenate(parts, axis=0)

    def along(self, e, j):
        target = lax.rem(self.t + e, self.ntok)
        return self.sent(
            "along", e * self.cap + j, self.o_s.at[target, j], self.g_s.at[self.t, self.me, j],
            {"tok": target},
        )

    def origin(self, e):
        return lax.rem(self.t + self.ntok - e, self.ntok)

    def placed(self, kind, e, j, slot, device):
        ref = self.g_s.at[self.origin(e), slot, j]
        return self.sent(kind, e * self.cap + j, ref, ref, device)

    def across(self, e, j):
        return self.placed("across", e, j, self.me, self.peer)

    def over(self, e, j):
        return self.placed("over", e, j, self.me, self.mate)

    def relay(self, e, j):
        return self.placed("relay", e, j, (1 - self.c) * self.reps + self.r, self.mate)

    def arrive(self, e):
        for j in range(self.cap):
            if e:
                self.along(e, j).wait_recv()
            self.across(e, j).start()
            self.over(e, j).start()

    def hand(self, e):
        for j in range(self.cap):
            self.across(e, j).wait_recv()
            self.relay(e, j).start()

    def take(self, e):
        for j in range(self.cap):
            self.over(e, j).wait_recv()
            self.relay(e, j).wait_recv()
        u = self.origin(e)
        parts = []
        for j in range(self.cap):
            places = [self.g_s[u, k, j] for k in range(self.cols * self.reps)]
            parts.append(jnp.concatenate(places, axis=-1))
        for m, values in enumerate(self.project(jnp.concatenate(parts, axis=0))):
            for j in range(self.cap):
                self.raw_s[m, u * self.cap + j] = values[j * self.block : (j + 1) * self.block]

    def move(self):
        for u in range(self.ntok):
            for j in range(self.cap):
                self.o_s[u, j] = self.x_ref[self.index_ref[u * self.cap + j]]
        for j in range(self.cap):
            self.g_s[self.t, self.me, j] = self.x_ref[self.index_ref[self.t * self.cap + j]]
        order = [0]
        for e in range(1, self.ntok // 2 + 1):
            order += [e] + ([self.ntok - e] if self.ntok - e != e else [])
        for j in range(self.cap):
            for e in order[1:]:
                self.along(e, j).start()
        self.arrive(0)
        self.split_weights()
        self.split_points()
        for at, e in enumerate(order[1:]):
            self.arrive(e)
            self.hand(order[at])
            if at:
                self.take(order[at - 1])
        self.hand(order[-1])
        for e in order[-2:]:
            self.take(e)

        def step(i, carry):
            def row(m):
                each = self.chunk // self.block
                blocks = [self.raw_s[m, self.source_ref[i * each + k]] for k in range(each)]
                return jnp.concatenate(blocks, axis=0)

            self.pack(piece(i, self.chunk), row(0), row(1), row(2))
            return carry

        lax.fori_loop(0, self.n, step, 0)

    def load_points(self):
        self.point = pltpu.make_async_copy(self.pw_ref, self.pw_f, self.wsem.at[4])
        self.point.start()

    def split_points(self):
        self.point.wait()

        def step(k, carry):
            at = piece(k, 64)
            for l in range(2):
                self.pw_s[0, l, at], self.pw_s[1, l, at] = split(self.pw_f[l, at])
            return carry

        lax.fori_loop(0, self.width // 64, step, 0)

    def cell_ids(self):
        count = self.pool_s.shape[0]
        p = lax.broadcasted_iota(jnp.int32, (count, 1), 0)
        wide = TC + 2 * HALO
        row = ((p.astype(jnp.float32) + 0.5) * (1.0 / wide)).astype(jnp.int32)
        col = row // TR
        x = col * TC - HALO + (p - row * wide)
        full = TC * self.cols
        y = row - col * TR
        return jnp.where((x >= 0) & (x < full), (self.t * TR + y) * full + x, -2)

    def feed(self, i):
        self.share(i).wait_recv()
        at = piece(i, self.chunk)
        x = self.a_s[at]
        high, low = split(self.mlp(x) + x * (1.0 / (self.cols * self.reps)))
        chosen = jnp.where(self.cell_ids() == self.pillar_ref[:, at], 1.0, 0.0).astype(jnp.bfloat16)
        self.pool_s[...] += bdot(chosen, high) + bdot(chosen, low)

    def tile_part(self, c, r, k):
        cells = self.pool_s.shape[0] // (self.cols * self.reps)
        start = (c * self.reps + r) * cells + k * self.edge
        return pl.ds(pl.multiple_of(start, 8), self.edge)

    def near3(self, w, k):
        c = self.c if w else 1 - self.c
        return self.sent(
            "near3", w * self.pieces + k, self.pool_s.at[self.tile_part(c, 1 - self.r, k)],
            self.n3_s.at[w, k], self.mate,
        )

    def far3(self, k):
        return self.sent("far3", k, self.s3_s.at[k], self.f3_s.at[k], self.peer)

    def inner(self):
        start = jnp.where(self.r == 0, self.pieces * self.edge, self.edge)
        src = self.tile_s.at[pl.ds(pl.multiple_of(start, 8), self.edge)]
        return self.sent("halo", 0, src, self.h_s.at[0], self.mate)

    def outer(self):
        start = jnp.where(self.r == 0, self.edge, self.pieces * self.edge)
        src = self.tile_s.at[pl.ds(pl.multiple_of(start, 8), self.edge)]
        return self.sent("halo", 1, src, self.h_s.at[1], self.partner)

    def scatter(self):
        order = [0, self.pieces - 1] + list(range(1, self.pieces - 1))
        for w in range(2):
            for k in order:
                self.near3(w, k).start()
        for k in order:
            self.near3(0, k).wait_recv()
            self.s3_s[k] = self.pool_s[self.tile_part(1 - self.c, self.r, k)] + self.n3_s[0, k]
            self.far3(k).start()
        for at, k in enumerate(order):
            self.near3(1, k).wait_recv()
            self.far3(k).wait_recv()
            own = self.pool_s[self.tile_part(self.c, self.r, k)] + self.n3_s[1, k]
            self.tile_s[pl.ds((k + 1) * self.edge, self.edge)] = own + self.f3_s[k]
            if at == 1:
                self.inner().start()
                self.outer().start()
        self.inner().wait()
        self.outer().wait()
        wrapped = jnp.where(self.r == 0, self.t == 0, self.t == self.ntok - 1)
        beyond = jnp.where(wrapped, 0.0, self.h_s[1])
        within = self.h_s[0]
        self.tile_s[: self.edge] = jnp.where(self.r == 0, beyond, within)
        self.tile_s[(self.pieces + 1) * self.edge :] = jnp.where(self.r == 0, within, beyond)

    def raster(self):
        wide = TC + 2 * HALO
        rows = self.tile_s.shape[0] // wide
        pad = (self.flat_s.shape[0] - rows * wide) // 2
        self.flat_s[:pad] = jnp.zeros((pad, self.width), jnp.float32)
        self.flat_s[pad + rows * wide :] = jnp.zeros((pad, self.width), jnp.float32)
        for l in range(2):
            old = pl.ds(l * wide, (rows - 2 * l) * wide)
            start, count = (l + 1) * wide, (rows - 2 * l - 2) * wide
            cells = self.tile_s[old]
            square = jnp.mean(cells * cells, axis=-1, keepdims=True)
            gain = self.rg_ref[pl.ds(l, 1)]
            self.flat_s[pl.ds(pad + l * wide, (rows - 2 * l) * wide)] = (
                cells * lax.rsqrt(square + EPSILON) * gain
            )
            mixed = jnp.zeros((count, self.width), jnp.float32)
            for a in range(3):
                for b in range(3):
                    shift = pad + start + (a - 1) * wide + b - 1
                    mixed = mixed + self.flat_s[pl.ds(shift, count)] * self.dw_ref[l, a, pl.ds(b, 1)]
            both = dot3(split(mixed), (self.pw_s[0, l], self.pw_s[1, l]))
            centre = self.tile_s[pl.ds(start, count)]
            result = centre + both[:, : self.width] * jax.nn.sigmoid(both[:, self.width :])
            if l == 0:
                p = lax.broadcasted_iota(jnp.int32, (count, 1), 0) + start
                row = ((p.astype(jnp.float32) + 0.5) * (1.0 / wide)).astype(jnp.int32)
                y = (self.t * self.reps + self.r) * (rows - 2 * HALO) - HALO + row
                x = self.c * TC - HALO + (p - row * wide)
                inside = (y >= 0) & (y < TR * self.ntok) & (x >= 0) & (x < TC * self.cols)
                result = jnp.where(inside, result, 0.0)
            self.tile_s[pl.ds(start, count)] = result
        for y in range(rows - 2 * HALO):
            self.out_ref[y] = self.tile_s[pl.ds((y + HALO) * wide + HALO, TC)]

    def body(self):
        self.block = self.x_ref.shape[1]
        self.cap = self.g_s.shape[2]
        self.pieces, self.edge = self.s3_s.shape[:2]
        step = jnp.where(self.r == 0, self.ntok - 1, 1)
        self.partner = {"tok": lax.rem(self.t + step, self.ntok), "rep": 1 - self.r}
        self.load_weights()
        self.load_points()
        greet([self.mate, self.peer, self.partner] + self.peers)
        self.move()
        self.pool_s[...] = jnp.zeros(self.pool_s.shape, jnp.float32)
        self.run([(6, self.feed), (5, self.reduce_far), (2, self.reduce_near), (1, self.finish)])
        self.scatter()
        self.raster()
        for copy in (self.near, self.far, self.share):
            for i in range(self.n):
                copy(i).wait_send()
        for j in range(self.cap):
            for e in range(self.ntok):
                if e:
                    self.along(e, j).wait_send()
                for copy in (self.across, self.over, self.relay):
                    copy(e, j).wait_send()
        for k in range(self.pieces):
            self.near3(0, k).wait_send()
            self.near3(1, k).wait_send()
            self.far3(k).wait_send()


def run_layer(kind, layer, inputs, outputs, weights, collective_id, extra, kinds, most):
    w_qkv, w_out, w_up, w_down, attn_gain, mlp_gain = weights
    lanes, width, hidden = w_qkv.shape[-1], w_qkv.shape[-2], w_up.shape[-1]
    heads, rows = lanes // HD, PATCH
    chunk = min(256, rows)
    dma, f32, b16 = pltpu.SemaphoreType.DMA, jnp.float32, jnp.bfloat16
    vmem = pl.BlockSpec(memory_space=pltpu.VMEM)
    hbm = pl.BlockSpec(memory_space=pl.ANY)
    smem = pl.BlockSpec(memory_space=pltpu.SMEM)
    inputs = dict(inputs)
    places = {name: vmem for name in inputs}
    inputs.update(ga_ref=attn_gain, gm_ref=mlp_gain)
    inputs.update(wqkv_ref=w_qkv, wo_ref=w_out, wu_ref=w_up, wd_ref=w_down)
    for name in ("index_ref", "source_ref"):
        places[name] = smem
    for name in ("wqkv_ref", "wo_ref", "wu_ref", "wd_ref", "pw_ref"):
        places[name] = hbm
    scratch = dict(
        wqkv_f=pltpu.VMEM((3, width, lanes), f32),
        wo_f=pltpu.VMEM((lanes, width), f32),
        wu_f=pltpu.VMEM((width, hidden), f32),
        wd_f=pltpu.VMEM((hidden, width), f32),
        wqkv_s=pltpu.VMEM((2, 3, width, lanes), b16),
        wo_s=pltpu.VMEM((2, lanes, width), b16),
        wu_s=pltpu.VMEM((2, width, hidden), b16),
        wd_s=pltpu.VMEM((2, hidden, width), b16),
        q_s=pltpu.VMEM((2, rows, 2 * lanes), b16),
        k_s=pltpu.VMEM((heads, rows, 2 * lanes), b16),
        v_s=pltpu.VMEM((heads, rows, 2 * lanes), b16),
        att_s=pltpu.VMEM((2, chunk, lanes), f32),
        p_s=pltpu.VMEM((rows, width), f32),
        n1_s=pltpu.VMEM((rows // 2, width), f32),
        s1_s=pltpu.VMEM((rows // 2, width), f32),
        f1_s=pltpu.VMEM((rows // 2, width), f32),
        a_s=pltpu.VMEM((rows, width), f32),
        sem=dma((len(kinds), 2, max(most, rows // chunk))),
        wsem=dma((5,)),
    )
    scratch.update(extra)
    names = list(inputs) + list(outputs) + list(scratch)

    def kernel(*refs):
        kind(layer, dict(zip(names, refs)), heads, chunk, kinds).body()

    return pl.pallas_call(
        kernel,
        out_shape=tuple(outputs.values()),
        in_specs=[places.get(name, vmem) for name in inputs],
        out_specs=tuple(vmem for _ in outputs),
        scratch_shapes=list(scratch.values()),
        compiler_params=pltpu.CompilerParams(
            collective_id=collective_id, has_side_effects=True, vmem_limit_bytes=VMEM_LIMIT
        ),
        name=kind.__name__.lower(),
    )(*inputs.values())


def first_layer(tokens, codes, weights, collective_id):
    rows, lanes = tokens.shape
    cols, reps = lax.axis_size("col"), lax.axis_size("rep")
    f32 = jnp.float32
    extra = dict(
        g_s=pltpu.VMEM((cols * reps, rows, lanes), f32),
        m_s=pltpu.VMEM((reps, cols, rows, lanes), f32),
        n2_s=pltpu.VMEM((cols, rows, lanes), f32),
        s2_s=pltpu.VMEM((rows, lanes), f32),
        f2_s=pltpu.VMEM((rows, lanes), f32),
    )
    kinds = ("near", "far", "share", "near2", "far2", "across", "over", "relay", "code")
    outputs = dict(
        out_ref=jax.ShapeDtypeStruct((rows, lanes), f32),
        arrived_ref=jax.ShapeDtypeStruct(codes.shape, codes.dtype),
    )
    inputs = dict(x_ref=tokens, code_ref=codes)
    return run_layer(First, 0, inputs, outputs, weights, collective_id, extra, kinds, lax.axis_size("tok"))


def second_layer(share, index, source, pillar, raster_weights, weights, collective_id):
    cols, reps, ntok = lax.axis_size("col"), lax.axis_size("rep"), lax.axis_size("tok")
    count, block, lanes = share.shape
    cap = index.shape[0] // ntok
    depth_weight, point_weight, raster_gain = raster_weights
    width = depth_weight.shape[-1]
    wide, rep_rows = TC + 2 * HALO, TR // reps
    edge, pieces = HALO * wide, rep_rows // HALO
    tile = (rep_rows + 2 * HALO) * wide
    f32 = jnp.float32
    extra = dict(
        o_s=pltpu.VMEM((ntok, cap, block, lanes), f32),
        g_s=pltpu.VMEM((ntok, cols * reps, cap, block, lanes), f32),
        raw_s=pltpu.VMEM((3, ntok * cap, block, lanes), f32),
        pw_f=pltpu.VMEM(point_weight.shape, f32),
        pw_s=pltpu.VMEM((2,) + point_weight.shape, jnp.bfloat16),
        pool_s=pltpu.VMEM((cols * reps * rep_rows * wide, width), f32),
        n3_s=pltpu.VMEM((2, pieces, edge, width), f32),
        s3_s=pltpu.VMEM((pieces, edge, width), f32),
        f3_s=pltpu.VMEM((pieces, edge, width), f32),
        h_s=pltpu.VMEM((2, edge, width), f32),
        tile_s=pltpu.VMEM((tile, width), f32),
        flat_s=pltpu.VMEM((tile + 16, width), f32),
    )
    kinds = ("near", "far", "share", "along", "across", "over", "relay", "near3", "far3", "halo")
    outputs = dict(out_ref=jax.ShapeDtypeStruct((rep_rows, TC, width), f32))
    inputs = dict(
        index_ref=index, source_ref=source, x_ref=share, pillar_ref=pillar[None, :],
        dw_ref=depth_weight, rg_ref=raster_gain, pw_ref=point_weight,
    )
    return run_layer(Second, 1, inputs, outputs, weights, collective_id, extra, kinds, ntok * cap)[0]


HALO = 2


def routes(dest_device, dest_slot):
    count = dest_device.shape[0]
    peers = lax.axis_size("tok")
    capacity = max(2, (count + peers - 4) // (peers - 1))
    order = jnp.arange(count, dtype=jnp.int32)
    earlier = (dest_device[:, None] == dest_device[None, :]) & (order[None, :] < order[:, None])
    place = dest_device * capacity + jnp.sum(earlier.astype(jnp.int32), axis=1)
    chosen = jnp.arange(peers * capacity, dtype=jnp.int32)[:, None] == place[None, :]
    index = jnp.sum(jnp.where(chosen, order[None, :], 0), axis=1)
    code = jnp.sum(jnp.where(chosen, dest_slot[None, :] + 1, 0), axis=1)
    code = jnp.pad(code.reshape(peers, capacity), ((0, 0), (0, 128 - capacity)))
    code = jnp.broadcast_to(code[:, None, :], (peers, 8, 128)).astype(jnp.float32)
    return index, code, capacity


def places(arrived, capacity, order):
    held = arrived[:, 0, :capacity].reshape(-1).astype(jnp.int32)
    found = held[None, :] == order[:, None] + 1
    return jnp.sum(jnp.where(found, jnp.arange(held.shape[0], dtype=jnp.int32)[None, :], 0), axis=1)


def raster_cells(extended, depth_weight, point_weight, gain_row):
    row_count = extended.shape[0] - 2
    col_count = extended.shape[1] - 2
    channels = extended.shape[2]
    normed = (
        extended
        * lax.rsqrt(jnp.mean(extended * extended, axis=-1, keepdims=True) + EPSILON)
        * gain_row
    )
    mixed = jnp.zeros((row_count, col_count, channels), jnp.float32)
    for a in range(3):
        for b in range(3):
            mixed = mixed + normed[a : a + row_count, b : b + col_count] * depth_weight[a, b]
    combined = matmul(mixed.reshape(row_count * col_count, channels), point_weight)
    combined = combined.reshape(row_count, col_count, 2 * channels)
    centre = extended[1:-1, 1:-1]
    return centre + combined[..., :channels] * jax.nn.sigmoid(combined[..., channels:])


def extended_cells(tok, members, rep_rows, full_width):
    cols, reps = members
    tile = []
    for col in range(cols):
        for rep in range(reps):
            y = rep * rep_rows - HALO + jnp.arange(rep_rows + 2 * HALO, dtype=jnp.int32)[:, None]
            x = col * TC - HALO + jnp.arange(TC + 2 * HALO, dtype=jnp.int32)[None, :]
            good = (y >= 0) & (y < TR) & (x >= 0) & (x < full_width)
            tile.append(jnp.where(good, (tok * TR + y) * full_width + x, -2).reshape(-1))
    return jnp.concatenate(tile)


def pool(partial, pillar, cells):
    onehot = (cells[:, None] == pillar[None, :]).astype(jnp.float32)
    return matmul(onehot, partial)


def exchange_rows(tile, ntok, reps):
    count = ntok * reps
    rep = lax.axis_index("rep")
    forward = [(i, i + 1) for i in range(count - 1)]
    backward = [(i + 1, i) for i in range(count - 1)]
    above = lax.ppermute(tile[-2 * HALO : -HALO], ("tok", "rep"), forward)
    below = lax.ppermute(tile[HALO : 2 * HALO], ("tok", "rep"), backward)
    above = jnp.where(rep == 0, above, tile[:HALO])
    below = jnp.where(rep == reps - 1, below, tile[-HALO:])
    return jnp.concatenate([above, tile[HALO:-HALO], below], axis=0)


def on_device(
    tokens,
    w_qkv,
    w_out,
    w_up,
    w_down,
    attn_gain,
    mlp_gain,
    dest_device,
    dest_slot,
    pillar,
    depth_weight,
    point_weight,
    raster_gain,
):
    members = (lax.axis_size("col"), lax.axis_size("rep"))
    group = members[0] * members[1]
    ntok = lax.axis_size("tok")
    block_count = dest_device.shape[0]
    order = jnp.arange(block_count, dtype=jnp.int32)
    index, codes, capacity = routes(dest_device, dest_slot)
    width = tokens.shape[1]
    weights = (w_qkv, w_out, w_up, w_down, attn_gain, mlp_gain)
    whole = (2 * members[1] * HALO * (TC + 2 * HALO)) % 8 == 0 and TR % (members[1] * HALO) == 0
    if members == (2, 2) and ntok > 1 and tokens.shape[0] == PATCH and whole:
        share, arrived = first_layer(tokens, codes, weights, 1)
        source = places(arrived, capacity, order)
        share = share.reshape(block_count, -1, width)
        raster_weights = (depth_weight, point_weight, raster_gain)
        return second_layer(share, index, source, pillar, raster_weights, weights, 5)
    blocks = gather(tokens, 1).reshape(1, group, block_count, -1, width)
    stream = attention_layer(blocks, order, 0, w_qkv, w_out, attn_gain, 2)
    share = scatter(mlp_partial(stream, 0, w_up, w_down, mlp_gain, group), 3)
    outgoing = pick(share.reshape(block_count, -1, width), index)
    outgoing = outgoing.reshape(ntok, -1, width)
    moved, arrived = move(outgoing, codes, 4)
    blocks = moved.reshape(ntok, group, capacity, -1, width)
    source = places(arrived, capacity, order)
    stream = attention_layer(blocks, source, 1, w_qkv, w_out, attn_gain, 5)
    partial = mlp_partial(stream, 1, w_up, w_down, mlp_gain, 1)[0]

    rep_rows = TR // members[1]
    full_width = TC * members[0]
    cells = extended_cells(lax.axis_index("tok"), members, rep_rows, full_width)
    pooled = pool(partial, pillar, cells)
    parts = pooled.reshape(group, -1, pooled.shape[1])
    edge = HALO * (TC + 2 * HALO)
    inside_kernel = members[0] > 1 and members[1] == 2 and ntok > 1 and edge % 8 == 0
    tile = scatter(parts, 6, edge if inside_kernel else 0)
    tile = tile.reshape(rep_rows + 2 * HALO, TC + 2 * HALO, -1)
    if not inside_kernel:
        tile = exchange_rows(tile, ntok, members[1])
    first = raster_cells(tile, depth_weight[0], point_weight[0], raster_gain[0])
    y = lax.axis_index(("tok", "rep")) * rep_rows - 1 + jnp.arange(rep_rows + 2)[:, None, None]
    x = lax.axis_index("col") * TC - 1 + jnp.arange(TC + 2)[None, :, None]
    inside = (y >= 0) & (y < TR * ntok) & (x >= 0) & (x < full_width)
    first = jnp.where(inside, first, 0.0)
    return raster_cells(first, depth_weight[1], point_weight[1], raster_gain[1])


def solution(mesh):
    placed = (
        P(("scene", "tok"), ("col", "rep")),
        P(None, None, None, ("col", "rep")),
        P(None, ("col", "rep"), None),
        P(None, None, ("col", "rep")),
        P(None, ("col", "rep"), None),
        P(),
        P(),
        P(("scene", "tok")),
        P(("scene", "tok")),
        P(("scene", "tok")),
        P(),
        P(),
        P(),
    )
    return jax.shard_map(
        on_device,
        mesh=mesh,
        in_specs=placed,
        out_specs=P(("scene", "tok", "rep"), "col", None),
        check_vma=False,
    )
```

```python
import functools
import math

import jax
import jax.numpy as jnp
from jax import lax
from jax.experimental import pallas as pl
from jax.experimental.pallas import tpu as pltpu
from jax.sharding import PartitionSpec as P

PATCH = 1024
TR = 16
TC = 16
HD = 16


MATMUL_PRECISION = lax.Precision.HIGH
EPSILON = 1e-05


def layer_norm(values, gain_row):
    average = jnp.mean(values, axis=-1, keepdims=True)
    centered = values - average
    variance = jnp.mean(centered * centered, axis=-1, keepdims=True)
    return centered * lax.rsqrt(variance + EPSILON) * gain_row


def split(values):
    high = values.astype(jnp.bfloat16)
    return high, (values - high.astype(jnp.float32)).astype(jnp.bfloat16)


def bdot(left, right, dims=(((1,), (0,)), ((), ()))):
    return lax.dot_general(left, right, dims, preferred_element_type=jnp.float32)


def dot3(left, right):
    lh, ll = left
    rh, rl = right
    return bdot(lh, rh) + bdot(lh, rl) + bdot(ll, rh)


def attention_kernel(share, source_ref, x_ref, gain_ref, w_ref, o_ref, out_ref, q_s, k_s, v_s, att_s):
    cols = w_ref.shape[-1]
    heads = cols // HD
    rows = out_ref.shape[0]
    chunk = att_s.shape[0]
    slots, each, block = x_ref.shape[1:4]
    first_block = pl.program_id(0) * (rows // block)

    def stream_rows(i):
        parts = []
        for n in range(chunk // block):
            at = source_ref[first_block + i * (chunk // block) + n]
            places = [x_ref[at // each, j, at % each] for j in range(slots)]
            parts.append(jnp.concatenate(places, axis=-1))
        return jnp.concatenate(parts, axis=0)

    lanes = q_s.shape[-1]

    r = lax.broadcasted_iota(jnp.int32, (cols, lanes), 0)
    c = lax.broadcasted_iota(jnp.int32, (cols, lanes), 1)
    lane = lax.broadcasted_iota(jnp.int32, (1, cols), 1)
    w = [split(w_ref[j]) for j in range(3)]
    for i in range(rows // chunk):
        at = pl.ds(i * chunk, chunk)
        normed = split(layer_norm(stream_rows(i), gain_ref[...]))
        qh, ql = split(dot3(normed, w[0]) * (HD ** (-0.5) * math.log2(math.e)))
        kh, kl = split(dot3(normed, w[1]))
        vh, vl = split(dot3(normed, w[2]))
        for h in range(heads):
            part = c // HD
            inside = (r // HD == h) & (r % HD == c % HD)
            first = (inside & ((part == 0) | (part == 1))).astype(jnp.bfloat16)
            third = (inside & (part == 2)).astype(jnp.bfloat16)
            outer = (inside & ((part == 0) | (part == 2))).astype(jnp.bfloat16)
            middle = (inside & (part == 1)).astype(jnp.bfloat16)
            q_s[h, at, :] = (bdot(qh, first) + bdot(ql, third)).astype(jnp.bfloat16)
            k_s[h, at, :] = (bdot(kh, outer) + bdot(kl, middle)).astype(jnp.bfloat16)
            own = lane // HD == h
            v_s[h, at, :cols] = jnp.where(own, vh.astype(jnp.float32), 0.0).astype(jnp.bfloat16)
            v_s[h, at, cols:] = jnp.where(own, vl.astype(jnp.float32), 1.0).astype(jnp.bfloat16)

    projection = split(o_ref[...])

    def query_rows(i, carry):
        at = pl.ds(pl.multiple_of(i * chunk, chunk), chunk)
        att_s[...] = jnp.zeros_like(att_s)

        def one_head(h, carry):
            scores = bdot(q_s[h, at, :], k_s[h], (((1,), (1,)), ((), ())))
            weights = jnp.exp2(scores - jnp.max(scores, axis=-1, keepdims=True))
            wh, wl = split(weights)
            sums = bdot(wh, v_s[h]) + bdot(wl, v_s[h])
            top, low = sums[:, :cols], sums[:, cols:]
            own = lane // HD == h
            total = jnp.max(jnp.where(own, 0.0, low), axis=-1, keepdims=True)
            att_s[...] += jnp.where(own, (top + low) / total, 0.0)
            return carry

        lax.fori_loop(0, heads, one_head, 0, unroll=4)
        out_ref[at, :] = dot3(split(att_s[...]), projection) + stream_rows(i) * share
        return carry

    lax.fori_loop(0, rows // chunk, query_rows, 0)


def attend(blocks, source, gain_row, weights, w_out, group):
    block, width = blocks.shape[3], blocks.shape[1] * blocks.shape[4]
    rows = source.shape[0] * block
    cols = weights.shape[-1]
    heads = cols // HD
    lanes = max(128, 3 * HD)
    return pl.pallas_call(
        functools.partial(attention_kernel, 1.0 / group),
        grid_spec=pltpu.PrefetchScalarGridSpec(
            num_scalar_prefetch=1,
            grid=(rows // PATCH,),
            in_specs=[
                pl.BlockSpec(blocks.shape, lambda i, source: (0, 0, 0, 0, 0)),
                pl.BlockSpec((1, width), lambda i, source: (0, 0)),
                pl.BlockSpec(weights.shape, lambda i, source: (0, 0, 0)),
                pl.BlockSpec(w_out.shape, lambda i, source: (0, 0)),
            ],
            out_specs=pl.BlockSpec((PATCH, width), lambda i, source: (i, 0)),
            scratch_shapes=[
                pltpu.VMEM((heads, PATCH, lanes), jnp.bfloat16),
                pltpu.VMEM((heads, PATCH, lanes), jnp.bfloat16),
                pltpu.VMEM((heads, PATCH, 2 * cols), jnp.bfloat16),
                pltpu.VMEM((256, cols), jnp.float32),
            ],
        ),
        out_shape=jax.ShapeDtypeStruct((rows, width), jnp.float32),
        compiler_params=pltpu.CompilerParams(vmem_limit_bytes=48 * 1024 * 1024),
        name="attend",
    )(source, blocks, gain_row[None, :], weights, w_out)


def matmul(left, right):
    return jnp.dot(left, right, precision=MATMUL_PRECISION, preferred_element_type=jnp.float32)


VMEM_LIMIT = 56 * 1024 * 1024
MESH = pl.DeviceIdType.MESH


def position():
    cols, reps = lax.axis_size("col"), lax.axis_size("rep")
    return cols, reps, lax.axis_index("col"), lax.axis_index("rep")


def greet(devices):
    barrier = pltpu.get_barrier_semaphore()
    for device in devices:
        pl.semaphore_signal(barrier, inc=1, device_id=device, device_id_type=MESH)
    pl.semaphore_wait(barrier, len(devices))


def remote(src, dst, send, recv, device):
    return pltpu.make_async_remote_copy(
        src_ref=src, dst_ref=dst, send_sem=send, recv_sem=recv, device_id=device, device_id_type=MESH
    )


def chunks_of(rows):
    for pieces in (8, 5, 4, 2):
        if rows % (8 * pieces) == 0:
            return pieces, rows // pieces
    return 1, rows


def gather_kernel(x_ref, out_ref, xs, xr, fs, fr, ps, pr, local):
    cols, reps, c, r = position()
    rows = x_ref.shape[0]
    pieces, size = chunks_of(rows)
    me = c * reps + r
    mate = {"col": c, "rep": 1 - r}
    others = [{"col": lax.rem(c + d, cols), "rep": r} for d in range(1, cols)]
    greet([mate] + others)
    across, onward = [], []
    for k in range(pieces):
        at = pl.ds(k * size, size)
        for d in range(1, cols):
            copy = remote(
                x_ref.at[at], out_ref.at[me, at], xs.at[d - 1, k], xr.at[d - 1, k], others[d - 1]
            )
            copy.start()
            across.append(copy)
    share = remote(x_ref, out_ref.at[me], ps, pr, mate)
    share.start()
    keep = pltpu.make_async_copy(x_ref, out_ref.at[me], local)
    keep.start()
    for k in range(pieces):
        at = pl.ds(k * size, size)
        for d in range(1, cols):
            across[k * (cols - 1) + d - 1].wait_recv()
            slot = lax.rem(c + cols - d, cols) * reps + r
            copy = remote(
                out_ref.at[slot, at], out_ref.at[slot, at], fs.at[d - 1, k], fr.at[d - 1, k], mate
            )
            copy.start()
            onward.append(copy)
    for copy in across:
        copy.wait_send()
    share.wait()
    keep.wait()
    for copy in onward:
        copy.wait()


def gather(block, collective_id):
    cols, reps = lax.axis_size("col"), lax.axis_size("rep")
    if reps != 2 or cols < 2:
        return lax.all_gather(block, ("col", "rep"), axis=0)
    pieces, _ = chunks_of(block.shape[0])
    dma = pltpu.SemaphoreType.DMA
    return pl.pallas_call(
        gather_kernel,
        out_shape=jax.ShapeDtypeStruct((cols * reps,) + block.shape, block.dtype),
        in_specs=[pl.BlockSpec(memory_space=pltpu.VMEM)],
        out_specs=pl.BlockSpec(memory_space=pltpu.VMEM),
        scratch_shapes=[dma((cols - 1, pieces))] * 4 + [dma, dma, dma],
        compiler_params=pltpu.CompilerParams(
            collective_id=collective_id, has_side_effects=True, vmem_limit_bytes=VMEM_LIMIT
        ),
        name="gather",
    )(block)


def scatter_kernel(edge, p_ref, out_ref, a_ref, s_ref, b_ref, a_s, a_r, b_s, b_r, *halo):
    cols, reps, c, r = position()
    rows = p_ref.shape[1]
    pieces, size = chunks_of(rows)
    mate = {"col": c, "rep": 1 - r}
    others = [{"col": lax.rem(c + d, cols), "rep": r} for d in range(1, cols)]
    greeted = [mate] + others
    if edge:
        ntok, t = lax.axis_size("tok"), lax.axis_index("tok")
        partner = {"tok": lax.rem(t + jnp.where(r == 0, ntok - 1, 1), ntok), "rep": 1 - r}
        greeted = greeted + [partner]
    greet(greeted)
    order = [(k, d) for k in range(pieces) for d in range(1, cols)]
    order += [(k, 0) for k in range(pieces)]
    near, far = {}, {}
    for k, d in order:
        at = pl.ds(k * size, size)
        slot = lax.rem(c + d, cols) * reps + 1 - r
        near[k, d] = remote(
            p_ref.at[slot, at], a_ref.at[d, at], a_s.at[d, k], a_r.at[d, k], mate
        )
        near[k, d].start()
    for k, d in order:
        at = pl.ds(k * size, size)
        slot = lax.rem(c + d, cols) * reps + r
        near[k, d].wait_recv()
        total = p_ref[slot, at] + a_ref[d, at]
        if d == 0:
            out_ref[at] = total
        else:
            s_ref[d - 1, at] = total
            far[k, d] = remote(
                s_ref.at[d - 1, at],
                b_ref.at[d - 1, at],
                b_s.at[d - 1, k],
                b_r.at[d - 1, k],
                others[d - 1],
            )
            far[k, d].start()
    for (k, d), copy in far.items():
        at = pl.ds(k * size, size)
        copy.wait_recv()
        out_ref[at] += b_ref[d - 1, at]
    if edge:
        h_ref, e_ref, h_s, h_r = halo
        inner = pl.multiple_of(jnp.where(r == 0, edge, rows - 2 * edge), 8)
        outer = pl.multiple_of(jnp.where(r == 0, 0, rows - edge), 8)
        e_ref[...] = out_ref[pl.ds(inner, edge)]
        copy = remote(e_ref, h_ref, h_s, h_r, partner)
        copy.start()
        copy.wait()
        wrapped = jnp.where(r == 0, t == 0, t == ntok - 1)
        out_ref[pl.ds(outer, edge)] = jnp.where(wrapped, 0.0, h_ref[...])
    for copy in list(near.values()) + list(far.values()):
        copy.wait_send()


def scatter(parts, collective_id, edge=0):
    cols, reps = lax.axis_size("col"), lax.axis_size("rep")
    if reps != 2 or cols < 2:
        return lax.psum_scatter(parts, ("col", "rep"), scatter_dimension=0)
    shape, kind = parts.shape[1:], parts.dtype
    pieces, _ = chunks_of(shape[0])
    dma = pltpu.SemaphoreType.DMA
    return pl.pallas_call(
        functools.partial(scatter_kernel, edge),
        out_shape=jax.ShapeDtypeStruct(shape, kind),
        in_specs=[pl.BlockSpec(memory_space=pltpu.VMEM)],
        out_specs=pl.BlockSpec(memory_space=pltpu.VMEM),
        scratch_shapes=[
            pltpu.VMEM((cols,) + shape, kind),
            pltpu.VMEM((cols - 1,) + shape, kind),
            pltpu.VMEM((cols - 1,) + shape, kind),
            dma((cols, pieces)),
            dma((cols, pieces)),
            dma((cols - 1, pieces)),
            dma((cols - 1, pieces)),
        ]
        + ([pltpu.VMEM((edge, shape[1]), kind)] * 2 + [dma, dma] if edge else []),
        compiler_params=pltpu.CompilerParams(
            collective_id=collective_id, has_side_effects=True, vmem_limit_bytes=VMEM_LIMIT
        ),
        name="scatter",
    )(parts)


def total_kernel(
    p_ref, out_ref, a_ref, s_ref, b_ref, a_s, a_r, b_s, b_r, xs, xr, fs, fr, ps, pr
):
    cols, reps, c, r = position()
    rows = p_ref.shape[1]
    pieces, size = chunks_of(rows)
    me = c * reps + r
    mate = {"col": c, "rep": 1 - r}
    others = [{"col": lax.rem(c + d, cols), "rep": r} for d in range(1, cols)]
    greet([mate] + others)
    order = [(k, d) for k in range(pieces) for d in range(1, cols)]
    order += [(k, 0) for k in range(pieces)]
    near, far, across, share, onward = {}, {}, {}, {}, {}
    for k, d in order:
        at = pl.ds(k * size, size)
        slot = lax.rem(c + d, cols) * reps + 1 - r
        near[k, d] = remote(
            p_ref.at[slot, at], a_ref.at[d, at], a_s.at[d, k], a_r.at[d, k], mate
        )
        near[k, d].start()
    for k, d in order:
        if d == 0:
            continue
        at = pl.ds(k * size, size)
        slot = lax.rem(c + d, cols) * reps + r
        near[k, d].wait_recv()
        s_ref[d - 1, at] = p_ref[slot, at] + a_ref[d, at]
        far[k, d] = remote(
            s_ref.at[d - 1, at], b_ref.at[d - 1, at], b_s.at[d - 1, k], b_r.at[d - 1, k], others[d - 1]
        )
        far[k, d].start()
    for k in range(pieces):
        at = pl.ds(k * size, size)
        near[k, 0].wait_recv()
        total = p_ref[me, at] + a_ref[0, at]
        for d in range(1, cols):
            far[k, d].wait_recv()
            total = total + b_ref[d - 1, at]
        out_ref[me, at] = total
        for d in range(1, cols):
            across[k, d] = remote(
                out_ref.at[me, at], out_ref.at[me, at], xs.at[d - 1, k], xr.at[d - 1, k], others[d - 1]
            )
            across[k, d].start()
        share[k] = remote(out_ref.at[me, at], out_ref.at[me, at], ps.at[k], pr.at[k], mate)
        share[k].start()
    for (k, d), copy in across.items():
        at = pl.ds(k * size, size)
        copy.wait_recv()
        slot = lax.rem(c + cols - d, cols) * reps + r
        onward[k, d] = remote(
            out_ref.at[slot, at], out_ref.at[slot, at], fs.at[d - 1, k], fr.at[d - 1, k], mate
        )
        onward[k, d].start()
    for copies in (near, far, across):
        for copy in copies.values():
            copy.wait_send()
    for copies in (share, onward):
        for copy in copies.values():
            copy.wait()


def total(parts, collective_id):
    cols, reps = lax.axis_size("col"), lax.axis_size("rep")
    if reps != 2 or cols < 2:
        return lax.psum(parts, ("col", "rep"))
    shape, kind = parts.shape[1:], parts.dtype
    pieces, _ = chunks_of(shape[0])
    dma = pltpu.SemaphoreType.DMA
    return pl.pallas_call(
        total_kernel,
        out_shape=jax.ShapeDtypeStruct(parts.shape, kind),
        in_specs=[pl.BlockSpec(memory_space=pltpu.VMEM)],
        out_specs=pl.BlockSpec(memory_space=pltpu.VMEM),
        scratch_shapes=[
            pltpu.VMEM((cols,) + shape, kind),
            pltpu.VMEM((cols - 1,) + shape, kind),
            pltpu.VMEM((cols - 1,) + shape, kind),
            dma((cols, pieces)),
            dma((cols, pieces)),
        ]
        + [dma((cols - 1, pieces))] * 6
        + [dma((pieces,))] * 2,
        compiler_params=pltpu.CompilerParams(
            collective_id=collective_id, has_side_effects=True, vmem_limit_bytes=VMEM_LIMIT
        ),
        name="total",
    )(parts)


def move_kernel(o_ref, code_ref, out_ref, arrived_ref, zs, zr, cs, cr, xs, xr, fs, fr, ps, pr, local):
    cols, reps, c, r = position()
    ntok, t = lax.axis_size("tok"), lax.axis_index("tok")
    me = c * reps + r
    mate = {"col": c, "rep": 1 - r}
    others = [{"col": lax.rem(c + d, cols), "rep": r} for d in range(1, cols)]
    peers = [{"tok": lax.rem(t + e, ntok)} for e in range(1, ntok)]
    greet([mate] + others + peers)
    along, codes, across, share, onward = [], [], {}, [], []
    for e in range(1, ntok):
        target = lax.rem(t + e, ntok)
        copy = remote(o_ref.at[target], out_ref.at[t, me], zs.at[e - 1], zr.at[e - 1], peers[e - 1])
        copy.start()
        along.append(copy)
        copy = remote(
            code_ref.at[target], arrived_ref.at[t], cs.at[e - 1], cr.at[e - 1], peers[e - 1]
        )
        copy.start()
        codes.append(copy)
    keep = pltpu.make_async_copy(o_ref.at[t], out_ref.at[t, me], local.at[0])
    keep.start()
    keep_code = pltpu.make_async_copy(code_ref.at[t], arrived_ref.at[t], local.at[1])
    keep_code.start()

    def hand_on(e):
        u = lax.rem(t + ntok - e, ntok)
        for d in range(1, cols):
            across[e, d].wait_recv()
            slot = lax.rem(c + cols - d, cols) * reps + r
            copy = remote(
                out_ref.at[u, slot], out_ref.at[u, slot], fs.at[e, d - 1], fr.at[e, d - 1], mate
            )
            copy.start()
            onward.append(copy)

    for e in range(ntok):
        u = lax.rem(t + ntok - e, ntok)
        if e:
            along[e - 1].wait_recv()
        origin = out_ref.at[u, me] if e else o_ref.at[t]
        for d in range(1, cols):
            across[e, d] = remote(
                origin, out_ref.at[u, me], xs.at[e, d - 1], xr.at[e, d - 1], others[d - 1]
            )
            across[e, d].start()
        copy = remote(origin, out_ref.at[u, me], ps.at[e], pr.at[e], mate)
        copy.start()
        share.append(copy)
        if e:
            hand_on(e - 1)
    hand_on(ntok - 1)
    keep.wait()
    keep_code.wait()
    for copy in along + list(across.values()):
        copy.wait_send()
    for copy in codes + share + onward:
        copy.wait()


def move(outgoing, codes, collective_id):
    cols, reps, ntok = lax.axis_size("col"), lax.axis_size("rep"), lax.axis_size("tok")
    if reps != 2 or cols < 2 or ntok < 2:
        incoming = lax.all_to_all(outgoing, "tok", split_axis=0, concat_axis=0, tiled=True)
        arrived = lax.all_to_all(codes, "tok", split_axis=0, concat_axis=0, tiled=True)
        return lax.all_gather(incoming, ("col", "rep"), axis=1), arrived
    dma = pltpu.SemaphoreType.DMA
    shape = (ntok, cols * reps) + outgoing.shape[1:]
    return pl.pallas_call(
        move_kernel,
        out_shape=(
            jax.ShapeDtypeStruct(shape, outgoing.dtype),
            jax.ShapeDtypeStruct(codes.shape, codes.dtype),
        ),
        in_specs=[pl.BlockSpec(memory_space=pltpu.VMEM)] * 2,
        out_specs=[pl.BlockSpec(memory_space=pltpu.VMEM)] * 2,
        scratch_shapes=[dma((ntok - 1,))] * 4
        + [dma((ntok, cols - 1))] * 4
        + [dma((ntok,))] * 2
        + [dma((2,))],
        compiler_params=pltpu.CompilerParams(
            collective_id=collective_id, has_side_effects=True, vmem_limit_bytes=VMEM_LIMIT
        ),
        name="move",
    )(outgoing, codes)


def pick_kernel(index_ref, x_ref, out_ref):
    for j in range(out_ref.shape[0]):
        out_ref[j] = x_ref[index_ref[j]]


def pick(blocks, index):
    return pl.pallas_call(
        pick_kernel,
        out_shape=jax.ShapeDtypeStruct(index.shape + blocks.shape[1:], blocks.dtype),
        in_specs=[pl.BlockSpec(memory_space=pltpu.SMEM), pl.BlockSpec(memory_space=pltpu.VMEM)],
        out_specs=pl.BlockSpec(memory_space=pltpu.VMEM),
        name="pick",
    )(index, blocks)


def attention_layer(blocks, source, layer, w_qkv, w_out, attn_gain, collective_id):
    group = blocks.shape[1]
    terms = attend(blocks, source, attn_gain[layer], w_qkv[layer], w_out[layer], group)
    rows, width = terms.shape
    return total(terms.reshape(group, rows // group, width), collective_id).reshape(rows, width)


def mlp_kernel(x_ref, gain_ref, up_ref, down_ref, share, out_ref):
    x = x_ref[...]
    hidden = dot3(split(layer_norm(x, gain_ref[...])), split(up_ref[...]))
    hidden = 0.5 * hidden * (1.0 + lax.erf(hidden * (0.5**0.5)))
    total = dot3(split(hidden), split(down_ref[...])) + x * share
    width = out_ref.shape[-1]
    for j in range(out_ref.shape[0]):
        out_ref[j] = total[:, j * width : (j + 1) * width]


def mlp_partial(stream, layer, w_up, w_down, mlp_gain, slots):
    rows, width = stream.shape
    tile = min(256, rows)
    hidden = w_up.shape[-1]
    group = lax.axis_size("col") * lax.axis_size("rep")

    def kernel(x_ref, gain_ref, up_ref, down_ref, out_ref):
        mlp_kernel(x_ref, gain_ref, up_ref, down_ref, 1.0 / group, out_ref)

    return pl.pallas_call(
        kernel,
        grid=(rows // tile,),
        in_specs=[
            pl.BlockSpec((tile, width), lambda i: (i, 0)),
            pl.BlockSpec((1, width), lambda i: (0, 0)),
            pl.BlockSpec((width, hidden), lambda i: (0, 0)),
            pl.BlockSpec((hidden, width), lambda i: (0, 0)),
        ],
        out_specs=pl.BlockSpec((slots, tile, width // slots), lambda i: (0, i, 0)),
        out_shape=jax.ShapeDtypeStruct((slots, rows, width // slots), jnp.float32),
        compiler_params=pltpu.CompilerParams(vmem_limit_bytes=48 * 1024 * 1024),
        name="mlp",
    )(stream, mlp_gain[layer][None, :], w_up[layer], w_down[layer])


def gelu(values):
    return 0.5 * values * (1.0 + lax.erf(values * (0.5**0.5)))


def piece(i, size):
    return pl.ds(pl.multiple_of(i * size, size), size)


class Layer:
    def __init__(self, layer, refs, heads, chunk, kinds):
        self.__dict__.update(refs)
        self.layer, self.heads, self.chunk, self.kinds = layer, heads, chunk, kinds
        self.cols, self.reps, self.c, self.r = position()
        self.ntok, self.t = lax.axis_size("tok"), lax.axis_index("tok")
        self.me = self.c * self.reps + self.r
        self.mate, self.peer = {"rep": 1 - self.r}, {"col": 1 - self.c}
        self.peers = [{"tok": lax.rem(self.t + e, self.ntok)} for e in range(1, self.ntok)]
        self.rows, self.width = self.a_s.shape
        self.lanes = self.q_s.shape[-1] // 2
        self.n = self.rows // chunk
        self.started = []

    def sent(self, kind, i, src, dst, device):
        k = self.kinds.index(kind)
        return remote(src, dst, self.sem.at[k, 0, i], self.sem.at[k, 1, i], device)

    def load_weights(self):
        pairs = (
            (self.wqkv_ref, self.wqkv_f), (self.wo_ref, self.wo_f),
            (self.wu_ref, self.wu_f), (self.wd_ref, self.wd_f),
        )
        self.loads = [
            pltpu.make_async_copy(src.at[self.layer], dst, self.wsem.at[j])
            for j, (src, dst) in enumerate(pairs)
        ]
        for load in self.loads:
            load.start()

    def split_weights(self):
        self.loads[0].wait()
        for m in range(3):
            self.wqkv_s[0, m], self.wqkv_s[1, m] = split(self.wqkv_f[m])
        rest = ((self.wo_f, self.wo_s), (self.wu_f, self.wu_s), (self.wd_f, self.wd_s))
        for load, (src, dst) in zip(self.loads[1:], rest):
            load.wait()
            dst[0], dst[1] = split(src[...])

    def project(self, stream):
        normed = split(layer_norm(stream, self.ga_ref[pl.ds(self.layer, 1)]))
        return [dot3(normed, (self.wqkv_s[0, m], self.wqkv_s[1, m])) for m in range(3)]

    def pack(self, at, q, k, v):
        lanes = self.lanes
        half_lanes = lanes // 2
        lane = lax.broadcasted_iota(jnp.int32, (1, lanes), 1)
        low = lane < half_lanes
        qh, ql = split(q * (HD ** (-0.5) * math.log2(math.e)))
        kh, kl = [part.astype(jnp.float32) for part in split(k)]
        vh, vl = [part.astype(jnp.float32) for part in split(v)]
        qf, qlf = qh.astype(jnp.float32), ql.astype(jnp.float32)
        q_s, k_s, v_s = self.q_s, self.k_s, self.v_s

        def roll(values):
            return pltpu.roll(values, half_lanes, 1)

        q_s[0, at, :lanes] = qh
        q_s[1, at, :lanes] = qh
        q_s[0, at, lanes:] = jnp.where(low, qf, roll(qlf)).astype(jnp.bfloat16)
        q_s[1, at, lanes:] = jnp.where(low, roll(qf), qlf).astype(jnp.bfloat16)
        k_s[0, at, :lanes] = kh.astype(jnp.bfloat16)
        k_s[1, at, :lanes] = kh.astype(jnp.bfloat16)
        k_s[0, at, lanes:] = jnp.where(low, kl, roll(kh)).astype(jnp.bfloat16)
        k_s[1, at, lanes:] = jnp.where(low, roll(kl), kh).astype(jnp.bfloat16)
        v_s[0, at, :lanes] = vh.astype(jnp.bfloat16)
        v_s[1, at, :lanes] = vh.astype(jnp.bfloat16)
        v_s[0, at, lanes:] = jnp.where(low, vl, 1.0).astype(jnp.bfloat16)
        v_s[1, at, lanes:] = jnp.where(low, 1.0, vl).astype(jnp.bfloat16)

    def near(self, i):
        half = self.chunk // 2
        start = pl.multiple_of(i * self.chunk + (1 - self.r) * half, half)
        return self.sent("near", i, self.p_s.at[pl.ds(start, half)], self.n1_s.at[piece(i, half)], self.mate)

    def far(self, i):
        at = piece(i, self.chunk // 2)
        return self.sent("far", i, self.s1_s.at[at], self.f1_s.at[at], self.peer)

    def own_half(self, i):
        half = self.chunk // 2
        return pl.ds(pl.multiple_of(i * self.chunk + self.r * half, half), half)

    def share(self, i):
        at = self.own_half(i)
        return self.sent("share", i, self.a_s.at[at], self.a_s.at[at], self.mate)

    def attention(self, k):
        lanes, half_heads, chunk = self.lanes, self.heads // 2, self.chunk
        wide = lax.broadcasted_iota(jnp.int32, (1, 2 * lanes), 1)
        lane = lax.broadcasted_iota(jnp.int32, (1, lanes), 1)
        i, half = k // 2, k % 2
        query = self.q_s[half, piece(i, chunk), :]
        queries = []
        for m in range(half_heads):
            first = (wide < lanes) & (wide // HD == half * half_heads + m)
            second = (wide >= lanes) & ((wide % (lanes // 2)) // HD == m)
            mask = jnp.where(first | second, 1.0, 0.0).astype(jnp.bfloat16)
            queries.append(query * mask)
        stacked = jnp.concatenate(queries, axis=0)
        scores = bdot(stacked, self.k_s[half], (((1,), (1,)), ((), ())))
        weights = jnp.exp2(scores - jnp.max(scores, axis=-1, keepdims=True))
        sums = bdot(jnp.concatenate(split(weights), axis=0), self.v_s[half])
        sums = sums[: half_heads * chunk] + sums[half_heads * chunk :]
        total = jnp.zeros((chunk, lanes), jnp.float32)
        for m in range(half_heads):
            own = sums[m * chunk : (m + 1) * chunk]
            top, low = own[:, :lanes], own[:, lanes:]
            ratio = (top + low) / pltpu.roll(low, lanes // 2, 1)
            total += jnp.where(lane // HD == half * half_heads + m, ratio, 0.0)
        self.att_s[half] = total

    def finish(self, i):
        projection = (self.wo_s[0], self.wo_s[1])
        self.p_s[piece(i, self.chunk)] = dot3(split(self.att_s[0] + self.att_s[1]), projection)
        self.near(i).start()

    def reduce_near(self, i):
        self.near(i).wait_recv()
        at = piece(i, self.chunk // 2)
        self.s1_s[at] = self.p_s[self.own_half(i)] + self.n1_s[at]
        self.far(i).start()

    def reduce_far(self, i):
        self.far(i).wait_recv()
        half = self.chunk // 2
        at = piece(i, half)
        stream = self.stream_rows(i * self.chunk + self.r * half, half)
        self.a_s[self.own_half(i)] = (self.s1_s[at] + self.f1_s[at]) + stream
        self.share(i).start()

    def mlp(self, x):
        normed = split(layer_norm(x, self.gm_ref[pl.ds(self.layer, 1)]))
        hidden = gelu(dot3(normed, (self.wu_s[0], self.wu_s[1])))
        return dot3(split(hidden), (self.wd_s[0], self.wd_s[1]))

    def run(self, stages):
        n = self.n

        def tick(k, carry):
            @pl.when(k < 2 * n)
            def _():
                self.attention(k)

            for offset, stage in stages:
                @pl.when((k >= offset) & (k < offset + 2 * n) & ((k - offset) % 2 == 0))
                def _(offset=offset, stage=stage):
                    stage((k - offset) // 2)

            return carry

        lax.fori_loop(0, 2 * n + stages[0][0] - 1, tick, 0)


class First(Layer):
    def stream_rows(self, start, count):
        at = pl.ds(pl.multiple_of(start, count), count)
        return jnp.concatenate([self.g_s[j, at] for j in range(self.cols * self.reps)], axis=-1)

    def across(self, i):
        at = piece(i, self.chunk)
        return self.sent("across", i, self.x_ref.at[at], self.g_s.at[self.me, at], self.peer)

    def over(self, i):
        at = piece(i, self.chunk)
        return self.sent("over", i, self.x_ref.at[at], self.g_s.at[self.me, at], self.mate)

    def relay(self, i):
        at = piece(i, self.chunk)
        slot = (1 - self.c) * self.reps + self.r
        return self.sent("relay", i, self.g_s.at[slot, at], self.g_s.at[slot, at], self.mate)

    def code(self, e):
        target = {"tok": lax.rem(self.t + e, self.ntok)}
        return self.sent("code", e, self.code_s, self.arrived_s.at[self.t], target)

    def route(self):
        device = self.dd_ref[...].astype(jnp.float32)
        slot = self.ds_ref[...].astype(jnp.float32)
        count = device.shape[1]
        row = lax.broadcasted_iota(jnp.int32, (count, count), 0)
        col = lax.broadcasted_iota(jnp.int32, (count, count), 1)

        def upright(values):
            return jnp.sum(jnp.where(row == col, values, 0.0), axis=1, keepdims=True)

        devices, slots = upright(device), upright(slot)
        earlier = jnp.where((devices == device) & (col < row), 1.0, 0.0)
        place = devices * self.cap + jnp.sum(earlier, axis=1, keepdims=True)
        at = lax.broadcasted_iota(jnp.int32, (count, 128), 1).astype(jnp.float32)
        block = lax.broadcasted_iota(jnp.int32, (count, 128), 0).astype(jnp.float32)
        index = jnp.sum(jnp.where(place == at, block, 0.0), axis=0, keepdims=True)
        code = jnp.sum(jnp.where(place == at, slots + 1.0, 0.0), axis=0, keepdims=True)
        self.index_ref[...] = index.astype(jnp.int32)
        self.code_s[...] = jnp.broadcast_to(code, self.code_s.shape)
        self.arrived_s[self.t] = jnp.broadcast_to(code, self.code_s.shape)

    def locate(self):
        row = lax.broadcasted_iota(jnp.int32, (128, 128), 0)
        col = lax.broadcasted_iota(jnp.int32, (128, 128), 1)
        first = self.t * self.cap
        valid = (row >= first) & (row < first + self.cap)
        source = jnp.zeros((1, 128), jnp.float32)
        for u in range(self.ntok):
            codes = self.arrived_s[u][:1]
            upright = jnp.sum(jnp.where(row == col, codes, 0.0), axis=1, keepdims=True)
            found = valid & (upright == (col + 1).astype(jnp.float32))
            entry = (row - first + u * self.cap).astype(jnp.float32)
            source += jnp.sum(jnp.where(found, entry, 0.0), axis=0, keepdims=True)
        self.source_ref[...] = source.astype(jnp.int32)

    def near2(self, i):
        at = piece(i, self.chunk)
        return self.sent("near2", i, self.m_s.at[1 - self.r, :, at], self.n2_s.at[:, at], self.mate)

    def far2(self, i):
        at = piece(i, self.chunk)
        return self.sent("far2", i, self.s2_s.at[at], self.f2_s.at[at], self.peer)

    def feed(self, i):
        self.share(i).wait_recv()
        at = piece(i, self.chunk)
        total = self.mlp(self.a_s[at])
        for j in range(self.cols * self.reps):
            self.m_s[j % self.reps, j // self.reps, at] = total[:, j * self.lanes : (j + 1) * self.lanes]
        self.near2(i).start()

    def scatter_near(self, i):
        self.near2(i).wait_recv()
        at = piece(i, self.chunk)
        self.s2_s[at] = self.m_s[self.r, 1 - self.c, at] + self.n2_s[1 - self.c, at]
        self.far2(i).start()

    def scatter_far(self, i):
        self.far2(i).wait_recv()
        at = piece(i, self.chunk)
        own = self.a_s[at, piece(self.me, self.lanes)]
        total = (self.m_s[self.r, self.c, at] + self.n2_s[self.c, at]) + self.f2_s[at]
        self.out_ref[at] = total + own

    def body(self):
        n = self.n
        self.load_weights()
        greet([self.mate, self.peer] + self.peers)
        for i in range(n):
            self.across(i).start()
        for i in range(n):
            self.over(i).start()
        self.cap = capacity_of(self.dd_ref.shape[1], self.ntok)
        self.route()
        self.g_s[self.me] = self.x_ref[...]
        self.split_weights()
        for e in range(1, self.ntok):
            self.code(e).start()

        def step(i, carry):
            @pl.when(i < n)
            def _():
                self.across(i).wait_recv()
                self.relay(i).start()

            @pl.when(i > 0)
            def _():
                self.over(i - 1).wait_recv()
                self.relay(i - 1).wait_recv()
                stream = self.stream_rows((i - 1) * self.chunk, self.chunk)
                self.pack(piece(i - 1, self.chunk), *self.project(stream))

            return carry

        lax.fori_loop(0, n + 1, step, 0)
        self.run(
            [
                (9, self.scatter_far), (7, self.scatter_near), (6, self.feed),
                (5, self.reduce_far), (2, self.reduce_near), (1, self.finish),
            ]
        )
        for copy in (
            self.near, self.far, self.share, self.near2, self.far2, self.across, self.over, self.relay
        ):
            for i in range(n):
                copy(i).wait_send()
        for e in range(1, self.ntok):
            self.code(e).wait()
        self.locate()


class Second(Layer):
    def stream_rows(self, start, count):
        parts = []
        for m in range(count // self.block):
            at = self.source_ref[0, start // self.block + m]
            places = [self.g_s[at // self.cap, j, at % self.cap] for j in range(self.cols * self.reps)]
            parts.append(jnp.concatenate(places, axis=-1))
        return jnp.concatenate(parts, axis=0)

    def along(self, e, j):
        target = lax.rem(self.t + e, self.ntok)
        return self.sent(
            "along", e * self.cap + j, self.o_s.at[target, j], self.g_s.at[self.t, self.me, j],
            {"tok": target},
        )

    def origin(self, e):
        return lax.rem(self.t + self.ntok - e, self.ntok)

    def placed(self, kind, e, j, slot, device):
        ref = self.g_s.at[self.origin(e), slot, j]
        return self.sent(kind, e * self.cap + j, ref, ref, device)

    def across(self, e, j):
        return self.placed("across", e, j, self.me, self.peer)

    def over(self, e, j):
        return self.placed("over", e, j, self.me, self.mate)

    def relay(self, e, j):
        return self.placed("relay", e, j, (1 - self.c) * self.reps + self.r, self.mate)

    def arrive(self, j):
        for e in self.order[1:]:
            self.along(e, j).wait_recv()
            self.across(e, j).start()
            self.over(e, j).start()

    def hand(self, j):
        for e in self.order:
            self.across(e, j).wait_recv()
            self.relay(e, j).start()

    def take(self, j):
        parts = []
        for e in self.order:
            self.over(e, j).wait_recv()
            self.relay(e, j).wait_recv()
            places = [self.g_s[self.origin(e), k, j] for k in range(self.cols * self.reps)]
            parts.append(jnp.concatenate(places, axis=-1))
        for m, values in enumerate(self.project(jnp.concatenate(parts, axis=0))):
            for at, e in enumerate(self.order):
                entry = self.origin(e) * self.cap + j
                self.raw_s[m, entry] = values[at * self.block : (at + 1) * self.block]

    def move(self):
        self.order = [0]
        for e in range(1, self.ntok // 2 + 1):
            self.order += [e] + ([self.ntok - e] if self.ntok - e != e else [])
        for u in range(self.ntok):
            for j in range(self.cap):
                self.o_s[u, j] = self.x_ref[self.index_ref[0, u * self.cap + j]]
        for j in range(self.cap):
            self.g_s[self.t, self.me, j] = self.x_ref[self.index_ref[0, self.t * self.cap + j]]
        for j in range(self.cap):
            for e in self.order[1:]:
                self.along(e, j).start()
        for j in range(self.cap):
            self.across(0, j).start()
            self.over(0, j).start()
        self.split_weights()
        for j in range(self.cap):
            self.arrive(j)
            if j == 0:
                self.split_points()
            if j >= 1:
                self.hand(j - 1)
            if j >= 2:
                self.take(j - 2)
        self.hand(self.cap - 1)
        for j in range(max(0, self.cap - 2), self.cap):
            self.take(j)

        def step(i, carry):
            def row(m):
                each = self.chunk // self.block
                blocks = [self.raw_s[m, self.source_ref[0, i * each + k]] for k in range(each)]
                return jnp.concatenate(blocks, axis=0)

            self.pack(piece(i, self.chunk), row(0), row(1), row(2))
            return carry

        lax.fori_loop(0, self.n, step, 0)

    def load_points(self):
        self.point = pltpu.make_async_copy(self.pw_ref, self.pw_f, self.wsem.at[4])
        self.point.start()

    def split_points(self):
        self.point.wait()

        def step(k, carry):
            at = piece(k, 64)
            for l in range(2):
                self.pw_s[0, l, at], self.pw_s[1, l, at] = split(self.pw_f[l, at])
            return carry

        lax.fori_loop(0, self.width // 64, step, 0)

    def cell_ids(self):
        count = self.pool_s.shape[0]
        p = lax.broadcasted_iota(jnp.int32, (count, 1), 0)
        wide = TC + 2 * HALO
        row = ((p.astype(jnp.float32) + 0.5) * (1.0 / wide)).astype(jnp.int32)
        col = row // TR
        x = col * TC - HALO + (p - row * wide)
        full = TC * self.cols
        y = row - col * TR
        return jnp.where((x >= 0) & (x < full), (self.t * TR + y) * full + x, -2)

    def feed(self, i):
        self.share(i).wait_recv()
        at = piece(i, self.chunk)
        x = self.a_s[at]
        high, low = split(self.mlp(x) + x * (1.0 / (self.cols * self.reps)))
        chosen = jnp.where(self.cell_ids() == self.pillar_ref[:, at], 1.0, 0.0).astype(jnp.bfloat16)
        self.pool_s[...] += bdot(chosen, high) + bdot(chosen, low)

    def tile_part(self, c, r, k):
        cells = self.pool_s.shape[0] // (self.cols * self.reps)
        start = (c * self.reps + r) * cells + k * self.edge
        return pl.ds(pl.multiple_of(start, 8), self.edge)

    def near3(self, w, k):
        c = self.c if w else 1 - self.c
        return self.sent(
            "near3", w * self.pieces + k, self.pool_s.at[self.tile_part(c, 1 - self.r, k)],
            self.n3_s.at[w, k], self.mate,
        )

    def far3(self, k):
        return self.sent("far3", k, self.s3_s.at[k], self.f3_s.at[k], self.peer)

    def inner(self):
        start = jnp.where(self.r == 0, self.pieces * self.edge, self.edge)
        src = self.tile_s.at[pl.ds(pl.multiple_of(start, 8), self.edge)]
        return self.sent("halo", 0, src, self.h_s.at[0], self.mate)

    def outer(self):
        start = jnp.where(self.r == 0, self.edge, self.pieces * self.edge)
        src = self.tile_s.at[pl.ds(pl.multiple_of(start, 8), self.edge)]
        return self.sent("halo", 1, src, self.h_s.at[1], self.partner)

    def scatter(self):
        order = [0, self.pieces - 1] + list(range(1, self.pieces - 1))
        for w in range(2):
            for k in order:
                self.near3(w, k).start()
        for k in order:
            self.near3(0, k).wait_recv()
            self.s3_s[k] = self.pool_s[self.tile_part(1 - self.c, self.r, k)] + self.n3_s[0, k]
            self.far3(k).start()
        for at, k in enumerate(order):
            self.near3(1, k).wait_recv()
            self.far3(k).wait_recv()
            own = self.pool_s[self.tile_part(self.c, self.r, k)] + self.n3_s[1, k]
            self.tile_s[pl.ds((k + 1) * self.edge, self.edge)] = own + self.f3_s[k]
            if at == 1:
                self.inner().start()
                self.outer().start()
        self.inner().wait()
        self.outer().wait()
        wrapped = jnp.where(self.r == 0, self.t == 0, self.t == self.ntok - 1)
        beyond = jnp.where(wrapped, 0.0, self.h_s[1])
        within = self.h_s[0]
        self.tile_s[: self.edge] = jnp.where(self.r == 0, beyond, within)
        self.tile_s[(self.pieces + 1) * self.edge :] = jnp.where(self.r == 0, within, beyond)

    def raster(self):
        wide = TC + 2 * HALO
        rows = self.tile_s.shape[0] // wide
        pad = (self.flat_s.shape[0] - rows * wide) // 2
        self.flat_s[:pad] = jnp.zeros((pad, self.width), jnp.float32)
        self.flat_s[pad + rows * wide :] = jnp.zeros((pad, self.width), jnp.float32)
        for l in range(2):
            old = pl.ds(l * wide, (rows - 2 * l) * wide)
            start, count = (l + 1) * wide, (rows - 2 * l - 2) * wide
            cells = self.tile_s[old]
            square = jnp.mean(cells * cells, axis=-1, keepdims=True)
            gain = self.rg_ref[pl.ds(l, 1)]
            self.flat_s[pl.ds(pad + l * wide, (rows - 2 * l) * wide)] = (
                cells * lax.rsqrt(square + EPSILON) * gain
            )
            mixed = jnp.zeros((count, self.width), jnp.float32)
            for a in range(3):
                for b in range(3):
                    shift = pad + start + (a - 1) * wide + b - 1
                    mixed = mixed + self.flat_s[pl.ds(shift, count)] * self.dw_ref[a, b, pl.ds(l, 1)]
            both = dot3(split(mixed), (self.pw_s[0, l], self.pw_s[1, l]))
            centre = self.tile_s[pl.ds(start, count)]
            result = centre + both[:, : self.width] * jax.nn.sigmoid(both[:, self.width :])
            if l == 0:
                p = lax.broadcasted_iota(jnp.int32, (count, 1), 0) + start
                row = ((p.astype(jnp.float32) + 0.5) * (1.0 / wide)).astype(jnp.int32)
                y = (self.t * self.reps + self.r) * (rows - 2 * HALO) - HALO + row
                x = self.c * TC - HALO + (p - row * wide)
                inside = (y >= 0) & (y < TR * self.ntok) & (x >= 0) & (x < TC * self.cols)
                result = jnp.where(inside, result, 0.0)
            self.tile_s[pl.ds(start, count)] = result
        for y in range(rows - 2 * HALO):
            self.out_ref[y] = self.tile_s[pl.ds((y + HALO) * wide + HALO, TC)]

    def body(self):
        self.block = self.x_ref.shape[1]
        self.cap = self.g_s.shape[2]
        self.pieces, self.edge = self.s3_s.shape[:2]
        step = jnp.where(self.r == 0, self.ntok - 1, 1)
        self.partner = {"tok": lax.rem(self.t + step, self.ntok), "rep": 1 - self.r}
        self.load_weights()
        self.load_points()
        greet([self.mate, self.peer, self.partner] + self.peers)
        self.move()
        self.pool_s[...] = jnp.zeros(self.pool_s.shape, jnp.float32)
        self.run([(6, self.feed), (5, self.reduce_far), (2, self.reduce_near), (1, self.finish)])
        self.scatter()
        self.raster()
        for copy in (self.near, self.far, self.share):
            for i in range(self.n):
                copy(i).wait_send()
        for j in range(self.cap):
            for e in range(self.ntok):
                if e:
                    self.along(e, j).wait_send()
                for copy in (self.across, self.over, self.relay):
                    copy(e, j).wait_send()
        for k in range(self.pieces):
            self.near3(0, k).wait_send()
            self.near3(1, k).wait_send()
            self.far3(k).wait_send()


def run_layer(kind, layer, inputs, outputs, weights, collective_id, extra, kinds, most):
    w_qkv, w_out, w_up, w_down, attn_gain, mlp_gain = weights
    lanes, width, hidden = w_qkv.shape[-1], w_qkv.shape[-2], w_up.shape[-1]
    heads, rows = lanes // HD, PATCH
    chunk = min(256, rows)
    dma, f32, b16 = pltpu.SemaphoreType.DMA, jnp.float32, jnp.bfloat16
    vmem = pl.BlockSpec(memory_space=pltpu.VMEM)
    hbm = pl.BlockSpec(memory_space=pl.ANY)
    smem = pl.BlockSpec(memory_space=pltpu.SMEM)
    inputs = dict(inputs)
    places = {name: vmem for name in inputs}
    inputs.update(ga_ref=attn_gain, gm_ref=mlp_gain)
    inputs.update(wqkv_ref=w_qkv, wo_ref=w_out, wu_ref=w_up, wd_ref=w_down)
    for name in ("index_ref", "source_ref"):
        if name in inputs:
            places[name] = smem
    for name in ("wqkv_ref", "wo_ref", "wu_ref", "wd_ref", "pw_ref"):
        places[name] = hbm
    scratch = dict(
        wqkv_f=pltpu.VMEM((3, width, lanes), f32),
        wo_f=pltpu.VMEM((lanes, width), f32),
        wu_f=pltpu.VMEM((width, hidden), f32),
        wd_f=pltpu.VMEM((hidden, width), f32),
        wqkv_s=pltpu.VMEM((2, 3, width, lanes), b16),
        wo_s=pltpu.VMEM((2, lanes, width), b16),
        wu_s=pltpu.VMEM((2, width, hidden), b16),
        wd_s=pltpu.VMEM((2, hidden, width), b16),
        q_s=pltpu.VMEM((2, rows, 2 * lanes), b16),
        k_s=pltpu.VMEM((2, rows, 2 * lanes), b16),
        v_s=pltpu.VMEM((2, rows, 2 * lanes), b16),
        att_s=pltpu.VMEM((2, chunk, lanes), f32),
        p_s=pltpu.VMEM((rows, width), f32),
        n1_s=pltpu.VMEM((rows // 2, width), f32),
        s1_s=pltpu.VMEM((rows // 2, width), f32),
        f1_s=pltpu.VMEM((rows // 2, width), f32),
        a_s=pltpu.VMEM((rows, width), f32),
        sem=dma((len(kinds), 2, max(most, rows // chunk))),
        wsem=dma((5,)),
    )
    scratch.update(extra)
    names = list(inputs) + list(outputs) + list(scratch)

    def kernel(*refs):
        kind(layer, dict(zip(names, refs)), heads, chunk, kinds).body()

    return pl.pallas_call(
        kernel,
        out_shape=tuple(outputs.values()),
        in_specs=[places.get(name, vmem) for name in inputs],
        out_specs=tuple(vmem for _ in outputs),
        scratch_shapes=list(scratch.values()),
        compiler_params=pltpu.CompilerParams(
            collective_id=collective_id, has_side_effects=True, vmem_limit_bytes=VMEM_LIMIT
        ),
        name=kind.__name__.lower(),
    )(*inputs.values())


def capacity_of(count, peers):
    return max(2, (count + peers - 4) // (peers - 1))


def first_layer(tokens, dest_device, dest_slot, weights, collective_id):
    rows, lanes = tokens.shape
    cols, reps, ntok = lax.axis_size("col"), lax.axis_size("rep"), lax.axis_size("tok")
    f32 = jnp.float32
    extra = dict(
        g_s=pltpu.VMEM((cols * reps, rows, lanes), f32),
        m_s=pltpu.VMEM((reps, cols, rows, lanes), f32),
        n2_s=pltpu.VMEM((cols, rows, lanes), f32),
        s2_s=pltpu.VMEM((rows, lanes), f32),
        f2_s=pltpu.VMEM((rows, lanes), f32),
        code_s=pltpu.VMEM((8, 128), f32),
        arrived_s=pltpu.VMEM((ntok, 8, 128), f32),
    )
    kinds = ("near", "far", "share", "near2", "far2", "across", "over", "relay", "code")
    table = jax.ShapeDtypeStruct((1, 128), jnp.int32)
    outputs = dict(
        out_ref=jax.ShapeDtypeStruct((rows, lanes), f32), index_ref=table, source_ref=table
    )
    inputs = dict(x_ref=tokens, dd_ref=dest_device[None, :], ds_ref=dest_slot[None, :])
    return run_layer(First, 0, inputs, outputs, weights, collective_id, extra, kinds, ntok)


def second_layer(share, index, source, cap, pillar, raster_weights, weights, collective_id):
    cols, reps, ntok = lax.axis_size("col"), lax.axis_size("rep"), lax.axis_size("tok")
    count, block, lanes = share.shape
    depth_weight, point_weight, raster_gain = raster_weights
    width = depth_weight.shape[-1]
    wide, rep_rows = TC + 2 * HALO, TR // reps
    edge, pieces = HALO * wide, rep_rows // HALO
    tile = (rep_rows + 2 * HALO) * wide
    f32 = jnp.float32
    extra = dict(
        o_s=pltpu.VMEM((ntok, cap, block, lanes), f32),
        g_s=pltpu.VMEM((ntok, cols * reps, cap, block, lanes), f32),
        raw_s=pltpu.VMEM((3, ntok * cap, block, lanes), f32),
        pw_f=pltpu.VMEM(point_weight.shape, f32),
        pw_s=pltpu.VMEM((2,) + point_weight.shape, jnp.bfloat16),
        pool_s=pltpu.VMEM((cols * reps * rep_rows * wide, width), f32),
        n3_s=pltpu.VMEM((2, pieces, edge, width), f32),
        s3_s=pltpu.VMEM((pieces, edge, width), f32),
        f3_s=pltpu.VMEM((pieces, edge, width), f32),
        h_s=pltpu.VMEM((2, edge, width), f32),
        tile_s=pltpu.VMEM((tile, width), f32),
        flat_s=pltpu.VMEM((tile + 16, width), f32),
    )
    kinds = ("near", "far", "share", "along", "across", "over", "relay", "near3", "far3", "halo")
    outputs = dict(out_ref=jax.ShapeDtypeStruct((rep_rows, TC, width), f32))
    inputs = dict(
        index_ref=index, source_ref=source, x_ref=share, pillar_ref=pillar[None, :],
        dw_ref=jnp.transpose(depth_weight, (1, 2, 0, 3)), rg_ref=raster_gain, pw_ref=point_weight,
    )
    return run_layer(Second, 1, inputs, outputs, weights, collective_id, extra, kinds, ntok * cap)[0]


HALO = 2


def routes(dest_device, dest_slot):
    count = dest_device.shape[0]
    peers = lax.axis_size("tok")
    capacity = capacity_of(count, peers)
    order = jnp.arange(count, dtype=jnp.int32)
    earlier = (dest_device[:, None] == dest_device[None, :]) & (order[None, :] < order[:, None])
    place = dest_device * capacity + jnp.sum(earlier.astype(jnp.int32), axis=1)
    chosen = jnp.arange(peers * capacity, dtype=jnp.int32)[:, None] == place[None, :]
    index = jnp.sum(jnp.where(chosen, order[None, :], 0), axis=1)
    code = jnp.sum(jnp.where(chosen, dest_slot[None, :] + 1, 0), axis=1)
    code = jnp.pad(code.reshape(peers, capacity), ((0, 0), (0, 128 - capacity)))
    code = jnp.broadcast_to(code[:, None, :], (peers, 8, 128)).astype(jnp.float32)
    return index, code, capacity


def places(arrived, capacity, order):
    held = arrived[:, 0, :capacity].reshape(-1).astype(jnp.int32)
    found = held[None, :] == order[:, None] + 1
    return jnp.sum(jnp.where(found, jnp.arange(held.shape[0], dtype=jnp.int32)[None, :], 0), axis=1)


def raster_cells(extended, depth_weight, point_weight, gain_row):
    row_count = extended.shape[0] - 2
    col_count = extended.shape[1] - 2
    channels = extended.shape[2]
    normed = (
        extended
        * lax.rsqrt(jnp.mean(extended * extended, axis=-1, keepdims=True) + EPSILON)
        * gain_row
    )
    mixed = jnp.zeros((row_count, col_count, channels), jnp.float32)
    for a in range(3):
        for b in range(3):
            mixed = mixed + normed[a : a + row_count, b : b + col_count] * depth_weight[a, b]
    combined = matmul(mixed.reshape(row_count * col_count, channels), point_weight)
    combined = combined.reshape(row_count, col_count, 2 * channels)
    centre = extended[1:-1, 1:-1]
    return centre + combined[..., :channels] * jax.nn.sigmoid(combined[..., channels:])


def extended_cells(tok, members, rep_rows, full_width):
    cols, reps = members
    tile = []
    for col in range(cols):
        for rep in range(reps):
            y = rep * rep_rows - HALO + jnp.arange(rep_rows + 2 * HALO, dtype=jnp.int32)[:, None]
            x = col * TC - HALO + jnp.arange(TC + 2 * HALO, dtype=jnp.int32)[None, :]
            good = (y >= 0) & (y < TR) & (x >= 0) & (x < full_width)
            tile.append(jnp.where(good, (tok * TR + y) * full_width + x, -2).reshape(-1))
    return jnp.concatenate(tile)


def pool(partial, pillar, cells):
    onehot = (cells[:, None] == pillar[None, :]).astype(jnp.float32)
    return matmul(onehot, partial)


def exchange_rows(tile, ntok, reps):
    count = ntok * reps
    rep = lax.axis_index("rep")
    forward = [(i, i + 1) for i in range(count - 1)]
    backward = [(i + 1, i) for i in range(count - 1)]
    above = lax.ppermute(tile[-2 * HALO : -HALO], ("tok", "rep"), forward)
    below = lax.ppermute(tile[HALO : 2 * HALO], ("tok", "rep"), backward)
    above = jnp.where(rep == 0, above, tile[:HALO])
    below = jnp.where(rep == reps - 1, below, tile[-HALO:])
    return jnp.concatenate([above, tile[HALO:-HALO], below], axis=0)


def on_device(
    tokens,
    w_qkv,
    w_out,
    w_up,
    w_down,
    attn_gain,
    mlp_gain,
    dest_device,
    dest_slot,
    pillar,
    depth_weight,
    point_weight,
    raster_gain,
):
    members = (lax.axis_size("col"), lax.axis_size("rep"))
    group = members[0] * members[1]
    ntok = lax.axis_size("tok")
    block_count = dest_device.shape[0]
    order = jnp.arange(block_count, dtype=jnp.int32)
    index, codes, capacity = routes(dest_device, dest_slot)
    width = tokens.shape[1]
    weights = (w_qkv, w_out, w_up, w_down, attn_gain, mlp_gain)
    whole = (2 * members[1] * HALO * (TC + 2 * HALO)) % 8 == 0 and TR % (members[1] * HALO) == 0
    if members == (2, 2) and ntok > 1 and tokens.shape[0] == PATCH and whole and ntok * capacity <= 128:
        share, index, source = first_layer(tokens, dest_device, dest_slot, weights, 1)
        share = share.reshape(block_count, -1, width)
        raster_weights = (depth_weight, point_weight, raster_gain)
        return second_layer(share, index, source, capacity, pillar, raster_weights, weights, 5)
    blocks = gather(tokens, 1).reshape(1, group, block_count, -1, width)
    stream = attention_layer(blocks, order, 0, w_qkv, w_out, attn_gain, 2)
    share = scatter(mlp_partial(stream, 0, w_up, w_down, mlp_gain, group), 3)
    outgoing = pick(share.reshape(block_count, -1, width), index)
    outgoing = outgoing.reshape(ntok, -1, width)
    moved, arrived = move(outgoing, codes, 4)
    blocks = moved.reshape(ntok, group, capacity, -1, width)
    source = places(arrived, capacity, order)
    stream = attention_layer(blocks, source, 1, w_qkv, w_out, attn_gain, 5)
    partial = mlp_partial(stream, 1, w_up, w_down, mlp_gain, 1)[0]

    rep_rows = TR // members[1]
    full_width = TC * members[0]
    cells = extended_cells(lax.axis_index("tok"), members, rep_rows, full_width)
    pooled = pool(partial, pillar, cells)
    parts = pooled.reshape(group, -1, pooled.shape[1])
    edge = HALO * (TC + 2 * HALO)
    inside_kernel = members[0] > 1 and members[1] == 2 and ntok > 1 and edge % 8 == 0
    tile = scatter(parts, 6, edge if inside_kernel else 0)
    tile = tile.reshape(rep_rows + 2 * HALO, TC + 2 * HALO, -1)
    if not inside_kernel:
        tile = exchange_rows(tile, ntok, members[1])
    first = raster_cells(tile, depth_weight[0], point_weight[0], raster_gain[0])
    y = lax.axis_index(("tok", "rep")) * rep_rows - 1 + jnp.arange(rep_rows + 2)[:, None, None]
    x = lax.axis_index("col") * TC - 1 + jnp.arange(TC + 2)[None, :, None]
    inside = (y >= 0) & (y < TR * ntok) & (x >= 0) & (x < full_width)
    first = jnp.where(inside, first, 0.0)
    return raster_cells(first, depth_weight[1], point_weight[1], raster_gain[1])


def solution(mesh):
    placed = (
        P(("scene", "tok"), ("col", "rep")),
        P(None, None, None, ("col", "rep")),
        P(None, ("col", "rep"), None),
        P(None, None, ("col", "rep")),
        P(None, ("col", "rep"), None),
        P(),
        P(),
        P(("scene", "tok")),
        P(("scene", "tok")),
        P(("scene", "tok")),
        P(),
        P(),
        P(),
    )
    return jax.shard_map(
        on_device,
        mesh=mesh,
        in_specs=placed,
        out_specs=P(("scene", "tok", "rep"), "col", None),
        check_vma=False,
    )
```

```python
import functools
import math

import jax
import jax.numpy as jnp
from jax import lax
from jax.experimental import pallas as pl
from jax.experimental.pallas import tpu as pltpu
from jax.sharding import PartitionSpec as P

PATCH = 1024
TR = 16
TC = 16
HD = 16


MATMUL_PRECISION = lax.Precision.HIGH
EPSILON = 1e-05


def layer_norm(values, gain_row):
    average = jnp.mean(values, axis=-1, keepdims=True)
    centered = values - average
    variance = jnp.mean(centered * centered, axis=-1, keepdims=True)
    return centered * lax.rsqrt(variance + EPSILON) * gain_row


def split(values):
    high = values.astype(jnp.bfloat16)
    return high, (values - high.astype(jnp.float32)).astype(jnp.bfloat16)


def bdot(left, right, dims=(((1,), (0,)), ((), ()))):
    return lax.dot_general(left, right, dims, preferred_element_type=jnp.float32)


def dot3(left, right):
    lh, ll = left
    rh, rl = right
    return bdot(lh, rh) + bdot(lh, rl) + bdot(ll, rh)


def attention_kernel(share, source_ref, x_ref, gain_ref, w_ref, o_ref, out_ref, q_s, k_s, v_s, att_s):
    cols = w_ref.shape[-1]
    heads = cols // HD
    rows = out_ref.shape[0]
    chunk = att_s.shape[0]
    slots, each, block = x_ref.shape[1:4]
    first_block = pl.program_id(0) * (rows // block)

    def stream_rows(i):
        parts = []
        for n in range(chunk // block):
            at = source_ref[first_block + i * (chunk // block) + n]
            places = [x_ref[at // each, j, at % each] for j in range(slots)]
            parts.append(jnp.concatenate(places, axis=-1))
        return jnp.concatenate(parts, axis=0)

    lanes = q_s.shape[-1]

    r = lax.broadcasted_iota(jnp.int32, (cols, lanes), 0)
    c = lax.broadcasted_iota(jnp.int32, (cols, lanes), 1)
    lane = lax.broadcasted_iota(jnp.int32, (1, cols), 1)
    w = [split(w_ref[j]) for j in range(3)]
    for i in range(rows // chunk):
        at = pl.ds(i * chunk, chunk)
        normed = split(layer_norm(stream_rows(i), gain_ref[...]))
        qh, ql = split(dot3(normed, w[0]) * (HD ** (-0.5) * math.log2(math.e)))
        kh, kl = split(dot3(normed, w[1]))
        vh, vl = split(dot3(normed, w[2]))
        for h in range(heads):
            part = c // HD
            inside = (r // HD == h) & (r % HD == c % HD)
            first = (inside & ((part == 0) | (part == 1))).astype(jnp.bfloat16)
            third = (inside & (part == 2)).astype(jnp.bfloat16)
            outer = (inside & ((part == 0) | (part == 2))).astype(jnp.bfloat16)
            middle = (inside & (part == 1)).astype(jnp.bfloat16)
            q_s[h, at, :] = (bdot(qh, first) + bdot(ql, third)).astype(jnp.bfloat16)
            k_s[h, at, :] = (bdot(kh, outer) + bdot(kl, middle)).astype(jnp.bfloat16)
            own = lane // HD == h
            v_s[h, at, :cols] = jnp.where(own, vh.astype(jnp.float32), 0.0).astype(jnp.bfloat16)
            v_s[h, at, cols:] = jnp.where(own, vl.astype(jnp.float32), 1.0).astype(jnp.bfloat16)

    projection = split(o_ref[...])

    def query_rows(i, carry):
        at = pl.ds(pl.multiple_of(i * chunk, chunk), chunk)
        att_s[...] = jnp.zeros_like(att_s)

        def one_head(h, carry):
            scores = bdot(q_s[h, at, :], k_s[h], (((1,), (1,)), ((), ())))
            weights = jnp.exp2(scores - jnp.max(scores, axis=-1, keepdims=True))
            wh, wl = split(weights)
            sums = bdot(wh, v_s[h]) + bdot(wl, v_s[h])
            top, low = sums[:, :cols], sums[:, cols:]
            own = lane // HD == h
            total = jnp.max(jnp.where(own, 0.0, low), axis=-1, keepdims=True)
            att_s[...] += jnp.where(own, (top + low) / total, 0.0)
            return carry

        lax.fori_loop(0, heads, one_head, 0, unroll=4)
        out_ref[at, :] = dot3(split(att_s[...]), projection) + stream_rows(i) * share
        return carry

    lax.fori_loop(0, rows // chunk, query_rows, 0)


def attend(blocks, source, gain_row, weights, w_out, group):
    block, width = blocks.shape[3], blocks.shape[1] * blocks.shape[4]
    rows = source.shape[0] * block
    cols = weights.shape[-1]
    heads = cols // HD
    lanes = max(128, 3 * HD)
    return pl.pallas_call(
        functools.partial(attention_kernel, 1.0 / group),
        grid_spec=pltpu.PrefetchScalarGridSpec(
            num_scalar_prefetch=1,
            grid=(rows // PATCH,),
            in_specs=[
                pl.BlockSpec(blocks.shape, lambda i, source: (0, 0, 0, 0, 0)),
                pl.BlockSpec((1, width), lambda i, source: (0, 0)),
                pl.BlockSpec(weights.shape, lambda i, source: (0, 0, 0)),
                pl.BlockSpec(w_out.shape, lambda i, source: (0, 0)),
            ],
            out_specs=pl.BlockSpec((PATCH, width), lambda i, source: (i, 0)),
            scratch_shapes=[
                pltpu.VMEM((heads, PATCH, lanes), jnp.bfloat16),
                pltpu.VMEM((heads, PATCH, lanes), jnp.bfloat16),
                pltpu.VMEM((heads, PATCH, 2 * cols), jnp.bfloat16),
                pltpu.VMEM((256, cols), jnp.float32),
            ],
        ),
        out_shape=jax.ShapeDtypeStruct((rows, width), jnp.float32),
        compiler_params=pltpu.CompilerParams(vmem_limit_bytes=48 * 1024 * 1024),
        name="attend",
    )(source, blocks, gain_row[None, :], weights, w_out)


def matmul(left, right):
    return jnp.dot(left, right, precision=MATMUL_PRECISION, preferred_element_type=jnp.float32)


VMEM_LIMIT = 56 * 1024 * 1024
MESH = pl.DeviceIdType.MESH


def position():
    cols, reps = lax.axis_size("col"), lax.axis_size("rep")
    return cols, reps, lax.axis_index("col"), lax.axis_index("rep")


def greet(devices):
    barrier = pltpu.get_barrier_semaphore()
    for device in devices:
        pl.semaphore_signal(barrier, inc=1, device_id=device, device_id_type=MESH)
    pl.semaphore_wait(barrier, len(devices))


def remote(src, dst, send, recv, device):
    return pltpu.make_async_remote_copy(
        src_ref=src, dst_ref=dst, send_sem=send, recv_sem=recv, device_id=device, device_id_type=MESH
    )


def chunks_of(rows):
    for pieces in (8, 5, 4, 2):
        if rows % (8 * pieces) == 0:
            return pieces, rows // pieces
    return 1, rows


def gather_kernel(x_ref, out_ref, xs, xr, fs, fr, ps, pr, local):
    cols, reps, c, r = position()
    rows = x_ref.shape[0]
    pieces, size = chunks_of(rows)
    me = c * reps + r
    mate = {"col": c, "rep": 1 - r}
    others = [{"col": lax.rem(c + d, cols), "rep": r} for d in range(1, cols)]
    greet([mate] + others)
    across, onward = [], []
    for k in range(pieces):
        at = pl.ds(k * size, size)
        for d in range(1, cols):
            copy = remote(
                x_ref.at[at], out_ref.at[me, at], xs.at[d - 1, k], xr.at[d - 1, k], others[d - 1]
            )
            copy.start()
            across.append(copy)
    share = remote(x_ref, out_ref.at[me], ps, pr, mate)
    share.start()
    keep = pltpu.make_async_copy(x_ref, out_ref.at[me], local)
    keep.start()
    for k in range(pieces):
        at = pl.ds(k * size, size)
        for d in range(1, cols):
            across[k * (cols - 1) + d - 1].wait_recv()
            slot = lax.rem(c + cols - d, cols) * reps + r
            copy = remote(
                out_ref.at[slot, at], out_ref.at[slot, at], fs.at[d - 1, k], fr.at[d - 1, k], mate
            )
            copy.start()
            onward.append(copy)
    for copy in across:
        copy.wait_send()
    share.wait()
    keep.wait()
    for copy in onward:
        copy.wait()


def gather(block, collective_id):
    cols, reps = lax.axis_size("col"), lax.axis_size("rep")
    if reps != 2 or cols < 2:
        return lax.all_gather(block, ("col", "rep"), axis=0)
    pieces, _ = chunks_of(block.shape[0])
    dma = pltpu.SemaphoreType.DMA
    return pl.pallas_call(
        gather_kernel,
        out_shape=jax.ShapeDtypeStruct((cols * reps,) + block.shape, block.dtype),
        in_specs=[pl.BlockSpec(memory_space=pltpu.VMEM)],
        out_specs=pl.BlockSpec(memory_space=pltpu.VMEM),
        scratch_shapes=[dma((cols - 1, pieces))] * 4 + [dma, dma, dma],
        compiler_params=pltpu.CompilerParams(
            collective_id=collective_id, has_side_effects=True, vmem_limit_bytes=VMEM_LIMIT
        ),
        name="gather",
    )(block)


def scatter_kernel(edge, p_ref, out_ref, a_ref, s_ref, b_ref, a_s, a_r, b_s, b_r, *halo):
    cols, reps, c, r = position()
    rows = p_ref.shape[1]
    pieces, size = chunks_of(rows)
    mate = {"col": c, "rep": 1 - r}
    others = [{"col": lax.rem(c + d, cols), "rep": r} for d in range(1, cols)]
    greeted = [mate] + others
    if edge:
        ntok, t = lax.axis_size("tok"), lax.axis_index("tok")
        partner = {"tok": lax.rem(t + jnp.where(r == 0, ntok - 1, 1), ntok), "rep": 1 - r}
        greeted = greeted + [partner]
    greet(greeted)
    order = [(k, d) for k in range(pieces) for d in range(1, cols)]
    order += [(k, 0) for k in range(pieces)]
    near, far = {}, {}
    for k, d in order:
        at = pl.ds(k * size, size)
        slot = lax.rem(c + d, cols) * reps + 1 - r
        near[k, d] = remote(
            p_ref.at[slot, at], a_ref.at[d, at], a_s.at[d, k], a_r.at[d, k], mate
        )
        near[k, d].start()
    for k, d in order:
        at = pl.ds(k * size, size)
        slot = lax.rem(c + d, cols) * reps + r
        near[k, d].wait_recv()
        total = p_ref[slot, at] + a_ref[d, at]
        if d == 0:
            out_ref[at] = total
        else:
            s_ref[d - 1, at] = total
            far[k, d] = remote(
                s_ref.at[d - 1, at],
                b_ref.at[d - 1, at],
                b_s.at[d - 1, k],
                b_r.at[d - 1, k],
                others[d - 1],
            )
            far[k, d].start()
    for (k, d), copy in far.items():
        at = pl.ds(k * size, size)
        copy.wait_recv()
        out_ref[at] += b_ref[d - 1, at]
    if edge:
        h_ref, e_ref, h_s, h_r = halo
        inner = pl.multiple_of(jnp.where(r == 0, edge, rows - 2 * edge), 8)
        outer = pl.multiple_of(jnp.where(r == 0, 0, rows - edge), 8)
        e_ref[...] = out_ref[pl.ds(inner, edge)]
        copy = remote(e_ref, h_ref, h_s, h_r, partner)
        copy.start()
        copy.wait()
        wrapped = jnp.where(r == 0, t == 0, t == ntok - 1)
        out_ref[pl.ds(outer, edge)] = jnp.where(wrapped, 0.0, h_ref[...])
    for copy in list(near.values()) + list(far.values()):
        copy.wait_send()


def scatter(parts, collective_id, edge=0):
    cols, reps = lax.axis_size("col"), lax.axis_size("rep")
    if reps != 2 or cols < 2:
        return lax.psum_scatter(parts, ("col", "rep"), scatter_dimension=0)
    shape, kind = parts.shape[1:], parts.dtype
    pieces, _ = chunks_of(shape[0])
    dma = pltpu.SemaphoreType.DMA
    return pl.pallas_call(
        functools.partial(scatter_kernel, edge),
        out_shape=jax.ShapeDtypeStruct(shape, kind),
        in_specs=[pl.BlockSpec(memory_space=pltpu.VMEM)],
        out_specs=pl.BlockSpec(memory_space=pltpu.VMEM),
        scratch_shapes=[
            pltpu.VMEM((cols,) + shape, kind),
            pltpu.VMEM((cols - 1,) + shape, kind),
            pltpu.VMEM((cols - 1,) + shape, kind),
            dma((cols, pieces)),
            dma((cols, pieces)),
            dma((cols - 1, pieces)),
            dma((cols - 1, pieces)),
        ]
        + ([pltpu.VMEM((edge, shape[1]), kind)] * 2 + [dma, dma] if edge else []),
        compiler_params=pltpu.CompilerParams(
            collective_id=collective_id, has_side_effects=True, vmem_limit_bytes=VMEM_LIMIT
        ),
        name="scatter",
    )(parts)


def total_kernel(
    p_ref, out_ref, a_ref, s_ref, b_ref, a_s, a_r, b_s, b_r, xs, xr, fs, fr, ps, pr
):
    cols, reps, c, r = position()
    rows = p_ref.shape[1]
    pieces, size = chunks_of(rows)
    me = c * reps + r
    mate = {"col": c, "rep": 1 - r}
    others = [{"col": lax.rem(c + d, cols), "rep": r} for d in range(1, cols)]
    greet([mate] + others)
    order = [(k, d) for k in range(pieces) for d in range(1, cols)]
    order += [(k, 0) for k in range(pieces)]
    near, far, across, share, onward = {}, {}, {}, {}, {}
    for k, d in order:
        at = pl.ds(k * size, size)
        slot = lax.rem(c + d, cols) * reps + 1 - r
        near[k, d] = remote(
            p_ref.at[slot, at], a_ref.at[d, at], a_s.at[d, k], a_r.at[d, k], mate
        )
        near[k, d].start()
    for k, d in order:
        if d == 0:
            continue
        at = pl.ds(k * size, size)
        slot = lax.rem(c + d, cols) * reps + r
        near[k, d].wait_recv()
        s_ref[d - 1, at] = p_ref[slot, at] + a_ref[d, at]
        far[k, d] = remote(
            s_ref.at[d - 1, at], b_ref.at[d - 1, at], b_s.at[d - 1, k], b_r.at[d - 1, k], others[d - 1]
        )
        far[k, d].start()
    for k in range(pieces):
        at = pl.ds(k * size, size)
        near[k, 0].wait_recv()
        total = p_ref[me, at] + a_ref[0, at]
        for d in range(1, cols):
            far[k, d].wait_recv()
            total = total + b_ref[d - 1, at]
        out_ref[me, at] = total
        for d in range(1, cols):
            across[k, d] = remote(
                out_ref.at[me, at], out_ref.at[me, at], xs.at[d - 1, k], xr.at[d - 1, k], others[d - 1]
            )
            across[k, d].start()
        share[k] = remote(out_ref.at[me, at], out_ref.at[me, at], ps.at[k], pr.at[k], mate)
        share[k].start()
    for (k, d), copy in across.items():
        at = pl.ds(k * size, size)
        copy.wait_recv()
        slot = lax.rem(c + cols - d, cols) * reps + r
        onward[k, d] = remote(
            out_ref.at[slot, at], out_ref.at[slot, at], fs.at[d - 1, k], fr.at[d - 1, k], mate
        )
        onward[k, d].start()
    for copies in (near, far, across):
        for copy in copies.values():
            copy.wait_send()
    for copies in (share, onward):
        for copy in copies.values():
            copy.wait()


def total(parts, collective_id):
    cols, reps = lax.axis_size("col"), lax.axis_size("rep")
    if reps != 2 or cols < 2:
        return lax.psum(parts, ("col", "rep"))
    shape, kind = parts.shape[1:], parts.dtype
    pieces, _ = chunks_of(shape[0])
    dma = pltpu.SemaphoreType.DMA
    return pl.pallas_call(
        total_kernel,
        out_shape=jax.ShapeDtypeStruct(parts.shape, kind),
        in_specs=[pl.BlockSpec(memory_space=pltpu.VMEM)],
        out_specs=pl.BlockSpec(memory_space=pltpu.VMEM),
        scratch_shapes=[
            pltpu.VMEM((cols,) + shape, kind),
            pltpu.VMEM((cols - 1,) + shape, kind),
            pltpu.VMEM((cols - 1,) + shape, kind),
            dma((cols, pieces)),
            dma((cols, pieces)),
        ]
        + [dma((cols - 1, pieces))] * 6
        + [dma((pieces,))] * 2,
        compiler_params=pltpu.CompilerParams(
            collective_id=collective_id, has_side_effects=True, vmem_limit_bytes=VMEM_LIMIT
        ),
        name="total",
    )(parts)


def move_kernel(o_ref, code_ref, out_ref, arrived_ref, zs, zr, cs, cr, xs, xr, fs, fr, ps, pr, local):
    cols, reps, c, r = position()
    ntok, t = lax.axis_size("tok"), lax.axis_index("tok")
    me = c * reps + r
    mate = {"col": c, "rep": 1 - r}
    others = [{"col": lax.rem(c + d, cols), "rep": r} for d in range(1, cols)]
    peers = [{"tok": lax.rem(t + e, ntok)} for e in range(1, ntok)]
    greet([mate] + others + peers)
    along, codes, across, share, onward = [], [], {}, [], []
    for e in range(1, ntok):
        target = lax.rem(t + e, ntok)
        copy = remote(o_ref.at[target], out_ref.at[t, me], zs.at[e - 1], zr.at[e - 1], peers[e - 1])
        copy.start()
        along.append(copy)
        copy = remote(
            code_ref.at[target], arrived_ref.at[t], cs.at[e - 1], cr.at[e - 1], peers[e - 1]
        )
        copy.start()
        codes.append(copy)
    keep = pltpu.make_async_copy(o_ref.at[t], out_ref.at[t, me], local.at[0])
    keep.start()
    keep_code = pltpu.make_async_copy(code_ref.at[t], arrived_ref.at[t], local.at[1])
    keep_code.start()

    def hand_on(e):
        u = lax.rem(t + ntok - e, ntok)
        for d in range(1, cols):
            across[e, d].wait_recv()
            slot = lax.rem(c + cols - d, cols) * reps + r
            copy = remote(
                out_ref.at[u, slot], out_ref.at[u, slot], fs.at[e, d - 1], fr.at[e, d - 1], mate
            )
            copy.start()
            onward.append(copy)

    for e in range(ntok):
        u = lax.rem(t + ntok - e, ntok)
        if e:
            along[e - 1].wait_recv()
        origin = out_ref.at[u, me] if e else o_ref.at[t]
        for d in range(1, cols):
            across[e, d] = remote(
                origin, out_ref.at[u, me], xs.at[e, d - 1], xr.at[e, d - 1], others[d - 1]
            )
            across[e, d].start()
        copy = remote(origin, out_ref.at[u, me], ps.at[e], pr.at[e], mate)
        copy.start()
        share.append(copy)
        if e:
            hand_on(e - 1)
    hand_on(ntok - 1)
    keep.wait()
    keep_code.wait()
    for copy in along + list(across.values()):
        copy.wait_send()
    for copy in codes + share + onward:
        copy.wait()


def move(outgoing, codes, collective_id):
    cols, reps, ntok = lax.axis_size("col"), lax.axis_size("rep"), lax.axis_size("tok")
    if reps != 2 or cols < 2 or ntok < 2:
        incoming = lax.all_to_all(outgoing, "tok", split_axis=0, concat_axis=0, tiled=True)
        arrived = lax.all_to_all(codes, "tok", split_axis=0, concat_axis=0, tiled=True)
        return lax.all_gather(incoming, ("col", "rep"), axis=1), arrived
    dma = pltpu.SemaphoreType.DMA
    shape = (ntok, cols * reps) + outgoing.shape[1:]
    return pl.pallas_call(
        move_kernel,
        out_shape=(
            jax.ShapeDtypeStruct(shape, outgoing.dtype),
            jax.ShapeDtypeStruct(codes.shape, codes.dtype),
        ),
        in_specs=[pl.BlockSpec(memory_space=pltpu.VMEM)] * 2,
        out_specs=[pl.BlockSpec(memory_space=pltpu.VMEM)] * 2,
        scratch_shapes=[dma((ntok - 1,))] * 4
        + [dma((ntok, cols - 1))] * 4
        + [dma((ntok,))] * 2
        + [dma((2,))],
        compiler_params=pltpu.CompilerParams(
            collective_id=collective_id, has_side_effects=True, vmem_limit_bytes=VMEM_LIMIT
        ),
        name="move",
    )(outgoing, codes)


def pick_kernel(index_ref, x_ref, out_ref):
    for j in range(out_ref.shape[0]):
        out_ref[j] = x_ref[index_ref[j]]


def pick(blocks, index):
    return pl.pallas_call(
        pick_kernel,
        out_shape=jax.ShapeDtypeStruct(index.shape + blocks.shape[1:], blocks.dtype),
        in_specs=[pl.BlockSpec(memory_space=pltpu.SMEM), pl.BlockSpec(memory_space=pltpu.VMEM)],
        out_specs=pl.BlockSpec(memory_space=pltpu.VMEM),
        name="pick",
    )(index, blocks)


def attention_layer(blocks, source, layer, w_qkv, w_out, attn_gain, collective_id):
    group = blocks.shape[1]
    terms = attend(blocks, source, attn_gain[layer], w_qkv[layer], w_out[layer], group)
    rows, width = terms.shape
    return total(terms.reshape(group, rows // group, width), collective_id).reshape(rows, width)


def mlp_kernel(x_ref, gain_ref, up_ref, down_ref, share, out_ref):
    x = x_ref[...]
    hidden = dot3(split(layer_norm(x, gain_ref[...])), split(up_ref[...]))
    hidden = 0.5 * hidden * (1.0 + lax.erf(hidden * (0.5**0.5)))
    total = dot3(split(hidden), split(down_ref[...])) + x * share
    width = out_ref.shape[-1]
    for j in range(out_ref.shape[0]):
        out_ref[j] = total[:, j * width : (j + 1) * width]


def mlp_partial(stream, layer, w_up, w_down, mlp_gain, slots):
    rows, width = stream.shape
    tile = min(256, rows)
    hidden = w_up.shape[-1]
    group = lax.axis_size("col") * lax.axis_size("rep")

    def kernel(x_ref, gain_ref, up_ref, down_ref, out_ref):
        mlp_kernel(x_ref, gain_ref, up_ref, down_ref, 1.0 / group, out_ref)

    return pl.pallas_call(
        kernel,
        grid=(rows // tile,),
        in_specs=[
            pl.BlockSpec((tile, width), lambda i: (i, 0)),
            pl.BlockSpec((1, width), lambda i: (0, 0)),
            pl.BlockSpec((width, hidden), lambda i: (0, 0)),
            pl.BlockSpec((hidden, width), lambda i: (0, 0)),
        ],
        out_specs=pl.BlockSpec((slots, tile, width // slots), lambda i: (0, i, 0)),
        out_shape=jax.ShapeDtypeStruct((slots, rows, width // slots), jnp.float32),
        compiler_params=pltpu.CompilerParams(vmem_limit_bytes=48 * 1024 * 1024),
        name="mlp",
    )(stream, mlp_gain[layer][None, :], w_up[layer], w_down[layer])


def gelu(values):
    return 0.5 * values * (1.0 + lax.erf(values * (0.5**0.5)))


def piece(i, size):
    return pl.ds(pl.multiple_of(i * size, size), size)


class Layer:
    def __init__(self, layer, refs, heads, chunk, kinds):
        self.__dict__.update(refs)
        self.layer, self.heads, self.chunk, self.kinds = layer, heads, chunk, kinds
        self.cols, self.reps, self.c, self.r = position()
        self.ntok, self.t = lax.axis_size("tok"), lax.axis_index("tok")
        self.me = self.c * self.reps + self.r
        self.mate, self.peer = {"rep": 1 - self.r}, {"col": 1 - self.c}
        self.peers = [{"tok": lax.rem(self.t + e, self.ntok)} for e in range(1, self.ntok)]
        self.rows, self.width = self.a_s.shape
        self.lanes = self.q_s.shape[-1] // 2
        self.n = self.rows // chunk
        self.started = []

    def sent(self, kind, i, src, dst, device):
        k = self.kinds.index(kind)
        return remote(src, dst, self.sem.at[k, 0, i], self.sem.at[k, 1, i], device)

    def load_weights(self):
        pairs = (
            (self.wqkv_ref, self.wqkv_f), (self.wo_ref, self.wo_f),
            (self.wu_ref, self.wu_f), (self.wd_ref, self.wd_f),
        )
        self.loads = [
            pltpu.make_async_copy(src.at[self.layer], dst, self.wsem.at[j])
            for j, (src, dst) in enumerate(pairs)
        ]
        for load in self.loads:
            load.start()

    def split_weights(self):
        self.loads[0].wait()
        for m in range(3):
            self.wqkv_s[0, m], self.wqkv_s[1, m] = split(self.wqkv_f[m])
        rest = ((self.wo_f, self.wo_s), (self.wu_f, self.wu_s), (self.wd_f, self.wd_s))
        for load, (src, dst) in zip(self.loads[1:], rest):
            load.wait()
            dst[0], dst[1] = split(src[...])

    def project(self, stream):
        normed = split(layer_norm(stream, self.ga_ref[pl.ds(self.layer, 1)]))
        return [dot3(normed, (self.wqkv_s[0, m], self.wqkv_s[1, m])) for m in range(3)]

    def pack(self, at, q, k, v):
        lanes = self.lanes
        half_lanes = lanes // 2
        lane = lax.broadcasted_iota(jnp.int32, (1, lanes), 1)
        low = lane < half_lanes
        qh, ql = split(q * (HD ** (-0.5) * math.log2(math.e)))
        kh, kl = [part.astype(jnp.float32) for part in split(k)]
        vh, vl = [part.astype(jnp.float32) for part in split(v)]
        qf, qlf = qh.astype(jnp.float32), ql.astype(jnp.float32)
        q_s, k_s, v_s = self.q_s, self.k_s, self.v_s

        def roll(values):
            return pltpu.roll(values, half_lanes, 1)

        q_s[0, at, :lanes] = qh
        q_s[1, at, :lanes] = qh
        q_s[0, at, lanes:] = jnp.where(low, qf, roll(qlf)).astype(jnp.bfloat16)
        q_s[1, at, lanes:] = jnp.where(low, roll(qf), qlf).astype(jnp.bfloat16)
        k_s[0, at, :lanes] = kh.astype(jnp.bfloat16)
        k_s[1, at, :lanes] = kh.astype(jnp.bfloat16)
        k_s[0, at, lanes:] = jnp.where(low, kl, roll(kh)).astype(jnp.bfloat16)
        k_s[1, at, lanes:] = jnp.where(low, roll(kl), kh).astype(jnp.bfloat16)
        v_s[0, at, :lanes] = vh.astype(jnp.bfloat16)
        v_s[1, at, :lanes] = vh.astype(jnp.bfloat16)
        v_s[0, at, lanes:] = jnp.where(low, vl, 1.0).astype(jnp.bfloat16)
        v_s[1, at, lanes:] = jnp.where(low, 1.0, vl).astype(jnp.bfloat16)

    def near(self, i):
        half = self.chunk // 2
        start = pl.multiple_of(i * self.chunk + (1 - self.r) * half, half)
        return self.sent("near", i, self.p_s.at[pl.ds(start, half)], self.n1_s.at[piece(i, half)], self.mate)

    def far(self, i):
        at = piece(i, self.chunk // 2)
        return self.sent("far", i, self.s1_s.at[at], self.f1_s.at[at], self.peer)

    def own_half(self, i):
        half = self.chunk // 2
        return pl.ds(pl.multiple_of(i * self.chunk + self.r * half, half), half)

    def share(self, i):
        at = self.own_half(i)
        return self.sent("share", i, self.a_s.at[at], self.a_s.at[at], self.mate)

    def attention(self, k):
        lanes, half_heads, chunk = self.lanes, self.heads // 2, self.chunk
        wide = lax.broadcasted_iota(jnp.int32, (1, 2 * lanes), 1)
        lane = lax.broadcasted_iota(jnp.int32, (1, lanes), 1)
        i, half = k // 2, k % 2
        query = self.q_s[half, piece(i, chunk), :]
        queries = []
        for m in range(half_heads):
            first = (wide < lanes) & (wide // HD == half * half_heads + m)
            second = (wide >= lanes) & ((wide % (lanes // 2)) // HD == m)
            mask = jnp.where(first | second, 1.0, 0.0).astype(jnp.bfloat16)
            queries.append(query * mask)
        stacked = jnp.concatenate(queries, axis=0)
        scores = bdot(stacked, self.k_s[half], (((1,), (1,)), ((), ())))
        weights = jnp.exp2(scores - jnp.max(scores, axis=-1, keepdims=True))
        sums = bdot(jnp.concatenate(split(weights), axis=0), self.v_s[half])
        sums = sums[: half_heads * chunk] + sums[half_heads * chunk :]
        total = jnp.zeros((chunk, lanes), jnp.float32)
        for m in range(half_heads):
            own = sums[m * chunk : (m + 1) * chunk]
            top, low = own[:, :lanes], own[:, lanes:]
            ratio = (top + low) / pltpu.roll(low, lanes // 2, 1)
            total += jnp.where(lane // HD == half * half_heads + m, ratio, 0.0)
        self.att_s[half] = total

    def finish(self, i):
        projection = (self.wo_s[0], self.wo_s[1])
        self.p_s[piece(i, self.chunk)] = dot3(split(self.att_s[0] + self.att_s[1]), projection)
        self.near(i).start()

    def reduce_near(self, i):
        self.near(i).wait_recv()
        at = piece(i, self.chunk // 2)
        self.s1_s[at] = self.p_s[self.own_half(i)] + self.n1_s[at]
        self.far(i).start()

    def reduce_far(self, i):
        self.far(i).wait_recv()
        half = self.chunk // 2
        at = piece(i, half)
        stream = self.stream_rows(i * self.chunk + self.r * half, half)
        self.a_s[self.own_half(i)] = (self.s1_s[at] + self.f1_s[at]) + stream
        self.share(i).start()

    def mlp(self, x):
        normed = split(layer_norm(x, self.gm_ref[pl.ds(self.layer, 1)]))
        hidden = gelu(dot3(normed, (self.wu_s[0], self.wu_s[1])))
        return dot3(split(hidden), (self.wd_s[0], self.wd_s[1]))

    def run(self, stages):
        n = self.n

        def tick(k, carry):
            @pl.when(k < 2 * n)
            def _():
                self.attention(k)

            for offset, stage in stages:
                @pl.when((k >= offset) & (k < offset + 2 * n) & ((k - offset) % 2 == 0))
                def _(offset=offset, stage=stage):
                    stage((k - offset) // 2)

            return carry

        lax.fori_loop(0, 2 * n + max(offset for offset, _ in stages) - 1, tick, 0)


class First(Layer):
    def stream_rows(self, start, count):
        at = pl.ds(pl.multiple_of(start, count), count)
        return jnp.concatenate([self.g_s[j, at] for j in range(self.cols * self.reps)], axis=-1)

    def across(self, i):
        at = piece(i, self.chunk)
        return self.sent("across", i, self.x_ref.at[at], self.g_s.at[self.me, at], self.peer)

    def over(self, i):
        at = piece(i, self.chunk)
        return self.sent("over", i, self.x_ref.at[at], self.g_s.at[self.me, at], self.mate)

    def relay(self, i):
        at = piece(i, self.chunk)
        slot = (1 - self.c) * self.reps + self.r
        return self.sent("relay", i, self.g_s.at[slot, at], self.g_s.at[slot, at], self.mate)

    def code(self, e):
        target = {"tok": lax.rem(self.t + e, self.ntok)}
        return self.sent("code", e, self.code_s, self.arrived_s.at[self.t], target)

    def route(self):
        device = self.dd_ref[...].astype(jnp.float32)
        slot = self.ds_ref[...].astype(jnp.float32)
        count = device.shape[1]
        row = lax.broadcasted_iota(jnp.int32, (count, count), 0)
        col = lax.broadcasted_iota(jnp.int32, (count, count), 1)

        def upright(values):
            return jnp.sum(jnp.where(row == col, values, 0.0), axis=1, keepdims=True)

        devices, slots = upright(device), upright(slot)
        earlier = jnp.where((devices == device) & (col < row), 1.0, 0.0)
        place = devices * self.cap + jnp.sum(earlier, axis=1, keepdims=True)
        at = lax.broadcasted_iota(jnp.int32, (count, 128), 1).astype(jnp.float32)
        block = lax.broadcasted_iota(jnp.int32, (count, 128), 0).astype(jnp.float32)
        index = jnp.sum(jnp.where(place == at, block, 0.0), axis=0, keepdims=True)
        code = jnp.sum(jnp.where(place == at, slots + 1.0, 0.0), axis=0, keepdims=True)
        self.index_ref[...] = index.astype(jnp.int32)
        self.code_s[...] = jnp.broadcast_to(code, self.code_s.shape)
        self.arrived_s[self.t] = jnp.broadcast_to(code, self.code_s.shape)

    def locate(self):
        row = lax.broadcasted_iota(jnp.int32, (128, 128), 0)
        col = lax.broadcasted_iota(jnp.int32, (128, 128), 1)
        first = self.t * self.cap
        valid = (row >= first) & (row < first + self.cap)
        source = jnp.zeros((1, 128), jnp.float32)
        for u in range(self.ntok):
            codes = self.arrived_s[u][:1]
            upright = jnp.sum(jnp.where(row == col, codes, 0.0), axis=1, keepdims=True)
            found = valid & (upright == (col + 1).astype(jnp.float32))
            entry = (row - first + u * self.cap).astype(jnp.float32)
            source += jnp.sum(jnp.where(found, entry, 0.0), axis=0, keepdims=True)
        self.source_ref[...] = source.astype(jnp.int32)

    def near2(self, i):
        at = piece(i, self.chunk)
        return self.sent("near2", i, self.m_s.at[1 - self.r, :, at], self.n2_s.at[:, at], self.mate)

    def far2(self, i):
        at = piece(i, self.chunk)
        return self.sent("far2", i, self.s2_s.at[at], self.f2_s.at[at], self.peer)

    def feed(self, i):
        self.share(i).wait_recv()
        at = piece(i, self.chunk)
        total = self.mlp(self.a_s[at])
        for j in range(self.cols * self.reps):
            self.m_s[j % self.reps, j // self.reps, at] = total[:, j * self.lanes : (j + 1) * self.lanes]
        self.near2(i).start()

    def scatter_near(self, i):
        self.near2(i).wait_recv()
        at = piece(i, self.chunk)
        self.s2_s[at] = self.m_s[self.r, 1 - self.c, at] + self.n2_s[1 - self.c, at]
        self.far2(i).start()

    def scatter_far(self, i):
        self.far2(i).wait_recv()
        at = piece(i, self.chunk)
        own = self.a_s[at, piece(self.me, self.lanes)]
        total = (self.m_s[self.r, self.c, at] + self.n2_s[self.c, at]) + self.f2_s[at]
        self.out_ref[at] = total + own

    def body(self):
        n = self.n
        self.load_weights()
        greet([self.mate, self.peer] + self.peers)
        for i in range(n):
            self.across(i).start()
        for i in range(n):
            self.over(i).start()
        self.cap = capacity_of(self.dd_ref.shape[1], self.ntok)
        self.route()
        self.g_s[self.me] = self.x_ref[...]
        self.split_weights()
        for e in range(1, self.ntok):
            self.code(e).start()

        def step(i, carry):
            @pl.when(i < n)
            def _():
                self.across(i).wait_recv()
                self.relay(i).start()

            @pl.when(i > 0)
            def _():
                self.over(i - 1).wait_recv()
                self.relay(i - 1).wait_recv()
                stream = self.stream_rows((i - 1) * self.chunk, self.chunk)
                self.pack(piece(i - 1, self.chunk), *self.project(stream))

            return carry

        lax.fori_loop(0, n + 1, step, 0)
        self.run(
            [
                (1, self.finish), (2, self.reduce_near), (9, self.scatter_near),
                (6, self.reduce_far), (7, self.feed), (13, self.scatter_far),
            ]
        )
        for copy in (
            self.near, self.far, self.share, self.near2, self.far2, self.across, self.over, self.relay
        ):
            for i in range(n):
                copy(i).wait_send()
        for e in range(1, self.ntok):
            self.code(e).wait()
        self.locate()


class Second(Layer):
    def stream_rows(self, start, count):
        parts = []
        for m in range(count // self.block):
            at = self.source_ref[0, start // self.block + m]
            places = [self.g_s[at // self.cap, j, at % self.cap] for j in range(self.cols * self.reps)]
            parts.append(jnp.concatenate(places, axis=-1))
        return jnp.concatenate(parts, axis=0)

    def along(self, e, j):
        target = lax.rem(self.t + e, self.ntok)
        return self.sent(
            "along", e * self.cap + j, self.o_s.at[target, j], self.g_s.at[self.t, self.me, j],
            {"tok": target},
        )

    def origin(self, e):
        return lax.rem(self.t + self.ntok - e, self.ntok)

    def placed(self, kind, e, j, slot, device):
        ref = self.g_s.at[self.origin(e), slot, j]
        return self.sent(kind, e * self.cap + j, ref, ref, device)

    def across(self, e, j):
        return self.placed("across", e, j, self.me, self.peer)

    def over(self, e, j):
        return self.placed("over", e, j, self.me, self.mate)

    def relay(self, e, j):
        return self.placed("relay", e, j, (1 - self.c) * self.reps + self.r, self.mate)

    def arrive(self, j):
        for e in self.order[1:]:
            self.along(e, j).wait_recv()
            self.across(e, j).start()
            self.over(e, j).start()

    def hand(self, j):
        for e in self.order:
            self.across(e, j).wait_recv()
            self.relay(e, j).start()

    def take(self, j):
        parts = []
        for e in self.order:
            self.over(e, j).wait_recv()
            self.relay(e, j).wait_recv()
            places = [self.g_s[self.origin(e), k, j] for k in range(self.cols * self.reps)]
            parts.append(jnp.concatenate(places, axis=-1))
        for m, values in enumerate(self.project(jnp.concatenate(parts, axis=0))):
            for at, e in enumerate(self.order):
                entry = self.origin(e) * self.cap + j
                self.raw_s[m, entry] = values[at * self.block : (at + 1) * self.block]

    def move(self):
        self.order = [0]
        for e in range(1, self.ntok // 2 + 1):
            self.order += [e] + ([self.ntok - e] if self.ntok - e != e else [])
        for u in range(self.ntok):
            for j in range(self.cap):
                self.o_s[u, j] = self.x_ref[self.index_ref[0, u * self.cap + j]]
        for j in range(self.cap):
            self.g_s[self.t, self.me, j] = self.x_ref[self.index_ref[0, self.t * self.cap + j]]
        for j in range(self.cap):
            for e in self.order[1:]:
                self.along(e, j).start()
        for j in range(self.cap):
            self.across(0, j).start()
            self.over(0, j).start()
        self.split_weights()
        for j in range(self.cap):
            self.arrive(j)
            if j == 0:
                self.split_points()
            if j >= 1:
                self.hand(j - 1)
            if j >= 2:
                self.take(j - 2)
        self.hand(self.cap - 1)
        for j in range(max(0, self.cap - 2), self.cap):
            self.take(j)

        def step(i, carry):
            def row(m):
                each = self.chunk // self.block
                blocks = [self.raw_s[m, self.source_ref[0, i * each + k]] for k in range(each)]
                return jnp.concatenate(blocks, axis=0)

            self.pack(piece(i, self.chunk), row(0), row(1), row(2))
            return carry

        lax.fori_loop(0, self.n, step, 0)

    def load_points(self):
        self.point = pltpu.make_async_copy(self.pw_ref, self.pw_f, self.wsem.at[4])
        self.point.start()

    def split_points(self):
        self.point.wait()

        def step(k, carry):
            at = piece(k, 64)
            for l in range(2):
                self.pw_s[0, l, at], self.pw_s[1, l, at] = split(self.pw_f[l, at])
            return carry

        lax.fori_loop(0, self.width // 64, step, 0)

    def cell_ids(self):
        count = self.pool_s.shape[0]
        p = lax.broadcasted_iota(jnp.int32, (count, 1), 0)
        wide = TC + 2 * HALO
        row = ((p.astype(jnp.float32) + 0.5) * (1.0 / wide)).astype(jnp.int32)
        col = row // TR
        x = col * TC - HALO + (p - row * wide)
        full = TC * self.cols
        y = row - col * TR
        return jnp.where((x >= 0) & (x < full), (self.t * TR + y) * full + x, -2)

    def feed(self, i):
        self.share(i).wait_recv()
        at = piece(i, self.chunk)
        x = self.a_s[at]
        high, low = split(self.mlp(x) + x * (1.0 / (self.cols * self.reps)))
        chosen = jnp.where(self.cell_ids() == self.pillar_ref[:, at], 1.0, 0.0).astype(jnp.bfloat16)
        self.pool_s[...] += bdot(chosen, high) + bdot(chosen, low)

    def tile_part(self, c, r, k):
        cells = self.pool_s.shape[0] // (self.cols * self.reps)
        start = (c * self.reps + r) * cells + k * self.edge
        return pl.ds(pl.multiple_of(start, 8), self.edge)

    def near3(self, w, k):
        c = self.c if w else 1 - self.c
        return self.sent(
            "near3", w * self.pieces + k, self.pool_s.at[self.tile_part(c, 1 - self.r, k)],
            self.n3_s.at[w, k], self.mate,
        )

    def far3(self, k):
        return self.sent("far3", k, self.s3_s.at[k], self.f3_s.at[k], self.peer)

    def inner(self):
        start = jnp.where(self.r == 0, self.pieces * self.edge, self.edge)
        src = self.tile_s.at[pl.ds(pl.multiple_of(start, 8), self.edge)]
        return self.sent("halo", 0, src, self.h_s.at[0], self.mate)

    def outer(self):
        start = jnp.where(self.r == 0, self.edge, self.pieces * self.edge)
        src = self.tile_s.at[pl.ds(pl.multiple_of(start, 8), self.edge)]
        return self.sent("halo", 1, src, self.h_s.at[1], self.partner)

    def scatter(self):
        order = [0, self.pieces - 1] + list(range(1, self.pieces - 1))
        for w in range(2):
            for k in order:
                self.near3(w, k).start()
        for k in order:
            self.near3(0, k).wait_recv()
            self.s3_s[k] = self.pool_s[self.tile_part(1 - self.c, self.r, k)] + self.n3_s[0, k]
            self.far3(k).start()
        for at, k in enumerate(order):
            self.near3(1, k).wait_recv()
            self.far3(k).wait_recv()
            own = self.pool_s[self.tile_part(self.c, self.r, k)] + self.n3_s[1, k]
            self.tile_s[pl.ds((k + 1) * self.edge, self.edge)] = own + self.f3_s[k]
            if at == 1:
                self.inner().start()
                self.outer().start()
        self.inner().wait()
        self.outer().wait()
        wrapped = jnp.where(self.r == 0, self.t == 0, self.t == self.ntok - 1)
        beyond = jnp.where(wrapped, 0.0, self.h_s[1])
        within = self.h_s[0]
        self.tile_s[: self.edge] = jnp.where(self.r == 0, beyond, within)
        self.tile_s[(self.pieces + 1) * self.edge :] = jnp.where(self.r == 0, within, beyond)

    def raster(self):
        wide = TC + 2 * HALO
        rows = self.tile_s.shape[0] // wide
        pad = (self.flat_s.shape[0] - rows * wide) // 2
        self.flat_s[:pad] = jnp.zeros((pad, self.width), jnp.float32)
        self.flat_s[pad + rows * wide :] = jnp.zeros((pad, self.width), jnp.float32)
        for l in range(2):
            old = pl.ds(l * wide, (rows - 2 * l) * wide)
            start, count = (l + 1) * wide, (rows - 2 * l - 2) * wide
            cells = self.tile_s[old]
            square = jnp.mean(cells * cells, axis=-1, keepdims=True)
            gain = self.rg_ref[pl.ds(l, 1)]
            self.flat_s[pl.ds(pad + l * wide, (rows - 2 * l) * wide)] = (
                cells * lax.rsqrt(square + EPSILON) * gain
            )
            mixed = jnp.zeros((count, self.width), jnp.float32)
            for a in range(3):
                for b in range(3):
                    shift = pad + start + (a - 1) * wide + b - 1
                    mixed = mixed + self.flat_s[pl.ds(shift, count)] * self.dw_ref[a, b, pl.ds(l, 1)]
            both = dot3(split(mixed), (self.pw_s[0, l], self.pw_s[1, l]))
            centre = self.tile_s[pl.ds(start, count)]
            result = centre + both[:, : self.width] * jax.nn.sigmoid(both[:, self.width :])
            if l == 0:
                p = lax.broadcasted_iota(jnp.int32, (count, 1), 0) + start
                row = ((p.astype(jnp.float32) + 0.5) * (1.0 / wide)).astype(jnp.int32)
                y = (self.t * self.reps + self.r) * (rows - 2 * HALO) - HALO + row
                x = self.c * TC - HALO + (p - row * wide)
                inside = (y >= 0) & (y < TR * self.ntok) & (x >= 0) & (x < TC * self.cols)
                result = jnp.where(inside, result, 0.0)
            self.tile_s[pl.ds(start, count)] = result
        for y in range(rows - 2 * HALO):
            self.out_ref[y] = self.tile_s[pl.ds((y + HALO) * wide + HALO, TC)]

    def body(self):
        self.block = self.x_ref.shape[1]
        self.cap = self.g_s.shape[2]
        self.pieces, self.edge = self.s3_s.shape[:2]
        step = jnp.where(self.r == 0, self.ntok - 1, 1)
        self.partner = {"tok": lax.rem(self.t + step, self.ntok), "rep": 1 - self.r}
        self.load_weights()
        self.load_points()
        greet([self.mate, self.peer, self.partner] + self.peers)
        self.move()
        self.pool_s[...] = jnp.zeros(self.pool_s.shape, jnp.float32)
        self.run([(1, self.finish), (2, self.reduce_near), (7, self.feed), (5, self.reduce_far)])
        self.scatter()
        self.raster()
        for copy in (self.near, self.far, self.share):
            for i in range(self.n):
                copy(i).wait_send()
        for j in range(self.cap):
            for e in range(self.ntok):
                if e:
                    self.along(e, j).wait_send()
                for copy in (self.across, self.over, self.relay):
                    copy(e, j).wait_send()
        for k in range(self.pieces):
            self.near3(0, k).wait_send()
            self.near3(1, k).wait_send()
            self.far3(k).wait_send()


def run_layer(kind, layer, inputs, outputs, weights, collective_id, extra, kinds, most):
    w_qkv, w_out, w_up, w_down, attn_gain, mlp_gain = weights
    lanes, width, hidden = w_qkv.shape[-1], w_qkv.shape[-2], w_up.shape[-1]
    heads, rows = lanes // HD, PATCH
    chunk = min(256, rows)
    dma, f32, b16 = pltpu.SemaphoreType.DMA, jnp.float32, jnp.bfloat16
    vmem = pl.BlockSpec(memory_space=pltpu.VMEM)
    hbm = pl.BlockSpec(memory_space=pl.ANY)
    smem = pl.BlockSpec(memory_space=pltpu.SMEM)
    inputs = dict(inputs)
    places = {name: vmem for name in inputs}
    inputs.update(ga_ref=attn_gain, gm_ref=mlp_gain)
    inputs.update(wqkv_ref=w_qkv, wo_ref=w_out, wu_ref=w_up, wd_ref=w_down)
    for name in ("index_ref", "source_ref"):
        if name in inputs:
            places[name] = smem
    for name in ("wqkv_ref", "wo_ref", "wu_ref", "wd_ref", "pw_ref"):
        places[name] = hbm
    scratch = dict(
        wqkv_f=pltpu.VMEM((3, width, lanes), f32),
        wo_f=pltpu.VMEM((lanes, width), f32),
        wu_f=pltpu.VMEM((width, hidden), f32),
        wd_f=pltpu.VMEM((hidden, width), f32),
        wqkv_s=pltpu.VMEM((2, 3, width, lanes), b16),
        wo_s=pltpu.VMEM((2, lanes, width), b16),
        wu_s=pltpu.VMEM((2, width, hidden), b16),
        wd_s=pltpu.VMEM((2, hidden, width), b16),
        q_s=pltpu.VMEM((2, rows, 2 * lanes), b16),
        k_s=pltpu.VMEM((2, rows, 2 * lanes), b16),
        v_s=pltpu.VMEM((2, rows, 2 * lanes), b16),
        att_s=pltpu.VMEM((2, chunk, lanes), f32),
        p_s=pltpu.VMEM((rows, width), f32),
        n1_s=pltpu.VMEM((rows // 2, width), f32),
        s1_s=pltpu.VMEM((rows // 2, width), f32),
        f1_s=pltpu.VMEM((rows // 2, width), f32),
        a_s=pltpu.VMEM((rows, width), f32),
        sem=dma((len(kinds), 2, max(most, rows // chunk))),
        wsem=dma((5,)),
    )
    scratch.update(extra)
    names = list(inputs) + list(outputs) + list(scratch)

    def kernel(*refs):
        kind(layer, dict(zip(names, refs)), heads, chunk, kinds).body()

    return pl.pallas_call(
        kernel,
        out_shape=tuple(outputs.values()),
        in_specs=[places.get(name, vmem) for name in inputs],
        out_specs=tuple(vmem for _ in outputs),
        scratch_shapes=list(scratch.values()),
        compiler_params=pltpu.CompilerParams(
            collective_id=collective_id, has_side_effects=True, vmem_limit_bytes=VMEM_LIMIT
        ),
        name=kind.__name__.lower(),
    )(*inputs.values())


def capacity_of(count, peers):
    return max(2, (count + peers - 4) // (peers - 1))


def first_layer(tokens, dest_device, dest_slot, weights, collective_id):
    rows, lanes = tokens.shape
    cols, reps, ntok = lax.axis_size("col"), lax.axis_size("rep"), lax.axis_size("tok")
    f32 = jnp.float32
    extra = dict(
        g_s=pltpu.VMEM((cols * reps, rows, lanes), f32),
        m_s=pltpu.VMEM((reps, cols, rows, lanes), f32),
        n2_s=pltpu.VMEM((cols, rows, lanes), f32),
        s2_s=pltpu.VMEM((rows, lanes), f32),
        f2_s=pltpu.VMEM((rows, lanes), f32),
        code_s=pltpu.VMEM((8, 128), f32),
        arrived_s=pltpu.VMEM((ntok, 8, 128), f32),
    )
    kinds = ("near", "far", "share", "near2", "far2", "across", "over", "relay", "code")
    table = jax.ShapeDtypeStruct((1, 128), jnp.int32)
    outputs = dict(
        out_ref=jax.ShapeDtypeStruct((rows, lanes), f32), index_ref=table, source_ref=table
    )
    inputs = dict(x_ref=tokens, dd_ref=dest_device[None, :], ds_ref=dest_slot[None, :])
    return run_layer(First, 0, inputs, outputs, weights, collective_id, extra, kinds, ntok)


def second_layer(share, index, source, cap, pillar, raster_weights, weights, collective_id):
    cols, reps, ntok = lax.axis_size("col"), lax.axis_size("rep"), lax.axis_size("tok")
    count, block, lanes = share.shape
    depth_weight, point_weight, raster_gain = raster_weights
    width = depth_weight.shape[-1]
    wide, rep_rows = TC + 2 * HALO, TR // reps
    edge, pieces = HALO * wide, rep_rows // HALO
    tile = (rep_rows + 2 * HALO) * wide
    f32 = jnp.float32
    extra = dict(
        o_s=pltpu.VMEM((ntok, cap, block, lanes), f32),
        g_s=pltpu.VMEM((ntok, cols * reps, cap, block, lanes), f32),
        raw_s=pltpu.VMEM((3, ntok * cap, block, lanes), f32),
        pw_f=pltpu.VMEM(point_weight.shape, f32),
        pw_s=pltpu.VMEM((2,) + point_weight.shape, jnp.bfloat16),
        pool_s=pltpu.VMEM((cols * reps * rep_rows * wide, width), f32),
        n3_s=pltpu.VMEM((2, pieces, edge, width), f32),
        s3_s=pltpu.VMEM((pieces, edge, width), f32),
        f3_s=pltpu.VMEM((pieces, edge, width), f32),
        h_s=pltpu.VMEM((2, edge, width), f32),
        tile_s=pltpu.VMEM((tile, width), f32),
        flat_s=pltpu.VMEM((tile + 16, width), f32),
    )
    kinds = ("near", "far", "share", "along", "across", "over", "relay", "near3", "far3", "halo")
    outputs = dict(out_ref=jax.ShapeDtypeStruct((rep_rows, TC, width), f32))
    inputs = dict(
        index_ref=index, source_ref=source, x_ref=share, pillar_ref=pillar[None, :],
        dw_ref=jnp.transpose(depth_weight, (1, 2, 0, 3)), rg_ref=raster_gain, pw_ref=point_weight,
    )
    return run_layer(Second, 1, inputs, outputs, weights, collective_id, extra, kinds, ntok * cap)[0]


HALO = 2


def routes(dest_device, dest_slot):
    count = dest_device.shape[0]
    peers = lax.axis_size("tok")
    capacity = capacity_of(count, peers)
    order = jnp.arange(count, dtype=jnp.int32)
    earlier = (dest_device[:, None] == dest_device[None, :]) & (order[None, :] < order[:, None])
    place = dest_device * capacity + jnp.sum(earlier.astype(jnp.int32), axis=1)
    chosen = jnp.arange(peers * capacity, dtype=jnp.int32)[:, None] == place[None, :]
    index = jnp.sum(jnp.where(chosen, order[None, :], 0), axis=1)
    code = jnp.sum(jnp.where(chosen, dest_slot[None, :] + 1, 0), axis=1)
    code = jnp.pad(code.reshape(peers, capacity), ((0, 0), (0, 128 - capacity)))
    code = jnp.broadcast_to(code[:, None, :], (peers, 8, 128)).astype(jnp.float32)
    return index, code, capacity


def places(arrived, capacity, order):
    held = arrived[:, 0, :capacity].reshape(-1).astype(jnp.int32)
    found = held[None, :] == order[:, None] + 1
    return jnp.sum(jnp.where(found, jnp.arange(held.shape[0], dtype=jnp.int32)[None, :], 0), axis=1)


def raster_cells(extended, depth_weight, point_weight, gain_row):
    row_count = extended.shape[0] - 2
    col_count = extended.shape[1] - 2
    channels = extended.shape[2]
    normed = (
        extended
        * lax.rsqrt(jnp.mean(extended * extended, axis=-1, keepdims=True) + EPSILON)
        * gain_row
    )
    mixed = jnp.zeros((row_count, col_count, channels), jnp.float32)
    for a in range(3):
        for b in range(3):
            mixed = mixed + normed[a : a + row_count, b : b + col_count] * depth_weight[a, b]
    combined = matmul(mixed.reshape(row_count * col_count, channels), point_weight)
    combined = combined.reshape(row_count, col_count, 2 * channels)
    centre = extended[1:-1, 1:-1]
    return centre + combined[..., :channels] * jax.nn.sigmoid(combined[..., channels:])


def extended_cells(tok, members, rep_rows, full_width):
    cols, reps = members
    tile = []
    for col in range(cols):
        for rep in range(reps):
            y = rep * rep_rows - HALO + jnp.arange(rep_rows + 2 * HALO, dtype=jnp.int32)[:, None]
            x = col * TC - HALO + jnp.arange(TC + 2 * HALO, dtype=jnp.int32)[None, :]
            good = (y >= 0) & (y < TR) & (x >= 0) & (x < full_width)
            tile.append(jnp.where(good, (tok * TR + y) * full_width + x, -2).reshape(-1))
    return jnp.concatenate(tile)


def pool(partial, pillar, cells):
    onehot = (cells[:, None] == pillar[None, :]).astype(jnp.float32)
    return matmul(onehot, partial)


def exchange_rows(tile, ntok, reps):
    count = ntok * reps
    rep = lax.axis_index("rep")
    forward = [(i, i + 1) for i in range(count - 1)]
    backward = [(i + 1, i) for i in range(count - 1)]
    above = lax.ppermute(tile[-2 * HALO : -HALO], ("tok", "rep"), forward)
    below = lax.ppermute(tile[HALO : 2 * HALO], ("tok", "rep"), backward)
    above = jnp.where(rep == 0, above, tile[:HALO])
    below = jnp.where(rep == reps - 1, below, tile[-HALO:])
    return jnp.concatenate([above, tile[HALO:-HALO], below], axis=0)


def on_device(
    tokens,
    w_qkv,
    w_out,
    w_up,
    w_down,
    attn_gain,
    mlp_gain,
    dest_device,
    dest_slot,
    pillar,
    depth_weight,
    point_weight,
    raster_gain,
):
    members = (lax.axis_size("col"), lax.axis_size("rep"))
    group = members[0] * members[1]
    ntok = lax.axis_size("tok")
    block_count = dest_device.shape[0]
    order = jnp.arange(block_count, dtype=jnp.int32)
    index, codes, capacity = routes(dest_device, dest_slot)
    width = tokens.shape[1]
    weights = (w_qkv, w_out, w_up, w_down, attn_gain, mlp_gain)
    whole = (2 * members[1] * HALO * (TC + 2 * HALO)) % 8 == 0 and TR % (members[1] * HALO) == 0
    if members == (2, 2) and ntok > 1 and tokens.shape[0] == PATCH and whole and ntok * capacity <= 128:
        share, index, source = first_layer(tokens, dest_device, dest_slot, weights, 1)
        share = share.reshape(block_count, -1, width)
        raster_weights = (depth_weight, point_weight, raster_gain)
        return second_layer(share, index, source, capacity, pillar, raster_weights, weights, 5)
    blocks = gather(tokens, 1).reshape(1, group, block_count, -1, width)
    stream = attention_layer(blocks, order, 0, w_qkv, w_out, attn_gain, 2)
    share = scatter(mlp_partial(stream, 0, w_up, w_down, mlp_gain, group), 3)
    outgoing = pick(share.reshape(block_count, -1, width), index)
    outgoing = outgoing.reshape(ntok, -1, width)
    moved, arrived = move(outgoing, codes, 4)
    blocks = moved.reshape(ntok, group, capacity, -1, width)
    source = places(arrived, capacity, order)
    stream = attention_layer(blocks, source, 1, w_qkv, w_out, attn_gain, 5)
    partial = mlp_partial(stream, 1, w_up, w_down, mlp_gain, 1)[0]

    rep_rows = TR // members[1]
    full_width = TC * members[0]
    cells = extended_cells(lax.axis_index("tok"), members, rep_rows, full_width)
    pooled = pool(partial, pillar, cells)
    parts = pooled.reshape(group, -1, pooled.shape[1])
    edge = HALO * (TC + 2 * HALO)
    inside_kernel = members[0] > 1 and members[1] == 2 and ntok > 1 and edge % 8 == 0
    tile = scatter(parts, 6, edge if inside_kernel else 0)
    tile = tile.reshape(rep_rows + 2 * HALO, TC + 2 * HALO, -1)
    if not inside_kernel:
        tile = exchange_rows(tile, ntok, members[1])
    first = raster_cells(tile, depth_weight[0], point_weight[0], raster_gain[0])
    y = lax.axis_index(("tok", "rep")) * rep_rows - 1 + jnp.arange(rep_rows + 2)[:, None, None]
    x = lax.axis_index("col") * TC - 1 + jnp.arange(TC + 2)[None, :, None]
    inside = (y >= 0) & (y < TR * ntok) & (x >= 0) & (x < full_width)
    first = jnp.where(inside, first, 0.0)
    return raster_cells(first, depth_weight[1], point_weight[1], raster_gain[1])


def solution(mesh):
    placed = (
        P(("scene", "tok"), ("col", "rep")),
        P(None, None, None, ("col", "rep")),
        P(None, ("col", "rep"), None),
        P(None, None, ("col", "rep")),
        P(None, ("col", "rep"), None),
        P(),
        P(),
        P(("scene", "tok")),
        P(("scene", "tok")),
        P(("scene", "tok")),
        P(),
        P(),
        P(),
    )
    return jax.shard_map(
        on_device,
        mesh=mesh,
        in_specs=placed,
        out_specs=P(("scene", "tok", "rep"), "col", None),
        check_vma=False,
    )
```

```python
import functools
import math

import jax
import jax.numpy as jnp
from jax import lax
from jax.experimental import pallas as pl
from jax.experimental.pallas import tpu as pltpu
from jax.sharding import PartitionSpec as P

PATCH = 1024
TR = 16
TC = 16
HD = 16


MATMUL_PRECISION = lax.Precision.HIGH
EPSILON = 1e-05


def layer_norm(values, gain_row):
    average = jnp.mean(values, axis=-1, keepdims=True)
    centered = values - average
    variance = jnp.mean(centered * centered, axis=-1, keepdims=True)
    return centered * lax.rsqrt(variance + EPSILON) * gain_row


def split(values):
    high = values.astype(jnp.bfloat16)
    return high, (values - high.astype(jnp.float32)).astype(jnp.bfloat16)


def bdot(left, right, dims=(((1,), (0,)), ((), ()))):
    return lax.dot_general(left, right, dims, preferred_element_type=jnp.float32)


def dot3(left, right):
    lh, ll = left
    rh, rl = right
    return bdot(lh, rh) + bdot(lh, rl) + bdot(ll, rh)


def attention_kernel(share, source_ref, x_ref, gain_ref, w_ref, o_ref, out_ref, q_s, k_s, v_s, att_s):
    cols = w_ref.shape[-1]
    heads = cols // HD
    rows = out_ref.shape[0]
    chunk = att_s.shape[0]
    slots, each, block = x_ref.shape[1:4]
    first_block = pl.program_id(0) * (rows // block)

    def stream_rows(i):
        parts = []
        for n in range(chunk // block):
            at = source_ref[first_block + i * (chunk // block) + n]
            places = [x_ref[at // each, j, at % each] for j in range(slots)]
            parts.append(jnp.concatenate(places, axis=-1))
        return jnp.concatenate(parts, axis=0)

    lanes = q_s.shape[-1]

    r = lax.broadcasted_iota(jnp.int32, (cols, lanes), 0)
    c = lax.broadcasted_iota(jnp.int32, (cols, lanes), 1)
    lane = lax.broadcasted_iota(jnp.int32, (1, cols), 1)
    w = [split(w_ref[j]) for j in range(3)]
    for i in range(rows // chunk):
        at = pl.ds(i * chunk, chunk)
        normed = split(layer_norm(stream_rows(i), gain_ref[...]))
        qh, ql = split(dot3(normed, w[0]) * (HD ** (-0.5) * math.log2(math.e)))
        kh, kl = split(dot3(normed, w[1]))
        vh, vl = split(dot3(normed, w[2]))
        for h in range(heads):
            part = c // HD
            inside = (r // HD == h) & (r % HD == c % HD)
            first = (inside & ((part == 0) | (part == 1))).astype(jnp.bfloat16)
            third = (inside & (part == 2)).astype(jnp.bfloat16)
            outer = (inside & ((part == 0) | (part == 2))).astype(jnp.bfloat16)
            middle = (inside & (part == 1)).astype(jnp.bfloat16)
            q_s[h, at, :] = (bdot(qh, first) + bdot(ql, third)).astype(jnp.bfloat16)
            k_s[h, at, :] = (bdot(kh, outer) + bdot(kl, middle)).astype(jnp.bfloat16)
            own = lane // HD == h
            v_s[h, at, :cols] = jnp.where(own, vh.astype(jnp.float32), 0.0).astype(jnp.bfloat16)
            v_s[h, at, cols:] = jnp.where(own, vl.astype(jnp.float32), 1.0).astype(jnp.bfloat16)

    projection = split(o_ref[...])

    def query_rows(i, carry):
        at = pl.ds(pl.multiple_of(i * chunk, chunk), chunk)
        att_s[...] = jnp.zeros_like(att_s)

        def one_head(h, carry):
            scores = bdot(q_s[h, at, :], k_s[h], (((1,), (1,)), ((), ())))
            weights = jnp.exp2(scores - jnp.max(scores, axis=-1, keepdims=True))
            wh, wl = split(weights)
            sums = bdot(wh, v_s[h]) + bdot(wl, v_s[h])
            top, low = sums[:, :cols], sums[:, cols:]
            own = lane // HD == h
            total = jnp.max(jnp.where(own, 0.0, low), axis=-1, keepdims=True)
            att_s[...] += jnp.where(own, (top + low) / total, 0.0)
            return carry

        lax.fori_loop(0, heads, one_head, 0, unroll=4)
        out_ref[at, :] = dot3(split(att_s[...]), projection) + stream_rows(i) * share
        return carry

    lax.fori_loop(0, rows // chunk, query_rows, 0)


def attend(blocks, source, gain_row, weights, w_out, group):
    block, width = blocks.shape[3], blocks.shape[1] * blocks.shape[4]
    rows = source.shape[0] * block
    cols = weights.shape[-1]
    heads = cols // HD
    lanes = max(128, 3 * HD)
    return pl.pallas_call(
        functools.partial(attention_kernel, 1.0 / group),
        grid_spec=pltpu.PrefetchScalarGridSpec(
            num_scalar_prefetch=1,
            grid=(rows // PATCH,),
            in_specs=[
                pl.BlockSpec(blocks.shape, lambda i, source: (0, 0, 0, 0, 0)),
                pl.BlockSpec((1, width), lambda i, source: (0, 0)),
                pl.BlockSpec(weights.shape, lambda i, source: (0, 0, 0)),
                pl.BlockSpec(w_out.shape, lambda i, source: (0, 0)),
            ],
            out_specs=pl.BlockSpec((PATCH, width), lambda i, source: (i, 0)),
            scratch_shapes=[
                pltpu.VMEM((heads, PATCH, lanes), jnp.bfloat16),
                pltpu.VMEM((heads, PATCH, lanes), jnp.bfloat16),
                pltpu.VMEM((heads, PATCH, 2 * cols), jnp.bfloat16),
                pltpu.VMEM((256, cols), jnp.float32),
            ],
        ),
        out_shape=jax.ShapeDtypeStruct((rows, width), jnp.float32),
        compiler_params=pltpu.CompilerParams(vmem_limit_bytes=48 * 1024 * 1024),
        name="attend",
    )(source, blocks, gain_row[None, :], weights, w_out)


def matmul(left, right):
    return jnp.dot(left, right, precision=MATMUL_PRECISION, preferred_element_type=jnp.float32)


VMEM_LIMIT = 56 * 1024 * 1024
MESH = pl.DeviceIdType.MESH


def position():
    cols, reps = lax.axis_size("col"), lax.axis_size("rep")
    return cols, reps, lax.axis_index("col"), lax.axis_index("rep")


def greet(devices):
    barrier = pltpu.get_barrier_semaphore()
    for device in devices:
        pl.semaphore_signal(barrier, inc=1, device_id=device, device_id_type=MESH)
    pl.semaphore_wait(barrier, len(devices))


def remote(src, dst, send, recv, device):
    return pltpu.make_async_remote_copy(
        src_ref=src, dst_ref=dst, send_sem=send, recv_sem=recv, device_id=device, device_id_type=MESH
    )


def chunks_of(rows):
    for pieces in (8, 5, 4, 2):
        if rows % (8 * pieces) == 0:
            return pieces, rows // pieces
    return 1, rows


def gather_kernel(x_ref, out_ref, xs, xr, fs, fr, ps, pr, local):
    cols, reps, c, r = position()
    rows = x_ref.shape[0]
    pieces, size = chunks_of(rows)
    me = c * reps + r
    mate = {"col": c, "rep": 1 - r}
    others = [{"col": lax.rem(c + d, cols), "rep": r} for d in range(1, cols)]
    greet([mate] + others)
    across, onward = [], []
    for k in range(pieces):
        at = pl.ds(k * size, size)
        for d in range(1, cols):
            copy = remote(
                x_ref.at[at], out_ref.at[me, at], xs.at[d - 1, k], xr.at[d - 1, k], others[d - 1]
            )
            copy.start()
            across.append(copy)
    share = remote(x_ref, out_ref.at[me], ps, pr, mate)
    share.start()
    keep = pltpu.make_async_copy(x_ref, out_ref.at[me], local)
    keep.start()
    for k in range(pieces):
        at = pl.ds(k * size, size)
        for d in range(1, cols):
            across[k * (cols - 1) + d - 1].wait_recv()
            slot = lax.rem(c + cols - d, cols) * reps + r
            copy = remote(
                out_ref.at[slot, at], out_ref.at[slot, at], fs.at[d - 1, k], fr.at[d - 1, k], mate
            )
            copy.start()
            onward.append(copy)
    for copy in across:
        copy.wait_send()
    share.wait()
    keep.wait()
    for copy in onward:
        copy.wait()


def gather(block, collective_id):
    cols, reps = lax.axis_size("col"), lax.axis_size("rep")
    if reps != 2 or cols < 2:
        return lax.all_gather(block, ("col", "rep"), axis=0)
    pieces, _ = chunks_of(block.shape[0])
    dma = pltpu.SemaphoreType.DMA
    return pl.pallas_call(
        gather_kernel,
        out_shape=jax.ShapeDtypeStruct((cols * reps,) + block.shape, block.dtype),
        in_specs=[pl.BlockSpec(memory_space=pltpu.VMEM)],
        out_specs=pl.BlockSpec(memory_space=pltpu.VMEM),
        scratch_shapes=[dma((cols - 1, pieces))] * 4 + [dma, dma, dma],
        compiler_params=pltpu.CompilerParams(
            collective_id=collective_id, has_side_effects=True, vmem_limit_bytes=VMEM_LIMIT
        ),
        name="gather",
    )(block)


def scatter_kernel(edge, p_ref, out_ref, a_ref, s_ref, b_ref, a_s, a_r, b_s, b_r, *halo):
    cols, reps, c, r = position()
    rows = p_ref.shape[1]
    pieces, size = chunks_of(rows)
    mate = {"col": c, "rep": 1 - r}
    others = [{"col": lax.rem(c + d, cols), "rep": r} for d in range(1, cols)]
    greeted = [mate] + others
    if edge:
        ntok, t = lax.axis_size("tok"), lax.axis_index("tok")
        partner = {"tok": lax.rem(t + jnp.where(r == 0, ntok - 1, 1), ntok), "rep": 1 - r}
        greeted = greeted + [partner]
    greet(greeted)
    order = [(k, d) for k in range(pieces) for d in range(1, cols)]
    order += [(k, 0) for k in range(pieces)]
    near, far = {}, {}
    for k, d in order:
        at = pl.ds(k * size, size)
        slot = lax.rem(c + d, cols) * reps + 1 - r
        near[k, d] = remote(
            p_ref.at[slot, at], a_ref.at[d, at], a_s.at[d, k], a_r.at[d, k], mate
        )
        near[k, d].start()
    for k, d in order:
        at = pl.ds(k * size, size)
        slot = lax.rem(c + d, cols) * reps + r
        near[k, d].wait_recv()
        total = p_ref[slot, at] + a_ref[d, at]
        if d == 0:
            out_ref[at] = total
        else:
            s_ref[d - 1, at] = total
            far[k, d] = remote(
                s_ref.at[d - 1, at],
                b_ref.at[d - 1, at],
                b_s.at[d - 1, k],
                b_r.at[d - 1, k],
                others[d - 1],
            )
            far[k, d].start()
    for (k, d), copy in far.items():
        at = pl.ds(k * size, size)
        copy.wait_recv()
        out_ref[at] += b_ref[d - 1, at]
    if edge:
        h_ref, e_ref, h_s, h_r = halo
        inner = pl.multiple_of(jnp.where(r == 0, edge, rows - 2 * edge), 8)
        outer = pl.multiple_of(jnp.where(r == 0, 0, rows - edge), 8)
        e_ref[...] = out_ref[pl.ds(inner, edge)]
        copy = remote(e_ref, h_ref, h_s, h_r, partner)
        copy.start()
        copy.wait()
        wrapped = jnp.where(r == 0, t == 0, t == ntok - 1)
        out_ref[pl.ds(outer, edge)] = jnp.where(wrapped, 0.0, h_ref[...])
    for copy in list(near.values()) + list(far.values()):
        copy.wait_send()


def scatter(parts, collective_id, edge=0):
    cols, reps = lax.axis_size("col"), lax.axis_size("rep")
    if reps != 2 or cols < 2:
        return lax.psum_scatter(parts, ("col", "rep"), scatter_dimension=0)
    shape, kind = parts.shape[1:], parts.dtype
    pieces, _ = chunks_of(shape[0])
    dma = pltpu.SemaphoreType.DMA
    return pl.pallas_call(
        functools.partial(scatter_kernel, edge),
        out_shape=jax.ShapeDtypeStruct(shape, kind),
        in_specs=[pl.BlockSpec(memory_space=pltpu.VMEM)],
        out_specs=pl.BlockSpec(memory_space=pltpu.VMEM),
        scratch_shapes=[
            pltpu.VMEM((cols,) + shape, kind),
            pltpu.VMEM((cols - 1,) + shape, kind),
            pltpu.VMEM((cols - 1,) + shape, kind),
            dma((cols, pieces)),
            dma((cols, pieces)),
            dma((cols - 1, pieces)),
            dma((cols - 1, pieces)),
        ]
        + ([pltpu.VMEM((edge, shape[1]), kind)] * 2 + [dma, dma] if edge else []),
        compiler_params=pltpu.CompilerParams(
            collective_id=collective_id, has_side_effects=True, vmem_limit_bytes=VMEM_LIMIT
        ),
        name="scatter",
    )(parts)


def total_kernel(
    p_ref, out_ref, a_ref, s_ref, b_ref, a_s, a_r, b_s, b_r, xs, xr, fs, fr, ps, pr
):
    cols, reps, c, r = position()
    rows = p_ref.shape[1]
    pieces, size = chunks_of(rows)
    me = c * reps + r
    mate = {"col": c, "rep": 1 - r}
    others = [{"col": lax.rem(c + d, cols), "rep": r} for d in range(1, cols)]
    greet([mate] + others)
    order = [(k, d) for k in range(pieces) for d in range(1, cols)]
    order += [(k, 0) for k in range(pieces)]
    near, far, across, share, onward = {}, {}, {}, {}, {}
    for k, d in order:
        at = pl.ds(k * size, size)
        slot = lax.rem(c + d, cols) * reps + 1 - r
        near[k, d] = remote(
            p_ref.at[slot, at], a_ref.at[d, at], a_s.at[d, k], a_r.at[d, k], mate
        )
        near[k, d].start()
    for k, d in order:
        if d == 0:
            continue
        at = pl.ds(k * size, size)
        slot = lax.rem(c + d, cols) * reps + r
        near[k, d].wait_recv()
        s_ref[d - 1, at] = p_ref[slot, at] + a_ref[d, at]
        far[k, d] = remote(
            s_ref.at[d - 1, at], b_ref.at[d - 1, at], b_s.at[d - 1, k], b_r.at[d - 1, k], others[d - 1]
        )
        far[k, d].start()
    for k in range(pieces):
        at = pl.ds(k * size, size)
        near[k, 0].wait_recv()
        total = p_ref[me, at] + a_ref[0, at]
        for d in range(1, cols):
            far[k, d].wait_recv()
            total = total + b_ref[d - 1, at]
        out_ref[me, at] = total
        for d in range(1, cols):
            across[k, d] = remote(
                out_ref.at[me, at], out_ref.at[me, at], xs.at[d - 1, k], xr.at[d - 1, k], others[d - 1]
            )
            across[k, d].start()
        share[k] = remote(out_ref.at[me, at], out_ref.at[me, at], ps.at[k], pr.at[k], mate)
        share[k].start()
    for (k, d), copy in across.items():
        at = pl.ds(k * size, size)
        copy.wait_recv()
        slot = lax.rem(c + cols - d, cols) * reps + r
        onward[k, d] = remote(
            out_ref.at[slot, at], out_ref.at[slot, at], fs.at[d - 1, k], fr.at[d - 1, k], mate
        )
        onward[k, d].start()
    for copies in (near, far, across):
        for copy in copies.values():
            copy.wait_send()
    for copies in (share, onward):
        for copy in copies.values():
            copy.wait()


def total(parts, collective_id):
    cols, reps = lax.axis_size("col"), lax.axis_size("rep")
    if reps != 2 or cols < 2:
        return lax.psum(parts, ("col", "rep"))
    shape, kind = parts.shape[1:], parts.dtype
    pieces, _ = chunks_of(shape[0])
    dma = pltpu.SemaphoreType.DMA
    return pl.pallas_call(
        total_kernel,
        out_shape=jax.ShapeDtypeStruct(parts.shape, kind),
        in_specs=[pl.BlockSpec(memory_space=pltpu.VMEM)],
        out_specs=pl.BlockSpec(memory_space=pltpu.VMEM),
        scratch_shapes=[
            pltpu.VMEM((cols,) + shape, kind),
            pltpu.VMEM((cols - 1,) + shape, kind),
            pltpu.VMEM((cols - 1,) + shape, kind),
            dma((cols, pieces)),
            dma((cols, pieces)),
        ]
        + [dma((cols - 1, pieces))] * 6
        + [dma((pieces,))] * 2,
        compiler_params=pltpu.CompilerParams(
            collective_id=collective_id, has_side_effects=True, vmem_limit_bytes=VMEM_LIMIT
        ),
        name="total",
    )(parts)


def move_kernel(o_ref, code_ref, out_ref, arrived_ref, zs, zr, cs, cr, xs, xr, fs, fr, ps, pr, local):
    cols, reps, c, r = position()
    ntok, t = lax.axis_size("tok"), lax.axis_index("tok")
    me = c * reps + r
    mate = {"col": c, "rep": 1 - r}
    others = [{"col": lax.rem(c + d, cols), "rep": r} for d in range(1, cols)]
    peers = [{"tok": lax.rem(t + e, ntok)} for e in range(1, ntok)]
    greet([mate] + others + peers)
    along, codes, across, share, onward = [], [], {}, [], []
    for e in range(1, ntok):
        target = lax.rem(t + e, ntok)
        copy = remote(o_ref.at[target], out_ref.at[t, me], zs.at[e - 1], zr.at[e - 1], peers[e - 1])
        copy.start()
        along.append(copy)
        copy = remote(
            code_ref.at[target], arrived_ref.at[t], cs.at[e - 1], cr.at[e - 1], peers[e - 1]
        )
        copy.start()
        codes.append(copy)
    keep = pltpu.make_async_copy(o_ref.at[t], out_ref.at[t, me], local.at[0])
    keep.start()
    keep_code = pltpu.make_async_copy(code_ref.at[t], arrived_ref.at[t], local.at[1])
    keep_code.start()

    def hand_on(e):
        u = lax.rem(t + ntok - e, ntok)
        for d in range(1, cols):
            across[e, d].wait_recv()
            slot = lax.rem(c + cols - d, cols) * reps + r
            copy = remote(
                out_ref.at[u, slot], out_ref.at[u, slot], fs.at[e, d - 1], fr.at[e, d - 1], mate
            )
            copy.start()
            onward.append(copy)

    for e in range(ntok):
        u = lax.rem(t + ntok - e, ntok)
        if e:
            along[e - 1].wait_recv()
        origin = out_ref.at[u, me] if e else o_ref.at[t]
        for d in range(1, cols):
            across[e, d] = remote(
                origin, out_ref.at[u, me], xs.at[e, d - 1], xr.at[e, d - 1], others[d - 1]
            )
            across[e, d].start()
        copy = remote(origin, out_ref.at[u, me], ps.at[e], pr.at[e], mate)
        copy.start()
        share.append(copy)
        if e:
            hand_on(e - 1)
    hand_on(ntok - 1)
    keep.wait()
    keep_code.wait()
    for copy in along + list(across.values()):
        copy.wait_send()
    for copy in codes + share + onward:
        copy.wait()


def move(outgoing, codes, collective_id):
    cols, reps, ntok = lax.axis_size("col"), lax.axis_size("rep"), lax.axis_size("tok")
    if reps != 2 or cols < 2 or ntok < 2:
        incoming = lax.all_to_all(outgoing, "tok", split_axis=0, concat_axis=0, tiled=True)
        arrived = lax.all_to_all(codes, "tok", split_axis=0, concat_axis=0, tiled=True)
        return lax.all_gather(incoming, ("col", "rep"), axis=1), arrived
    dma = pltpu.SemaphoreType.DMA
    shape = (ntok, cols * reps) + outgoing.shape[1:]
    return pl.pallas_call(
        move_kernel,
        out_shape=(
            jax.ShapeDtypeStruct(shape, outgoing.dtype),
            jax.ShapeDtypeStruct(codes.shape, codes.dtype),
        ),
        in_specs=[pl.BlockSpec(memory_space=pltpu.VMEM)] * 2,
        out_specs=[pl.BlockSpec(memory_space=pltpu.VMEM)] * 2,
        scratch_shapes=[dma((ntok - 1,))] * 4
        + [dma((ntok, cols - 1))] * 4
        + [dma((ntok,))] * 2
        + [dma((2,))],
        compiler_params=pltpu.CompilerParams(
            collective_id=collective_id, has_side_effects=True, vmem_limit_bytes=VMEM_LIMIT
        ),
        name="move",
    )(outgoing, codes)


def pick_kernel(index_ref, x_ref, out_ref):
    for j in range(out_ref.shape[0]):
        out_ref[j] = x_ref[index_ref[j]]


def pick(blocks, index):
    return pl.pallas_call(
        pick_kernel,
        out_shape=jax.ShapeDtypeStruct(index.shape + blocks.shape[1:], blocks.dtype),
        in_specs=[pl.BlockSpec(memory_space=pltpu.SMEM), pl.BlockSpec(memory_space=pltpu.VMEM)],
        out_specs=pl.BlockSpec(memory_space=pltpu.VMEM),
        name="pick",
    )(index, blocks)


def attention_layer(blocks, source, layer, w_qkv, w_out, attn_gain, collective_id):
    group = blocks.shape[1]
    terms = attend(blocks, source, attn_gain[layer], w_qkv[layer], w_out[layer], group)
    rows, width = terms.shape
    return total(terms.reshape(group, rows // group, width), collective_id).reshape(rows, width)


def mlp_kernel(x_ref, gain_ref, up_ref, down_ref, share, out_ref):
    x = x_ref[...]
    hidden = dot3(split(layer_norm(x, gain_ref[...])), split(up_ref[...]))
    hidden = 0.5 * hidden * (1.0 + lax.erf(hidden * (0.5**0.5)))
    total = dot3(split(hidden), split(down_ref[...])) + x * share
    width = out_ref.shape[-1]
    for j in range(out_ref.shape[0]):
        out_ref[j] = total[:, j * width : (j + 1) * width]


def mlp_partial(stream, layer, w_up, w_down, mlp_gain, slots):
    rows, width = stream.shape
    tile = min(256, rows)
    hidden = w_up.shape[-1]
    group = lax.axis_size("col") * lax.axis_size("rep")

    def kernel(x_ref, gain_ref, up_ref, down_ref, out_ref):
        mlp_kernel(x_ref, gain_ref, up_ref, down_ref, 1.0 / group, out_ref)

    return pl.pallas_call(
        kernel,
        grid=(rows // tile,),
        in_specs=[
            pl.BlockSpec((tile, width), lambda i: (i, 0)),
            pl.BlockSpec((1, width), lambda i: (0, 0)),
            pl.BlockSpec((width, hidden), lambda i: (0, 0)),
            pl.BlockSpec((hidden, width), lambda i: (0, 0)),
        ],
        out_specs=pl.BlockSpec((slots, tile, width // slots), lambda i: (0, i, 0)),
        out_shape=jax.ShapeDtypeStruct((slots, rows, width // slots), jnp.float32),
        compiler_params=pltpu.CompilerParams(vmem_limit_bytes=48 * 1024 * 1024),
        name="mlp",
    )(stream, mlp_gain[layer][None, :], w_up[layer], w_down[layer])


def gelu(values):
    return 0.5 * values * (1.0 + lax.erf(values * (0.5**0.5)))


def piece(i, size):
    return pl.ds(pl.multiple_of(i * size, size), size)


class Layer:
    def __init__(self, layer, refs, heads, chunk):
        self.__dict__.update(refs)
        self.layer, self.heads, self.chunk = layer, heads, chunk
        self.tag = "_sem" + str(layer)
        self.cols, self.reps, self.c, self.r = position()
        self.ntok, self.t = lax.axis_size("tok"), lax.axis_index("tok")
        self.me = self.c * self.reps + self.r
        self.mate, self.peer = {"rep": 1 - self.r}, {"col": 1 - self.c}
        self.peers = [{"tok": lax.rem(self.t + e, self.ntok)} for e in range(1, self.ntok)]
        self.rows, self.width = self.a_s.shape
        self.lanes = self.q_s.shape[-1] // 2
        self.n = self.rows // chunk
        self.block = self.y_s.shape[1]
        self.cap = self.o_s.shape[1]

    def sent(self, kind, i, src, dst, device):
        sem = getattr(self, kind + self.tag)
        return remote(src, dst, sem.at[0, i], sem.at[1, i], device)

    def load_weights(self):
        pairs = (
            (self.wqkv_ref, self.wqkv_f), (self.wo_ref, self.wo_f),
            (self.wu_ref, self.wu_f), (self.wd_ref, self.wd_f),
        )
        self.loads = [
            pltpu.make_async_copy(src.at[self.layer], dst.at[self.layer], self.wsem.at[self.layer, j])
            for j, (src, dst) in enumerate(pairs)
        ]
        for load in self.loads:
            load.start()

    def split_weights(self):
        layer = self.layer
        self.loads[0].wait()
        for m in range(3):
            self.wqkv_s[layer, 0, m], self.wqkv_s[layer, 1, m] = split(self.wqkv_f[layer, m])
        rest = ((self.wo_f, self.wo_s), (self.wu_f, self.wu_s), (self.wd_f, self.wd_s))
        for load, (src, dst) in zip(self.loads[1:], rest):
            load.wait()
            dst[layer, 0], dst[layer, 1] = split(src[layer])

    def pair(self, ref):
        return ref[self.layer, 0], ref[self.layer, 1]

    def project(self, stream):
        normed = split(layer_norm(stream, self.ga_ref[pl.ds(self.layer, 1)]))
        return [dot3(normed, (self.wqkv_s[self.layer, 0, m], self.wqkv_s[self.layer, 1, m])) for m in range(3)]

    def pack(self, at, q, k, v):
        lanes = self.lanes
        half_lanes = lanes // 2
        lane = lax.broadcasted_iota(jnp.int32, (1, lanes), 1)
        low = lane < half_lanes
        qh, ql = split(q * (HD ** (-0.5) * math.log2(math.e)))
        kh, kl = [part.astype(jnp.float32) for part in split(k)]
        vh, vl = [part.astype(jnp.float32) for part in split(v)]
        qf, qlf = qh.astype(jnp.float32), ql.astype(jnp.float32)
        q_s, k_s, v_s = self.q_s, self.k_s, self.v_s

        def roll(values):
            return pltpu.roll(values, half_lanes, 1)

        q_s[0, at, :lanes] = qh
        q_s[1, at, :lanes] = qh
        q_s[0, at, lanes:] = jnp.where(low, qf, roll(qlf)).astype(jnp.bfloat16)
        q_s[1, at, lanes:] = jnp.where(low, roll(qf), qlf).astype(jnp.bfloat16)
        k_s[0, at, :lanes] = kh.astype(jnp.bfloat16)
        k_s[1, at, :lanes] = kh.astype(jnp.bfloat16)
        k_s[0, at, lanes:] = jnp.where(low, kl, roll(kh)).astype(jnp.bfloat16)
        k_s[1, at, lanes:] = jnp.where(low, roll(kl), kh).astype(jnp.bfloat16)
        v_s[0, at, :lanes] = vh.astype(jnp.bfloat16)
        v_s[1, at, :lanes] = vh.astype(jnp.bfloat16)
        v_s[0, at, lanes:] = jnp.where(low, vl, 1.0).astype(jnp.bfloat16)
        v_s[1, at, lanes:] = jnp.where(low, 1.0, vl).astype(jnp.bfloat16)

    def near(self, i):
        half = self.chunk // 2
        start = pl.multiple_of(i * self.chunk + (1 - self.r) * half, half)
        return self.sent("near", i, self.p_s.at[pl.ds(start, half)], self.n1_s.at[piece(i, half)], self.mate)

    def far(self, i):
        at = piece(i, self.chunk // 2)
        return self.sent("far", i, self.s1_s.at[at], self.f1_s.at[at], self.peer)

    def own_half(self, i):
        half = self.chunk // 2
        return pl.ds(pl.multiple_of(i * self.chunk + self.r * half, half), half)

    def share(self, i):
        at = self.own_half(i)
        return self.sent("share", i, self.a_s.at[at], self.a_s.at[at], self.mate)

    def attention(self, k):
        lanes, half_heads, chunk = self.lanes, self.heads // 2, self.chunk
        wide = lax.broadcasted_iota(jnp.int32, (1, 2 * lanes), 1)
        lane = lax.broadcasted_iota(jnp.int32, (1, lanes), 1)
        i, half = k // 2, k % 2
        query = self.q_s[half, piece(i, chunk), :]
        queries = []
        for m in range(half_heads):
            first = (wide < lanes) & (wide // HD == half * half_heads + m)
            second = (wide >= lanes) & ((wide % (lanes // 2)) // HD == m)
            mask = jnp.where(first | second, 1.0, 0.0).astype(jnp.bfloat16)
            queries.append(query * mask)
        stacked = jnp.concatenate(queries, axis=0)
        scores = bdot(stacked, self.k_s[half], (((1,), (1,)), ((), ())))
        weights = jnp.exp2(scores - jnp.max(scores, axis=-1, keepdims=True))
        sums = bdot(jnp.concatenate(split(weights), axis=0), self.v_s[half])
        sums = sums[: half_heads * chunk] + sums[half_heads * chunk :]
        total = jnp.zeros((chunk, lanes), jnp.float32)
        for m in range(half_heads):
            own = sums[m * chunk : (m + 1) * chunk]
            top, low = own[:, :lanes], own[:, lanes:]
            ratio = (top + low) / pltpu.roll(low, lanes // 2, 1)
            total += jnp.where(lane // HD == half * half_heads + m, ratio, 0.0)
        self.att_s[half] = total

    def finish(self, i):
        projection = self.pair(self.wo_s)
        self.p_s[piece(i, self.chunk)] = dot3(split(self.att_s[0] + self.att_s[1]), projection)
        self.near(i).start()

    def reduce_near(self, i):
        self.near(i).wait_recv()
        at = piece(i, self.chunk // 2)
        self.s1_s[at] = self.p_s[self.own_half(i)] + self.n1_s[at]
        self.far(i).start()

    def reduce_far(self, i):
        self.far(i).wait_recv()
        half = self.chunk // 2
        at = piece(i, half)
        stream = self.stream_rows(i * self.chunk + self.r * half, half)
        self.a_s[self.own_half(i)] = (self.s1_s[at] + self.f1_s[at]) + stream
        self.share(i).start()

    def mlp(self, x):
        normed = split(layer_norm(x, self.gm_ref[pl.ds(self.layer, 1)]))
        hidden = gelu(dot3(normed, self.pair(self.wu_s)))
        return dot3(split(hidden), self.pair(self.wd_s))

    def run(self, stages):
        n = self.n

        def tick(k, carry):
            @pl.when(k < 2 * n)
            def _():
                self.attention(k)

            for offset, stage in stages:
                @pl.when((k >= offset) & (k < offset + 2 * n) & ((k - offset) % 2 == 0))
                def _(offset=offset, stage=stage):
                    stage((k - offset) // 2)

            return carry

        lax.fori_loop(0, 2 * n + max(offset for offset, _ in stages) - 1, tick, 0)


class First(Layer):
    def stream_rows(self, start, count):
        at = pl.ds(pl.multiple_of(start, count), count)
        return jnp.concatenate([self.g0_s[j, at] for j in range(self.cols * self.reps)], axis=-1)

    def across(self, i):
        at = piece(i, self.chunk)
        return self.sent("across", i, self.tokens_ref.at[at], self.g0_s.at[self.me, at], self.peer)

    def over(self, i):
        at = piece(i, self.chunk)
        return self.sent("over", i, self.tokens_ref.at[at], self.g0_s.at[self.me, at], self.mate)

    def relay(self, i):
        at = piece(i, self.chunk)
        slot = (1 - self.c) * self.reps + self.r
        return self.sent("relay", i, self.g0_s.at[slot, at], self.g0_s.at[slot, at], self.mate)

    def code(self, e):
        target = {"tok": lax.rem(self.t + e, self.ntok)}
        return self.sent("code", e, self.code_s, self.arrived_s.at[self.t], target)

    def route(self):
        device = self.dd_ref[...].astype(jnp.float32)
        slot = self.ds_ref[...].astype(jnp.float32)
        count = device.shape[1]
        row = lax.broadcasted_iota(jnp.int32, (count, count), 0)
        col = lax.broadcasted_iota(jnp.int32, (count, count), 1)

        def upright(values):
            return jnp.sum(jnp.where(row == col, values, 0.0), axis=1, keepdims=True)

        devices, slots = upright(device), upright(slot)
        earlier = jnp.where((devices == device) & (col < row), 1.0, 0.0)
        place = devices * self.cap + jnp.sum(earlier, axis=1, keepdims=True)
        at = lax.broadcasted_iota(jnp.int32, (count, 128), 1).astype(jnp.float32)
        block = lax.broadcasted_iota(jnp.int32, (count, 128), 0).astype(jnp.float32)
        index = jnp.sum(jnp.where(place == at, block, 0.0), axis=0, keepdims=True)
        code = jnp.sum(jnp.where(place == at, slots + 1.0, 0.0), axis=0, keepdims=True)
        self.index_v[...] = index.astype(jnp.int32)
        self.code_s[...] = jnp.broadcast_to(code, self.code_s.shape)
        self.arrived_s[self.t] = jnp.broadcast_to(code, self.code_s.shape)

    def locate(self):
        row = lax.broadcasted_iota(jnp.int32, (128, 128), 0)
        col = lax.broadcasted_iota(jnp.int32, (128, 128), 1)
        first = self.t * self.cap
        valid = (row >= first) & (row < first + self.cap)
        source = jnp.zeros((1, 128), jnp.float32)
        for u in range(self.ntok):
            codes = self.arrived_s[u][:1]
            upright = jnp.sum(jnp.where(row == col, codes, 0.0), axis=1, keepdims=True)
            found = valid & (upright == (col + 1).astype(jnp.float32))
            entry = (row - first + u * self.cap).astype(jnp.float32)
            source += jnp.sum(jnp.where(found, entry, 0.0), axis=0, keepdims=True)
        self.source_v[...] = source.astype(jnp.int32)

    def near2(self, i):
        at = piece(i, self.chunk)
        return self.sent("near2", i, self.m_s.at[1 - self.r, :, at], self.n2_s.at[:, at], self.mate)

    def far2(self, i):
        at = piece(i, self.chunk)
        return self.sent("far2", i, self.s2_s.at[at], self.f2_s.at[at], self.peer)

    def feed(self, i):
        self.share(i).wait_recv()
        at = piece(i, self.chunk)
        total = self.mlp(self.a_s[at])
        for j in range(self.cols * self.reps):
            self.m_s[j % self.reps, j // self.reps, at] = total[:, j * self.lanes : (j + 1) * self.lanes]
        self.near2(i).start()

    def scatter_near(self, i):
        self.near2(i).wait_recv()
        at = piece(i, self.chunk)
        self.s2_s[at] = self.m_s[self.r, 1 - self.c, at] + self.n2_s[1 - self.c, at]
        self.far2(i).start()

    def scatter_far(self, i):
        self.far2(i).wait_recv()
        at = piece(i, self.chunk)
        own = self.a_s[at, piece(self.me, self.lanes)]
        total = (self.m_s[self.r, self.c, at] + self.n2_s[self.c, at]) + self.f2_s[at]
        count = self.chunk // self.block
        self.y_s[piece(i, count)] = (total + own).reshape(count, self.block, self.lanes)

    def body(self, second):
        n = self.n
        for i in range(n):
            self.across(i).start()
        for i in range(n):
            self.over(i).start()
        keep = pltpu.make_async_copy(self.tokens_ref, self.g0_s.at[self.me], self.tsem.at[0])
        keep.start()
        self.route()
        table = pltpu.make_async_copy(self.index_v, self.index_m, self.tsem.at[1])
        table.start()
        self.split_weights()
        for e in range(1, self.ntok):
            self.code(e).start()
        second.split_weights()
        second.split_points()
        keep.wait()
        table.wait()

        def step(i, carry):
            @pl.when(i < n)
            def _():
                self.across(i).wait_recv()
                self.relay(i).start()

            @pl.when(i > 0)
            def _():
                self.over(i - 1).wait_recv()
                self.relay(i - 1).wait_recv()
                stream = self.stream_rows((i - 1) * self.chunk, self.chunk)
                self.pack(piece(i - 1, self.chunk), *self.project(stream))

            return carry

        lax.fori_loop(0, n + 1, step, 0)
        self.run(
            [
                (1, self.finish), (2, self.reduce_near), (9, self.scatter_near),
                (6, self.reduce_far), (7, self.feed), (13, self.scatter_far),
            ]
        )
        for copy in (
            self.near, self.far, self.share, self.near2, self.far2, self.across, self.over, self.relay
        ):
            for i in range(n):
                copy(i).wait_send()
        for e in range(1, self.ntok):
            self.code(e).wait()
        self.locate()
        table = pltpu.make_async_copy(self.source_v, self.source_m, self.tsem.at[2])
        table.start()
        table.wait()


class Second(Layer):
    def entry(self, k):
        return jnp.clip(self.source_m[0, k], 0, self.ntok * self.cap - 1)

    def chosen(self, u, j):
        return jnp.clip(self.index_m[0, u * self.cap + j], 0, self.y_s.shape[0] - 1)

    def stream_rows(self, start, count):
        parts = []
        for m in range(count // self.block):
            at = self.entry(start // self.block + m)
            places = [self.g_s[at // self.cap, j, at % self.cap] for j in range(self.cols * self.reps)]
            parts.append(jnp.concatenate(places, axis=-1))
        return jnp.concatenate(parts, axis=0)

    def along(self, e, j):
        target = lax.rem(self.t + e, self.ntok)
        return self.sent(
            "along", e * self.cap + j, self.o_s.at[target, j], self.g_s.at[self.t, self.me, j],
            {"tok": target},
        )

    def origin(self, e):
        return lax.rem(self.t + self.ntok - e, self.ntok)

    def placed(self, kind, e, j, slot, device):
        ref = self.g_s.at[self.origin(e), slot, j]
        return self.sent(kind, e * self.cap + j, ref, ref, device)

    def across(self, e, j):
        return self.placed("across", e, j, self.me, self.peer)

    def over(self, e, j):
        return self.placed("over", e, j, self.me, self.mate)

    def relay(self, e, j):
        return self.placed("relay", e, j, (1 - self.c) * self.reps + self.r, self.mate)

    def arrive(self, j):
        for e in self.order[1:]:
            self.along(e, j).wait_recv()
            self.across(e, j).start()
            self.over(e, j).start()

    def hand(self, j):
        for e in self.order:
            self.across(e, j).wait_recv()
            self.relay(e, j).start()

    def take(self, j):
        parts = []
        for e in self.order:
            self.over(e, j).wait_recv()
            self.relay(e, j).wait_recv()
            places = [self.g_s[self.origin(e), k, j] for k in range(self.cols * self.reps)]
            parts.append(jnp.concatenate(places, axis=-1))
        for m, values in enumerate(self.project(jnp.concatenate(parts, axis=0))):
            for at, e in enumerate(self.order):
                entry = self.origin(e) * self.cap + j
                self.raw_s[m, entry] = values[at * self.block : (at + 1) * self.block]

    def move(self):
        self.order = [0]
        for e in range(1, self.ntok // 2 + 1):
            self.order += [e] + ([self.ntok - e] if self.ntok - e != e else [])
        for u in range(self.ntok):
            for j in range(self.cap):
                self.o_s[u, j] = self.y_s[self.chosen(u, j)]
        for j in range(self.cap):
            self.g_s[self.t, self.me, j] = self.y_s[self.chosen(self.t, j)]
        for j in range(self.cap):
            for e in self.order[1:]:
                self.along(e, j).start()
        for j in range(self.cap):
            self.across(0, j).start()
            self.over(0, j).start()
        for j in range(self.cap):
            self.arrive(j)
            if j >= 1:
                self.hand(j - 1)
            if j >= 2:
                self.take(j - 2)
        self.hand(self.cap - 1)
        for j in range(max(0, self.cap - 2), self.cap):
            self.take(j)

        def step(i, carry):
            def row(m):
                each = self.chunk // self.block
                blocks = [self.raw_s[m, self.entry(i * each + k)] for k in range(each)]
                return jnp.concatenate(blocks, axis=0)

            self.pack(piece(i, self.chunk), row(0), row(1), row(2))
            return carry

        lax.fori_loop(0, self.n, step, 0)

    def load_points(self):
        self.point = pltpu.make_async_copy(self.pw_ref, self.pw_f, self.tsem.at[3])
        self.point.start()

    def split_points(self):
        self.point.wait()

        def step(k, carry):
            at = piece(k, 64)
            for l in range(2):
                self.pw_s[0, l, at], self.pw_s[1, l, at] = split(self.pw_f[l, at])
            return carry

        lax.fori_loop(0, self.width // 64, step, 0)

    def cell_ids(self):
        count = self.pool_s.shape[0]
        p = lax.broadcasted_iota(jnp.int32, (count, 1), 0)
        wide = TC + 2 * HALO
        row = ((p.astype(jnp.float32) + 0.5) * (1.0 / wide)).astype(jnp.int32)
        col = row // TR
        x = col * TC - HALO + (p - row * wide)
        full = TC * self.cols
        y = row - col * TR
        return jnp.where((x >= 0) & (x < full), (self.t * TR + y) * full + x, -2)

    def feed(self, i):
        self.share(i).wait_recv()
        at = piece(i, self.chunk)
        x = self.a_s[at]
        high, low = split(self.mlp(x) + x * (1.0 / (self.cols * self.reps)))
        chosen = jnp.where(self.cell_ids() == self.pillar_ref[:, at], 1.0, 0.0).astype(jnp.bfloat16)
        self.pool_s[...] += bdot(chosen, high) + bdot(chosen, low)

    def tile_part(self, c, r, k):
        cells = self.pool_s.shape[0] // (self.cols * self.reps)
        start = (c * self.reps + r) * cells + k * self.edge
        return pl.ds(pl.multiple_of(start, 8), self.edge)

    def near3(self, w, k):
        c = self.c if w else 1 - self.c
        return self.sent(
            "near3", w * self.pieces + k, self.pool_s.at[self.tile_part(c, 1 - self.r, k)],
            self.n3_s.at[w, k], self.mate,
        )

    def far3(self, k):
        return self.sent("far3", k, self.s3_s.at[k], self.f3_s.at[k], self.peer)

    def inner(self):
        start = jnp.where(self.r == 0, self.pieces * self.edge, self.edge)
        src = self.tile_s.at[pl.ds(pl.multiple_of(start, 8), self.edge)]
        return self.sent("halo", 0, src, self.h_s.at[0], self.mate)

    def outer(self):
        start = jnp.where(self.r == 0, self.edge, self.pieces * self.edge)
        src = self.tile_s.at[pl.ds(pl.multiple_of(start, 8), self.edge)]
        return self.sent("halo", 1, src, self.h_s.at[1], self.partner)

    def scatter(self):
        order = [0, self.pieces - 1] + list(range(1, self.pieces - 1))
        for w in range(2):
            for k in order:
                self.near3(w, k).start()
        for k in order:
            self.near3(0, k).wait_recv()
            self.s3_s[k] = self.pool_s[self.tile_part(1 - self.c, self.r, k)] + self.n3_s[0, k]
            self.far3(k).start()
        for at, k in enumerate(order):
            self.near3(1, k).wait_recv()
            self.far3(k).wait_recv()
            own = self.pool_s[self.tile_part(self.c, self.r, k)] + self.n3_s[1, k]
            self.tile_s[pl.ds((k + 1) * self.edge, self.edge)] = own + self.f3_s[k]
            if at == 1:
                self.inner().start()
                self.outer().start()
        self.inner().wait()
        self.outer().wait()
        wrapped = jnp.where(self.r == 0, self.t == 0, self.t == self.ntok - 1)
        beyond = jnp.where(wrapped, 0.0, self.h_s[1])
        within = self.h_s[0]
        self.tile_s[: self.edge] = jnp.where(self.r == 0, beyond, within)
        self.tile_s[(self.pieces + 1) * self.edge :] = jnp.where(self.r == 0, within, beyond)

    def raster(self):
        wide = TC + 2 * HALO
        rows = self.tile_s.shape[0] // wide
        pad = (self.flat_s.shape[0] - rows * wide) // 2
        self.flat_s[:pad] = jnp.zeros((pad, self.width), jnp.float32)
        self.flat_s[pad + rows * wide :] = jnp.zeros((pad, self.width), jnp.float32)
        for l in range(2):
            old = pl.ds(l * wide, (rows - 2 * l) * wide)
            start, count = (l + 1) * wide, (rows - 2 * l - 2) * wide
            cells = self.tile_s[old]
            square = jnp.mean(cells * cells, axis=-1, keepdims=True)
            gain = self.rg_ref[pl.ds(l, 1)]
            self.flat_s[pl.ds(pad + l * wide, (rows - 2 * l) * wide)] = (
                cells * lax.rsqrt(square + EPSILON) * gain
            )
            mixed = jnp.zeros((count, self.width), jnp.float32)
            for a in range(3):
                for b in range(3):
                    shift = pad + start + (a - 1) * wide + b - 1
                    mixed = mixed + self.flat_s[pl.ds(shift, count)] * self.dw_ref[a, b, pl.ds(l, 1)]
            both = dot3(split(mixed), (self.pw_s[0, l], self.pw_s[1, l]))
            centre = self.tile_s[pl.ds(start, count)]
            result = centre + both[:, : self.width] * jax.nn.sigmoid(both[:, self.width :])
            if l == 0:
                p = lax.broadcasted_iota(jnp.int32, (count, 1), 0) + start
                row = ((p.astype(jnp.float32) + 0.5) * (1.0 / wide)).astype(jnp.int32)
                y = (self.t * self.reps + self.r) * (rows - 2 * HALO) - HALO + row
                x = self.c * TC - HALO + (p - row * wide)
                inside = (y >= 0) & (y < TR * self.ntok) & (x >= 0) & (x < TC * self.cols)
                result = jnp.where(inside, result, 0.0)
            self.tile_s[pl.ds(start, count)] = result
        for y in range(rows - 2 * HALO):
            self.out_ref[y] = self.tile_s[pl.ds((y + HALO) * wide + HALO, TC)]

    def body(self):
        self.pieces, self.edge = self.s3_s.shape[:2]
        self.move()
        self.pool_s[...] = jnp.zeros(self.pool_s.shape, jnp.float32)
        self.run([(1, self.finish), (2, self.reduce_near), (7, self.feed), (5, self.reduce_far)])
        self.scatter()
        self.raster()
        for copy in (self.near, self.far, self.share):
            for i in range(self.n):
                copy(i).wait_send()
        for j in range(self.cap):
            for e in range(self.ntok):
                if e:
                    self.along(e, j).wait_send()
                for copy in (self.across, self.over, self.relay):
                    copy(e, j).wait_send()
        for k in range(self.pieces):
            self.near3(0, k).wait_send()
            self.near3(1, k).wait_send()
            self.far3(k).wait_send()


def capacity_of(count, peers):
    return max(2, (count + peers - 4) // (peers - 1))


def both_layers(tokens, dest_device, dest_slot, cap, pillar, raster_weights, weights, collective_id):
    w_qkv, w_out, w_up, w_down, attn_gain, mlp_gain = weights
    depth_weight, point_weight, raster_gain = raster_weights
    cols, reps, ntok = lax.axis_size("col"), lax.axis_size("rep"), lax.axis_size("tok")
    rows, lanes = tokens.shape
    width, hidden, count = w_qkv.shape[-2], w_up.shape[-1], dest_device.shape[0]
    block, heads, chunk = rows // count, lanes // HD, min(256, rows)
    n = rows // chunk
    wide, rep_rows = TC + 2 * HALO, TR // reps
    edge, pieces = HALO * wide, rep_rows // HALO
    tile = (rep_rows + 2 * HALO) * wide
    dma, f32, b16 = pltpu.SemaphoreType.DMA, jnp.float32, jnp.bfloat16
    places = {True: pl.BlockSpec(memory_space=pltpu.VMEM), False: pl.BlockSpec(memory_space=pl.ANY)}
    inputs = dict(
        tokens_ref=tokens, wqkv_ref=w_qkv, wo_ref=w_out, wu_ref=w_up, wd_ref=w_down, pw_ref=point_weight,
        ga_ref=attn_gain, gm_ref=mlp_gain, dd_ref=dest_device[None, :], ds_ref=dest_slot[None, :],
        pillar_ref=pillar[None, :], dw_ref=jnp.transpose(depth_weight, (1, 2, 0, 3)), rg_ref=raster_gain,
    )
    far_away = ("tokens_ref", "wqkv_ref", "wo_ref", "wu_ref", "wd_ref", "pw_ref")
    floats = dict(
        wqkv_f=(2, 3, width, lanes), wo_f=(2, lanes, width), wu_f=(2, width, hidden),
        wd_f=(2, hidden, width), att_s=(2, chunk, lanes), p_s=(rows, width), n1_s=(rows // 2, width),
        s1_s=(rows // 2, width), f1_s=(rows // 2, width), a_s=(rows, width),
        g0_s=(cols * reps, rows, lanes), m_s=(reps, cols, rows, lanes), n2_s=(cols, rows, lanes),
        s2_s=(rows, lanes), f2_s=(rows, lanes), code_s=(8, 128), arrived_s=(ntok, 8, 128),
        y_s=(count, block, lanes), o_s=(ntok, cap, block, lanes),
        g_s=(ntok, cols * reps, cap, block, lanes), raw_s=(3, ntok * cap, block, lanes),
        pw_f=point_weight.shape, pool_s=(cols * reps * rep_rows * wide, width),
        n3_s=(2, pieces, edge, width), s3_s=(pieces, edge, width), f3_s=(pieces, edge, width),
        h_s=(2, edge, width), tile_s=(tile, width), flat_s=(tile + 16, width),
    )
    halves = dict(
        wqkv_s=(2, 2, 3, width, lanes), wo_s=(2, 2, lanes, width), wu_s=(2, 2, width, hidden),
        wd_s=(2, 2, hidden, width), q_s=(2, rows, 2 * lanes), k_s=(2, rows, 2 * lanes),
        v_s=(2, rows, 2 * lanes), pw_s=(2,) + point_weight.shape,
    )
    scratch = {name: pltpu.VMEM(shape, f32) for name, shape in floats.items()}
    scratch.update({name: pltpu.VMEM(shape, b16) for name, shape in halves.items()})
    for name in ("index", "source"):
        scratch[name + "_v"] = pltpu.VMEM((1, 128), jnp.int32)
        scratch[name + "_m"] = pltpu.SMEM((1, 128), jnp.int32)
    for kind in ("near", "far", "share", "near2", "far2", "across", "over", "relay"):
        scratch[kind + "_sem0"] = dma((2, n))
    scratch["code_sem0"] = dma((2, ntok))
    for kind in ("near", "far", "share"):
        scratch[kind + "_sem1"] = dma((2, n))
    for kind in ("along", "across", "over", "relay"):
        scratch[kind + "_sem1"] = dma((2, ntok * cap))
    scratch["near3_sem1"] = dma((2, 2 * pieces))
    scratch["far3_sem1"] = dma((2, pieces))
    scratch["halo_sem1"] = dma((2, 2))
    scratch["wsem"], scratch["tsem"] = dma((2, 4)), dma((4,))
    names = list(inputs) + ["out_ref"] + list(scratch)

    def kernel(*refs):
        refs = dict(zip(names, refs))
        first, second = First(0, refs, heads, chunk), Second(1, refs, heads, chunk)
        step = jnp.where(first.r == 0, ntok - 1, 1)
        second.partner = {"tok": lax.rem(first.t + step, ntok), "rep": 1 - first.r}
        first.load_weights()
        second.load_weights()
        second.load_points()
        greet([first.mate, first.peer, second.partner] + first.peers)
        first.body(second)
        second.body()

    return pl.pallas_call(
        kernel,
        out_shape=jax.ShapeDtypeStruct((rep_rows, TC, width), f32),
        in_specs=[places[name not in far_away] for name in inputs],
        out_specs=places[True],
        scratch_shapes=list(scratch.values()),
        compiler_params=pltpu.CompilerParams(
            collective_id=collective_id, has_side_effects=True, vmem_limit_bytes=VMEM_LIMIT
        ),
        name="layers",
    )(*inputs.values())


HALO = 2


def routes(dest_device, dest_slot):
    count = dest_device.shape[0]
    peers = lax.axis_size("tok")
    capacity = capacity_of(count, peers)
    order = jnp.arange(count, dtype=jnp.int32)
    earlier = (dest_device[:, None] == dest_device[None, :]) & (order[None, :] < order[:, None])
    place = dest_device * capacity + jnp.sum(earlier.astype(jnp.int32), axis=1)
    chosen = jnp.arange(peers * capacity, dtype=jnp.int32)[:, None] == place[None, :]
    index = jnp.sum(jnp.where(chosen, order[None, :], 0), axis=1)
    code = jnp.sum(jnp.where(chosen, dest_slot[None, :] + 1, 0), axis=1)
    code = jnp.pad(code.reshape(peers, capacity), ((0, 0), (0, 128 - capacity)))
    code = jnp.broadcast_to(code[:, None, :], (peers, 8, 128)).astype(jnp.float32)
    return index, code, capacity


def places(arrived, capacity, order):
    held = arrived[:, 0, :capacity].reshape(-1).astype(jnp.int32)
    found = held[None, :] == order[:, None] + 1
    return jnp.sum(jnp.where(found, jnp.arange(held.shape[0], dtype=jnp.int32)[None, :], 0), axis=1)


def raster_cells(extended, depth_weight, point_weight, gain_row):
    row_count = extended.shape[0] - 2
    col_count = extended.shape[1] - 2
    channels = extended.shape[2]
    normed = (
        extended
        * lax.rsqrt(jnp.mean(extended * extended, axis=-1, keepdims=True) + EPSILON)
        * gain_row
    )
    mixed = jnp.zeros((row_count, col_count, channels), jnp.float32)
    for a in range(3):
        for b in range(3):
            mixed = mixed + normed[a : a + row_count, b : b + col_count] * depth_weight[a, b]
    combined = matmul(mixed.reshape(row_count * col_count, channels), point_weight)
    combined = combined.reshape(row_count, col_count, 2 * channels)
    centre = extended[1:-1, 1:-1]
    return centre + combined[..., :channels] * jax.nn.sigmoid(combined[..., channels:])


def extended_cells(tok, members, rep_rows, full_width):
    cols, reps = members
    tile = []
    for col in range(cols):
        for rep in range(reps):
            y = rep * rep_rows - HALO + jnp.arange(rep_rows + 2 * HALO, dtype=jnp.int32)[:, None]
            x = col * TC - HALO + jnp.arange(TC + 2 * HALO, dtype=jnp.int32)[None, :]
            good = (y >= 0) & (y < TR) & (x >= 0) & (x < full_width)
            tile.append(jnp.where(good, (tok * TR + y) * full_width + x, -2).reshape(-1))
    return jnp.concatenate(tile)


def pool(partial, pillar, cells):
    onehot = (cells[:, None] == pillar[None, :]).astype(jnp.float32)
    return matmul(onehot, partial)


def exchange_rows(tile, ntok, reps):
    count = ntok * reps
    rep = lax.axis_index("rep")
    forward = [(i, i + 1) for i in range(count - 1)]
    backward = [(i + 1, i) for i in range(count - 1)]
    above = lax.ppermute(tile[-2 * HALO : -HALO], ("tok", "rep"), forward)
    below = lax.ppermute(tile[HALO : 2 * HALO], ("tok", "rep"), backward)
    above = jnp.where(rep == 0, above, tile[:HALO])
    below = jnp.where(rep == reps - 1, below, tile[-HALO:])
    return jnp.concatenate([above, tile[HALO:-HALO], below], axis=0)


def on_device(
    tokens,
    w_qkv,
    w_out,
    w_up,
    w_down,
    attn_gain,
    mlp_gain,
    dest_device,
    dest_slot,
    pillar,
    depth_weight,
    point_weight,
    raster_gain,
):
    members = (lax.axis_size("col"), lax.axis_size("rep"))
    group = members[0] * members[1]
    ntok = lax.axis_size("tok")
    block_count = dest_device.shape[0]
    order = jnp.arange(block_count, dtype=jnp.int32)
    index, codes, capacity = routes(dest_device, dest_slot)
    width = tokens.shape[1]
    weights = (w_qkv, w_out, w_up, w_down, attn_gain, mlp_gain)
    whole = (2 * members[1] * HALO * (TC + 2 * HALO)) % 8 == 0 and TR % (members[1] * HALO) == 0
    if members == (2, 2) and ntok > 1 and tokens.shape[0] == PATCH and whole and ntok * capacity <= 128:
        raster_weights = (depth_weight, point_weight, raster_gain)
        return both_layers(tokens, dest_device, dest_slot, capacity, pillar, raster_weights, weights, 1)
    blocks = gather(tokens, 1).reshape(1, group, block_count, -1, width)
    stream = attention_layer(blocks, order, 0, w_qkv, w_out, attn_gain, 2)
    share = scatter(mlp_partial(stream, 0, w_up, w_down, mlp_gain, group), 3)
    outgoing = pick(share.reshape(block_count, -1, width), index)
    outgoing = outgoing.reshape(ntok, -1, width)
    moved, arrived = move(outgoing, codes, 4)
    blocks = moved.reshape(ntok, group, capacity, -1, width)
    source = places(arrived, capacity, order)
    stream = attention_layer(blocks, source, 1, w_qkv, w_out, attn_gain, 5)
    partial = mlp_partial(stream, 1, w_up, w_down, mlp_gain, 1)[0]

    rep_rows = TR // members[1]
    full_width = TC * members[0]
    cells = extended_cells(lax.axis_index("tok"), members, rep_rows, full_width)
    pooled = pool(partial, pillar, cells)
    parts = pooled.reshape(group, -1, pooled.shape[1])
    edge = HALO * (TC + 2 * HALO)
    inside_kernel = members[0] > 1 and members[1] == 2 and ntok > 1 and edge % 8 == 0
    tile = scatter(parts, 6, edge if inside_kernel else 0)
    tile = tile.reshape(rep_rows + 2 * HALO, TC + 2 * HALO, -1)
    if not inside_kernel:
        tile = exchange_rows(tile, ntok, members[1])
    first = raster_cells(tile, depth_weight[0], point_weight[0], raster_gain[0])
    y = lax.axis_index(("tok", "rep")) * rep_rows - 1 + jnp.arange(rep_rows + 2)[:, None, None]
    x = lax.axis_index("col") * TC - 1 + jnp.arange(TC + 2)[None, :, None]
    inside = (y >= 0) & (y < TR * ntok) & (x >= 0) & (x < full_width)
    first = jnp.where(inside, first, 0.0)
    return raster_cells(first, depth_weight[1], point_weight[1], raster_gain[1])


def solution(mesh):
    placed = (
        P(("scene", "tok"), ("col", "rep")),
        P(None, None, None, ("col", "rep")),
        P(None, ("col", "rep"), None),
        P(None, None, ("col", "rep")),
        P(None, ("col", "rep"), None),
        P(),
        P(),
        P(("scene", "tok")),
        P(("scene", "tok")),
        P(("scene", "tok")),
        P(),
        P(),
        P(),
    )
    return jax.shard_map(
        on_device,
        mesh=mesh,
        in_specs=placed,
        out_specs=P(("scene", "tok", "rep"), "col", None),
        check_vma=False,
    )
```

```python
import functools
import math

import jax
import jax.numpy as jnp
from jax import lax
from jax.experimental import pallas as pl
from jax.experimental.pallas import tpu as pltpu
from jax.sharding import PartitionSpec as P

PATCH = 1024
TR = 16
TC = 16
HD = 16


MATMUL_PRECISION = lax.Precision.HIGH
EPSILON = 1e-05


def layer_norm(values, gain_row):
    average = jnp.mean(values, axis=-1, keepdims=True)
    centered = values - average
    variance = jnp.mean(centered * centered, axis=-1, keepdims=True)
    return centered * lax.rsqrt(variance + EPSILON) * gain_row


def split(values):
    high = values.astype(jnp.bfloat16)
    return high, (values - high.astype(jnp.float32)).astype(jnp.bfloat16)


def bdot(left, right, dims=(((1,), (0,)), ((), ()))):
    return lax.dot_general(left, right, dims, preferred_element_type=jnp.float32)


def dot3(left, right):
    lh, ll = left
    rh, rl = right
    return bdot(lh, rh) + bdot(lh, rl) + bdot(ll, rh)


def attention_kernel(share, source_ref, x_ref, gain_ref, w_ref, o_ref, out_ref, q_s, k_s, v_s, att_s):
    cols = w_ref.shape[-1]
    heads = cols // HD
    rows = out_ref.shape[0]
    chunk = att_s.shape[0]
    slots, each, block = x_ref.shape[1:4]
    first_block = pl.program_id(0) * (rows // block)

    def stream_rows(i):
        parts = []
        for n in range(chunk // block):
            at = source_ref[first_block + i * (chunk // block) + n]
            places = [x_ref[at // each, j, at % each] for j in range(slots)]
            parts.append(jnp.concatenate(places, axis=-1))
        return jnp.concatenate(parts, axis=0)

    lanes = q_s.shape[-1]

    r = lax.broadcasted_iota(jnp.int32, (cols, lanes), 0)
    c = lax.broadcasted_iota(jnp.int32, (cols, lanes), 1)
    lane = lax.broadcasted_iota(jnp.int32, (1, cols), 1)
    w = [split(w_ref[j]) for j in range(3)]
    for i in range(rows // chunk):
        at = pl.ds(i * chunk, chunk)
        normed = split(layer_norm(stream_rows(i), gain_ref[...]))
        qh, ql = split(dot3(normed, w[0]) * (HD ** (-0.5) * math.log2(math.e)))
        kh, kl = split(dot3(normed, w[1]))
        vh, vl = split(dot3(normed, w[2]))
        for h in range(heads):
            part = c // HD
            inside = (r // HD == h) & (r % HD == c % HD)
            first = (inside & ((part == 0) | (part == 1))).astype(jnp.bfloat16)
            third = (inside & (part == 2)).astype(jnp.bfloat16)
            outer = (inside & ((part == 0) | (part == 2))).astype(jnp.bfloat16)
            middle = (inside & (part == 1)).astype(jnp.bfloat16)
            q_s[h, at, :] = (bdot(qh, first) + bdot(ql, third)).astype(jnp.bfloat16)
            k_s[h, at, :] = (bdot(kh, outer) + bdot(kl, middle)).astype(jnp.bfloat16)
            own = lane // HD == h
            v_s[h, at, :cols] = jnp.where(own, vh.astype(jnp.float32), 0.0).astype(jnp.bfloat16)
            v_s[h, at, cols:] = jnp.where(own, vl.astype(jnp.float32), 1.0).astype(jnp.bfloat16)

    projection = split(o_ref[...])

    def query_rows(i, carry):
        at = pl.ds(pl.multiple_of(i * chunk, chunk), chunk)
        att_s[...] = jnp.zeros_like(att_s)

        def one_head(h, carry):
            scores = bdot(q_s[h, at, :], k_s[h], (((1,), (1,)), ((), ())))
            weights = jnp.exp2(scores - jnp.max(scores, axis=-1, keepdims=True))
            wh, wl = split(weights)
            sums = bdot(wh, v_s[h]) + bdot(wl, v_s[h])
            top, low = sums[:, :cols], sums[:, cols:]
            own = lane // HD == h
            total = jnp.max(jnp.where(own, 0.0, low), axis=-1, keepdims=True)
            att_s[...] += jnp.where(own, (top + low) / total, 0.0)
            return carry

        lax.fori_loop(0, heads, one_head, 0, unroll=4)
        out_ref[at, :] = dot3(split(att_s[...]), projection) + stream_rows(i) * share
        return carry

    lax.fori_loop(0, rows // chunk, query_rows, 0)


def attend(blocks, source, gain_row, weights, w_out, group):
    block, width = blocks.shape[3], blocks.shape[1] * blocks.shape[4]
    rows = source.shape[0] * block
    cols = weights.shape[-1]
    heads = cols // HD
    lanes = max(128, 3 * HD)
    return pl.pallas_call(
        functools.partial(attention_kernel, 1.0 / group),
        grid_spec=pltpu.PrefetchScalarGridSpec(
            num_scalar_prefetch=1,
            grid=(rows // PATCH,),
            in_specs=[
                pl.BlockSpec(blocks.shape, lambda i, source: (0, 0, 0, 0, 0)),
                pl.BlockSpec((1, width), lambda i, source: (0, 0)),
                pl.BlockSpec(weights.shape, lambda i, source: (0, 0, 0)),
                pl.BlockSpec(w_out.shape, lambda i, source: (0, 0)),
            ],
            out_specs=pl.BlockSpec((PATCH, width), lambda i, source: (i, 0)),
            scratch_shapes=[
                pltpu.VMEM((heads, PATCH, lanes), jnp.bfloat16),
                pltpu.VMEM((heads, PATCH, lanes), jnp.bfloat16),
                pltpu.VMEM((heads, PATCH, 2 * cols), jnp.bfloat16),
                pltpu.VMEM((256, cols), jnp.float32),
            ],
        ),
        out_shape=jax.ShapeDtypeStruct((rows, width), jnp.float32),
        compiler_params=pltpu.CompilerParams(vmem_limit_bytes=48 * 1024 * 1024),
        name="attend",
    )(source, blocks, gain_row[None, :], weights, w_out)


def matmul(left, right):
    return jnp.dot(left, right, precision=MATMUL_PRECISION, preferred_element_type=jnp.float32)


VMEM_LIMIT = 56 * 1024 * 1024
MESH = pl.DeviceIdType.MESH


def position():
    cols, reps = lax.axis_size("col"), lax.axis_size("rep")
    return cols, reps, lax.axis_index("col"), lax.axis_index("rep")


def greet(devices):
    barrier = pltpu.get_barrier_semaphore()
    for device in devices:
        pl.semaphore_signal(barrier, inc=1, device_id=device, device_id_type=MESH)
    pl.semaphore_wait(barrier, len(devices))


def remote(src, dst, send, recv, device):
    return pltpu.make_async_remote_copy(
        src_ref=src, dst_ref=dst, send_sem=send, recv_sem=recv, device_id=device, device_id_type=MESH
    )


def chunks_of(rows):
    for pieces in (8, 5, 4, 2):
        if rows % (8 * pieces) == 0:
            return pieces, rows // pieces
    return 1, rows


def gather_kernel(x_ref, out_ref, xs, xr, fs, fr, ps, pr, local):
    cols, reps, c, r = position()
    rows = x_ref.shape[0]
    pieces, size = chunks_of(rows)
    me = c * reps + r
    mate = {"col": c, "rep": 1 - r}
    others = [{"col": lax.rem(c + d, cols), "rep": r} for d in range(1, cols)]
    greet([mate] + others)
    across, onward = [], []
    for k in range(pieces):
        at = pl.ds(k * size, size)
        for d in range(1, cols):
            copy = remote(
                x_ref.at[at], out_ref.at[me, at], xs.at[d - 1, k], xr.at[d - 1, k], others[d - 1]
            )
            copy.start()
            across.append(copy)
    share = remote(x_ref, out_ref.at[me], ps, pr, mate)
    share.start()
    keep = pltpu.make_async_copy(x_ref, out_ref.at[me], local)
    keep.start()
    for k in range(pieces):
        at = pl.ds(k * size, size)
        for d in range(1, cols):
            across[k * (cols - 1) + d - 1].wait_recv()
            slot = lax.rem(c + cols - d, cols) * reps + r
            copy = remote(
                out_ref.at[slot, at], out_ref.at[slot, at], fs.at[d - 1, k], fr.at[d - 1, k], mate
            )
            copy.start()
            onward.append(copy)
    for copy in across:
        copy.wait_send()
    share.wait()
    keep.wait()
    for copy in onward:
        copy.wait()


def gather(block, collective_id):
    cols, reps = lax.axis_size("col"), lax.axis_size("rep")
    if reps != 2 or cols < 2:
        return lax.all_gather(block, ("col", "rep"), axis=0)
    pieces, _ = chunks_of(block.shape[0])
    dma = pltpu.SemaphoreType.DMA
    return pl.pallas_call(
        gather_kernel,
        out_shape=jax.ShapeDtypeStruct((cols * reps,) + block.shape, block.dtype),
        in_specs=[pl.BlockSpec(memory_space=pltpu.VMEM)],
        out_specs=pl.BlockSpec(memory_space=pltpu.VMEM),
        scratch_shapes=[dma((cols - 1, pieces))] * 4 + [dma, dma, dma],
        compiler_params=pltpu.CompilerParams(
            collective_id=collective_id, has_side_effects=True, vmem_limit_bytes=VMEM_LIMIT
        ),
        name="gather",
    )(block)


def scatter_kernel(edge, p_ref, out_ref, a_ref, s_ref, b_ref, a_s, a_r, b_s, b_r, *halo):
    cols, reps, c, r = position()
    rows = p_ref.shape[1]
    pieces, size = chunks_of(rows)
    mate = {"col": c, "rep": 1 - r}
    others = [{"col": lax.rem(c + d, cols), "rep": r} for d in range(1, cols)]
    greeted = [mate] + others
    if edge:
        ntok, t = lax.axis_size("tok"), lax.axis_index("tok")
        partner = {"tok": lax.rem(t + jnp.where(r == 0, ntok - 1, 1), ntok), "rep": 1 - r}
        greeted = greeted + [partner]
    greet(greeted)
    order = [(k, d) for k in range(pieces) for d in range(1, cols)]
    order += [(k, 0) for k in range(pieces)]
    near, far = {}, {}
    for k, d in order:
        at = pl.ds(k * size, size)
        slot = lax.rem(c + d, cols) * reps + 1 - r
        near[k, d] = remote(
            p_ref.at[slot, at], a_ref.at[d, at], a_s.at[d, k], a_r.at[d, k], mate
        )
        near[k, d].start()
    for k, d in order:
        at = pl.ds(k * size, size)
        slot = lax.rem(c + d, cols) * reps + r
        near[k, d].wait_recv()
        total = p_ref[slot, at] + a_ref[d, at]
        if d == 0:
            out_ref[at] = total
        else:
            s_ref[d - 1, at] = total
            far[k, d] = remote(
                s_ref.at[d - 1, at],
                b_ref.at[d - 1, at],
                b_s.at[d - 1, k],
                b_r.at[d - 1, k],
                others[d - 1],
            )
            far[k, d].start()
    for (k, d), copy in far.items():
        at = pl.ds(k * size, size)
        copy.wait_recv()
        out_ref[at] += b_ref[d - 1, at]
    if edge:
        h_ref, e_ref, h_s, h_r = halo
        inner = pl.multiple_of(jnp.where(r == 0, edge, rows - 2 * edge), 8)
        outer = pl.multiple_of(jnp.where(r == 0, 0, rows - edge), 8)
        e_ref[...] = out_ref[pl.ds(inner, edge)]
        copy = remote(e_ref, h_ref, h_s, h_r, partner)
        copy.start()
        copy.wait()
        wrapped = jnp.where(r == 0, t == 0, t == ntok - 1)
        out_ref[pl.ds(outer, edge)] = jnp.where(wrapped, 0.0, h_ref[...])
    for copy in list(near.values()) + list(far.values()):
        copy.wait_send()


def scatter(parts, collective_id, edge=0):
    cols, reps = lax.axis_size("col"), lax.axis_size("rep")
    if reps != 2 or cols < 2:
        return lax.psum_scatter(parts, ("col", "rep"), scatter_dimension=0)
    shape, kind = parts.shape[1:], parts.dtype
    pieces, _ = chunks_of(shape[0])
    dma = pltpu.SemaphoreType.DMA
    return pl.pallas_call(
        functools.partial(scatter_kernel, edge),
        out_shape=jax.ShapeDtypeStruct(shape, kind),
        in_specs=[pl.BlockSpec(memory_space=pltpu.VMEM)],
        out_specs=pl.BlockSpec(memory_space=pltpu.VMEM),
        scratch_shapes=[
            pltpu.VMEM((cols,) + shape, kind),
            pltpu.VMEM((cols - 1,) + shape, kind),
            pltpu.VMEM((cols - 1,) + shape, kind),
            dma((cols, pieces)),
            dma((cols, pieces)),
            dma((cols - 1, pieces)),
            dma((cols - 1, pieces)),
        ]
        + ([pltpu.VMEM((edge, shape[1]), kind)] * 2 + [dma, dma] if edge else []),
        compiler_params=pltpu.CompilerParams(
            collective_id=collective_id, has_side_effects=True, vmem_limit_bytes=VMEM_LIMIT
        ),
        name="scatter",
    )(parts)


def total_kernel(
    p_ref, out_ref, a_ref, s_ref, b_ref, a_s, a_r, b_s, b_r, xs, xr, fs, fr, ps, pr
):
    cols, reps, c, r = position()
    rows = p_ref.shape[1]
    pieces, size = chunks_of(rows)
    me = c * reps + r
    mate = {"col": c, "rep": 1 - r}
    others = [{"col": lax.rem(c + d, cols), "rep": r} for d in range(1, cols)]
    greet([mate] + others)
    order = [(k, d) for k in range(pieces) for d in range(1, cols)]
    order += [(k, 0) for k in range(pieces)]
    near, far, across, share, onward = {}, {}, {}, {}, {}
    for k, d in order:
        at = pl.ds(k * size, size)
        slot = lax.rem(c + d, cols) * reps + 1 - r
        near[k, d] = remote(
            p_ref.at[slot, at], a_ref.at[d, at], a_s.at[d, k], a_r.at[d, k], mate
        )
        near[k, d].start()
    for k, d in order:
        if d == 0:
            continue
        at = pl.ds(k * size, size)
        slot = lax.rem(c + d, cols) * reps + r
        near[k, d].wait_recv()
        s_ref[d - 1, at] = p_ref[slot, at] + a_ref[d, at]
        far[k, d] = remote(
            s_ref.at[d - 1, at], b_ref.at[d - 1, at], b_s.at[d - 1, k], b_r.at[d - 1, k], others[d - 1]
        )
        far[k, d].start()
    for k in range(pieces):
        at = pl.ds(k * size, size)
        near[k, 0].wait_recv()
        total = p_ref[me, at] + a_ref[0, at]
        for d in range(1, cols):
            far[k, d].wait_recv()
            total = total + b_ref[d - 1, at]
        out_ref[me, at] = total
        for d in range(1, cols):
            across[k, d] = remote(
                out_ref.at[me, at], out_ref.at[me, at], xs.at[d - 1, k], xr.at[d - 1, k], others[d - 1]
            )
            across[k, d].start()
        share[k] = remote(out_ref.at[me, at], out_ref.at[me, at], ps.at[k], pr.at[k], mate)
        share[k].start()
    for (k, d), copy in across.items():
        at = pl.ds(k * size, size)
        copy.wait_recv()
        slot = lax.rem(c + cols - d, cols) * reps + r
        onward[k, d] = remote(
            out_ref.at[slot, at], out_ref.at[slot, at], fs.at[d - 1, k], fr.at[d - 1, k], mate
        )
        onward[k, d].start()
    for copies in (near, far, across):
        for copy in copies.values():
            copy.wait_send()
    for copies in (share, onward):
        for copy in copies.values():
            copy.wait()


def total(parts, collective_id):
    cols, reps = lax.axis_size("col"), lax.axis_size("rep")
    if reps != 2 or cols < 2:
        return lax.psum(parts, ("col", "rep"))
    shape, kind = parts.shape[1:], parts.dtype
    pieces, _ = chunks_of(shape[0])
    dma = pltpu.SemaphoreType.DMA
    return pl.pallas_call(
        total_kernel,
        out_shape=jax.ShapeDtypeStruct(parts.shape, kind),
        in_specs=[pl.BlockSpec(memory_space=pltpu.VMEM)],
        out_specs=pl.BlockSpec(memory_space=pltpu.VMEM),
        scratch_shapes=[
            pltpu.VMEM((cols,) + shape, kind),
            pltpu.VMEM((cols - 1,) + shape, kind),
            pltpu.VMEM((cols - 1,) + shape, kind),
            dma((cols, pieces)),
            dma((cols, pieces)),
        ]
        + [dma((cols - 1, pieces))] * 6
        + [dma((pieces,))] * 2,
        compiler_params=pltpu.CompilerParams(
            collective_id=collective_id, has_side_effects=True, vmem_limit_bytes=VMEM_LIMIT
        ),
        name="total",
    )(parts)


def move_kernel(o_ref, code_ref, out_ref, arrived_ref, zs, zr, cs, cr, xs, xr, fs, fr, ps, pr, local):
    cols, reps, c, r = position()
    ntok, t = lax.axis_size("tok"), lax.axis_index("tok")
    me = c * reps + r
    mate = {"col": c, "rep": 1 - r}
    others = [{"col": lax.rem(c + d, cols), "rep": r} for d in range(1, cols)]
    peers = [{"tok": lax.rem(t + e, ntok)} for e in range(1, ntok)]
    greet([mate] + others + peers)
    along, codes, across, share, onward = [], [], {}, [], []
    for e in range(1, ntok):
        target = lax.rem(t + e, ntok)
        copy = remote(o_ref.at[target], out_ref.at[t, me], zs.at[e - 1], zr.at[e - 1], peers[e - 1])
        copy.start()
        along.append(copy)
        copy = remote(
            code_ref.at[target], arrived_ref.at[t], cs.at[e - 1], cr.at[e - 1], peers[e - 1]
        )
        copy.start()
        codes.append(copy)
    keep = pltpu.make_async_copy(o_ref.at[t], out_ref.at[t, me], local.at[0])
    keep.start()
    keep_code = pltpu.make_async_copy(code_ref.at[t], arrived_ref.at[t], local.at[1])
    keep_code.start()

    def hand_on(e):
        u = lax.rem(t + ntok - e, ntok)
        for d in range(1, cols):
            across[e, d].wait_recv()
            slot = lax.rem(c + cols - d, cols) * reps + r
            copy = remote(
                out_ref.at[u, slot], out_ref.at[u, slot], fs.at[e, d - 1], fr.at[e, d - 1], mate
            )
            copy.start()
            onward.append(copy)

    for e in range(ntok):
        u = lax.rem(t + ntok - e, ntok)
        if e:
            along[e - 1].wait_recv()
        origin = out_ref.at[u, me] if e else o_ref.at[t]
        for d in range(1, cols):
            across[e, d] = remote(
                origin, out_ref.at[u, me], xs.at[e, d - 1], xr.at[e, d - 1], others[d - 1]
            )
            across[e, d].start()
        copy = remote(origin, out_ref.at[u, me], ps.at[e], pr.at[e], mate)
        copy.start()
        share.append(copy)
        if e:
            hand_on(e - 1)
    hand_on(ntok - 1)
    keep.wait()
    keep_code.wait()
    for copy in along + list(across.values()):
        copy.wait_send()
    for copy in codes + share + onward:
        copy.wait()


def move(outgoing, codes, collective_id):
    cols, reps, ntok = lax.axis_size("col"), lax.axis_size("rep"), lax.axis_size("tok")
    if reps != 2 or cols < 2 or ntok < 2:
        incoming = lax.all_to_all(outgoing, "tok", split_axis=0, concat_axis=0, tiled=True)
        arrived = lax.all_to_all(codes, "tok", split_axis=0, concat_axis=0, tiled=True)
        return lax.all_gather(incoming, ("col", "rep"), axis=1), arrived
    dma = pltpu.SemaphoreType.DMA
    shape = (ntok, cols * reps) + outgoing.shape[1:]
    return pl.pallas_call(
        move_kernel,
        out_shape=(
            jax.ShapeDtypeStruct(shape, outgoing.dtype),
            jax.ShapeDtypeStruct(codes.shape, codes.dtype),
        ),
        in_specs=[pl.BlockSpec(memory_space=pltpu.VMEM)] * 2,
        out_specs=[pl.BlockSpec(memory_space=pltpu.VMEM)] * 2,
        scratch_shapes=[dma((ntok - 1,))] * 4
        + [dma((ntok, cols - 1))] * 4
        + [dma((ntok,))] * 2
        + [dma((2,))],
        compiler_params=pltpu.CompilerParams(
            collective_id=collective_id, has_side_effects=True, vmem_limit_bytes=VMEM_LIMIT
        ),
        name="move",
    )(outgoing, codes)


def pick_kernel(index_ref, x_ref, out_ref):
    for j in range(out_ref.shape[0]):
        out_ref[j] = x_ref[index_ref[j]]


def pick(blocks, index):
    return pl.pallas_call(
        pick_kernel,
        out_shape=jax.ShapeDtypeStruct(index.shape + blocks.shape[1:], blocks.dtype),
        in_specs=[pl.BlockSpec(memory_space=pltpu.SMEM), pl.BlockSpec(memory_space=pltpu.VMEM)],
        out_specs=pl.BlockSpec(memory_space=pltpu.VMEM),
        name="pick",
    )(index, blocks)


def attention_layer(blocks, source, layer, w_qkv, w_out, attn_gain, collective_id):
    group = blocks.shape[1]
    terms = attend(blocks, source, attn_gain[layer], w_qkv[layer], w_out[layer], group)
    rows, width = terms.shape
    return total(terms.reshape(group, rows // group, width), collective_id).reshape(rows, width)


def mlp_kernel(x_ref, gain_ref, up_ref, down_ref, share, out_ref):
    x = x_ref[...]
    hidden = dot3(split(layer_norm(x, gain_ref[...])), split(up_ref[...]))
    hidden = 0.5 * hidden * (1.0 + lax.erf(hidden * (0.5**0.5)))
    total = dot3(split(hidden), split(down_ref[...])) + x * share
    width = out_ref.shape[-1]
    for j in range(out_ref.shape[0]):
        out_ref[j] = total[:, j * width : (j + 1) * width]


def mlp_partial(stream, layer, w_up, w_down, mlp_gain, slots):
    rows, width = stream.shape
    tile = min(256, rows)
    hidden = w_up.shape[-1]
    group = lax.axis_size("col") * lax.axis_size("rep")

    def kernel(x_ref, gain_ref, up_ref, down_ref, out_ref):
        mlp_kernel(x_ref, gain_ref, up_ref, down_ref, 1.0 / group, out_ref)

    return pl.pallas_call(
        kernel,
        grid=(rows // tile,),
        in_specs=[
            pl.BlockSpec((tile, width), lambda i: (i, 0)),
            pl.BlockSpec((1, width), lambda i: (0, 0)),
            pl.BlockSpec((width, hidden), lambda i: (0, 0)),
            pl.BlockSpec((hidden, width), lambda i: (0, 0)),
        ],
        out_specs=pl.BlockSpec((slots, tile, width // slots), lambda i: (0, i, 0)),
        out_shape=jax.ShapeDtypeStruct((slots, rows, width // slots), jnp.float32),
        compiler_params=pltpu.CompilerParams(vmem_limit_bytes=48 * 1024 * 1024),
        name="mlp",
    )(stream, mlp_gain[layer][None, :], w_up[layer], w_down[layer])


def gelu(values):
    return 0.5 * values * (1.0 + lax.erf(values * (0.5**0.5)))


def piece(i, size):
    return pl.ds(pl.multiple_of(i * size, size), size)


class Layer:
    def __init__(self, layer, refs, heads, chunk):
        self.__dict__.update(refs)
        self.layer, self.heads, self.chunk = layer, heads, chunk
        self.tag = "_sem" + str(layer)
        self.cols, self.reps, self.c, self.r = position()
        self.ntok, self.t = lax.axis_size("tok"), lax.axis_index("tok")
        self.me = self.c * self.reps + self.r
        self.mate, self.peer = {"rep": 1 - self.r}, {"col": 1 - self.c}
        self.peers = [{"tok": lax.rem(self.t + e, self.ntok)} for e in range(1, self.ntok)]
        self.rows, self.width = self.a_s.shape
        self.lanes = self.q_s.shape[-1] // 2
        self.n = self.rows // chunk
        self.block = self.y_s.shape[1]
        self.cap = self.o_s.shape[1]

    def sent(self, kind, i, src, dst, device):
        sem = getattr(self, kind + self.tag)
        return remote(src, dst, sem.at[0, i], sem.at[1, i], device)

    def load_weights(self):
        pairs = (
            (self.wqkv_ref, self.wqkv_f), (self.wo_ref, self.wo_f),
            (self.wu_ref, self.wu_f), (self.wd_ref, self.wd_f),
        )
        self.loads = [
            pltpu.make_async_copy(src.at[self.layer], dst.at[self.layer], self.wsem.at[self.layer, j])
            for j, (src, dst) in enumerate(pairs)
        ]
        for load in self.loads:
            load.start()

    def split_weights(self):
        layer = self.layer
        self.loads[0].wait()
        for m in range(3):
            self.wqkv_s[layer, 0, m], self.wqkv_s[layer, 1, m] = split(self.wqkv_f[layer, m])
        rest = ((self.wo_f, self.wo_s), (self.wu_f, self.wu_s), (self.wd_f, self.wd_s))
        for load, (src, dst) in zip(self.loads[1:], rest):
            load.wait()
            dst[layer, 0], dst[layer, 1] = split(src[layer])

    def pair(self, ref):
        return ref[self.layer, 0], ref[self.layer, 1]

    def project(self, stream):
        normed = split(layer_norm(stream, self.ga_ref[pl.ds(self.layer, 1)]))
        return [dot3(normed, (self.wqkv_s[self.layer, 0, m], self.wqkv_s[self.layer, 1, m])) for m in range(3)]

    def pack(self, at, q, k, v):
        lanes = self.lanes
        half_lanes = lanes // 2
        lane = lax.broadcasted_iota(jnp.int32, (1, lanes), 1)
        low = lane < half_lanes
        qh, ql = split(q * (HD ** (-0.5) * math.log2(math.e)))
        kh, kl = [part.astype(jnp.float32) for part in split(k)]
        vh, vl = [part.astype(jnp.float32) for part in split(v)]
        qf, qlf = qh.astype(jnp.float32), ql.astype(jnp.float32)
        q_s, k_s, v_s = self.q_s, self.k_s, self.v_s

        def roll(values):
            return pltpu.roll(values, half_lanes, 1)

        q_s[0, at, :lanes] = qh
        q_s[1, at, :lanes] = qh
        q_s[0, at, lanes:] = jnp.where(low, qf, roll(qlf)).astype(jnp.bfloat16)
        q_s[1, at, lanes:] = jnp.where(low, roll(qf), qlf).astype(jnp.bfloat16)
        k_s[0, at, :lanes] = kh.astype(jnp.bfloat16)
        k_s[1, at, :lanes] = kh.astype(jnp.bfloat16)
        k_s[0, at, lanes:] = jnp.where(low, kl, roll(kh)).astype(jnp.bfloat16)
        k_s[1, at, lanes:] = jnp.where(low, roll(kl), kh).astype(jnp.bfloat16)
        v_s[0, at, :lanes] = vh.astype(jnp.bfloat16)
        v_s[1, at, :lanes] = vh.astype(jnp.bfloat16)
        v_s[0, at, lanes:] = jnp.where(low, vl, 1.0).astype(jnp.bfloat16)
        v_s[1, at, lanes:] = jnp.where(low, 1.0, vl).astype(jnp.bfloat16)

    def near(self, i):
        half = self.chunk // 2
        start = pl.multiple_of(i * self.chunk + (1 - self.r) * half, half)
        return self.sent("near", i, self.p_s.at[pl.ds(start, half)], self.n1_s.at[piece(i, half)], self.mate)

    def far(self, i):
        at = piece(i, self.chunk // 2)
        return self.sent("far", i, self.s1_s.at[at], self.f1_s.at[at], self.peer)

    def own_half(self, i):
        half = self.chunk // 2
        return pl.ds(pl.multiple_of(i * self.chunk + self.r * half, half), half)

    def share(self, i):
        at = self.own_half(i)
        return self.sent("share", i, self.a_s.at[at], self.a_s.at[at], self.mate)

    def attention(self, k):
        lanes, half_heads, chunk = self.lanes, self.heads // 2, self.chunk
        wide = lax.broadcasted_iota(jnp.int32, (1, 2 * lanes), 1)
        lane = lax.broadcasted_iota(jnp.int32, (1, lanes), 1)
        i, half = k // 2, k % 2
        query = self.q_s[half, piece(i, chunk), :]
        queries = []
        for m in range(half_heads):
            first = (wide < lanes) & (wide // HD == half * half_heads + m)
            second = (wide >= lanes) & ((wide % (lanes // 2)) // HD == m)
            mask = jnp.where(first | second, 1.0, 0.0).astype(jnp.bfloat16)
            queries.append(query * mask)
        stacked = jnp.concatenate(queries, axis=0)
        scores = bdot(stacked, self.k_s[half], (((1,), (1,)), ((), ())))
        weights = jnp.exp2(scores - jnp.max(scores, axis=-1, keepdims=True))
        sums = bdot(jnp.concatenate(split(weights), axis=0), self.v_s[half])
        sums = sums[: half_heads * chunk] + sums[half_heads * chunk :]
        total = jnp.zeros((chunk, lanes), jnp.float32)
        for m in range(half_heads):
            own = sums[m * chunk : (m + 1) * chunk]
            top, low = own[:, :lanes], own[:, lanes:]
            ratio = (top + low) / pltpu.roll(low, lanes // 2, 1)
            total += jnp.where(lane // HD == half * half_heads + m, ratio, 0.0)
        self.att_s[half] = total

    def finish(self, i):
        projection = self.pair(self.wo_s)
        self.p_s[piece(i, self.chunk)] = dot3(split(self.att_s[0] + self.att_s[1]), projection)
        self.near(i).start()

    def reduce_near(self, i):
        self.near(i).wait_recv()
        at = piece(i, self.chunk // 2)
        self.s1_s[at] = self.p_s[self.own_half(i)] + self.n1_s[at]
        self.far(i).start()

    def reduce_far(self, i):
        self.far(i).wait_recv()
        half = self.chunk // 2
        at = piece(i, half)
        stream = self.stream_rows(i * self.chunk + self.r * half, half)
        self.a_s[self.own_half(i)] = (self.s1_s[at] + self.f1_s[at]) + stream
        self.share(i).start()

    def mlp(self, x):
        normed = split(layer_norm(x, self.gm_ref[pl.ds(self.layer, 1)]))
        hidden = gelu(dot3(normed, self.pair(self.wu_s)))
        return dot3(split(hidden), self.pair(self.wd_s))

    def run(self, stages):
        n = self.n

        def tick(k, carry):
            @pl.when(k < 2 * n)
            def _():
                self.attention(k)

            for offset, stage in stages:
                @pl.when((k >= offset) & (k < offset + 2 * n) & ((k - offset) % 2 == 0))
                def _(offset=offset, stage=stage):
                    stage((k - offset) // 2)

            return carry

        lax.fori_loop(0, 2 * n + max(offset for offset, _ in stages) - 1, tick, 0)


class First(Layer):
    def stream_rows(self, start, count):
        at = pl.ds(pl.multiple_of(start, count), count)
        return jnp.concatenate([self.g0_s[j, at] for j in range(self.cols * self.reps)], axis=-1)

    def across(self, i):
        at = piece(i, self.chunk)
        return self.sent("across", i, self.tokens_ref.at[at], self.g0_s.at[self.me, at], self.peer)

    def over(self, i):
        at = piece(i, self.chunk)
        return self.sent("over", i, self.tokens_ref.at[at], self.g0_s.at[self.me, at], self.mate)

    def relay(self, i):
        at = piece(i, self.chunk)
        slot = (1 - self.c) * self.reps + self.r
        return self.sent("relay", i, self.g0_s.at[slot, at], self.g0_s.at[slot, at], self.mate)

    def code(self, e):
        target = {"tok": lax.rem(self.t + e, self.ntok)}
        return self.sent("code", e, self.code_s, self.arrived_s.at[self.t], target)

    def route(self):
        device = self.dd_ref[...].astype(jnp.float32)
        slot = self.ds_ref[...].astype(jnp.float32)
        count = device.shape[1]
        row = lax.broadcasted_iota(jnp.int32, (count, count), 0)
        col = lax.broadcasted_iota(jnp.int32, (count, count), 1)

        def upright(values):
            return jnp.sum(jnp.where(row == col, values, 0.0), axis=1, keepdims=True)

        devices, slots = upright(device), upright(slot)
        earlier = jnp.where((devices == device) & (col < row), 1.0, 0.0)
        place = devices * self.cap + jnp.sum(earlier, axis=1, keepdims=True)
        at = lax.broadcasted_iota(jnp.int32, (count, 128), 1).astype(jnp.float32)
        block = lax.broadcasted_iota(jnp.int32, (count, 128), 0).astype(jnp.float32)
        index = jnp.sum(jnp.where(place == at, block, 0.0), axis=0, keepdims=True)
        code = jnp.sum(jnp.where(place == at, slots + 1.0, 0.0), axis=0, keepdims=True)
        self.index_v[...] = index.astype(jnp.int32)
        self.code_s[...] = jnp.broadcast_to(code, self.code_s.shape)
        self.arrived_s[self.t] = jnp.broadcast_to(code, self.code_s.shape)

    def locate(self):
        row = lax.broadcasted_iota(jnp.int32, (128, 128), 0)
        col = lax.broadcasted_iota(jnp.int32, (128, 128), 1)
        first = self.t * self.cap
        valid = (row >= first) & (row < first + self.cap)
        source = jnp.zeros((1, 128), jnp.float32)
        for u in range(self.ntok):
            codes = self.arrived_s[u][:1]
            upright = jnp.sum(jnp.where(row == col, codes, 0.0), axis=1, keepdims=True)
            found = valid & (upright == (col + 1).astype(jnp.float32))
            entry = (row - first + u * self.cap).astype(jnp.float32)
            source += jnp.sum(jnp.where(found, entry, 0.0), axis=0, keepdims=True)
        self.source_v[...] = source.astype(jnp.int32)

    def near2(self, i):
        at = piece(i, self.chunk)
        return self.sent("near2", i, self.m_s.at[1 - self.r, :, at], self.n2_s.at[:, at], self.mate)

    def far2(self, i):
        at = piece(i, self.chunk)
        return self.sent("far2", i, self.s2_s.at[at], self.f2_s.at[at], self.peer)

    def feed(self, i):
        self.share(i).wait_recv()
        at = piece(i, self.chunk)
        total = self.mlp(self.a_s[at])
        for j in range(self.cols * self.reps):
            self.m_s[j % self.reps, j // self.reps, at] = total[:, j * self.lanes : (j + 1) * self.lanes]
        self.near2(i).start()

    def scatter_near(self, i):
        self.near2(i).wait_recv()
        at = piece(i, self.chunk)
        self.s2_s[at] = self.m_s[self.r, 1 - self.c, at] + self.n2_s[1 - self.c, at]
        self.far2(i).start()

    def scatter_far(self, i):
        self.far2(i).wait_recv()
        at = piece(i, self.chunk)
        own = self.a_s[at, piece(self.me, self.lanes)]
        total = (self.m_s[self.r, self.c, at] + self.n2_s[self.c, at]) + self.f2_s[at]
        count = self.chunk // self.block
        self.y_s[piece(i, count)] = (total + own).reshape(count, self.block, self.lanes)

    def body(self, second):
        n = self.n
        for i in range(n):
            self.across(i).start()
        for i in range(n):
            self.over(i).start()
        keep = pltpu.make_async_copy(self.tokens_ref, self.g0_s.at[self.me], self.tsem.at[0])
        keep.start()
        self.route()
        table = pltpu.make_async_copy(self.index_v, self.index_m, self.tsem.at[1])
        table.start()
        self.split_weights()
        for e in range(1, self.ntok):
            self.code(e).start()
        second.split_weights()
        second.split_points()
        self.pool_s[...] = jnp.zeros(self.pool_s.shape, jnp.float32)
        keep.wait()
        table.wait()

        def step(i, carry):
            @pl.when(i < n)
            def _():
                self.across(i).wait_recv()
                self.relay(i).start()

            @pl.when(i > 0)
            def _():
                self.over(i - 1).wait_recv()
                self.relay(i - 1).wait_recv()
                stream = self.stream_rows((i - 1) * self.chunk, self.chunk)
                self.pack(piece(i - 1, self.chunk), *self.project(stream))

            return carry

        lax.fori_loop(0, n + 1, step, 0)
        self.run(
            [
                (1, self.finish), (2, self.reduce_near), (9, self.scatter_near),
                (6, self.reduce_far), (7, self.feed), (13, self.scatter_far),
            ]
        )
        for copy in (
            self.near, self.far, self.share, self.near2, self.far2, self.across, self.over, self.relay
        ):
            for i in range(n):
                copy(i).wait_send()

    def tables(self):
        for e in range(1, self.ntok):
            self.code(e).wait()
        self.locate()
        table = pltpu.make_async_copy(self.source_v, self.source_m, self.tsem.at[2])
        table.start()
        return table


class Second(Layer):
    def entry(self, k):
        return jnp.clip(self.source_m[0, k], 0, self.ntok * self.cap - 1)

    def chosen(self, u, j):
        return jnp.clip(self.index_m[0, u * self.cap + j], 0, self.y_s.shape[0] - 1)

    def stream_rows(self, start, count):
        parts = []
        for m in range(count // self.block):
            at = self.entry(start // self.block + m)
            places = [self.g_s[at // self.cap, j, at % self.cap] for j in range(self.cols * self.reps)]
            parts.append(jnp.concatenate(places, axis=-1))
        return jnp.concatenate(parts, axis=0)

    def along(self, e, j):
        target = lax.rem(self.t + e, self.ntok)
        return self.sent(
            "along", e * self.cap + j, self.o_s.at[target, j], self.g_s.at[self.t, self.me, j],
            {"tok": target},
        )

    def origin(self, e):
        return lax.rem(self.t + self.ntok - e, self.ntok)

    def placed(self, kind, e, j, slot, device):
        ref = self.g_s.at[self.origin(e), slot, j]
        return self.sent(kind, e * self.cap + j, ref, ref, device)

    def across(self, e, j):
        return self.placed("across", e, j, self.me, self.peer)

    def over(self, e, j):
        return self.placed("over", e, j, self.me, self.mate)

    def relay(self, e, j):
        return self.placed("relay", e, j, (1 - self.c) * self.reps + self.r, self.mate)

    def arrive(self, j):
        for e in self.order[1:]:
            self.along(e, j).wait_recv()
            self.across(e, j).start()
            self.over(e, j).start()

    def hand(self, j):
        for e in self.order:
            self.across(e, j).wait_recv()
            self.relay(e, j).start()

    def take(self, j):
        parts = []
        for e in self.order:
            self.over(e, j).wait_recv()
            self.relay(e, j).wait_recv()
            places = [self.g_s[self.origin(e), k, j] for k in range(self.cols * self.reps)]
            parts.append(jnp.concatenate(places, axis=-1))
        for m, values in enumerate(self.project(jnp.concatenate(parts, axis=0))):
            for at, e in enumerate(self.order):
                entry = self.origin(e) * self.cap + j
                self.raw_s[m, entry] = values[at * self.block : (at + 1) * self.block]

    def move(self, first):
        self.order = [0]
        for e in range(1, self.ntok // 2 + 1):
            self.order += [e] + ([self.ntok - e] if self.ntok - e != e else [])
        for j in range(self.cap):
            for u in range(self.ntok):
                self.o_s[u, j] = self.y_s[self.chosen(u, j)]
            for e in self.order[1:]:
                self.along(e, j).start()
        for j in range(self.cap):
            self.g_s[self.t, self.me, j] = self.y_s[self.chosen(self.t, j)]
            self.across(0, j).start()
            self.over(0, j).start()
        table = first.tables()
        for j in range(self.cap):
            self.arrive(j)
            if j >= 1:
                self.hand(j - 1)
            if j >= 2:
                self.take(j - 2)
        self.take(self.cap - 2)
        self.hand(self.cap - 1)
        self.take(self.cap - 1)
        table.wait()

        def step(i, carry):
            def row(m):
                each = self.chunk // self.block
                blocks = [self.raw_s[m, self.entry(i * each + k)] for k in range(each)]
                return jnp.concatenate(blocks, axis=0)

            self.pack(piece(i, self.chunk), row(0), row(1), row(2))
            return carry

        lax.fori_loop(0, self.n, step, 0)

    def load_points(self):
        self.point = pltpu.make_async_copy(self.pw_ref, self.pw_f, self.tsem.at[3])
        self.point.start()

    def split_points(self):
        self.point.wait()

        def step(k, carry):
            at = piece(k, 64)
            for l in range(2):
                self.pw_s[0, l, at], self.pw_s[1, l, at] = split(self.pw_f[l, at])
            return carry

        lax.fori_loop(0, self.width // 64, step, 0)

    def cell_ids(self):
        count = self.pool_s.shape[0]
        p = lax.broadcasted_iota(jnp.int32, (count, 1), 0)
        wide = TC + 2 * HALO
        row = ((p.astype(jnp.float32) + 0.5) * (1.0 / wide)).astype(jnp.int32)
        col = row // TR
        x = col * TC - HALO + (p - row * wide)
        full = TC * self.cols
        y = row - col * TR
        return jnp.where((x >= 0) & (x < full), (self.t * TR + y) * full + x, -2)

    def feed(self, i):
        self.share(i).wait_recv()
        at = piece(i, self.chunk)
        x = self.a_s[at]
        high, low = split(self.mlp(x) + x * (1.0 / (self.cols * self.reps)))
        chosen = jnp.where(self.cell_ids() == self.pillar_ref[:, at], 1.0, 0.0).astype(jnp.bfloat16)
        self.pool_s[...] += bdot(chosen, high) + bdot(chosen, low)

    def tile_part(self, c, r, k):
        cells = self.pool_s.shape[0] // (self.cols * self.reps)
        start = (c * self.reps + r) * cells + k * self.edge
        return pl.ds(pl.multiple_of(start, 8), self.edge)

    def near3(self, w, k):
        c = self.c if w else 1 - self.c
        return self.sent(
            "near3", w * self.pieces + k, self.pool_s.at[self.tile_part(c, 1 - self.r, k)],
            self.n3_s.at[w, k], self.mate,
        )

    def far3(self, k):
        return self.sent("far3", k, self.s3_s.at[k], self.f3_s.at[k], self.peer)

    def inner(self):
        start = jnp.where(self.r == 0, self.pieces * self.edge, self.edge)
        src = self.tile_s.at[pl.ds(pl.multiple_of(start, 8), self.edge)]
        return self.sent("halo", 0, src, self.h_s.at[0], self.mate)

    def outer(self):
        start = jnp.where(self.r == 0, self.edge, self.pieces * self.edge)
        src = self.tile_s.at[pl.ds(pl.multiple_of(start, 8), self.edge)]
        return self.sent("halo", 1, src, self.h_s.at[1], self.partner)

    def scatter(self):
        order = [0, self.pieces - 1] + list(range(1, self.pieces - 1))
        for w in range(2):
            for k in order:
                self.near3(w, k).start()
        for k in order:
            self.near3(0, k).wait_recv()
            self.s3_s[k] = self.pool_s[self.tile_part(1 - self.c, self.r, k)] + self.n3_s[0, k]
            self.far3(k).start()
        for at, k in enumerate(order):
            self.near3(1, k).wait_recv()
            self.far3(k).wait_recv()
            own = self.pool_s[self.tile_part(self.c, self.r, k)] + self.n3_s[1, k]
            self.tile_s[pl.ds((k + 1) * self.edge, self.edge)] = own + self.f3_s[k]
            if at == 1:
                self.inner().start()
                self.outer().start()
        self.inner().wait()
        self.outer().wait()
        wrapped = jnp.where(self.r == 0, self.t == 0, self.t == self.ntok - 1)
        beyond = jnp.where(wrapped, 0.0, self.h_s[1])
        within = self.h_s[0]
        self.tile_s[: self.edge] = jnp.where(self.r == 0, beyond, within)
        self.tile_s[(self.pieces + 1) * self.edge :] = jnp.where(self.r == 0, within, beyond)

    def raster(self):
        wide = TC + 2 * HALO
        rows = self.tile_s.shape[0] // wide
        pad = (self.flat_s.shape[0] - rows * wide) // 2
        self.flat_s[:pad] = jnp.zeros((pad, self.width), jnp.float32)
        self.flat_s[pad + rows * wide :] = jnp.zeros((pad, self.width), jnp.float32)
        for l in range(2):
            old = pl.ds(l * wide, (rows - 2 * l) * wide)
            start, count = (l + 1) * wide, (rows - 2 * l - 2) * wide
            cells = self.tile_s[old]
            square = jnp.mean(cells * cells, axis=-1, keepdims=True)
            gain = self.rg_ref[pl.ds(l, 1)]
            self.flat_s[pl.ds(pad + l * wide, (rows - 2 * l) * wide)] = (
                cells * lax.rsqrt(square + EPSILON) * gain
            )
            mixed = jnp.zeros((count, self.width), jnp.float32)
            for a in range(3):
                for b in range(3):
                    shift = pad + start + (a - 1) * wide + b - 1
                    mixed = mixed + self.flat_s[pl.ds(shift, count)] * self.dw_ref[a, b, pl.ds(l, 1)]
            both = dot3(split(mixed), (self.pw_s[0, l], self.pw_s[1, l]))
            centre = self.tile_s[pl.ds(start, count)]
            result = centre + both[:, : self.width] * jax.nn.sigmoid(both[:, self.width :])
            if l == 0:
                p = lax.broadcasted_iota(jnp.int32, (count, 1), 0) + start
                row = ((p.astype(jnp.float32) + 0.5) * (1.0 / wide)).astype(jnp.int32)
                y = (self.t * self.reps + self.r) * (rows - 2 * HALO) - HALO + row
                x = self.c * TC - HALO + (p - row * wide)
                inside = (y >= 0) & (y < TR * self.ntok) & (x >= 0) & (x < TC * self.cols)
                result = jnp.where(inside, result, 0.0)
            self.tile_s[pl.ds(start, count)] = result
        for y in range(rows - 2 * HALO):
            self.out_ref[y] = self.tile_s[pl.ds((y + HALO) * wide + HALO, TC)]

    def body(self, first):
        self.pieces, self.edge = self.s3_s.shape[:2]
        self.move(first)
        self.run([(1, self.finish), (2, self.reduce_near), (7, self.feed), (5, self.reduce_far)])
        self.scatter()
        self.raster()
        for copy in (self.near, self.far, self.share):
            for i in range(self.n):
                copy(i).wait_send()
        for j in range(self.cap):
            for e in range(self.ntok):
                if e:
                    self.along(e, j).wait_send()
                for copy in (self.across, self.over, self.relay):
                    copy(e, j).wait_send()
        for k in range(self.pieces):
            self.near3(0, k).wait_send()
            self.near3(1, k).wait_send()
            self.far3(k).wait_send()


def capacity_of(count, peers):
    return max(2, (count + peers - 4) // (peers - 1))


def both_layers(tokens, dest_device, dest_slot, cap, pillar, raster_weights, weights, collective_id):
    w_qkv, w_out, w_up, w_down, attn_gain, mlp_gain = weights
    depth_weight, point_weight, raster_gain = raster_weights
    cols, reps, ntok = lax.axis_size("col"), lax.axis_size("rep"), lax.axis_size("tok")
    rows, lanes = tokens.shape
    width, hidden, count = w_qkv.shape[-2], w_up.shape[-1], dest_device.shape[0]
    block, heads, chunk = rows // count, lanes // HD, min(256, rows)
    n = rows // chunk
    wide, rep_rows = TC + 2 * HALO, TR // reps
    edge, pieces = HALO * wide, rep_rows // HALO
    tile = (rep_rows + 2 * HALO) * wide
    dma, f32, b16 = pltpu.SemaphoreType.DMA, jnp.float32, jnp.bfloat16
    places = {True: pl.BlockSpec(memory_space=pltpu.VMEM), False: pl.BlockSpec(memory_space=pl.ANY)}
    inputs = dict(
        tokens_ref=tokens, wqkv_ref=w_qkv, wo_ref=w_out, wu_ref=w_up, wd_ref=w_down, pw_ref=point_weight,
        ga_ref=attn_gain, gm_ref=mlp_gain, dd_ref=dest_device[None, :], ds_ref=dest_slot[None, :],
        pillar_ref=pillar[None, :], dw_ref=jnp.transpose(depth_weight, (1, 2, 0, 3)), rg_ref=raster_gain,
    )
    far_away = ("tokens_ref", "wqkv_ref", "wo_ref", "wu_ref", "wd_ref", "pw_ref")
    floats = dict(
        wqkv_f=(2, 3, width, lanes), wo_f=(2, lanes, width), wu_f=(2, width, hidden),
        wd_f=(2, hidden, width), att_s=(2, chunk, lanes), p_s=(rows, width), n1_s=(rows // 2, width),
        s1_s=(rows // 2, width), f1_s=(rows // 2, width), a_s=(rows, width),
        g0_s=(cols * reps, rows, lanes), m_s=(reps, cols, rows, lanes), n2_s=(cols, rows, lanes),
        s2_s=(rows, lanes), f2_s=(rows, lanes), code_s=(8, 128), arrived_s=(ntok, 8, 128),
        y_s=(count, block, lanes), o_s=(ntok, cap, block, lanes),
        g_s=(ntok, cols * reps, cap, block, lanes), raw_s=(3, ntok * cap, block, lanes),
        pw_f=point_weight.shape, pool_s=(cols * reps * rep_rows * wide, width),
        n3_s=(2, pieces, edge, width), s3_s=(pieces, edge, width), f3_s=(pieces, edge, width),
        h_s=(2, edge, width), tile_s=(tile, width), flat_s=(tile + 16, width),
    )
    halves = dict(
        wqkv_s=(2, 2, 3, width, lanes), wo_s=(2, 2, lanes, width), wu_s=(2, 2, width, hidden),
        wd_s=(2, 2, hidden, width), q_s=(2, rows, 2 * lanes), k_s=(2, rows, 2 * lanes),
        v_s=(2, rows, 2 * lanes), pw_s=(2,) + point_weight.shape,
    )
    scratch = {name: pltpu.VMEM(shape, f32) for name, shape in floats.items()}
    scratch.update({name: pltpu.VMEM(shape, b16) for name, shape in halves.items()})
    for name in ("index", "source"):
        scratch[name + "_v"] = pltpu.VMEM((1, 128), jnp.int32)
        scratch[name + "_m"] = pltpu.SMEM((1, 128), jnp.int32)
    for kind in ("near", "far", "share", "near2", "far2", "across", "over", "relay"):
        scratch[kind + "_sem0"] = dma((2, n))
    scratch["code_sem0"] = dma((2, ntok))
    for kind in ("near", "far", "share"):
        scratch[kind + "_sem1"] = dma((2, n))
    for kind in ("along", "across", "over", "relay"):
        scratch[kind + "_sem1"] = dma((2, ntok * cap))
    scratch["near3_sem1"] = dma((2, 2 * pieces))
    scratch["far3_sem1"] = dma((2, pieces))
    scratch["halo_sem1"] = dma((2, 2))
    scratch["wsem"], scratch["tsem"] = dma((2, 4)), dma((4,))
    names = list(inputs) + ["out_ref"] + list(scratch)

    def kernel(*refs):
        refs = dict(zip(names, refs))
        first, second = First(0, refs, heads, chunk), Second(1, refs, heads, chunk)
        step = jnp.where(first.r == 0, ntok - 1, 1)
        second.partner = {"tok": lax.rem(first.t + step, ntok), "rep": 1 - first.r}
        first.load_weights()
        second.load_weights()
        second.load_points()
        greet([first.mate, first.peer, second.partner] + first.peers)
        first.body(second)
        second.body(first)

    return pl.pallas_call(
        kernel,
        out_shape=jax.ShapeDtypeStruct((rep_rows, TC, width), f32),
        in_specs=[places[name not in far_away] for name in inputs],
        out_specs=places[True],
        scratch_shapes=list(scratch.values()),
        compiler_params=pltpu.CompilerParams(
            collective_id=collective_id, has_side_effects=True, vmem_limit_bytes=VMEM_LIMIT
        ),
        name="layers",
    )(*inputs.values())


HALO = 2


def routes(dest_device, dest_slot):
    count = dest_device.shape[0]
    peers = lax.axis_size("tok")
    capacity = capacity_of(count, peers)
    order = jnp.arange(count, dtype=jnp.int32)
    earlier = (dest_device[:, None] == dest_device[None, :]) & (order[None, :] < order[:, None])
    place = dest_device * capacity + jnp.sum(earlier.astype(jnp.int32), axis=1)
    chosen = jnp.arange(peers * capacity, dtype=jnp.int32)[:, None] == place[None, :]
    index = jnp.sum(jnp.where(chosen, order[None, :], 0), axis=1)
    code = jnp.sum(jnp.where(chosen, dest_slot[None, :] + 1, 0), axis=1)
    code = jnp.pad(code.reshape(peers, capacity), ((0, 0), (0, 128 - capacity)))
    code = jnp.broadcast_to(code[:, None, :], (peers, 8, 128)).astype(jnp.float32)
    return index, code, capacity


def places(arrived, capacity, order):
    held = arrived[:, 0, :capacity].reshape(-1).astype(jnp.int32)
    found = held[None, :] == order[:, None] + 1
    return jnp.sum(jnp.where(found, jnp.arange(held.shape[0], dtype=jnp.int32)[None, :], 0), axis=1)


def raster_cells(extended, depth_weight, point_weight, gain_row):
    row_count = extended.shape[0] - 2
    col_count = extended.shape[1] - 2
    channels = extended.shape[2]
    normed = (
        extended
        * lax.rsqrt(jnp.mean(extended * extended, axis=-1, keepdims=True) + EPSILON)
        * gain_row
    )
    mixed = jnp.zeros((row_count, col_count, channels), jnp.float32)
    for a in range(3):
        for b in range(3):
            mixed = mixed + normed[a : a + row_count, b : b + col_count] * depth_weight[a, b]
    combined = matmul(mixed.reshape(row_count * col_count, channels), point_weight)
    combined = combined.reshape(row_count, col_count, 2 * channels)
    centre = extended[1:-1, 1:-1]
    return centre + combined[..., :channels] * jax.nn.sigmoid(combined[..., channels:])


def extended_cells(tok, members, rep_rows, full_width):
    cols, reps = members
    tile = []
    for col in range(cols):
        for rep in range(reps):
            y = rep * rep_rows - HALO + jnp.arange(rep_rows + 2 * HALO, dtype=jnp.int32)[:, None]
            x = col * TC - HALO + jnp.arange(TC + 2 * HALO, dtype=jnp.int32)[None, :]
            good = (y >= 0) & (y < TR) & (x >= 0) & (x < full_width)
            tile.append(jnp.where(good, (tok * TR + y) * full_width + x, -2).reshape(-1))
    return jnp.concatenate(tile)


def pool(partial, pillar, cells):
    onehot = (cells[:, None] == pillar[None, :]).astype(jnp.float32)
    return matmul(onehot, partial)


def exchange_rows(tile, ntok, reps):
    count = ntok * reps
    rep = lax.axis_index("rep")
    forward = [(i, i + 1) for i in range(count - 1)]
    backward = [(i + 1, i) for i in range(count - 1)]
    above = lax.ppermute(tile[-2 * HALO : -HALO], ("tok", "rep"), forward)
    below = lax.ppermute(tile[HALO : 2 * HALO], ("tok", "rep"), backward)
    above = jnp.where(rep == 0, above, tile[:HALO])
    below = jnp.where(rep == reps - 1, below, tile[-HALO:])
    return jnp.concatenate([above, tile[HALO:-HALO], below], axis=0)


def on_device(
    tokens,
    w_qkv,
    w_out,
    w_up,
    w_down,
    attn_gain,
    mlp_gain,
    dest_device,
    dest_slot,
    pillar,
    depth_weight,
    point_weight,
    raster_gain,
):
    members = (lax.axis_size("col"), lax.axis_size("rep"))
    group = members[0] * members[1]
    ntok = lax.axis_size("tok")
    block_count = dest_device.shape[0]
    order = jnp.arange(block_count, dtype=jnp.int32)
    index, codes, capacity = routes(dest_device, dest_slot)
    width = tokens.shape[1]
    weights = (w_qkv, w_out, w_up, w_down, attn_gain, mlp_gain)
    whole = (2 * members[1] * HALO * (TC + 2 * HALO)) % 8 == 0 and TR % (members[1] * HALO) == 0
    if members == (2, 2) and ntok > 1 and tokens.shape[0] == PATCH and whole and ntok * capacity <= 128:
        raster_weights = (depth_weight, point_weight, raster_gain)
        return both_layers(tokens, dest_device, dest_slot, capacity, pillar, raster_weights, weights, 1)
    blocks = gather(tokens, 1).reshape(1, group, block_count, -1, width)
    stream = attention_layer(blocks, order, 0, w_qkv, w_out, attn_gain, 2)
    share = scatter(mlp_partial(stream, 0, w_up, w_down, mlp_gain, group), 3)
    outgoing = pick(share.reshape(block_count, -1, width), index)
    outgoing = outgoing.reshape(ntok, -1, width)
    moved, arrived = move(outgoing, codes, 4)
    blocks = moved.reshape(ntok, group, capacity, -1, width)
    source = places(arrived, capacity, order)
    stream = attention_layer(blocks, source, 1, w_qkv, w_out, attn_gain, 5)
    partial = mlp_partial(stream, 1, w_up, w_down, mlp_gain, 1)[0]

    rep_rows = TR // members[1]
    full_width = TC * members[0]
    cells = extended_cells(lax.axis_index("tok"), members, rep_rows, full_width)
    pooled = pool(partial, pillar, cells)
    parts = pooled.reshape(group, -1, pooled.shape[1])
    edge = HALO * (TC + 2 * HALO)
    inside_kernel = members[0] > 1 and members[1] == 2 and ntok > 1 and edge % 8 == 0
    tile = scatter(parts, 6, edge if inside_kernel else 0)
    tile = tile.reshape(rep_rows + 2 * HALO, TC + 2 * HALO, -1)
    if not inside_kernel:
        tile = exchange_rows(tile, ntok, members[1])
    first = raster_cells(tile, depth_weight[0], point_weight[0], raster_gain[0])
    y = lax.axis_index(("tok", "rep")) * rep_rows - 1 + jnp.arange(rep_rows + 2)[:, None, None]
    x = lax.axis_index("col") * TC - 1 + jnp.arange(TC + 2)[None, :, None]
    inside = (y >= 0) & (y < TR * ntok) & (x >= 0) & (x < full_width)
    first = jnp.where(inside, first, 0.0)
    return raster_cells(first, depth_weight[1], point_weight[1], raster_gain[1])


def solution(mesh):
    placed = (
        P(("scene", "tok"), ("col", "rep")),
        P(None, None, None, ("col", "rep")),
        P(None, ("col", "rep"), None),
        P(None, None, ("col", "rep")),
        P(None, ("col", "rep"), None),
        P(),
        P(),
        P(("scene", "tok")),
        P(("scene", "tok")),
        P(("scene", "tok")),
        P(),
        P(),
        P(),
    )
    return jax.shard_map(
        on_device,
        mesh=mesh,
        in_specs=placed,
        out_specs=P(("scene", "tok", "rep"), "col", None),
        check_vma=False,
    )
```

```python
import functools
import math

import jax
import jax.numpy as jnp
from jax import lax
from jax.experimental import pallas as pl
from jax.experimental.pallas import tpu as pltpu
from jax.sharding import PartitionSpec as P

PATCH = 1024
TR = 16
TC = 16
HD = 16


MATMUL_PRECISION = lax.Precision.HIGH
EPSILON = 1e-05


def layer_norm(values, gain_row):
    average = jnp.mean(values, axis=-1, keepdims=True)
    centered = values - average
    variance = jnp.mean(centered * centered, axis=-1, keepdims=True)
    return centered * lax.rsqrt(variance + EPSILON) * gain_row


def split(values):
    high = values.astype(jnp.bfloat16)
    return high, (values - high.astype(jnp.float32)).astype(jnp.bfloat16)


def bdot(left, right, dims=(((1,), (0,)), ((), ()))):
    return lax.dot_general(left, right, dims, preferred_element_type=jnp.float32)


def dot3(left, right):
    lh, ll = left
    rh, rl = right
    return bdot(lh, rh) + bdot(lh, rl) + bdot(ll, rh)


def attention_kernel(share, source_ref, x_ref, gain_ref, w_ref, o_ref, out_ref, q_s, k_s, v_s, att_s):
    cols = w_ref.shape[-1]
    heads = cols // HD
    rows = out_ref.shape[0]
    chunk = att_s.shape[0]
    slots, each, block = x_ref.shape[1:4]
    first_block = pl.program_id(0) * (rows // block)

    def stream_rows(i):
        parts = []
        for n in range(chunk // block):
            at = source_ref[first_block + i * (chunk // block) + n]
            places = [x_ref[at // each, j, at % each] for j in range(slots)]
            parts.append(jnp.concatenate(places, axis=-1))
        return jnp.concatenate(parts, axis=0)

    lanes = q_s.shape[-1]

    r = lax.broadcasted_iota(jnp.int32, (cols, lanes), 0)
    c = lax.broadcasted_iota(jnp.int32, (cols, lanes), 1)
    lane = lax.broadcasted_iota(jnp.int32, (1, cols), 1)
    w = [split(w_ref[j]) for j in range(3)]
    for i in range(rows // chunk):
        at = pl.ds(i * chunk, chunk)
        normed = split(layer_norm(stream_rows(i), gain_ref[...]))
        qh, ql = split(dot3(normed, w[0]) * (HD ** (-0.5) * math.log2(math.e)))
        kh, kl = split(dot3(normed, w[1]))
        vh, vl = split(dot3(normed, w[2]))
        for h in range(heads):
            part = c // HD
            inside = (r // HD == h) & (r % HD == c % HD)
            first = (inside & ((part == 0) | (part == 1))).astype(jnp.bfloat16)
            third = (inside & (part == 2)).astype(jnp.bfloat16)
            outer = (inside & ((part == 0) | (part == 2))).astype(jnp.bfloat16)
            middle = (inside & (part == 1)).astype(jnp.bfloat16)
            q_s[h, at, :] = (bdot(qh, first) + bdot(ql, third)).astype(jnp.bfloat16)
            k_s[h, at, :] = (bdot(kh, outer) + bdot(kl, middle)).astype(jnp.bfloat16)
            own = lane // HD == h
            v_s[h, at, :cols] = jnp.where(own, vh.astype(jnp.float32), 0.0).astype(jnp.bfloat16)
            v_s[h, at, cols:] = jnp.where(own, vl.astype(jnp.float32), 1.0).astype(jnp.bfloat16)

    projection = split(o_ref[...])

    def query_rows(i, carry):
        at = pl.ds(pl.multiple_of(i * chunk, chunk), chunk)
        att_s[...] = jnp.zeros_like(att_s)

        def one_head(h, carry):
            scores = bdot(q_s[h, at, :], k_s[h], (((1,), (1,)), ((), ())))
            weights = jnp.exp2(scores - jnp.max(scores, axis=-1, keepdims=True))
            wh, wl = split(weights)
            sums = bdot(wh, v_s[h]) + bdot(wl, v_s[h])
            top, low = sums[:, :cols], sums[:, cols:]
            own = lane // HD == h
            total = jnp.max(jnp.where(own, 0.0, low), axis=-1, keepdims=True)
            att_s[...] += jnp.where(own, (top + low) / total, 0.0)
            return carry

        lax.fori_loop(0, heads, one_head, 0, unroll=4)
        out_ref[at, :] = dot3(split(att_s[...]), projection) + stream_rows(i) * share
        return carry

    lax.fori_loop(0, rows // chunk, query_rows, 0)


def attend(blocks, source, gain_row, weights, w_out, group):
    block, width = blocks.shape[3], blocks.shape[1] * blocks.shape[4]
    rows = source.shape[0] * block
    cols = weights.shape[-1]
    heads = cols // HD
    lanes = max(128, 3 * HD)
    return pl.pallas_call(
        functools.partial(attention_kernel, 1.0 / group),
        grid_spec=pltpu.PrefetchScalarGridSpec(
            num_scalar_prefetch=1,
            grid=(rows // PATCH,),
            in_specs=[
                pl.BlockSpec(blocks.shape, lambda i, source: (0, 0, 0, 0, 0)),
                pl.BlockSpec((1, width), lambda i, source: (0, 0)),
                pl.BlockSpec(weights.shape, lambda i, source: (0, 0, 0)),
                pl.BlockSpec(w_out.shape, lambda i, source: (0, 0)),
            ],
            out_specs=pl.BlockSpec((PATCH, width), lambda i, source: (i, 0)),
            scratch_shapes=[
                pltpu.VMEM((heads, PATCH, lanes), jnp.bfloat16),
                pltpu.VMEM((heads, PATCH, lanes), jnp.bfloat16),
                pltpu.VMEM((heads, PATCH, 2 * cols), jnp.bfloat16),
                pltpu.VMEM((256, cols), jnp.float32),
            ],
        ),
        out_shape=jax.ShapeDtypeStruct((rows, width), jnp.float32),
        compiler_params=pltpu.CompilerParams(vmem_limit_bytes=48 * 1024 * 1024),
        name="attend",
    )(source, blocks, gain_row[None, :], weights, w_out)


def matmul(left, right):
    return jnp.dot(left, right, precision=MATMUL_PRECISION, preferred_element_type=jnp.float32)


VMEM_LIMIT = 56 * 1024 * 1024
MESH = pl.DeviceIdType.MESH


def position():
    cols, reps = lax.axis_size("col"), lax.axis_size("rep")
    return cols, reps, lax.axis_index("col"), lax.axis_index("rep")


def greet(devices):
    barrier = pltpu.get_barrier_semaphore()
    for device in devices:
        pl.semaphore_signal(barrier, inc=1, device_id=device, device_id_type=MESH)
    pl.semaphore_wait(barrier, len(devices))


def remote(src, dst, send, recv, device):
    return pltpu.make_async_remote_copy(
        src_ref=src, dst_ref=dst, send_sem=send, recv_sem=recv, device_id=device, device_id_type=MESH
    )


def chunks_of(rows):
    for pieces in (8, 5, 4, 2):
        if rows % (8 * pieces) == 0:
            return pieces, rows // pieces
    return 1, rows


def gather_kernel(x_ref, out_ref, xs, xr, fs, fr, ps, pr, local):
    cols, reps, c, r = position()
    rows = x_ref.shape[0]
    pieces, size = chunks_of(rows)
    me = c * reps + r
    mate = {"col": c, "rep": 1 - r}
    others = [{"col": lax.rem(c + d, cols), "rep": r} for d in range(1, cols)]
    greet([mate] + others)
    across, onward = [], []
    for k in range(pieces):
        at = pl.ds(k * size, size)
        for d in range(1, cols):
            copy = remote(
                x_ref.at[at], out_ref.at[me, at], xs.at[d - 1, k], xr.at[d - 1, k], others[d - 1]
            )
            copy.start()
            across.append(copy)
    share = remote(x_ref, out_ref.at[me], ps, pr, mate)
    share.start()
    keep = pltpu.make_async_copy(x_ref, out_ref.at[me], local)
    keep.start()
    for k in range(pieces):
        at = pl.ds(k * size, size)
        for d in range(1, cols):
            across[k * (cols - 1) + d - 1].wait_recv()
            slot = lax.rem(c + cols - d, cols) * reps + r
            copy = remote(
                out_ref.at[slot, at], out_ref.at[slot, at], fs.at[d - 1, k], fr.at[d - 1, k], mate
            )
            copy.start()
            onward.append(copy)
    for copy in across:
        copy.wait_send()
    share.wait()
    keep.wait()
    for copy in onward:
        copy.wait()


def gather(block, collective_id):
    cols, reps = lax.axis_size("col"), lax.axis_size("rep")
    if reps != 2 or cols < 2:
        return lax.all_gather(block, ("col", "rep"), axis=0)
    pieces, _ = chunks_of(block.shape[0])
    dma = pltpu.SemaphoreType.DMA
    return pl.pallas_call(
        gather_kernel,
        out_shape=jax.ShapeDtypeStruct((cols * reps,) + block.shape, block.dtype),
        in_specs=[pl.BlockSpec(memory_space=pltpu.VMEM)],
        out_specs=pl.BlockSpec(memory_space=pltpu.VMEM),
        scratch_shapes=[dma((cols - 1, pieces))] * 4 + [dma, dma, dma],
        compiler_params=pltpu.CompilerParams(
            collective_id=collective_id, has_side_effects=True, vmem_limit_bytes=VMEM_LIMIT
        ),
        name="gather",
    )(block)


def scatter_kernel(edge, p_ref, out_ref, a_ref, s_ref, b_ref, a_s, a_r, b_s, b_r, *halo):
    cols, reps, c, r = position()
    rows = p_ref.shape[1]
    pieces, size = chunks_of(rows)
    mate = {"col": c, "rep": 1 - r}
    others = [{"col": lax.rem(c + d, cols), "rep": r} for d in range(1, cols)]
    greeted = [mate] + others
    if edge:
        ntok, t = lax.axis_size("tok"), lax.axis_index("tok")
        partner = {"tok": lax.rem(t + jnp.where(r == 0, ntok - 1, 1), ntok), "rep": 1 - r}
        greeted = greeted + [partner]
    greet(greeted)
    order = [(k, d) for k in range(pieces) for d in range(1, cols)]
    order += [(k, 0) for k in range(pieces)]
    near, far = {}, {}
    for k, d in order:
        at = pl.ds(k * size, size)
        slot = lax.rem(c + d, cols) * reps + 1 - r
        near[k, d] = remote(
            p_ref.at[slot, at], a_ref.at[d, at], a_s.at[d, k], a_r.at[d, k], mate
        )
        near[k, d].start()
    for k, d in order:
        at = pl.ds(k * size, size)
        slot = lax.rem(c + d, cols) * reps + r
        near[k, d].wait_recv()
        total = p_ref[slot, at] + a_ref[d, at]
        if d == 0:
            out_ref[at] = total
        else:
            s_ref[d - 1, at] = total
            far[k, d] = remote(
                s_ref.at[d - 1, at],
                b_ref.at[d - 1, at],
                b_s.at[d - 1, k],
                b_r.at[d - 1, k],
                others[d - 1],
            )
            far[k, d].start()
    for (k, d), copy in far.items():
        at = pl.ds(k * size, size)
        copy.wait_recv()
        out_ref[at] += b_ref[d - 1, at]
    if edge:
        h_ref, e_ref, h_s, h_r = halo
        inner = pl.multiple_of(jnp.where(r == 0, edge, rows - 2 * edge), 8)
        outer = pl.multiple_of(jnp.where(r == 0, 0, rows - edge), 8)
        e_ref[...] = out_ref[pl.ds(inner, edge)]
        copy = remote(e_ref, h_ref, h_s, h_r, partner)
        copy.start()
        copy.wait()
        wrapped = jnp.where(r == 0, t == 0, t == ntok - 1)
        out_ref[pl.ds(outer, edge)] = jnp.where(wrapped, 0.0, h_ref[...])
    for copy in list(near.values()) + list(far.values()):
        copy.wait_send()


def scatter(parts, collective_id, edge=0):
    cols, reps = lax.axis_size("col"), lax.axis_size("rep")
    if reps != 2 or cols < 2:
        return lax.psum_scatter(parts, ("col", "rep"), scatter_dimension=0)
    shape, kind = parts.shape[1:], parts.dtype
    pieces, _ = chunks_of(shape[0])
    dma = pltpu.SemaphoreType.DMA
    return pl.pallas_call(
        functools.partial(scatter_kernel, edge),
        out_shape=jax.ShapeDtypeStruct(shape, kind),
        in_specs=[pl.BlockSpec(memory_space=pltpu.VMEM)],
        out_specs=pl.BlockSpec(memory_space=pltpu.VMEM),
        scratch_shapes=[
            pltpu.VMEM((cols,) + shape, kind),
            pltpu.VMEM((cols - 1,) + shape, kind),
            pltpu.VMEM((cols - 1,) + shape, kind),
            dma((cols, pieces)),
            dma((cols, pieces)),
            dma((cols - 1, pieces)),
            dma((cols - 1, pieces)),
        ]
        + ([pltpu.VMEM((edge, shape[1]), kind)] * 2 + [dma, dma] if edge else []),
        compiler_params=pltpu.CompilerParams(
            collective_id=collective_id, has_side_effects=True, vmem_limit_bytes=VMEM_LIMIT
        ),
        name="scatter",
    )(parts)


def total_kernel(
    p_ref, out_ref, a_ref, s_ref, b_ref, a_s, a_r, b_s, b_r, xs, xr, fs, fr, ps, pr
):
    cols, reps, c, r = position()
    rows = p_ref.shape[1]
    pieces, size = chunks_of(rows)
    me = c * reps + r
    mate = {"col": c, "rep": 1 - r}
    others = [{"col": lax.rem(c + d, cols), "rep": r} for d in range(1, cols)]
    greet([mate] + others)
    order = [(k, d) for k in range(pieces) for d in range(1, cols)]
    order += [(k, 0) for k in range(pieces)]
    near, far, across, share, onward = {}, {}, {}, {}, {}
    for k, d in order:
        at = pl.ds(k * size, size)
        slot = lax.rem(c + d, cols) * reps + 1 - r
        near[k, d] = remote(
            p_ref.at[slot, at], a_ref.at[d, at], a_s.at[d, k], a_r.at[d, k], mate
        )
        near[k, d].start()
    for k, d in order:
        if d == 0:
            continue
        at = pl.ds(k * size, size)
        slot = lax.rem(c + d, cols) * reps + r
        near[k, d].wait_recv()
        s_ref[d - 1, at] = p_ref[slot, at] + a_ref[d, at]
        far[k, d] = remote(
            s_ref.at[d - 1, at], b_ref.at[d - 1, at], b_s.at[d - 1, k], b_r.at[d - 1, k], others[d - 1]
        )
        far[k, d].start()
    for k in range(pieces):
        at = pl.ds(k * size, size)
        near[k, 0].wait_recv()
        total = p_ref[me, at] + a_ref[0, at]
        for d in range(1, cols):
            far[k, d].wait_recv()
            total = total + b_ref[d - 1, at]
        out_ref[me, at] = total
        for d in range(1, cols):
            across[k, d] = remote(
                out_ref.at[me, at], out_ref.at[me, at], xs.at[d - 1, k], xr.at[d - 1, k], others[d - 1]
            )
            across[k, d].start()
        share[k] = remote(out_ref.at[me, at], out_ref.at[me, at], ps.at[k], pr.at[k], mate)
        share[k].start()
    for (k, d), copy in across.items():
        at = pl.ds(k * size, size)
        copy.wait_recv()
        slot = lax.rem(c + cols - d, cols) * reps + r
        onward[k, d] = remote(
            out_ref.at[slot, at], out_ref.at[slot, at], fs.at[d - 1, k], fr.at[d - 1, k], mate
        )
        onward[k, d].start()
    for copies in (near, far, across):
        for copy in copies.values():
            copy.wait_send()
    for copies in (share, onward):
        for copy in copies.values():
            copy.wait()


def total(parts, collective_id):
    cols, reps = lax.axis_size("col"), lax.axis_size("rep")
    if reps != 2 or cols < 2:
        return lax.psum(parts, ("col", "rep"))
    shape, kind = parts.shape[1:], parts.dtype
    pieces, _ = chunks_of(shape[0])
    dma = pltpu.SemaphoreType.DMA
    return pl.pallas_call(
        total_kernel,
        out_shape=jax.ShapeDtypeStruct(parts.shape, kind),
        in_specs=[pl.BlockSpec(memory_space=pltpu.VMEM)],
        out_specs=pl.BlockSpec(memory_space=pltpu.VMEM),
        scratch_shapes=[
            pltpu.VMEM((cols,) + shape, kind),
            pltpu.VMEM((cols - 1,) + shape, kind),
            pltpu.VMEM((cols - 1,) + shape, kind),
            dma((cols, pieces)),
            dma((cols, pieces)),
        ]
        + [dma((cols - 1, pieces))] * 6
        + [dma((pieces,))] * 2,
        compiler_params=pltpu.CompilerParams(
            collective_id=collective_id, has_side_effects=True, vmem_limit_bytes=VMEM_LIMIT
        ),
        name="total",
    )(parts)


def move_kernel(o_ref, code_ref, out_ref, arrived_ref, zs, zr, cs, cr, xs, xr, fs, fr, ps, pr, local):
    cols, reps, c, r = position()
    ntok, t = lax.axis_size("tok"), lax.axis_index("tok")
    me = c * reps + r
    mate = {"col": c, "rep": 1 - r}
    others = [{"col": lax.rem(c + d, cols), "rep": r} for d in range(1, cols)]
    peers = [{"tok": lax.rem(t + e, ntok)} for e in range(1, ntok)]
    greet([mate] + others + peers)
    along, codes, across, share, onward = [], [], {}, [], []
    for e in range(1, ntok):
        target = lax.rem(t + e, ntok)
        copy = remote(o_ref.at[target], out_ref.at[t, me], zs.at[e - 1], zr.at[e - 1], peers[e - 1])
        copy.start()
        along.append(copy)
        copy = remote(
            code_ref.at[target], arrived_ref.at[t], cs.at[e - 1], cr.at[e - 1], peers[e - 1]
        )
        copy.start()
        codes.append(copy)
    keep = pltpu.make_async_copy(o_ref.at[t], out_ref.at[t, me], local.at[0])
    keep.start()
    keep_code = pltpu.make_async_copy(code_ref.at[t], arrived_ref.at[t], local.at[1])
    keep_code.start()

    def hand_on(e):
        u = lax.rem(t + ntok - e, ntok)
        for d in range(1, cols):
            across[e, d].wait_recv()
            slot = lax.rem(c + cols - d, cols) * reps + r
            copy = remote(
                out_ref.at[u, slot], out_ref.at[u, slot], fs.at[e, d - 1], fr.at[e, d - 1], mate
            )
            copy.start()
            onward.append(copy)

    for e in range(ntok):
        u = lax.rem(t + ntok - e, ntok)
        if e:
            along[e - 1].wait_recv()
        origin = out_ref.at[u, me] if e else o_ref.at[t]
        for d in range(1, cols):
            across[e, d] = remote(
                origin, out_ref.at[u, me], xs.at[e, d - 1], xr.at[e, d - 1], others[d - 1]
            )
            across[e, d].start()
        copy = remote(origin, out_ref.at[u, me], ps.at[e], pr.at[e], mate)
        copy.start()
        share.append(copy)
        if e:
            hand_on(e - 1)
    hand_on(ntok - 1)
    keep.wait()
    keep_code.wait()
    for copy in along + list(across.values()):
        copy.wait_send()
    for copy in codes + share + onward:
        copy.wait()


def move(outgoing, codes, collective_id):
    cols, reps, ntok = lax.axis_size("col"), lax.axis_size("rep"), lax.axis_size("tok")
    if reps != 2 or cols < 2 or ntok < 2:
        incoming = lax.all_to_all(outgoing, "tok", split_axis=0, concat_axis=0, tiled=True)
        arrived = lax.all_to_all(codes, "tok", split_axis=0, concat_axis=0, tiled=True)
        return lax.all_gather(incoming, ("col", "rep"), axis=1), arrived
    dma = pltpu.SemaphoreType.DMA
    shape = (ntok, cols * reps) + outgoing.shape[1:]
    return pl.pallas_call(
        move_kernel,
        out_shape=(
            jax.ShapeDtypeStruct(shape, outgoing.dtype),
            jax.ShapeDtypeStruct(codes.shape, codes.dtype),
        ),
        in_specs=[pl.BlockSpec(memory_space=pltpu.VMEM)] * 2,
        out_specs=[pl.BlockSpec(memory_space=pltpu.VMEM)] * 2,
        scratch_shapes=[dma((ntok - 1,))] * 4
        + [dma((ntok, cols - 1))] * 4
        + [dma((ntok,))] * 2
        + [dma((2,))],
        compiler_params=pltpu.CompilerParams(
            collective_id=collective_id, has_side_effects=True, vmem_limit_bytes=VMEM_LIMIT
        ),
        name="move",
    )(outgoing, codes)


def pick_kernel(index_ref, x_ref, out_ref):
    for j in range(out_ref.shape[0]):
        out_ref[j] = x_ref[index_ref[j]]


def pick(blocks, index):
    return pl.pallas_call(
        pick_kernel,
        out_shape=jax.ShapeDtypeStruct(index.shape + blocks.shape[1:], blocks.dtype),
        in_specs=[pl.BlockSpec(memory_space=pltpu.SMEM), pl.BlockSpec(memory_space=pltpu.VMEM)],
        out_specs=pl.BlockSpec(memory_space=pltpu.VMEM),
        name="pick",
    )(index, blocks)


def attention_layer(blocks, source, layer, w_qkv, w_out, attn_gain, collective_id):
    group = blocks.shape[1]
    terms = attend(blocks, source, attn_gain[layer], w_qkv[layer], w_out[layer], group)
    rows, width = terms.shape
    return total(terms.reshape(group, rows // group, width), collective_id).reshape(rows, width)


def mlp_kernel(x_ref, gain_ref, up_ref, down_ref, share, out_ref):
    x = x_ref[...]
    hidden = dot3(split(layer_norm(x, gain_ref[...])), split(up_ref[...]))
    hidden = 0.5 * hidden * (1.0 + lax.erf(hidden * (0.5**0.5)))
    total = dot3(split(hidden), split(down_ref[...])) + x * share
    width = out_ref.shape[-1]
    for j in range(out_ref.shape[0]):
        out_ref[j] = total[:, j * width : (j + 1) * width]


def mlp_partial(stream, layer, w_up, w_down, mlp_gain, slots):
    rows, width = stream.shape
    tile = min(256, rows)
    hidden = w_up.shape[-1]
    group = lax.axis_size("col") * lax.axis_size("rep")

    def kernel(x_ref, gain_ref, up_ref, down_ref, out_ref):
        mlp_kernel(x_ref, gain_ref, up_ref, down_ref, 1.0 / group, out_ref)

    return pl.pallas_call(
        kernel,
        grid=(rows // tile,),
        in_specs=[
            pl.BlockSpec((tile, width), lambda i: (i, 0)),
            pl.BlockSpec((1, width), lambda i: (0, 0)),
            pl.BlockSpec((width, hidden), lambda i: (0, 0)),
            pl.BlockSpec((hidden, width), lambda i: (0, 0)),
        ],
        out_specs=pl.BlockSpec((slots, tile, width // slots), lambda i: (0, i, 0)),
        out_shape=jax.ShapeDtypeStruct((slots, rows, width // slots), jnp.float32),
        compiler_params=pltpu.CompilerParams(vmem_limit_bytes=48 * 1024 * 1024),
        name="mlp",
    )(stream, mlp_gain[layer][None, :], w_up[layer], w_down[layer])


def gelu(values):
    return 0.5 * values * (1.0 + lax.erf(values * (0.5**0.5)))


def piece(i, size):
    return pl.ds(pl.multiple_of(i * size, size), size)


class Layer:
    def __init__(self, layer, refs, heads, chunk):
        self.__dict__.update(refs)
        self.layer, self.heads, self.chunk = layer, heads, chunk
        self.tag = "_sem" + str(layer)
        self.cols, self.reps, self.c, self.r = position()
        self.ntok, self.t = lax.axis_size("tok"), lax.axis_index("tok")
        self.me = self.c * self.reps + self.r
        self.mate, self.peer = {"rep": 1 - self.r}, {"col": 1 - self.c}
        self.peers = [{"tok": lax.rem(self.t + e, self.ntok)} for e in range(1, self.ntok)]
        self.rows, self.width = self.a_s.shape
        self.lanes = self.q_s.shape[-1] // 2
        self.n = self.rows // chunk
        self.part = chunk // 2
        self.block = self.y_s.shape[1]
        self.cap = self.o_s.shape[1]

    def sent(self, kind, i, src, dst, device):
        sem = getattr(self, kind + self.tag)
        return remote(src, dst, sem.at[0, i], sem.at[1, i], device)

    def load_weights(self):
        pairs = (
            (self.wqkv_ref, self.wqkv_f), (self.wo_ref, self.wo_f),
            (self.wu_ref, self.wu_f), (self.wd_ref, self.wd_f),
        )
        self.loads = [
            pltpu.make_async_copy(src.at[self.layer], dst.at[self.layer], self.wsem.at[self.layer, j])
            for j, (src, dst) in enumerate(pairs)
        ]
        for load in self.loads:
            load.start()

    def split_weights(self):
        layer = self.layer
        self.loads[0].wait()
        for m in range(3):
            self.wqkv_s[layer, 0, m], self.wqkv_s[layer, 1, m] = split(self.wqkv_f[layer, m])
        rest = ((self.wo_f, self.wo_s), (self.wu_f, self.wu_s), (self.wd_f, self.wd_s))
        for load, (src, dst) in zip(self.loads[1:], rest):
            load.wait()
            dst[layer, 0], dst[layer, 1] = split(src[layer])

    def pair(self, ref):
        return ref[self.layer, 0], ref[self.layer, 1]

    def project(self, stream):
        normed = split(layer_norm(stream, self.ga_ref[pl.ds(self.layer, 1)]))
        return [dot3(normed, (self.wqkv_s[self.layer, 0, m], self.wqkv_s[self.layer, 1, m])) for m in range(3)]

    def pack(self, at, q, k, v):
        lanes = self.lanes
        half_lanes = lanes // 2
        lane = lax.broadcasted_iota(jnp.int32, (1, lanes), 1)
        low = lane < half_lanes
        qh, ql = split(q * (HD ** (-0.5) * math.log2(math.e)))
        kh, kl = [part.astype(jnp.float32) for part in split(k)]
        vh, vl = [part.astype(jnp.float32) for part in split(v)]
        qf, qlf = qh.astype(jnp.float32), ql.astype(jnp.float32)
        q_s, k_s, v_s = self.q_s, self.k_s, self.v_s

        def roll(values):
            return pltpu.roll(values, half_lanes, 1)

        q_s[0, at, :lanes] = qh
        q_s[1, at, :lanes] = qh
        q_s[0, at, lanes:] = jnp.where(low, qf, roll(qlf)).astype(jnp.bfloat16)
        q_s[1, at, lanes:] = jnp.where(low, roll(qf), qlf).astype(jnp.bfloat16)
        k_s[0, at, :lanes] = kh.astype(jnp.bfloat16)
        k_s[1, at, :lanes] = kh.astype(jnp.bfloat16)
        k_s[0, at, lanes:] = jnp.where(low, kl, roll(kh)).astype(jnp.bfloat16)
        k_s[1, at, lanes:] = jnp.where(low, roll(kl), kh).astype(jnp.bfloat16)
        v_s[0, at, :lanes] = vh.astype(jnp.bfloat16)
        v_s[1, at, :lanes] = vh.astype(jnp.bfloat16)
        v_s[0, at, lanes:] = jnp.where(low, vl, 1.0).astype(jnp.bfloat16)
        v_s[1, at, lanes:] = jnp.where(low, 1.0, vl).astype(jnp.bfloat16)

    def near(self, i):
        half = self.chunk // 2
        start = pl.multiple_of(i * self.chunk + (1 - self.r) * half, half)
        return self.sent("near", i, self.p_s.at[pl.ds(start, half)], self.n1_s.at[piece(i, half)], self.mate)

    def far(self, i):
        at = piece(i, self.chunk // 2)
        return self.sent("far", i, self.s1_s.at[at], self.f1_s.at[at], self.peer)

    def own_half(self, i):
        half = self.chunk // 2
        return pl.ds(pl.multiple_of(i * self.chunk + self.r * half, half), half)

    def share(self, i):
        at = self.own_half(i)
        return self.sent("share", i, self.a_s.at[at], self.a_s.at[at], self.mate)

    def attention(self, k):
        lanes, half_heads, chunk = self.lanes, self.heads // 2, self.chunk
        wide = lax.broadcasted_iota(jnp.int32, (1, 2 * lanes), 1)
        lane = lax.broadcasted_iota(jnp.int32, (1, lanes), 1)
        i, half = k // 2, k % 2
        query = self.q_s[half, piece(i, chunk), :]
        queries = []
        for m in range(half_heads):
            first = (wide < lanes) & (wide // HD == half * half_heads + m)
            second = (wide >= lanes) & ((wide % (lanes // 2)) // HD == m)
            mask = jnp.where(first | second, 1.0, 0.0).astype(jnp.bfloat16)
            queries.append(query * mask)
        stacked = jnp.concatenate(queries, axis=0)
        scores = bdot(stacked, self.k_s[half], (((1,), (1,)), ((), ())))
        weights = jnp.exp2(scores - jnp.max(scores, axis=-1, keepdims=True))
        sums = bdot(jnp.concatenate(split(weights), axis=0), self.v_s[half])
        sums = sums[: half_heads * chunk] + sums[half_heads * chunk :]
        total = jnp.zeros((chunk, lanes), jnp.float32)
        for m in range(half_heads):
            own = sums[m * chunk : (m + 1) * chunk]
            top, low = own[:, :lanes], own[:, lanes:]
            ratio = (top + low) / pltpu.roll(low, lanes // 2, 1)
            total += jnp.where(lane // HD == half * half_heads + m, ratio, 0.0)
        self.att_s[half] = total

    def finish(self, i):
        projection = self.pair(self.wo_s)
        self.p_s[piece(i, self.chunk)] = dot3(split(self.att_s[0] + self.att_s[1]), projection)
        self.near(i).start()

    def reduce_near(self, i):
        self.near(i).wait_recv()
        at = piece(i, self.chunk // 2)
        self.s1_s[at] = self.p_s[self.own_half(i)] + self.n1_s[at]
        self.far(i).start()

    def reduce_far(self, i):
        self.far(i).wait_recv()
        half = self.chunk // 2
        at = piece(i, half)
        stream = self.stream_rows(i * self.chunk + self.r * half, half)
        self.a_s[self.own_half(i)] = (self.s1_s[at] + self.f1_s[at]) + stream
        self.share(i).start()

    def mlp(self, x):
        normed = split(layer_norm(x, self.gm_ref[pl.ds(self.layer, 1)]))
        hidden = gelu(dot3(normed, self.pair(self.wu_s)))
        return dot3(split(hidden), self.pair(self.wd_s))

    def run(self, stages):
        n = self.n

        def tick(k, carry):
            @pl.when(k < 2 * n)
            def _():
                self.attention(k)

            for offset, stage in stages:
                @pl.when((k >= offset) & (k < offset + 2 * n) & ((k - offset) % 2 == 0))
                def _(offset=offset, stage=stage):
                    stage((k - offset) // 2)

            return carry

        lax.fori_loop(0, 2 * n + max(offset for offset, _ in stages) - 1, tick, 0)


class First(Layer):
    def stream_rows(self, start, count):
        at = pl.ds(pl.multiple_of(start, count), count)
        return jnp.concatenate([self.g0_s[j, at] for j in range(self.cols * self.reps)], axis=-1)

    def across(self, i):
        at = piece(i, self.part)
        return self.sent("across", i, self.tokens_ref.at[at], self.g0_s.at[self.me, at], self.peer)

    def over(self, i):
        at = piece(i, self.part)
        return self.sent("over", i, self.tokens_ref.at[at], self.g0_s.at[self.me, at], self.mate)

    def relay(self, i):
        at = piece(i, self.part)
        slot = (1 - self.c) * self.reps + self.r
        return self.sent("relay", i, self.g0_s.at[slot, at], self.g0_s.at[slot, at], self.mate)

    def code(self, e):
        target = {"tok": lax.rem(self.t + e, self.ntok)}
        return self.sent("code", e, self.code_s, self.arrived_s.at[self.t], target)

    def route(self):
        device = self.dd_ref[...].astype(jnp.float32)
        slot = self.ds_ref[...].astype(jnp.float32)
        count = device.shape[1]
        row = lax.broadcasted_iota(jnp.int32, (count, count), 0)
        col = lax.broadcasted_iota(jnp.int32, (count, count), 1)

        def upright(values):
            return jnp.sum(jnp.where(row == col, values, 0.0), axis=1, keepdims=True)

        devices, slots = upright(device), upright(slot)
        earlier = jnp.where((devices == device) & (col < row), 1.0, 0.0)
        place = devices * self.cap + jnp.sum(earlier, axis=1, keepdims=True)
        at = lax.broadcasted_iota(jnp.int32, (count, 128), 1).astype(jnp.float32)
        block = lax.broadcasted_iota(jnp.int32, (count, 128), 0).astype(jnp.float32)
        index = jnp.sum(jnp.where(place == at, block, 0.0), axis=0, keepdims=True)
        code = jnp.sum(jnp.where(place == at, slots + 1.0, 0.0), axis=0, keepdims=True)
        self.index_v[...] = index.astype(jnp.int32)
        self.code_s[...] = jnp.broadcast_to(code, self.code_s.shape)
        self.arrived_s[self.t] = jnp.broadcast_to(code, self.code_s.shape)

    def locate(self):
        row = lax.broadcasted_iota(jnp.int32, (128, 128), 0)
        col = lax.broadcasted_iota(jnp.int32, (128, 128), 1)
        first = self.t * self.cap
        valid = (row >= first) & (row < first + self.cap)
        source = jnp.zeros((1, 128), jnp.float32)
        for u in range(self.ntok):
            codes = self.arrived_s[u][:1]
            upright = jnp.sum(jnp.where(row == col, codes, 0.0), axis=1, keepdims=True)
            found = valid & (upright == (col + 1).astype(jnp.float32))
            entry = (row - first + u * self.cap).astype(jnp.float32)
            source += jnp.sum(jnp.where(found, entry, 0.0), axis=0, keepdims=True)
        self.source_v[...] = source.astype(jnp.int32)

    def near2(self, i):
        at = piece(i, self.chunk)
        return self.sent("near2", i, self.m_s.at[1 - self.r, :, at], self.n2_s.at[:, at], self.mate)

    def far2(self, i):
        at = piece(i, self.chunk)
        return self.sent("far2", i, self.s2_s.at[at], self.f2_s.at[at], self.peer)

    def feed(self, i):
        self.share(i).wait_recv()
        at = piece(i, self.chunk)
        total = self.mlp(self.a_s[at])
        for j in range(self.cols * self.reps):
            self.m_s[j % self.reps, j // self.reps, at] = total[:, j * self.lanes : (j + 1) * self.lanes]
        self.near2(i).start()

    def scatter_near(self, i):
        self.near2(i).wait_recv()
        at = piece(i, self.chunk)
        self.s2_s[at] = self.m_s[self.r, 1 - self.c, at] + self.n2_s[1 - self.c, at]
        self.far2(i).start()

    def scatter_far(self, i):
        self.far2(i).wait_recv()
        at = piece(i, self.chunk)
        own = self.a_s[at, piece(self.me, self.lanes)]
        total = (self.m_s[self.r, self.c, at] + self.n2_s[self.c, at]) + self.f2_s[at]
        count = self.chunk // self.block
        self.y_s[piece(i, count)] = (total + own).reshape(count, self.block, self.lanes)

    def body(self, second):
        n = self.rows // self.part
        for i in range(n):
            self.across(i).start()
        for i in range(n):
            self.over(i).start()
        keep = pltpu.make_async_copy(self.tokens_ref, self.g0_s.at[self.me], self.tsem.at[0])
        keep.start()
        self.route()
        table = pltpu.make_async_copy(self.index_v, self.index_m, self.tsem.at[1])
        table.start()
        self.split_weights()
        for e in range(1, self.ntok):
            self.code(e).start()
        second.split_weights()
        second.split_points()
        self.pool_s[...] = jnp.zeros(self.pool_s.shape, jnp.float32)
        keep.wait()
        table.wait()

        def step(i, carry):
            @pl.when(i < n)
            def _():
                self.across(i).wait_recv()
                self.relay(i).start()

            @pl.when(i > 0)
            def _():
                self.over(i - 1).wait_recv()
                self.relay(i - 1).wait_recv()
                stream = self.stream_rows((i - 1) * self.part, self.part)
                self.pack(piece(i - 1, self.part), *self.project(stream))

            return carry

        lax.fori_loop(0, n + 1, step, 0)
        self.run(
            [
                (1, self.finish), (2, self.reduce_near), (10, self.scatter_near),
                (7, self.reduce_far), (8, self.feed), (15, self.scatter_far),
            ]
        )
        for copy in (self.near, self.far, self.share, self.near2, self.far2):
            for i in range(self.n):
                copy(i).wait_send()
        for copy in (self.across, self.over, self.relay):
            for i in range(n):
                copy(i).wait_send()

    def tables(self):
        for e in range(1, self.ntok):
            self.code(e).wait()
        self.locate()
        table = pltpu.make_async_copy(self.source_v, self.source_m, self.tsem.at[2])
        table.start()
        return table


class Second(Layer):
    def entry(self, k):
        return jnp.clip(self.source_m[0, k], 0, self.ntok * self.cap - 1)

    def chosen(self, u, j):
        return jnp.clip(self.index_m[0, u * self.cap + j], 0, self.y_s.shape[0] - 1)

    def stream_rows(self, start, count):
        parts = []
        for m in range(count // self.block):
            at = self.entry(start // self.block + m)
            places = [self.g_s[at // self.cap, j, at % self.cap] for j in range(self.cols * self.reps)]
            parts.append(jnp.concatenate(places, axis=-1))
        return jnp.concatenate(parts, axis=0)

    def along(self, e, j):
        target = lax.rem(self.t + e, self.ntok)
        return self.sent(
            "along", e * self.cap + j, self.o_s.at[target, j], self.g_s.at[self.t, self.me, j],
            {"tok": target},
        )

    def origin(self, e):
        return lax.rem(self.t + self.ntok - e, self.ntok)

    def placed(self, kind, e, j, slot, device):
        ref = self.g_s.at[self.origin(e), slot, j]
        return self.sent(kind, e * self.cap + j, ref, ref, device)

    def across(self, e, j):
        return self.placed("across", e, j, self.me, self.peer)

    def over(self, e, j):
        return self.placed("over", e, j, self.me, self.mate)

    def relay(self, e, j):
        return self.placed("relay", e, j, (1 - self.c) * self.reps + self.r, self.mate)

    def arrive(self, j):
        for e in self.order[1:]:
            self.along(e, j).wait_recv()
            self.across(e, j).start()
            self.over(e, j).start()

    def hand(self, j):
        for e in self.order:
            self.across(e, j).wait_recv()
            self.relay(e, j).start()

    def take(self, j):
        parts = []
        for e in self.order:
            self.over(e, j).wait_recv()
            self.relay(e, j).wait_recv()
            places = [self.g_s[self.origin(e), k, j] for k in range(self.cols * self.reps)]
            parts.append(jnp.concatenate(places, axis=-1))
        for m, values in enumerate(self.project(jnp.concatenate(parts, axis=0))):
            for at, e in enumerate(self.order):
                entry = self.origin(e) * self.cap + j
                self.raw_s[m, entry] = values[at * self.block : (at + 1) * self.block]

    def move(self, first):
        self.order = [0]
        for e in range(1, self.ntok // 2 + 1):
            self.order += [e] + ([self.ntok - e] if self.ntok - e != e else [])
        for j in range(self.cap):
            for u in range(self.ntok):
                self.o_s[u, j] = self.y_s[self.chosen(u, j)]
            for e in self.order[1:]:
                self.along(e, j).start()
        for j in range(self.cap):
            self.g_s[self.t, self.me, j] = self.y_s[self.chosen(self.t, j)]
            self.across(0, j).start()
            self.over(0, j).start()
        table = first.tables()
        for j in range(self.cap):
            self.arrive(j)
            if j >= 1:
                self.hand(j - 1)
            if j >= 2:
                self.take(j - 2)
        self.take(self.cap - 2)
        self.hand(self.cap - 1)
        self.take(self.cap - 1)
        table.wait()

        def step(i, carry):
            def row(m):
                each = self.chunk // self.block
                blocks = [self.raw_s[m, self.entry(i * each + k)] for k in range(each)]
                return jnp.concatenate(blocks, axis=0)

            self.pack(piece(i, self.chunk), row(0), row(1), row(2))
            return carry

        lax.fori_loop(0, self.n, step, 0)

    def load_points(self):
        self.point = pltpu.make_async_copy(self.pw_ref, self.pw_f, self.tsem.at[3])
        self.point.start()

    def split_points(self):
        self.point.wait()

        def step(k, carry):
            at = piece(k, 64)
            for l in range(2):
                self.pw_s[0, l, at], self.pw_s[1, l, at] = split(self.pw_f[l, at])
            return carry

        lax.fori_loop(0, self.width // 64, step, 0)

    def cell_ids(self):
        count = self.pool_s.shape[0]
        p = lax.broadcasted_iota(jnp.int32, (count, 1), 0)
        wide = TC + 2 * HALO
        row = ((p.astype(jnp.float32) + 0.5) * (1.0 / wide)).astype(jnp.int32)
        col = row // TR
        x = col * TC - HALO + (p - row * wide)
        full = TC * self.cols
        y = row - col * TR
        return jnp.where((x >= 0) & (x < full), (self.t * TR + y) * full + x, -2)

    def feed(self, i):
        self.share(i).wait_recv()
        at = piece(i, self.chunk)
        x = self.a_s[at]
        high, low = split(self.mlp(x) + x * (1.0 / (self.cols * self.reps)))
        chosen = jnp.where(self.cell_ids() == self.pillar_ref[:, at], 1.0, 0.0).astype(jnp.bfloat16)
        self.pool_s[...] += bdot(chosen, high) + bdot(chosen, low)

    def tile_part(self, c, r, k):
        cells = self.pool_s.shape[0] // (self.cols * self.reps)
        start = (c * self.reps + r) * cells + k * self.edge
        return pl.ds(pl.multiple_of(start, 8), self.edge)

    def near3(self, w, k):
        c = self.c if w else 1 - self.c
        return self.sent(
            "near3", w * self.pieces + k, self.pool_s.at[self.tile_part(c, 1 - self.r, k)],
            self.n3_s.at[w, k], self.mate,
        )

    def far3(self, k):
        return self.sent("far3", k, self.s3_s.at[k], self.f3_s.at[k], self.peer)

    def inner(self):
        start = jnp.where(self.r == 0, self.pieces * self.edge, self.edge)
        src = self.tile_s.at[pl.ds(pl.multiple_of(start, 8), self.edge)]
        return self.sent("halo", 0, src, self.h_s.at[0], self.mate)

    def outer(self):
        start = jnp.where(self.r == 0, self.edge, self.pieces * self.edge)
        src = self.tile_s.at[pl.ds(pl.multiple_of(start, 8), self.edge)]
        return self.sent("halo", 1, src, self.h_s.at[1], self.partner)

    def scatter(self):
        order = [0, self.pieces - 1] + list(range(1, self.pieces - 1))
        for w in range(2):
            for k in order:
                self.near3(w, k).start()
        for k in order:
            self.near3(0, k).wait_recv()
            self.s3_s[k] = self.pool_s[self.tile_part(1 - self.c, self.r, k)] + self.n3_s[0, k]
            self.far3(k).start()
        for at, k in enumerate(order):
            self.near3(1, k).wait_recv()
            self.far3(k).wait_recv()
            own = self.pool_s[self.tile_part(self.c, self.r, k)] + self.n3_s[1, k]
            self.tile_s[pl.ds((k + 1) * self.edge, self.edge)] = own + self.f3_s[k]
            if at == 1:
                self.inner().start()
                self.outer().start()
        self.inner().wait()
        self.outer().wait()
        wrapped = jnp.where(self.r == 0, self.t == 0, self.t == self.ntok - 1)
        beyond = jnp.where(wrapped, 0.0, self.h_s[1])
        within = self.h_s[0]
        self.tile_s[: self.edge] = jnp.where(self.r == 0, beyond, within)
        self.tile_s[(self.pieces + 1) * self.edge :] = jnp.where(self.r == 0, within, beyond)

    def raster(self):
        wide = TC + 2 * HALO
        rows = self.tile_s.shape[0] // wide
        pad = (self.flat_s.shape[0] - rows * wide) // 2
        self.flat_s[:pad] = jnp.zeros((pad, self.width), jnp.float32)
        self.flat_s[pad + rows * wide :] = jnp.zeros((pad, self.width), jnp.float32)
        for l in range(2):
            old = pl.ds(l * wide, (rows - 2 * l) * wide)
            start, count = (l + 1) * wide, (rows - 2 * l - 2) * wide
            cells = self.tile_s[old]
            square = jnp.mean(cells * cells, axis=-1, keepdims=True)
            gain = self.rg_ref[pl.ds(l, 1)]
            self.flat_s[pl.ds(pad + l * wide, (rows - 2 * l) * wide)] = (
                cells * lax.rsqrt(square + EPSILON) * gain
            )
            mixed = jnp.zeros((count, self.width), jnp.float32)
            for a in range(3):
                for b in range(3):
                    shift = pad + start + (a - 1) * wide + b - 1
                    mixed = mixed + self.flat_s[pl.ds(shift, count)] * self.dw_ref[a, b, pl.ds(l, 1)]
            both = dot3(split(mixed), (self.pw_s[0, l], self.pw_s[1, l]))
            centre = self.tile_s[pl.ds(start, count)]
            result = centre + both[:, : self.width] * jax.nn.sigmoid(both[:, self.width :])
            if l == 0:
                p = lax.broadcasted_iota(jnp.int32, (count, 1), 0) + start
                row = ((p.astype(jnp.float32) + 0.5) * (1.0 / wide)).astype(jnp.int32)
                y = (self.t * self.reps + self.r) * (rows - 2 * HALO) - HALO + row
                x = self.c * TC - HALO + (p - row * wide)
                inside = (y >= 0) & (y < TR * self.ntok) & (x >= 0) & (x < TC * self.cols)
                result = jnp.where(inside, result, 0.0)
            self.tile_s[pl.ds(start, count)] = result
        for y in range(rows - 2 * HALO):
            self.out_ref[y] = self.tile_s[pl.ds((y + HALO) * wide + HALO, TC)]

    def body(self, first):
        self.pieces, self.edge = self.s3_s.shape[:2]
        self.move(first)
        self.run([(1, self.finish), (2, self.reduce_near), (8, self.feed), (6, self.reduce_far)])
        self.scatter()
        self.raster()
        for copy in (self.near, self.far, self.share):
            for i in range(self.n):
                copy(i).wait_send()
        for j in range(self.cap):
            for e in range(self.ntok):
                if e:
                    self.along(e, j).wait_send()
                for copy in (self.across, self.over, self.relay):
                    copy(e, j).wait_send()
        for k in range(self.pieces):
            self.near3(0, k).wait_send()
            self.near3(1, k).wait_send()
            self.far3(k).wait_send()


def capacity_of(count, peers):
    return max(2, (count + peers - 4) // (peers - 1))


def both_layers(tokens, dest_device, dest_slot, cap, pillar, raster_weights, weights, collective_id):
    w_qkv, w_out, w_up, w_down, attn_gain, mlp_gain = weights
    depth_weight, point_weight, raster_gain = raster_weights
    cols, reps, ntok = lax.axis_size("col"), lax.axis_size("rep"), lax.axis_size("tok")
    rows, lanes = tokens.shape
    width, hidden, count = w_qkv.shape[-2], w_up.shape[-1], dest_device.shape[0]
    block, heads, chunk = rows // count, lanes // HD, min(256, rows)
    n = rows // chunk
    wide, rep_rows = TC + 2 * HALO, TR // reps
    edge, pieces = HALO * wide, rep_rows // HALO
    tile = (rep_rows + 2 * HALO) * wide
    dma, f32, b16 = pltpu.SemaphoreType.DMA, jnp.float32, jnp.bfloat16
    places = {True: pl.BlockSpec(memory_space=pltpu.VMEM), False: pl.BlockSpec(memory_space=pl.ANY)}
    inputs = dict(
        tokens_ref=tokens, wqkv_ref=w_qkv, wo_ref=w_out, wu_ref=w_up, wd_ref=w_down, pw_ref=point_weight,
        ga_ref=attn_gain, gm_ref=mlp_gain, dd_ref=dest_device[None, :], ds_ref=dest_slot[None, :],
        pillar_ref=pillar[None, :], dw_ref=jnp.transpose(depth_weight, (1, 2, 0, 3)), rg_ref=raster_gain,
    )
    far_away = ("tokens_ref", "wqkv_ref", "wo_ref", "wu_ref", "wd_ref", "pw_ref")
    floats = dict(
        wqkv_f=(2, 3, width, lanes), wo_f=(2, lanes, width), wu_f=(2, width, hidden),
        wd_f=(2, hidden, width), att_s=(2, chunk, lanes), p_s=(rows, width), n1_s=(rows // 2, width),
        s1_s=(rows // 2, width), f1_s=(rows // 2, width), a_s=(rows, width),
        g0_s=(cols * reps, rows, lanes), m_s=(reps, cols, rows, lanes), n2_s=(cols, rows, lanes),
        s2_s=(rows, lanes), f2_s=(rows, lanes), code_s=(8, 128), arrived_s=(ntok, 8, 128),
        y_s=(count, block, lanes), o_s=(ntok, cap, block, lanes),
        g_s=(ntok, cols * reps, cap, block, lanes), raw_s=(3, ntok * cap, block, lanes),
        pw_f=point_weight.shape, pool_s=(cols * reps * rep_rows * wide, width),
        n3_s=(2, pieces, edge, width), s3_s=(pieces, edge, width), f3_s=(pieces, edge, width),
        h_s=(2, edge, width), tile_s=(tile, width), flat_s=(tile + 16, width),
    )
    halves = dict(
        wqkv_s=(2, 2, 3, width, lanes), wo_s=(2, 2, lanes, width), wu_s=(2, 2, width, hidden),
        wd_s=(2, 2, hidden, width), q_s=(2, rows, 2 * lanes), k_s=(2, rows, 2 * lanes),
        v_s=(2, rows, 2 * lanes), pw_s=(2,) + point_weight.shape,
    )
    scratch = {name: pltpu.VMEM(shape, f32) for name, shape in floats.items()}
    scratch.update({name: pltpu.VMEM(shape, b16) for name, shape in halves.items()})
    for name in ("index", "source"):
        scratch[name + "_v"] = pltpu.VMEM((1, 128), jnp.int32)
        scratch[name + "_m"] = pltpu.SMEM((1, 128), jnp.int32)
    for kind in ("near", "far", "share", "near2", "far2"):
        scratch[kind + "_sem0"] = dma((2, n))
    for kind in ("across", "over", "relay"):
        scratch[kind + "_sem0"] = dma((2, 2 * n))
    scratch["code_sem0"] = dma((2, ntok))
    for kind in ("near", "far", "share"):
        scratch[kind + "_sem1"] = dma((2, n))
    for kind in ("along", "across", "over", "relay"):
        scratch[kind + "_sem1"] = dma((2, ntok * cap))
    scratch["near3_sem1"] = dma((2, 2 * pieces))
    scratch["far3_sem1"] = dma((2, pieces))
    scratch["halo_sem1"] = dma((2, 2))
    scratch["wsem"], scratch["tsem"] = dma((2, 4)), dma((4,))
    names = list(inputs) + ["out_ref"] + list(scratch)

    def kernel(*refs):
        refs = dict(zip(names, refs))
        first, second = First(0, refs, heads, chunk), Second(1, refs, heads, chunk)
        step = jnp.where(first.r == 0, ntok - 1, 1)
        second.partner = {"tok": lax.rem(first.t + step, ntok), "rep": 1 - first.r}
        first.load_weights()
        second.load_weights()
        second.load_points()
        greet([first.mate, first.peer, second.partner] + first.peers)
        first.body(second)
        second.body(first)

    return pl.pallas_call(
        kernel,
        out_shape=jax.ShapeDtypeStruct((rep_rows, TC, width), f32),
        in_specs=[places[name not in far_away] for name in inputs],
        out_specs=places[True],
        scratch_shapes=list(scratch.values()),
        compiler_params=pltpu.CompilerParams(
            collective_id=collective_id, has_side_effects=True, vmem_limit_bytes=VMEM_LIMIT
        ),
        name="layers",
    )(*inputs.values())


HALO = 2


def routes(dest_device, dest_slot):
    count = dest_device.shape[0]
    peers = lax.axis_size("tok")
    capacity = capacity_of(count, peers)
    order = jnp.arange(count, dtype=jnp.int32)
    earlier = (dest_device[:, None] == dest_device[None, :]) & (order[None, :] < order[:, None])
    place = dest_device * capacity + jnp.sum(earlier.astype(jnp.int32), axis=1)
    chosen = jnp.arange(peers * capacity, dtype=jnp.int32)[:, None] == place[None, :]
    index = jnp.sum(jnp.where(chosen, order[None, :], 0), axis=1)
    code = jnp.sum(jnp.where(chosen, dest_slot[None, :] + 1, 0), axis=1)
    code = jnp.pad(code.reshape(peers, capacity), ((0, 0), (0, 128 - capacity)))
    code = jnp.broadcast_to(code[:, None, :], (peers, 8, 128)).astype(jnp.float32)
    return index, code, capacity


def places(arrived, capacity, order):
    held = arrived[:, 0, :capacity].reshape(-1).astype(jnp.int32)
    found = held[None, :] == order[:, None] + 1
    return jnp.sum(jnp.where(found, jnp.arange(held.shape[0], dtype=jnp.int32)[None, :], 0), axis=1)


def raster_cells(extended, depth_weight, point_weight, gain_row):
    row_count = extended.shape[0] - 2
    col_count = extended.shape[1] - 2
    channels = extended.shape[2]
    normed = (
        extended
        * lax.rsqrt(jnp.mean(extended * extended, axis=-1, keepdims=True) + EPSILON)
        * gain_row
    )
    mixed = jnp.zeros((row_count, col_count, channels), jnp.float32)
    for a in range(3):
        for b in range(3):
            mixed = mixed + normed[a : a + row_count, b : b + col_count] * depth_weight[a, b]
    combined = matmul(mixed.reshape(row_count * col_count, channels), point_weight)
    combined = combined.reshape(row_count, col_count, 2 * channels)
    centre = extended[1:-1, 1:-1]
    return centre + combined[..., :channels] * jax.nn.sigmoid(combined[..., channels:])


def extended_cells(tok, members, rep_rows, full_width):
    cols, reps = members
    tile = []
    for col in range(cols):
        for rep in range(reps):
            y = rep * rep_rows - HALO + jnp.arange(rep_rows + 2 * HALO, dtype=jnp.int32)[:, None]
            x = col * TC - HALO + jnp.arange(TC + 2 * HALO, dtype=jnp.int32)[None, :]
            good = (y >= 0) & (y < TR) & (x >= 0) & (x < full_width)
            tile.append(jnp.where(good, (tok * TR + y) * full_width + x, -2).reshape(-1))
    return jnp.concatenate(tile)


def pool(partial, pillar, cells):
    onehot = (cells[:, None] == pillar[None, :]).astype(jnp.float32)
    return matmul(onehot, partial)


def exchange_rows(tile, ntok, reps):
    count = ntok * reps
    rep = lax.axis_index("rep")
    forward = [(i, i + 1) for i in range(count - 1)]
    backward = [(i + 1, i) for i in range(count - 1)]
    above = lax.ppermute(tile[-2 * HALO : -HALO], ("tok", "rep"), forward)
    below = lax.ppermute(tile[HALO : 2 * HALO], ("tok", "rep"), backward)
    above = jnp.where(rep == 0, above, tile[:HALO])
    below = jnp.where(rep == reps - 1, below, tile[-HALO:])
    return jnp.concatenate([above, tile[HALO:-HALO], below], axis=0)


def on_device(
    tokens,
    w_qkv,
    w_out,
    w_up,
    w_down,
    attn_gain,
    mlp_gain,
    dest_device,
    dest_slot,
    pillar,
    depth_weight,
    point_weight,
    raster_gain,
):
    members = (lax.axis_size("col"), lax.axis_size("rep"))
    group = members[0] * members[1]
    ntok = lax.axis_size("tok")
    block_count = dest_device.shape[0]
    order = jnp.arange(block_count, dtype=jnp.int32)
    index, codes, capacity = routes(dest_device, dest_slot)
    width = tokens.shape[1]
    weights = (w_qkv, w_out, w_up, w_down, attn_gain, mlp_gain)
    whole = (2 * members[1] * HALO * (TC + 2 * HALO)) % 8 == 0 and TR % (members[1] * HALO) == 0
    if members == (2, 2) and ntok > 1 and tokens.shape[0] == PATCH and whole and ntok * capacity <= 128:
        raster_weights = (depth_weight, point_weight, raster_gain)
        return both_layers(tokens, dest_device, dest_slot, capacity, pillar, raster_weights, weights, 1)
    blocks = gather(tokens, 1).reshape(1, group, block_count, -1, width)
    stream = attention_layer(blocks, order, 0, w_qkv, w_out, attn_gain, 2)
    share = scatter(mlp_partial(stream, 0, w_up, w_down, mlp_gain, group), 3)
    outgoing = pick(share.reshape(block_count, -1, width), index)
    outgoing = outgoing.reshape(ntok, -1, width)
    moved, arrived = move(outgoing, codes, 4)
    blocks = moved.reshape(ntok, group, capacity, -1, width)
    source = places(arrived, capacity, order)
    stream = attention_layer(blocks, source, 1, w_qkv, w_out, attn_gain, 5)
    partial = mlp_partial(stream, 1, w_up, w_down, mlp_gain, 1)[0]

    rep_rows = TR // members[1]
    full_width = TC * members[0]
    cells = extended_cells(lax.axis_index("tok"), members, rep_rows, full_width)
    pooled = pool(partial, pillar, cells)
    parts = pooled.reshape(group, -1, pooled.shape[1])
    edge = HALO * (TC + 2 * HALO)
    inside_kernel = members[0] > 1 and members[1] == 2 and ntok > 1 and edge % 8 == 0
    tile = scatter(parts, 6, edge if inside_kernel else 0)
    tile = tile.reshape(rep_rows + 2 * HALO, TC + 2 * HALO, -1)
    if not inside_kernel:
        tile = exchange_rows(tile, ntok, members[1])
    first = raster_cells(tile, depth_weight[0], point_weight[0], raster_gain[0])
    y = lax.axis_index(("tok", "rep")) * rep_rows - 1 + jnp.arange(rep_rows + 2)[:, None, None]
    x = lax.axis_index("col") * TC - 1 + jnp.arange(TC + 2)[None, :, None]
    inside = (y >= 0) & (y < TR * ntok) & (x >= 0) & (x < full_width)
    first = jnp.where(inside, first, 0.0)
    return raster_cells(first, depth_weight[1], point_weight[1], raster_gain[1])


def solution(mesh):
    placed = (
        P(("scene", "tok"), ("col", "rep")),
        P(None, None, None, ("col", "rep")),
        P(None, ("col", "rep"), None),
        P(None, None, ("col", "rep")),
        P(None, ("col", "rep"), None),
        P(),
        P(),
        P(("scene", "tok")),
        P(("scene", "tok")),
        P(("scene", "tok")),
        P(),
        P(),
        P(),
    )
    return jax.shard_map(
        on_device,
        mesh=mesh,
        in_specs=placed,
        out_specs=P(("scene", "tok", "rep"), "col", None),
        check_vma=False,
    )
```

```python
import functools
import math

import jax
import jax.numpy as jnp
from jax import lax
from jax.experimental import pallas as pl
from jax.experimental.pallas import tpu as pltpu
from jax.sharding import PartitionSpec as P

PATCH = 1024
TR = 16
TC = 16
HD = 16


MATMUL_PRECISION = lax.Precision.HIGH
EPSILON = 1e-05


def layer_norm(values, gain_row):
    average = jnp.mean(values, axis=-1, keepdims=True)
    centered = values - average
    variance = jnp.mean(centered * centered, axis=-1, keepdims=True)
    return centered * lax.rsqrt(variance + EPSILON) * gain_row


def split(values):
    high = values.astype(jnp.bfloat16)
    return high, (values - high.astype(jnp.float32)).astype(jnp.bfloat16)


def bdot(left, right, dims=(((1,), (0,)), ((), ()))):
    return lax.dot_general(left, right, dims, preferred_element_type=jnp.float32)


def dot3(left, right):
    lh, ll = left
    rh, rl = right
    return bdot(lh, rh) + bdot(lh, rl) + bdot(ll, rh)


def attention_kernel(share, source_ref, x_ref, gain_ref, w_ref, o_ref, out_ref, q_s, k_s, v_s, att_s):
    cols = w_ref.shape[-1]
    heads = cols // HD
    rows = out_ref.shape[0]
    chunk = att_s.shape[0]
    slots, each, block = x_ref.shape[1:4]
    first_block = pl.program_id(0) * (rows // block)

    def stream_rows(i):
        parts = []
        for n in range(chunk // block):
            at = source_ref[first_block + i * (chunk // block) + n]
            places = [x_ref[at // each, j, at % each] for j in range(slots)]
            parts.append(jnp.concatenate(places, axis=-1))
        return jnp.concatenate(parts, axis=0)

    lanes = q_s.shape[-1]

    r = lax.broadcasted_iota(jnp.int32, (cols, lanes), 0)
    c = lax.broadcasted_iota(jnp.int32, (cols, lanes), 1)
    lane = lax.broadcasted_iota(jnp.int32, (1, cols), 1)
    w = [split(w_ref[j]) for j in range(3)]
    for i in range(rows // chunk):
        at = pl.ds(i * chunk, chunk)
        normed = split(layer_norm(stream_rows(i), gain_ref[...]))
        qh, ql = split(dot3(normed, w[0]) * (HD ** (-0.5) * math.log2(math.e)))
        kh, kl = split(dot3(normed, w[1]))
        vh, vl = split(dot3(normed, w[2]))
        for h in range(heads):
            part = c // HD
            inside = (r // HD == h) & (r % HD == c % HD)
            first = (inside & ((part == 0) | (part == 1))).astype(jnp.bfloat16)
            third = (inside & (part == 2)).astype(jnp.bfloat16)
            outer = (inside & ((part == 0) | (part == 2))).astype(jnp.bfloat16)
            middle = (inside & (part == 1)).astype(jnp.bfloat16)
            q_s[h, at, :] = (bdot(qh, first) + bdot(ql, third)).astype(jnp.bfloat16)
            k_s[h, at, :] = (bdot(kh, outer) + bdot(kl, middle)).astype(jnp.bfloat16)
            own = lane // HD == h
            v_s[h, at, :cols] = jnp.where(own, vh.astype(jnp.float32), 0.0).astype(jnp.bfloat16)
            v_s[h, at, cols:] = jnp.where(own, vl.astype(jnp.float32), 1.0).astype(jnp.bfloat16)

    projection = split(o_ref[...])

    def query_rows(i, carry):
        at = pl.ds(pl.multiple_of(i * chunk, chunk), chunk)
        att_s[...] = jnp.zeros_like(att_s)

        def one_head(h, carry):
            scores = bdot(q_s[h, at, :], k_s[h], (((1,), (1,)), ((), ())))
            weights = jnp.exp2(scores - jnp.max(scores, axis=-1, keepdims=True))
            wh, wl = split(weights)
            sums = bdot(wh, v_s[h]) + bdot(wl, v_s[h])
            top, low = sums[:, :cols], sums[:, cols:]
            own = lane // HD == h
            total = jnp.max(jnp.where(own, 0.0, low), axis=-1, keepdims=True)
            att_s[...] += jnp.where(own, (top + low) / total, 0.0)
            return carry

        lax.fori_loop(0, heads, one_head, 0, unroll=4)
        out_ref[at, :] = dot3(split(att_s[...]), projection) + stream_rows(i) * share
        return carry

    lax.fori_loop(0, rows // chunk, query_rows, 0)


def attend(blocks, source, gain_row, weights, w_out, group):
    block, width = blocks.shape[3], blocks.shape[1] * blocks.shape[4]
    rows = source.shape[0] * block
    cols = weights.shape[-1]
    heads = cols // HD
    lanes = max(128, 3 * HD)
    return pl.pallas_call(
        functools.partial(attention_kernel, 1.0 / group),
        grid_spec=pltpu.PrefetchScalarGridSpec(
            num_scalar_prefetch=1,
            grid=(rows // PATCH,),
            in_specs=[
                pl.BlockSpec(blocks.shape, lambda i, source: (0, 0, 0, 0, 0)),
                pl.BlockSpec((1, width), lambda i, source: (0, 0)),
                pl.BlockSpec(weights.shape, lambda i, source: (0, 0, 0)),
                pl.BlockSpec(w_out.shape, lambda i, source: (0, 0)),
            ],
            out_specs=pl.BlockSpec((PATCH, width), lambda i, source: (i, 0)),
            scratch_shapes=[
                pltpu.VMEM((heads, PATCH, lanes), jnp.bfloat16),
                pltpu.VMEM((heads, PATCH, lanes), jnp.bfloat16),
                pltpu.VMEM((heads, PATCH, 2 * cols), jnp.bfloat16),
                pltpu.VMEM((256, cols), jnp.float32),
            ],
        ),
        out_shape=jax.ShapeDtypeStruct((rows, width), jnp.float32),
        compiler_params=pltpu.CompilerParams(vmem_limit_bytes=48 * 1024 * 1024),
        name="attend",
    )(source, blocks, gain_row[None, :], weights, w_out)


def matmul(left, right):
    return jnp.dot(left, right, precision=MATMUL_PRECISION, preferred_element_type=jnp.float32)


VMEM_LIMIT = 56 * 1024 * 1024
MESH = pl.DeviceIdType.MESH


def position():
    cols, reps = lax.axis_size("col"), lax.axis_size("rep")
    return cols, reps, lax.axis_index("col"), lax.axis_index("rep")


def greet(devices):
    barrier = pltpu.get_barrier_semaphore()
    for device in devices:
        pl.semaphore_signal(barrier, inc=1, device_id=device, device_id_type=MESH)
    pl.semaphore_wait(barrier, len(devices))


def remote(src, dst, send, recv, device):
    return pltpu.make_async_remote_copy(
        src_ref=src, dst_ref=dst, send_sem=send, recv_sem=recv, device_id=device, device_id_type=MESH
    )


def chunks_of(rows):
    for pieces in (8, 5, 4, 2):
        if rows % (8 * pieces) == 0:
            return pieces, rows // pieces
    return 1, rows


def gather_kernel(x_ref, out_ref, xs, xr, fs, fr, ps, pr, local):
    cols, reps, c, r = position()
    rows = x_ref.shape[0]
    pieces, size = chunks_of(rows)
    me = c * reps + r
    mate = {"col": c, "rep": 1 - r}
    others = [{"col": lax.rem(c + d, cols), "rep": r} for d in range(1, cols)]
    greet([mate] + others)
    across, onward = [], []
    for k in range(pieces):
        at = pl.ds(k * size, size)
        for d in range(1, cols):
            copy = remote(
                x_ref.at[at], out_ref.at[me, at], xs.at[d - 1, k], xr.at[d - 1, k], others[d - 1]
            )
            copy.start()
            across.append(copy)
    share = remote(x_ref, out_ref.at[me], ps, pr, mate)
    share.start()
    keep = pltpu.make_async_copy(x_ref, out_ref.at[me], local)
    keep.start()
    for k in range(pieces):
        at = pl.ds(k * size, size)
        for d in range(1, cols):
            across[k * (cols - 1) + d - 1].wait_recv()
            slot = lax.rem(c + cols - d, cols) * reps + r
            copy = remote(
                out_ref.at[slot, at], out_ref.at[slot, at], fs.at[d - 1, k], fr.at[d - 1, k], mate
            )
            copy.start()
            onward.append(copy)
    for copy in across:
        copy.wait_send()
    share.wait()
    keep.wait()
    for copy in onward:
        copy.wait()


def gather(block, collective_id):
    cols, reps = lax.axis_size("col"), lax.axis_size("rep")
    if reps != 2 or cols < 2:
        return lax.all_gather(block, ("col", "rep"), axis=0)
    pieces, _ = chunks_of(block.shape[0])
    dma = pltpu.SemaphoreType.DMA
    return pl.pallas_call(
        gather_kernel,
        out_shape=jax.ShapeDtypeStruct((cols * reps,) + block.shape, block.dtype),
        in_specs=[pl.BlockSpec(memory_space=pltpu.VMEM)],
        out_specs=pl.BlockSpec(memory_space=pltpu.VMEM),
        scratch_shapes=[dma((cols - 1, pieces))] * 4 + [dma, dma, dma],
        compiler_params=pltpu.CompilerParams(
            collective_id=collective_id, has_side_effects=True, vmem_limit_bytes=VMEM_LIMIT
        ),
        name="gather",
    )(block)


def scatter_kernel(edge, p_ref, out_ref, a_ref, s_ref, b_ref, a_s, a_r, b_s, b_r, *halo):
    cols, reps, c, r = position()
    rows = p_ref.shape[1]
    pieces, size = chunks_of(rows)
    mate = {"col": c, "rep": 1 - r}
    others = [{"col": lax.rem(c + d, cols), "rep": r} for d in range(1, cols)]
    greeted = [mate] + others
    if edge:
        ntok, t = lax.axis_size("tok"), lax.axis_index("tok")
        partner = {"tok": lax.rem(t + jnp.where(r == 0, ntok - 1, 1), ntok), "rep": 1 - r}
        greeted = greeted + [partner]
    greet(greeted)
    order = [(k, d) for k in range(pieces) for d in range(1, cols)]
    order += [(k, 0) for k in range(pieces)]
    near, far = {}, {}
    for k, d in order:
        at = pl.ds(k * size, size)
        slot = lax.rem(c + d, cols) * reps + 1 - r
        near[k, d] = remote(
            p_ref.at[slot, at], a_ref.at[d, at], a_s.at[d, k], a_r.at[d, k], mate
        )
        near[k, d].start()
    for k, d in order:
        at = pl.ds(k * size, size)
        slot = lax.rem(c + d, cols) * reps + r
        near[k, d].wait_recv()
        total = p_ref[slot, at] + a_ref[d, at]
        if d == 0:
            out_ref[at] = total
        else:
            s_ref[d - 1, at] = total
            far[k, d] = remote(
                s_ref.at[d - 1, at],
                b_ref.at[d - 1, at],
                b_s.at[d - 1, k],
                b_r.at[d - 1, k],
                others[d - 1],
            )
            far[k, d].start()
    for (k, d), copy in far.items():
        at = pl.ds(k * size, size)
        copy.wait_recv()
        out_ref[at] += b_ref[d - 1, at]
    if edge:
        h_ref, e_ref, h_s, h_r = halo
        inner = pl.multiple_of(jnp.where(r == 0, edge, rows - 2 * edge), 8)
        outer = pl.multiple_of(jnp.where(r == 0, 0, rows - edge), 8)
        e_ref[...] = out_ref[pl.ds(inner, edge)]
        copy = remote(e_ref, h_ref, h_s, h_r, partner)
        copy.start()
        copy.wait()
        wrapped = jnp.where(r == 0, t == 0, t == ntok - 1)
        out_ref[pl.ds(outer, edge)] = jnp.where(wrapped, 0.0, h_ref[...])
    for copy in list(near.values()) + list(far.values()):
        copy.wait_send()


def scatter(parts, collective_id, edge=0):
    cols, reps = lax.axis_size("col"), lax.axis_size("rep")
    if reps != 2 or cols < 2:
        return lax.psum_scatter(parts, ("col", "rep"), scatter_dimension=0)
    shape, kind = parts.shape[1:], parts.dtype
    pieces, _ = chunks_of(shape[0])
    dma = pltpu.SemaphoreType.DMA
    return pl.pallas_call(
        functools.partial(scatter_kernel, edge),
        out_shape=jax.ShapeDtypeStruct(shape, kind),
        in_specs=[pl.BlockSpec(memory_space=pltpu.VMEM)],
        out_specs=pl.BlockSpec(memory_space=pltpu.VMEM),
        scratch_shapes=[
            pltpu.VMEM((cols,) + shape, kind),
            pltpu.VMEM((cols - 1,) + shape, kind),
            pltpu.VMEM((cols - 1,) + shape, kind),
            dma((cols, pieces)),
            dma((cols, pieces)),
            dma((cols - 1, pieces)),
            dma((cols - 1, pieces)),
        ]
        + ([pltpu.VMEM((edge, shape[1]), kind)] * 2 + [dma, dma] if edge else []),
        compiler_params=pltpu.CompilerParams(
            collective_id=collective_id, has_side_effects=True, vmem_limit_bytes=VMEM_LIMIT
        ),
        name="scatter",
    )(parts)


def total_kernel(
    p_ref, out_ref, a_ref, s_ref, b_ref, a_s, a_r, b_s, b_r, xs, xr, fs, fr, ps, pr
):
    cols, reps, c, r = position()
    rows = p_ref.shape[1]
    pieces, size = chunks_of(rows)
    me = c * reps + r
    mate = {"col": c, "rep": 1 - r}
    others = [{"col": lax.rem(c + d, cols), "rep": r} for d in range(1, cols)]
    greet([mate] + others)
    order = [(k, d) for k in range(pieces) for d in range(1, cols)]
    order += [(k, 0) for k in range(pieces)]
    near, far, across, share, onward = {}, {}, {}, {}, {}
    for k, d in order:
        at = pl.ds(k * size, size)
        slot = lax.rem(c + d, cols) * reps + 1 - r
        near[k, d] = remote(
            p_ref.at[slot, at], a_ref.at[d, at], a_s.at[d, k], a_r.at[d, k], mate
        )
        near[k, d].start()
    for k, d in order:
        if d == 0:
            continue
        at = pl.ds(k * size, size)
        slot = lax.rem(c + d, cols) * reps + r
        near[k, d].wait_recv()
        s_ref[d - 1, at] = p_ref[slot, at] + a_ref[d, at]
        far[k, d] = remote(
            s_ref.at[d - 1, at], b_ref.at[d - 1, at], b_s.at[d - 1, k], b_r.at[d - 1, k], others[d - 1]
        )
        far[k, d].start()
    for k in range(pieces):
        at = pl.ds(k * size, size)
        near[k, 0].wait_recv()
        total = p_ref[me, at] + a_ref[0, at]
        for d in range(1, cols):
            far[k, d].wait_recv()
            total = total + b_ref[d - 1, at]
        out_ref[me, at] = total
        for d in range(1, cols):
            across[k, d] = remote(
                out_ref.at[me, at], out_ref.at[me, at], xs.at[d - 1, k], xr.at[d - 1, k], others[d - 1]
            )
            across[k, d].start()
        share[k] = remote(out_ref.at[me, at], out_ref.at[me, at], ps.at[k], pr.at[k], mate)
        share[k].start()
    for (k, d), copy in across.items():
        at = pl.ds(k * size, size)
        copy.wait_recv()
        slot = lax.rem(c + cols - d, cols) * reps + r
        onward[k, d] = remote(
            out_ref.at[slot, at], out_ref.at[slot, at], fs.at[d - 1, k], fr.at[d - 1, k], mate
        )
        onward[k, d].start()
    for copies in (near, far, across):
        for copy in copies.values():
            copy.wait_send()
    for copies in (share, onward):
        for copy in copies.values():
            copy.wait()


def total(parts, collective_id):
    cols, reps = lax.axis_size("col"), lax.axis_size("rep")
    if reps != 2 or cols < 2:
        return lax.psum(parts, ("col", "rep"))
    shape, kind = parts.shape[1:], parts.dtype
    pieces, _ = chunks_of(shape[0])
    dma = pltpu.SemaphoreType.DMA
    return pl.pallas_call(
        total_kernel,
        out_shape=jax.ShapeDtypeStruct(parts.shape, kind),
        in_specs=[pl.BlockSpec(memory_space=pltpu.VMEM)],
        out_specs=pl.BlockSpec(memory_space=pltpu.VMEM),
        scratch_shapes=[
            pltpu.VMEM((cols,) + shape, kind),
            pltpu.VMEM((cols - 1,) + shape, kind),
            pltpu.VMEM((cols - 1,) + shape, kind),
            dma((cols, pieces)),
            dma((cols, pieces)),
        ]
        + [dma((cols - 1, pieces))] * 6
        + [dma((pieces,))] * 2,
        compiler_params=pltpu.CompilerParams(
            collective_id=collective_id, has_side_effects=True, vmem_limit_bytes=VMEM_LIMIT
        ),
        name="total",
    )(parts)


def move_kernel(o_ref, code_ref, out_ref, arrived_ref, zs, zr, cs, cr, xs, xr, fs, fr, ps, pr, local):
    cols, reps, c, r = position()
    ntok, t = lax.axis_size("tok"), lax.axis_index("tok")
    me = c * reps + r
    mate = {"col": c, "rep": 1 - r}
    others = [{"col": lax.rem(c + d, cols), "rep": r} for d in range(1, cols)]
    peers = [{"tok": lax.rem(t + e, ntok)} for e in range(1, ntok)]
    greet([mate] + others + peers)
    along, codes, across, share, onward = [], [], {}, [], []
    for e in range(1, ntok):
        target = lax.rem(t + e, ntok)
        copy = remote(o_ref.at[target], out_ref.at[t, me], zs.at[e - 1], zr.at[e - 1], peers[e - 1])
        copy.start()
        along.append(copy)
        copy = remote(
            code_ref.at[target], arrived_ref.at[t], cs.at[e - 1], cr.at[e - 1], peers[e - 1]
        )
        copy.start()
        codes.append(copy)
    keep = pltpu.make_async_copy(o_ref.at[t], out_ref.at[t, me], local.at[0])
    keep.start()
    keep_code = pltpu.make_async_copy(code_ref.at[t], arrived_ref.at[t], local.at[1])
    keep_code.start()

    def hand_on(e):
        u = lax.rem(t + ntok - e, ntok)
        for d in range(1, cols):
            across[e, d].wait_recv()
            slot = lax.rem(c + cols - d, cols) * reps + r
            copy = remote(
                out_ref.at[u, slot], out_ref.at[u, slot], fs.at[e, d - 1], fr.at[e, d - 1], mate
            )
            copy.start()
            onward.append(copy)

    for e in range(ntok):
        u = lax.rem(t + ntok - e, ntok)
        if e:
            along[e - 1].wait_recv()
        origin = out_ref.at[u, me] if e else o_ref.at[t]
        for d in range(1, cols):
            across[e, d] = remote(
                origin, out_ref.at[u, me], xs.at[e, d - 1], xr.at[e, d - 1], others[d - 1]
            )
            across[e, d].start()
        copy = remote(origin, out_ref.at[u, me], ps.at[e], pr.at[e], mate)
        copy.start()
        share.append(copy)
        if e:
            hand_on(e - 1)
    hand_on(ntok - 1)
    keep.wait()
    keep_code.wait()
    for copy in along + list(across.values()):
        copy.wait_send()
    for copy in codes + share + onward:
        copy.wait()


def move(outgoing, codes, collective_id):
    cols, reps, ntok = lax.axis_size("col"), lax.axis_size("rep"), lax.axis_size("tok")
    if reps != 2 or cols < 2 or ntok < 2:
        incoming = lax.all_to_all(outgoing, "tok", split_axis=0, concat_axis=0, tiled=True)
        arrived = lax.all_to_all(codes, "tok", split_axis=0, concat_axis=0, tiled=True)
        return lax.all_gather(incoming, ("col", "rep"), axis=1), arrived
    dma = pltpu.SemaphoreType.DMA
    shape = (ntok, cols * reps) + outgoing.shape[1:]
    return pl.pallas_call(
        move_kernel,
        out_shape=(
            jax.ShapeDtypeStruct(shape, outgoing.dtype),
            jax.ShapeDtypeStruct(codes.shape, codes.dtype),
        ),
        in_specs=[pl.BlockSpec(memory_space=pltpu.VMEM)] * 2,
        out_specs=[pl.BlockSpec(memory_space=pltpu.VMEM)] * 2,
        scratch_shapes=[dma((ntok - 1,))] * 4
        + [dma((ntok, cols - 1))] * 4
        + [dma((ntok,))] * 2
        + [dma((2,))],
        compiler_params=pltpu.CompilerParams(
            collective_id=collective_id, has_side_effects=True, vmem_limit_bytes=VMEM_LIMIT
        ),
        name="move",
    )(outgoing, codes)


def pick_kernel(index_ref, x_ref, out_ref):
    for j in range(out_ref.shape[0]):
        out_ref[j] = x_ref[index_ref[j]]


def pick(blocks, index):
    return pl.pallas_call(
        pick_kernel,
        out_shape=jax.ShapeDtypeStruct(index.shape + blocks.shape[1:], blocks.dtype),
        in_specs=[pl.BlockSpec(memory_space=pltpu.SMEM), pl.BlockSpec(memory_space=pltpu.VMEM)],
        out_specs=pl.BlockSpec(memory_space=pltpu.VMEM),
        name="pick",
    )(index, blocks)


def attention_layer(blocks, source, layer, w_qkv, w_out, attn_gain, collective_id):
    group = blocks.shape[1]
    terms = attend(blocks, source, attn_gain[layer], w_qkv[layer], w_out[layer], group)
    rows, width = terms.shape
    return total(terms.reshape(group, rows // group, width), collective_id).reshape(rows, width)


def mlp_kernel(x_ref, gain_ref, up_ref, down_ref, share, out_ref):
    x = x_ref[...]
    hidden = dot3(split(layer_norm(x, gain_ref[...])), split(up_ref[...]))
    hidden = 0.5 * hidden * (1.0 + lax.erf(hidden * (0.5**0.5)))
    total = dot3(split(hidden), split(down_ref[...])) + x * share
    width = out_ref.shape[-1]
    for j in range(out_ref.shape[0]):
        out_ref[j] = total[:, j * width : (j + 1) * width]


def mlp_partial(stream, layer, w_up, w_down, mlp_gain, slots):
    rows, width = stream.shape
    tile = min(256, rows)
    hidden = w_up.shape[-1]
    group = lax.axis_size("col") * lax.axis_size("rep")

    def kernel(x_ref, gain_ref, up_ref, down_ref, out_ref):
        mlp_kernel(x_ref, gain_ref, up_ref, down_ref, 1.0 / group, out_ref)

    return pl.pallas_call(
        kernel,
        grid=(rows // tile,),
        in_specs=[
            pl.BlockSpec((tile, width), lambda i: (i, 0)),
            pl.BlockSpec((1, width), lambda i: (0, 0)),
            pl.BlockSpec((width, hidden), lambda i: (0, 0)),
            pl.BlockSpec((hidden, width), lambda i: (0, 0)),
        ],
        out_specs=pl.BlockSpec((slots, tile, width // slots), lambda i: (0, i, 0)),
        out_shape=jax.ShapeDtypeStruct((slots, rows, width // slots), jnp.float32),
        compiler_params=pltpu.CompilerParams(vmem_limit_bytes=48 * 1024 * 1024),
        name="mlp",
    )(stream, mlp_gain[layer][None, :], w_up[layer], w_down[layer])


def gelu(values):
    return 0.5 * values * (1.0 + lax.erf(values * (0.5**0.5)))


def piece(i, size):
    return pl.ds(pl.multiple_of(i * size, size), size)


class Layer:
    def __init__(self, layer, refs, heads, chunk):
        self.__dict__.update(refs)
        self.layer, self.heads, self.chunk = layer, heads, chunk
        self.tag = "_sem" + str(layer)
        self.cols, self.reps, self.c, self.r = position()
        self.ntok, self.t = lax.axis_size("tok"), lax.axis_index("tok")
        self.me = self.c * self.reps + self.r
        self.mate, self.peer = {"rep": 1 - self.r}, {"col": 1 - self.c}
        self.peers = [{"tok": lax.rem(self.t + e, self.ntok)} for e in range(1, self.ntok)]
        self.rows, self.width = self.a_s.shape
        self.lanes = self.q_s.shape[-1] // 2
        self.n = self.rows // chunk
        self.block = self.y_s.shape[1]
        self.cap = self.o_s.shape[1]

    def sent(self, kind, i, src, dst, device):
        sem = getattr(self, kind + self.tag)
        return remote(src, dst, sem.at[0, i], sem.at[1, i], device)

    def load_weights(self):
        pairs = (
            (self.wqkv_ref, self.wqkv_f), (self.wo_ref, self.wo_f),
            (self.wu_ref, self.wu_f), (self.wd_ref, self.wd_f),
        )
        self.loads = [
            pltpu.make_async_copy(src.at[self.layer], dst.at[self.layer], self.wsem.at[self.layer, j])
            for j, (src, dst) in enumerate(pairs)
        ]
        for load in self.loads:
            load.start()

    def split_weights(self):
        layer = self.layer
        self.loads[0].wait()
        for m in range(3):
            self.wqkv_s[layer, 0, m], self.wqkv_s[layer, 1, m] = split(self.wqkv_f[layer, m])
        rest = ((self.wo_f, self.wo_s), (self.wu_f, self.wu_s), (self.wd_f, self.wd_s))
        for load, (src, dst) in zip(self.loads[1:], rest):
            load.wait()
            dst[layer, 0], dst[layer, 1] = split(src[layer])

    def pair(self, ref):
        return ref[self.layer, 0], ref[self.layer, 1]

    def project(self, stream):
        normed = split(layer_norm(stream, self.ga_ref[pl.ds(self.layer, 1)]))
        return [dot3(normed, (self.wqkv_s[self.layer, 0, m], self.wqkv_s[self.layer, 1, m])) for m in range(3)]

    def pack(self, at, q, k, v):
        lanes = self.lanes
        half_lanes = lanes // 2
        lane = lax.broadcasted_iota(jnp.int32, (1, lanes), 1)
        low = lane < half_lanes
        qh, ql = split(q * (HD ** (-0.5) * math.log2(math.e)))
        kh, kl = [part.astype(jnp.float32) for part in split(k)]
        vh, vl = [part.astype(jnp.float32) for part in split(v)]
        qf, qlf = qh.astype(jnp.float32), ql.astype(jnp.float32)
        q_s, k_s, v_s = self.q_s, self.k_s, self.v_s

        def roll(values):
            return pltpu.roll(values, half_lanes, 1)

        q_s[0, at, :lanes] = qh
        q_s[1, at, :lanes] = qh
        q_s[0, at, lanes:] = jnp.where(low, qf, roll(qlf)).astype(jnp.bfloat16)
        q_s[1, at, lanes:] = jnp.where(low, roll(qf), qlf).astype(jnp.bfloat16)
        k_s[0, at, :lanes] = kh.astype(jnp.bfloat16)
        k_s[1, at, :lanes] = kh.astype(jnp.bfloat16)
        k_s[0, at, lanes:] = jnp.where(low, kl, roll(kh)).astype(jnp.bfloat16)
        k_s[1, at, lanes:] = jnp.where(low, roll(kl), kh).astype(jnp.bfloat16)
        v_s[0, at, :lanes] = vh.astype(jnp.bfloat16)
        v_s[1, at, :lanes] = vh.astype(jnp.bfloat16)
        v_s[0, at, lanes:] = jnp.where(low, vl, 1.0).astype(jnp.bfloat16)
        v_s[1, at, lanes:] = jnp.where(low, 1.0, vl).astype(jnp.bfloat16)

    def near(self, i):
        half = self.chunk // 2
        start = pl.multiple_of(i * self.chunk + (1 - self.r) * half, half)
        return self.sent("near", i, self.p_s.at[pl.ds(start, half)], self.n1_s.at[piece(i, half)], self.mate)

    def far(self, i):
        at = piece(i, self.chunk // 2)
        return self.sent("far", i, self.s1_s.at[at], self.f1_s.at[at], self.peer)

    def own_half(self, i):
        half = self.chunk // 2
        return pl.ds(pl.multiple_of(i * self.chunk + self.r * half, half), half)

    def share(self, i):
        at = self.own_half(i)
        return self.sent("share", i, self.a_s.at[at], self.a_s.at[at], self.mate)

    def attention(self, k):
        lanes, half_heads, chunk = self.lanes, self.heads // 2, self.chunk
        wide = lax.broadcasted_iota(jnp.int32, (1, 2 * lanes), 1)
        lane = lax.broadcasted_iota(jnp.int32, (1, lanes), 1)
        i, half = k // 2, k % 2
        query = self.q_s[half, piece(i, chunk), :]
        queries = []
        for m in range(half_heads):
            first = (wide < lanes) & (wide // HD == half * half_heads + m)
            second = (wide >= lanes) & ((wide % (lanes // 2)) // HD == m)
            mask = jnp.where(first | second, 1.0, 0.0).astype(jnp.bfloat16)
            queries.append(query * mask)
        stacked = jnp.concatenate(queries, axis=0)
        scores = bdot(stacked, self.k_s[half], (((1,), (1,)), ((), ())))
        weights = jnp.exp2(scores - jnp.max(scores, axis=-1, keepdims=True))
        sums = bdot(jnp.concatenate(split(weights), axis=0), self.v_s[half])
        sums = sums[: half_heads * chunk] + sums[half_heads * chunk :]
        total = jnp.zeros((chunk, lanes), jnp.float32)
        for m in range(half_heads):
            own = sums[m * chunk : (m + 1) * chunk]
            top, low = own[:, :lanes], own[:, lanes:]
            ratio = (top + low) / pltpu.roll(low, lanes // 2, 1)
            total += jnp.where(lane // HD == half * half_heads + m, ratio, 0.0)
        self.att_s[half] = total

    def finish(self, i):
        projection = self.pair(self.wo_s)
        self.p_s[piece(i, self.chunk)] = dot3(split(self.att_s[0] + self.att_s[1]), projection)
        self.near(i).start()

    def reduce_near(self, i):
        self.near(i).wait_recv()
        at = piece(i, self.chunk // 2)
        self.s1_s[at] = self.p_s[self.own_half(i)] + self.n1_s[at]
        self.far(i).start()

    def reduce_far(self, i):
        self.far(i).wait_recv()
        half = self.chunk // 2
        at = piece(i, half)
        stream = self.stream_rows(i * self.chunk + self.r * half, half)
        self.a_s[self.own_half(i)] = (self.s1_s[at] + self.f1_s[at]) + stream
        self.share(i).start()

    def mlp(self, x):
        normed = split(layer_norm(x, self.gm_ref[pl.ds(self.layer, 1)]))
        hidden = gelu(dot3(normed, self.pair(self.wu_s)))
        return dot3(split(hidden), self.pair(self.wd_s))

    def run(self, stages):
        n = self.n

        def tick(k, carry):
            @pl.when(k < 2 * n)
            def _():
                self.attention(k)

            for offset, stage in stages:
                @pl.when((k >= offset) & (k < offset + 2 * n) & ((k - offset) % 2 == 0))
                def _(offset=offset, stage=stage):
                    stage((k - offset) // 2)

            return carry

        lax.fori_loop(0, 2 * n + max(offset for offset, _ in stages) - 1, tick, 0)


class First(Layer):
    def stream_rows(self, start, count):
        at = pl.ds(pl.multiple_of(start, count), count)
        return jnp.concatenate([self.g0_s[j, at] for j in range(self.cols * self.reps)], axis=-1)

    def across(self, i):
        at = piece(i, self.chunk)
        return self.sent("across", i, self.tokens_ref.at[at], self.g0_s.at[self.me, at], self.peer)

    def over(self, i):
        at = piece(i, self.chunk)
        return self.sent("over", i, self.tokens_ref.at[at], self.g0_s.at[self.me, at], self.mate)

    def relay(self, i):
        at = piece(i, self.chunk)
        slot = (1 - self.c) * self.reps + self.r
        return self.sent("relay", i, self.g0_s.at[slot, at], self.g0_s.at[slot, at], self.mate)

    def code(self, e):
        target = {"tok": lax.rem(self.t + e, self.ntok)}
        return self.sent("code", e, self.code_s, self.arrived_s.at[self.t], target)

    def route(self):
        device = self.dd_ref[...].astype(jnp.float32)
        slot = self.ds_ref[...].astype(jnp.float32)
        count = device.shape[1]
        row = lax.broadcasted_iota(jnp.int32, (count, count), 0)
        col = lax.broadcasted_iota(jnp.int32, (count, count), 1)

        def upright(values):
            return jnp.sum(jnp.where(row == col, values, 0.0), axis=1, keepdims=True)

        devices, slots = upright(device), upright(slot)
        earlier = jnp.where((devices == device) & (col < row), 1.0, 0.0)
        place = devices * self.cap + jnp.sum(earlier, axis=1, keepdims=True)
        at = lax.broadcasted_iota(jnp.int32, (count, 128), 1).astype(jnp.float32)
        block = lax.broadcasted_iota(jnp.int32, (count, 128), 0).astype(jnp.float32)
        index = jnp.sum(jnp.where(place == at, block, 0.0), axis=0, keepdims=True)
        code = jnp.sum(jnp.where(place == at, slots + 1.0, 0.0), axis=0, keepdims=True)
        self.index_v[...] = index.astype(jnp.int32)
        self.code_s[...] = jnp.broadcast_to(code, self.code_s.shape)
        self.arrived_s[self.t] = jnp.broadcast_to(code, self.code_s.shape)

    def locate(self):
        row = lax.broadcasted_iota(jnp.int32, (128, 128), 0)
        col = lax.broadcasted_iota(jnp.int32, (128, 128), 1)
        first = self.t * self.cap
        valid = (row >= first) & (row < first + self.cap)
        source = jnp.zeros((1, 128), jnp.float32)
        for u in range(self.ntok):
            codes = self.arrived_s[u][:1]
            upright = jnp.sum(jnp.where(row == col, codes, 0.0), axis=1, keepdims=True)
            found = valid & (upright == (col + 1).astype(jnp.float32))
            entry = (row - first + u * self.cap).astype(jnp.float32)
            source += jnp.sum(jnp.where(found, entry, 0.0), axis=0, keepdims=True)
        self.source_v[...] = source.astype(jnp.int32)

    def near2(self, i):
        at = piece(i, self.chunk)
        return self.sent("near2", i, self.m_s.at[1 - self.r, :, at], self.n2_s.at[:, at], self.mate)

    def far2(self, i):
        at = piece(i, self.chunk)
        return self.sent("far2", i, self.s2_s.at[at], self.f2_s.at[at], self.peer)

    def feed(self, i):
        self.share(i).wait_recv()
        at = piece(i, self.chunk)
        total = self.mlp(self.a_s[at])
        for j in range(self.cols * self.reps):
            self.m_s[j % self.reps, j // self.reps, at] = total[:, j * self.lanes : (j + 1) * self.lanes]
        self.near2(i).start()

    def scatter_near(self, i):
        self.near2(i).wait_recv()
        at = piece(i, self.chunk)
        self.s2_s[at] = self.m_s[self.r, 1 - self.c, at] + self.n2_s[1 - self.c, at]
        self.far2(i).start()

    def scatter_far(self, i):
        self.far2(i).wait_recv()
        at = piece(i, self.chunk)
        own = self.a_s[at, piece(self.me, self.lanes)]
        total = (self.m_s[self.r, self.c, at] + self.n2_s[self.c, at]) + self.f2_s[at]
        count = self.chunk // self.block
        self.y_s[piece(i, count)] = (total + own).reshape(count, self.block, self.lanes)

    def body(self, second):
        n = self.n
        for i in range(n):
            self.across(i).start()
        for i in range(n):
            self.over(i).start()
        keep = pltpu.make_async_copy(self.tokens_ref, self.g0_s.at[self.me], self.tsem.at[0])
        keep.start()
        self.route()
        table = pltpu.make_async_copy(self.index_v, self.index_m, self.tsem.at[1])
        table.start()
        self.split_weights()
        for e in range(1, self.ntok):
            self.code(e).start()
        second.split_weights()
        second.split_points()
        second.choose()
        self.pool_s[...] = jnp.zeros(self.pool_s.shape, jnp.float32)
        keep.wait()
        table.wait()

        def step(i, carry):
            @pl.when(i < n)
            def _():
                self.across(i).wait_recv()
                self.relay(i).start()

            @pl.when(i > 0)
            def _():
                self.over(i - 1).wait_recv()
                self.relay(i - 1).wait_recv()
                stream = self.stream_rows((i - 1) * self.chunk, self.chunk)
                self.pack(piece(i - 1, self.chunk), *self.project(stream))

            return carry

        lax.fori_loop(0, n + 1, step, 0)
        self.run(
            [
                (1, self.finish), (2, self.reduce_near), (9, self.scatter_near),
                (6, self.reduce_far), (7, self.feed), (13, self.scatter_far),
            ]
        )
        for copy in (
            self.near, self.far, self.share, self.near2, self.far2, self.across, self.over, self.relay
        ):
            for i in range(n):
                copy(i).wait_send()

    def tables(self):
        for e in range(1, self.ntok):
            self.code(e).wait()
        self.locate()
        table = pltpu.make_async_copy(self.source_v, self.source_m, self.tsem.at[2])
        table.start()
        return table


class Second(Layer):
    def entry(self, k):
        return jnp.clip(self.source_m[0, k], 0, self.ntok * self.cap - 1)

    def chosen(self, u, j):
        return jnp.clip(self.index_m[0, u * self.cap + j], 0, self.y_s.shape[0] - 1)

    def stream_rows(self, start, count):
        parts = []
        for m in range(count // self.block):
            at = self.entry(start // self.block + m)
            places = [self.g_s[at // self.cap, j, at % self.cap] for j in range(self.cols * self.reps)]
            parts.append(jnp.concatenate(places, axis=-1))
        return jnp.concatenate(parts, axis=0)

    def along(self, e, j):
        target = lax.rem(self.t + e, self.ntok)
        return self.sent(
            "along", e * self.cap + j, self.o_s.at[target, j], self.g_s.at[self.t, self.me, j],
            {"tok": target},
        )

    def origin(self, e):
        return lax.rem(self.t + self.ntok - e, self.ntok)

    def placed(self, kind, e, j, slot, device):
        ref = self.g_s.at[self.origin(e), slot, j]
        return self.sent(kind, e * self.cap + j, ref, ref, device)

    def across(self, e, j):
        return self.placed("across", e, j, self.me, self.peer)

    def over(self, e, j):
        return self.placed("over", e, j, self.me, self.mate)

    def relay(self, e, j):
        return self.placed("relay", e, j, (1 - self.c) * self.reps + self.r, self.mate)

    def arrive(self, j):
        for e in self.order[1:]:
            self.along(e, j).wait_recv()
            self.across(e, j).start()
            self.over(e, j).start()

    def hand(self, j):
        for e in self.order:
            self.across(e, j).wait_recv()
            self.relay(e, j).start()

    def take(self, j):
        parts = []
        for e in self.order:
            self.over(e, j).wait_recv()
            self.relay(e, j).wait_recv()
            places = [self.g_s[self.origin(e), k, j] for k in range(self.cols * self.reps)]
            parts.append(jnp.concatenate(places, axis=-1))
        for m, values in enumerate(self.project(jnp.concatenate(parts, axis=0))):
            for at, e in enumerate(self.order):
                entry = self.origin(e) * self.cap + j
                self.raw_s[m, entry] = values[at * self.block : (at + 1) * self.block]

    def move(self, first):
        self.order = [0]
        for e in range(1, self.ntok // 2 + 1):
            self.order += [e] + ([self.ntok - e] if self.ntok - e != e else [])
        for j in range(self.cap):
            for u in range(self.ntok):
                self.o_s[u, j] = self.y_s[self.chosen(u, j)]
            for e in self.order[1:]:
                self.along(e, j).start()
        for j in range(self.cap):
            self.g_s[self.t, self.me, j] = self.y_s[self.chosen(self.t, j)]
            self.across(0, j).start()
            self.over(0, j).start()
        table = first.tables()
        for j in range(self.cap):
            self.arrive(j)
            if j >= 1:
                self.hand(j - 1)
            if j >= 2:
                self.take(j - 2)
        self.take(self.cap - 2)
        self.hand(self.cap - 1)
        self.take(self.cap - 1)
        table.wait()

        def step(i, carry):
            def row(m):
                each = self.chunk // self.block
                blocks = [self.raw_s[m, self.entry(i * each + k)] for k in range(each)]
                return jnp.concatenate(blocks, axis=0)

            self.pack(piece(i, self.chunk), row(0), row(1), row(2))
            return carry

        lax.fori_loop(0, self.n, step, 0)

    def load_points(self):
        self.point = pltpu.make_async_copy(self.pw_ref, self.pw_f, self.tsem.at[3])
        self.point.start()

    def split_points(self):
        self.point.wait()

        def step(k, carry):
            at = piece(k, 64)
            for l in range(2):
                self.pw_s[0, l, at], self.pw_s[1, l, at] = split(self.pw_f[l, at])
            return carry

        lax.fori_loop(0, self.width // 64, step, 0)

    def cell_ids(self):
        count = self.pool_s.shape[0]
        p = lax.broadcasted_iota(jnp.int32, (count, 1), 0)
        wide = TC + 2 * HALO
        row = ((p.astype(jnp.float32) + 0.5) * (1.0 / wide)).astype(jnp.int32)
        col = row // TR
        x = col * TC - HALO + (p - row * wide)
        full = TC * self.cols
        y = row - col * TR
        return jnp.where((x >= 0) & (x < full), (self.t * TR + y) * full + x, -2)

    def feed(self, i):
        self.share(i).wait_recv()
        at = piece(i, self.chunk)
        x = self.a_s[at]
        high, low = split(self.mlp(x) + x * (1.0 / (self.cols * self.reps)))
        chosen = self.hot_s[i]
        self.pool_s[...] += bdot(chosen, high) + bdot(chosen, low)

    def choose(self):
        for i in range(self.n):
            pillar = self.pillar_ref[:, i * self.chunk : (i + 1) * self.chunk]
            self.hot_s[i] = jnp.where(self.cell_ids() == pillar, 1.0, 0.0).astype(jnp.bfloat16)

    def tile_part(self, c, r, k):
        cells = self.pool_s.shape[0] // (self.cols * self.reps)
        start = (c * self.reps + r) * cells + k * self.edge
        return pl.ds(pl.multiple_of(start, 8), self.edge)

    def near3(self, w, k):
        c = self.c if w else 1 - self.c
        return self.sent(
            "near3", w * self.pieces + k, self.pool_s.at[self.tile_part(c, 1 - self.r, k)],
            self.n3_s.at[w, k], self.mate,
        )

    def far3(self, k):
        return self.sent("far3", k, self.s3_s.at[k], self.f3_s.at[k], self.peer)

    def inner(self):
        start = jnp.where(self.r == 0, self.pieces * self.edge, self.edge)
        src = self.tile_s.at[pl.ds(pl.multiple_of(start, 8), self.edge)]
        return self.sent("halo", 0, src, self.h_s.at[0], self.mate)

    def outer(self):
        start = jnp.where(self.r == 0, self.edge, self.pieces * self.edge)
        src = self.tile_s.at[pl.ds(pl.multiple_of(start, 8), self.edge)]
        return self.sent("halo", 1, src, self.h_s.at[1], self.partner)

    def scatter(self):
        order = [0, self.pieces - 1] + list(range(1, self.pieces - 1))
        for w in range(2):
            for k in order:
                self.near3(w, k).start()
        for k in order:
            self.near3(0, k).wait_recv()
            self.s3_s[k] = self.pool_s[self.tile_part(1 - self.c, self.r, k)] + self.n3_s[0, k]
            self.far3(k).start()
        for at, k in enumerate(order):
            self.near3(1, k).wait_recv()
            self.far3(k).wait_recv()
            own = self.pool_s[self.tile_part(self.c, self.r, k)] + self.n3_s[1, k]
            self.tile_s[pl.ds((k + 1) * self.edge, self.edge)] = own + self.f3_s[k]
            if at == 1:
                self.inner().start()
                self.outer().start()
        self.inner().wait()
        self.outer().wait()
        wrapped = jnp.where(self.r == 0, self.t == 0, self.t == self.ntok - 1)
        beyond = jnp.where(wrapped, 0.0, self.h_s[1])
        within = self.h_s[0]
        self.tile_s[: self.edge] = jnp.where(self.r == 0, beyond, within)
        self.tile_s[(self.pieces + 1) * self.edge :] = jnp.where(self.r == 0, within, beyond)

    def raster(self):
        wide = TC + 2 * HALO
        rows = self.tile_s.shape[0] // wide
        pad = (self.flat_s.shape[0] - rows * wide) // 2
        self.flat_s[:pad] = jnp.zeros((pad, self.width), jnp.float32)
        self.flat_s[pad + rows * wide :] = jnp.zeros((pad, self.width), jnp.float32)
        for l in range(2):
            old = pl.ds(l * wide, (rows - 2 * l) * wide)
            start, count = (l + 1) * wide, (rows - 2 * l - 2) * wide
            cells = self.tile_s[old]
            square = jnp.mean(cells * cells, axis=-1, keepdims=True)
            gain = self.rg_ref[pl.ds(l, 1)]
            self.flat_s[pl.ds(pad + l * wide, (rows - 2 * l) * wide)] = (
                cells * lax.rsqrt(square + EPSILON) * gain
            )
            mixed = jnp.zeros((count, self.width), jnp.float32)
            for a in range(3):
                for b in range(3):
                    shift = pad + start + (a - 1) * wide + b - 1
                    mixed = mixed + self.flat_s[pl.ds(shift, count)] * self.dw_ref[a, b, pl.ds(l, 1)]
            both = dot3(split(mixed), (self.pw_s[0, l], self.pw_s[1, l]))
            centre = self.tile_s[pl.ds(start, count)]
            result = centre + both[:, : self.width] * jax.nn.sigmoid(both[:, self.width :])
            if l == 0:
                p = lax.broadcasted_iota(jnp.int32, (count, 1), 0) + start
                row = ((p.astype(jnp.float32) + 0.5) * (1.0 / wide)).astype(jnp.int32)
                y = (self.t * self.reps + self.r) * (rows - 2 * HALO) - HALO + row
                x = self.c * TC - HALO + (p - row * wide)
                inside = (y >= 0) & (y < TR * self.ntok) & (x >= 0) & (x < TC * self.cols)
                result = jnp.where(inside, result, 0.0)
            self.tile_s[pl.ds(start, count)] = result
        for y in range(rows - 2 * HALO):
            self.out_ref[y] = self.tile_s[pl.ds((y + HALO) * wide + HALO, TC)]

    def body(self, first):
        self.pieces, self.edge = self.s3_s.shape[:2]
        self.move(first)
        self.run([(1, self.finish), (2, self.reduce_near), (7, self.feed), (5, self.reduce_far)])
        self.scatter()
        self.raster()
        for copy in (self.near, self.far, self.share):
            for i in range(self.n):
                copy(i).wait_send()
        for j in range(self.cap):
            for e in range(self.ntok):
                if e:
                    self.along(e, j).wait_send()
                for copy in (self.across, self.over, self.relay):
                    copy(e, j).wait_send()
        for k in range(self.pieces):
            self.near3(0, k).wait_send()
            self.near3(1, k).wait_send()
            self.far3(k).wait_send()


def capacity_of(count, peers):
    return max(2, (count + peers - 4) // (peers - 1))


def both_layers(tokens, dest_device, dest_slot, cap, pillar, raster_weights, weights, collective_id):
    w_qkv, w_out, w_up, w_down, attn_gain, mlp_gain = weights
    depth_weight, point_weight, raster_gain = raster_weights
    cols, reps, ntok = lax.axis_size("col"), lax.axis_size("rep"), lax.axis_size("tok")
    rows, lanes = tokens.shape
    width, hidden, count = w_qkv.shape[-2], w_up.shape[-1], dest_device.shape[0]
    block, heads, chunk = rows // count, lanes // HD, min(256, rows)
    n = rows // chunk
    wide, rep_rows = TC + 2 * HALO, TR // reps
    edge, pieces = HALO * wide, rep_rows // HALO
    tile = (rep_rows + 2 * HALO) * wide
    dma, f32, b16 = pltpu.SemaphoreType.DMA, jnp.float32, jnp.bfloat16
    places = {True: pl.BlockSpec(memory_space=pltpu.VMEM), False: pl.BlockSpec(memory_space=pl.ANY)}
    inputs = dict(
        tokens_ref=tokens, wqkv_ref=w_qkv, wo_ref=w_out, wu_ref=w_up, wd_ref=w_down, pw_ref=point_weight,
        ga_ref=attn_gain, gm_ref=mlp_gain, dd_ref=dest_device[None, :], ds_ref=dest_slot[None, :],
        pillar_ref=pillar[None, :], dw_ref=jnp.transpose(depth_weight, (1, 2, 0, 3)), rg_ref=raster_gain,
    )
    far_away = ("tokens_ref", "wqkv_ref", "wo_ref", "wu_ref", "wd_ref", "pw_ref")
    floats = dict(
        wqkv_f=(2, 3, width, lanes), wo_f=(2, lanes, width), wu_f=(2, width, hidden),
        wd_f=(2, hidden, width), att_s=(2, chunk, lanes), p_s=(rows, width), n1_s=(rows // 2, width),
        s1_s=(rows // 2, width), f1_s=(rows // 2, width), a_s=(rows, width),
        g0_s=(cols * reps, rows, lanes), m_s=(reps, cols, rows, lanes), n2_s=(cols, rows, lanes),
        s2_s=(rows, lanes), f2_s=(rows, lanes), code_s=(8, 128), arrived_s=(ntok, 8, 128),
        y_s=(count, block, lanes), o_s=(ntok, cap, block, lanes),
        g_s=(ntok, cols * reps, cap, block, lanes), raw_s=(3, ntok * cap, block, lanes),
        pw_f=point_weight.shape, pool_s=(cols * reps * rep_rows * wide, width),
        n3_s=(2, pieces, edge, width), s3_s=(pieces, edge, width), f3_s=(pieces, edge, width),
        h_s=(2, edge, width), tile_s=(tile, width), flat_s=(tile + 16, width),
    )
    halves = dict(
        wqkv_s=(2, 2, 3, width, lanes), wo_s=(2, 2, lanes, width), wu_s=(2, 2, width, hidden),
        wd_s=(2, 2, hidden, width), q_s=(2, rows, 2 * lanes), k_s=(2, rows, 2 * lanes),
        v_s=(2, rows, 2 * lanes), pw_s=(2,) + point_weight.shape,
        hot_s=(n, cols * reps * rep_rows * wide, chunk),
    )
    scratch = {name: pltpu.VMEM(shape, f32) for name, shape in floats.items()}
    scratch.update({name: pltpu.VMEM(shape, b16) for name, shape in halves.items()})
    for name in ("index", "source"):
        scratch[name + "_v"] = pltpu.VMEM((1, 128), jnp.int32)
        scratch[name + "_m"] = pltpu.SMEM((1, 128), jnp.int32)
    for kind in ("near", "far", "share", "near2", "far2", "across", "over", "relay"):
        scratch[kind + "_sem0"] = dma((2, n))
    scratch["code_sem0"] = dma((2, ntok))
    for kind in ("near", "far", "share"):
        scratch[kind + "_sem1"] = dma((2, n))
    for kind in ("along", "across", "over", "relay"):
        scratch[kind + "_sem1"] = dma((2, ntok * cap))
    scratch["near3_sem1"] = dma((2, 2 * pieces))
    scratch["far3_sem1"] = dma((2, pieces))
    scratch["halo_sem1"] = dma((2, 2))
    scratch["wsem"], scratch["tsem"] = dma((2, 4)), dma((4,))
    names = list(inputs) + ["out_ref"] + list(scratch)

    def kernel(*refs):
        refs = dict(zip(names, refs))
        first, second = First(0, refs, heads, chunk), Second(1, refs, heads, chunk)
        step = jnp.where(first.r == 0, ntok - 1, 1)
        second.partner = {"tok": lax.rem(first.t + step, ntok), "rep": 1 - first.r}
        first.load_weights()
        second.load_weights()
        second.load_points()
        greet([first.mate, first.peer, second.partner] + first.peers)
        first.body(second)
        second.body(first)

    return pl.pallas_call(
        kernel,
        out_shape=jax.ShapeDtypeStruct((rep_rows, TC, width), f32),
        in_specs=[places[name not in far_away] for name in inputs],
        out_specs=places[True],
        scratch_shapes=list(scratch.values()),
        compiler_params=pltpu.CompilerParams(
            collective_id=collective_id, has_side_effects=True, vmem_limit_bytes=VMEM_LIMIT
        ),
        name="layers",
    )(*inputs.values())


HALO = 2


def routes(dest_device, dest_slot):
    count = dest_device.shape[0]
    peers = lax.axis_size("tok")
    capacity = capacity_of(count, peers)
    order = jnp.arange(count, dtype=jnp.int32)
    earlier = (dest_device[:, None] == dest_device[None, :]) & (order[None, :] < order[:, None])
    place = dest_device * capacity + jnp.sum(earlier.astype(jnp.int32), axis=1)
    chosen = jnp.arange(peers * capacity, dtype=jnp.int32)[:, None] == place[None, :]
    index = jnp.sum(jnp.where(chosen, order[None, :], 0), axis=1)
    code = jnp.sum(jnp.where(chosen, dest_slot[None, :] + 1, 0), axis=1)
    code = jnp.pad(code.reshape(peers, capacity), ((0, 0), (0, 128 - capacity)))
    code = jnp.broadcast_to(code[:, None, :], (peers, 8, 128)).astype(jnp.float32)
    return index, code, capacity


def places(arrived, capacity, order):
    held = arrived[:, 0, :capacity].reshape(-1).astype(jnp.int32)
    found = held[None, :] == order[:, None] + 1
    return jnp.sum(jnp.where(found, jnp.arange(held.shape[0], dtype=jnp.int32)[None, :], 0), axis=1)


def raster_cells(extended, depth_weight, point_weight, gain_row):
    row_count = extended.shape[0] - 2
    col_count = extended.shape[1] - 2
    channels = extended.shape[2]
    normed = (
        extended
        * lax.rsqrt(jnp.mean(extended * extended, axis=-1, keepdims=True) + EPSILON)
        * gain_row
    )
    mixed = jnp.zeros((row_count, col_count, channels), jnp.float32)
    for a in range(3):
        for b in range(3):
            mixed = mixed + normed[a : a + row_count, b : b + col_count] * depth_weight[a, b]
    combined = matmul(mixed.reshape(row_count * col_count, channels), point_weight)
    combined = combined.reshape(row_count, col_count, 2 * channels)
    centre = extended[1:-1, 1:-1]
    return centre + combined[..., :channels] * jax.nn.sigmoid(combined[..., channels:])


def extended_cells(tok, members, rep_rows, full_width):
    cols, reps = members
    tile = []
    for col in range(cols):
        for rep in range(reps):
            y = rep * rep_rows - HALO + jnp.arange(rep_rows + 2 * HALO, dtype=jnp.int32)[:, None]
            x = col * TC - HALO + jnp.arange(TC + 2 * HALO, dtype=jnp.int32)[None, :]
            good = (y >= 0) & (y < TR) & (x >= 0) & (x < full_width)
            tile.append(jnp.where(good, (tok * TR + y) * full_width + x, -2).reshape(-1))
    return jnp.concatenate(tile)


def pool(partial, pillar, cells):
    onehot = (cells[:, None] == pillar[None, :]).astype(jnp.float32)
    return matmul(onehot, partial)


def exchange_rows(tile, ntok, reps):
    count = ntok * reps
    rep = lax.axis_index("rep")
    forward = [(i, i + 1) for i in range(count - 1)]
    backward = [(i + 1, i) for i in range(count - 1)]
    above = lax.ppermute(tile[-2 * HALO : -HALO], ("tok", "rep"), forward)
    below = lax.ppermute(tile[HALO : 2 * HALO], ("tok", "rep"), backward)
    above = jnp.where(rep == 0, above, tile[:HALO])
    below = jnp.where(rep == reps - 1, below, tile[-HALO:])
    return jnp.concatenate([above, tile[HALO:-HALO], below], axis=0)


def on_device(
    tokens,
    w_qkv,
    w_out,
    w_up,
    w_down,
    attn_gain,
    mlp_gain,
    dest_device,
    dest_slot,
    pillar,
    depth_weight,
    point_weight,
    raster_gain,
):
    members = (lax.axis_size("col"), lax.axis_size("rep"))
    group = members[0] * members[1]
    ntok = lax.axis_size("tok")
    block_count = dest_device.shape[0]
    order = jnp.arange(block_count, dtype=jnp.int32)
    index, codes, capacity = routes(dest_device, dest_slot)
    width = tokens.shape[1]
    weights = (w_qkv, w_out, w_up, w_down, attn_gain, mlp_gain)
    whole = (2 * members[1] * HALO * (TC + 2 * HALO)) % 8 == 0 and TR % (members[1] * HALO) == 0
    if members == (2, 2) and ntok > 1 and tokens.shape[0] == PATCH and whole and ntok * capacity <= 128:
        raster_weights = (depth_weight, point_weight, raster_gain)
        return both_layers(tokens, dest_device, dest_slot, capacity, pillar, raster_weights, weights, 1)
    blocks = gather(tokens, 1).reshape(1, group, block_count, -1, width)
    stream = attention_layer(blocks, order, 0, w_qkv, w_out, attn_gain, 2)
    share = scatter(mlp_partial(stream, 0, w_up, w_down, mlp_gain, group), 3)
    outgoing = pick(share.reshape(block_count, -1, width), index)
    outgoing = outgoing.reshape(ntok, -1, width)
    moved, arrived = move(outgoing, codes, 4)
    blocks = moved.reshape(ntok, group, capacity, -1, width)
    source = places(arrived, capacity, order)
    stream = attention_layer(blocks, source, 1, w_qkv, w_out, attn_gain, 5)
    partial = mlp_partial(stream, 1, w_up, w_down, mlp_gain, 1)[0]

    rep_rows = TR // members[1]
    full_width = TC * members[0]
    cells = extended_cells(lax.axis_index("tok"), members, rep_rows, full_width)
    pooled = pool(partial, pillar, cells)
    parts = pooled.reshape(group, -1, pooled.shape[1])
    edge = HALO * (TC + 2 * HALO)
    inside_kernel = members[0] > 1 and members[1] == 2 and ntok > 1 and edge % 8 == 0
    tile = scatter(parts, 6, edge if inside_kernel else 0)
    tile = tile.reshape(rep_rows + 2 * HALO, TC + 2 * HALO, -1)
    if not inside_kernel:
        tile = exchange_rows(tile, ntok, members[1])
    first = raster_cells(tile, depth_weight[0], point_weight[0], raster_gain[0])
    y = lax.axis_index(("tok", "rep")) * rep_rows - 1 + jnp.arange(rep_rows + 2)[:, None, None]
    x = lax.axis_index("col") * TC - 1 + jnp.arange(TC + 2)[None, :, None]
    inside = (y >= 0) & (y < TR * ntok) & (x >= 0) & (x < full_width)
    first = jnp.where(inside, first, 0.0)
    return raster_cells(first, depth_weight[1], point_weight[1], raster_gain[1])


def solution(mesh):
    placed = (
        P(("scene", "tok"), ("col", "rep")),
        P(None, None, None, ("col", "rep")),
        P(None, ("col", "rep"), None),
        P(None, None, ("col", "rep")),
        P(None, ("col", "rep"), None),
        P(),
        P(),
        P(("scene", "tok")),
        P(("scene", "tok")),
        P(("scene", "tok")),
        P(),
        P(),
        P(),
    )
    return jax.shard_map(
        on_device,
        mesh=mesh,
        in_specs=placed,
        out_specs=P(("scene", "tok", "rep"), "col", None),
        check_vma=False,
    )
```
